32 devices in a mesh: rep: 2 (over x), fsdp: 2 (over core), seq: 8 (over z, y).
Axes of the slice: x: 2, y: 2, z: 4, core: 2. Of those that a mesh axis runs over, the one named last changes fastest.
Arguments:
- tokens: bfloat16 [2, 4, 2048, 768], P(None, ('rep', 'fsdp'), 'seq'), may hold values from -6 to 6
- lengths: int32 [2, 4, 8], P(None, ('rep', 'fsdp')), may hold values from 1 to 1024, 2048 in all within a row
- ln1_gain: bfloat16 [768], P('fsdp'), may hold values from 0.099609375 to 1.8984375
- ln1_bias: bfloat16 [768], P('fsdp'), may hold values from -3 to 3
- qkv_weight: bfloat16 [768, 2304], P('fsdp'), may hold values from -0.21875 to 0.21875
- q_gain: bfloat16 [64], P('fsdp'), may hold values from 0.099609375 to 1.8984375
- k_gain: bfloat16 [64], P('fsdp'), may hold values from 0.099609375 to 1.8984375
- out_weight: bfloat16 [768, 768], P('fsdp'), may hold values from -1.75 to 1.75
- ln2_gain: bfloat16 [768], P('fsdp'), may hold values from 0.099609375 to 1.8984375
- ln2_bias: bfloat16 [768], P('fsdp'), may hold values from -3 to 3
- up_weight: bfloat16 [768, 3072], P('fsdp'), may hold values from -0.21875 to 0.21875
- down_weight: bfloat16 [3072, 768], P('fsdp'), may hold values from -0.109375 to 0.109375
- cotangent: bfloat16 [2, 4, 2048, 768], P(None, ('rep', 'fsdp'), 'seq'), may hold values from -6 to 6
Outputs:
- output: bfloat16 [2, 4, 2048, 768], P(None, ('rep', 'fsdp'), 'seq')
- grad_tokens: float32 [2, 4, 2048, 768], P(None, ('rep', 'fsdp'), 'seq')
- grad_ln1_gain: float32 [768], P('fsdp')
- grad_ln1_bias: float32 [768], P('fsdp')
- grad_qkv_weight: float32 [768, 2304], P('fsdp')
- grad_q_gain: float32 [64], P('fsdp')
- grad_k_gain: float32 [64], P('fsdp')
- grad_out_weight: float32 [768, 768], P('fsdp')
- grad_ln2_gain: float32 [768], P('fsdp')
- grad_ln2_bias: float32 [768], P('fsdp')
- grad_up_weight: float32 [768, 3072], P('fsdp')
- grad_down_weight: float32 [3072, 768], P('fsdp')
The draws below stay inside these ranges and needn't reach their ends.
Inputs may be any that keep to these rules, and one draw needn't show every extreme that they name: In each row the first 7 entries are the lengths of its pictures in order and the last one is the padding at the row's end; each row's entries sum to 2048, and each row's largest entry is 1024.
All inputs are finite; a program needn't handle non-finite values.
Results may differ from the reference program's by a relative error of at most 0.014.
Values may be sent and summed in bfloat16 or wider, within the bound.
No kernel may reach another device: no remote copies, remote signals or barrier semaphores. Data moves between devices by JAX's collectives and lax.ppermute only.
A program may use at most 320 MiB of HBM per device.

```python
import math
import jax
import jax.numpy as jnp
import numpy as np
from jax import lax

D = 768
H = 12
HD = 64
FF = 3072
ROW = 2048
PICS = 8
MOST = 1024
MB = 2
BATCH = 4


def block_scale(own_key, dims, shards, least, largest):
    factor_of = 1.0
    for axis_at, parts in shards:
        draws = jax.random.uniform(jax.random.fold_in(jax.random.fold_in(own_key, 6), axis_at), (parts,), jnp.float32, least / len(shards), largest / len(shards))
        factor_of = factor_of * jnp.repeat(jnp.exp(draws), dims[axis_at] // parts).reshape((-1,) + (1,) * (len(dims) - 1 - axis_at))
    return factor_of


def length_profile(number_of, total, bound, slope):
    loads = [(1 << 20) // math.isqrt(standing ** slope) + 1 for standing in range(2, number_of + 1)]
    rest, holding = total - bound - (number_of - 1), [1] * (number_of - 1)
    while rest > 0:
        free = [i for i in range(number_of - 1) if holding[i] < bound]
        mass, left = sum([loads[i] for i in free]), rest
        for i in free:
            addition = min(bound - holding[i], max(1, left * loads[i] // mass), rest)
            holding[i] = holding[i] + addition
            rest = rest - addition
    return np.array([bound] + holding)


def uneven_parts(rng, count, total, most, lean):
    if count == 2:
        one = jax.random.randint(rng, (), max(1, total - most), min(most, total - 1) + 1)
        return jnp.stack([one, total - one])
    tallies = jnp.asarray(length_profile(count, total, most, lean), jnp.int32)
    pairs = (count - 1) // 2
    source_of, taker = tallies[1:1 + 2 * pairs:2], tallies[2:2 + 2 * pairs:2]
    margin = jnp.minimum(source_of - 1, most - taker)
    shifted = jax.random.randint(jax.random.fold_in(rng, 1), (pairs,), 0, 1 << 20) % (margin + 1)
    tallies = tallies.at[1:1 + 2 * pairs:2].set(source_of - shifted).at[2:2 + 2 * pairs:2].set(taker + shifted)
    return tallies[jax.random.permutation(jax.random.fold_in(rng, 2), count)]


def gaussian(own_key, dims, deviation, limit, pieces=(), kind=jnp.bfloat16):
    values = deviation * jax.random.normal(own_key, dims, jnp.float32)
    if pieces:
        values = values * block_scale(own_key, dims, pieces, -0.22, 0.18)
    return jnp.clip(values, -limit, limit).astype(kind)


def setup_inputs(seed: int = 0) -> dict:
    arg_keys = jax.random.split(jax.random.key(seed), 14)
    tokens = gaussian(arg_keys[0], (MB, BATCH, ROW, D), 1.0, 6.0, ((1, 4), (2, 8)))
    lengths = jax.vmap(lambda own: uneven_parts(own, PICS, ROW, MOST, 1))(jax.random.split(arg_keys[1], MB * BATCH)).reshape((MB, BATCH, PICS)).astype(jnp.int32)
    ln1_gain = jnp.clip(1.0 + 0.18 * jax.random.normal(arg_keys[2], (D,), jnp.float32), 0.099609375, 1.8984375).astype(jnp.bfloat16)
    ln1_bias = gaussian(arg_keys[3], (D,), 0.5, 3.0, ((0, 2),))
    qkv_weight = gaussian(arg_keys[4], (D, 3 * D), D ** -0.5, 0.21875, ((0, 2),))
    q_gain = jnp.clip(1.0 + 0.18 * jax.random.normal(arg_keys[5], (HD,), jnp.float32), 0.099609375, 1.8984375).astype(jnp.bfloat16)
    k_gain = jnp.clip(1.0 + 0.18 * jax.random.normal(arg_keys[6], (HD,), jnp.float32), 0.099609375, 1.8984375).astype(jnp.bfloat16)
    out_weight = gaussian(arg_keys[7], (D, D), (D // 64) ** -0.5, 1.75, ((0, 2),))
    ln2_gain = jnp.clip(1.0 + 0.18 * jax.random.normal(arg_keys[8], (D,), jnp.float32), 0.099609375, 1.8984375).astype(jnp.bfloat16)
    ln2_bias = gaussian(arg_keys[9], (D,), 0.5, 3.0, ((0, 2),))
    up_weight = gaussian(arg_keys[10], (D, FF), D ** -0.5, 0.21875, ((0, 2),))
    down_weight = gaussian(arg_keys[11], (FF, D), FF ** -0.5, 0.109375, ((0, 2),))
    cotangent = gaussian(arg_keys[12], (MB, BATCH, ROW, D), 1.0, 6.0, ((1, 4), (2, 8)))
    return dict(tokens=tokens, lengths=lengths, ln1_gain=ln1_gain, ln1_bias=ln1_bias, qkv_weight=qkv_weight, q_gain=q_gain, k_gain=k_gain, out_weight=out_weight, ln2_gain=ln2_gain, ln2_bias=ln2_bias, up_weight=up_weight, down_weight=down_weight, cotangent=cotangent)


@jax.custom_vjp
def low(v):
    return lax.optimization_barrier(v.astype(jnp.bfloat16)).astype(jnp.float32)

@jax.custom_vjp
def low_back(v):
    return v

def low_keep(v):
    return (low(v), None)

def low_pass(kept, grad):
    return (grad,)

def back_keep(v):
    return (v, None)

def back_low(kept, grad):
    return (low(grad),)
low.defvjp(low_keep, low_pass)
low_back.defvjp(back_keep, back_low)
EPS = 1e-06
MASKED = -1000000000.0
HIGH = lax.Precision.HIGHEST

def layer_norm(values, gain, shift):
    center = lax.optimization_barrier(jnp.mean(values, axis=-1, keepdims=True))
    centred = values - center
    spread = lax.optimization_barrier(jnp.mean(centred * centred, axis=-1, keepdims=True))
    return centred * lax.rsqrt(spread + EPS) * gain + shift

def picture_ids(lengths_row):
    bounds = jnp.cumsum(lengths_row).astype(jnp.int32)
    places = jnp.arange(ROW, dtype=jnp.int32)
    ident = lax.optimization_barrier(jnp.sum((places[:, None] >= bounds[None, :-1]).astype(jnp.int32), axis=1)).astype(jnp.int32)
    return jnp.where(ident == PICS - 1, -1, ident).astype(jnp.int32)

def row_forward(x_row, params, same, valid):
    ln1_gain, ln1_bias, qkv_weight, q_gain, k_gain, out_weight, ln2_gain, ln2_bias, up_weight, down_weight = params
    scale = HD ** (-0.5)
    first = low(layer_norm(x_row, ln1_gain, ln1_bias))
    qkv = low_back(jnp.dot(first, qkv_weight, precision=HIGH))
    q_raw = qkv[:, :D].reshape(ROW, H, HD)
    k_raw = qkv[:, D:2 * D].reshape(ROW, H, HD)
    v_raw = qkv[:, 2 * D:].reshape(ROW, H, HD)
    queries = low(layer_norm(q_raw, q_gain, 0.0))
    keys = low(layer_norm(k_raw, k_gain, 0.0))
    values = low(v_raw)

    def one_head(inputs):
        q_head, k_head, v_head = inputs
        scores = low_back(jnp.dot(q_head, k_head.T, precision=HIGH) * scale)
        scores = jnp.where(same, scores, MASKED)
        top = lax.optimization_barrier(jnp.max(scores, axis=-1, keepdims=True))
        expo = jnp.exp(scores - top)
        probs = expo / lax.optimization_barrier(jnp.sum(expo, axis=-1, keepdims=True))
        return jnp.dot(low(probs), v_head, precision=HIGH)
    heads = lax.map(jax.checkpoint(one_head), (jnp.swapaxes(queries, 0, 1), jnp.swapaxes(keys, 0, 1), jnp.swapaxes(values, 0, 1)))
    attn = jnp.swapaxes(heads, 0, 1).reshape(ROW, D) * valid[:, None]
    attn = low_back(low(attn))
    middle = x_row + low_back(jnp.dot(attn, out_weight, precision=HIGH))
    second = low(layer_norm(middle, ln2_gain, ln2_bias))
    upper = low_back(jnp.dot(second, up_weight, precision=HIGH))
    active = low(jax.nn.gelu(upper, approximate=False))
    return middle + jnp.dot(active, down_weight, precision=HIGH)

def reference(tokens, lengths, ln1_gain, ln1_bias, qkv_weight, q_gain, k_gain, out_weight, ln2_gain, ln2_bias, up_weight, down_weight, cotangent):
    params = (ln1_gain.astype(jnp.float32), ln1_bias.astype(jnp.float32), qkv_weight.astype(jnp.float32), q_gain.astype(jnp.float32), k_gain.astype(jnp.float32), out_weight.astype(jnp.float32), ln2_gain.astype(jnp.float32), ln2_bias.astype(jnp.float32), up_weight.astype(jnp.float32), down_weight.astype(jnp.float32))
    rows_x = tokens.reshape(MB * BATCH, ROW, D)
    rows_len = lengths.reshape(MB * BATCH, PICS)
    rows_dy = cotangent.reshape(MB * BATCH, ROW, D)
    zeros = tuple((jnp.zeros(member.shape, jnp.float32) for member in params))

    def step(totals, inputs):
        x_row, len_row, dy_row = inputs
        ident = picture_ids(len_row)
        same = (ident[:, None] == ident[None, :]) & (ident[None, :] >= 0)
        valid = (ident >= 0).astype(jnp.float32)

        def forward(x_value, param_value):
            return row_forward(x_value, param_value, same, valid)
        result, pullback = jax.vjp(forward, x_row.astype(jnp.float32), params)
        grad_x, grad_params = pullback(dy_row.astype(jnp.float32))
        totals = tuple((acc + part for acc, part in zip(totals, grad_params)))
        return (totals, (result.astype(jnp.bfloat16), grad_x.astype(jnp.float32)))
    totals, (results, grads_x) = lax.scan(step, zeros, (rows_x, rows_len, rows_dy))
    output = results.reshape(MB, BATCH, ROW, D)
    grad_tokens = grads_x.reshape(MB, BATCH, ROW, D)
    return (output, grad_tokens, totals[0], totals[1], totals[2], totals[3], totals[4], totals[5], totals[6], totals[7], totals[8], totals[9])
```

```python
import functools

import jax
import jax.numpy as jnp
from jax import lax
from jax.experimental import pallas as pl
from jax.experimental.pallas import tpu as pltpu
from jax.sharding import PartitionSpec as P

H = 12
EPS = 1e-06
LOG2E = 1.4426950408889634
SHIFT = 512.0
BLK = 256
NN = (((1,), (0,)), ((), ()))
NT = (((1,), (1,)), ((), ()))
TN = (((0,), (0,)), ((), ()))
F32 = jnp.float32
BF16 = jnp.bfloat16


def mm(a, b, dims=NN):
    return lax.dot_general(a, b, dims, preferred_element_type=F32)


def params(**kw):
    return pltpu.CompilerParams(vmem_limit_bytes=60 * 1024 * 1024, **kw)


def norm_rows(v):
    center = jnp.mean(v, axis=-1, keepdims=True)
    centred = v - center
    inv = lax.rsqrt(jnp.mean(centred * centred, axis=-1, keepdims=True) + EPS)
    return centred * inv, inv


def norm_cols(v):
    center = jnp.mean(v, axis=0, keepdims=True)
    centred = v - center
    inv = lax.rsqrt(jnp.mean(centred * centred, axis=0, keepdims=True) + EPS)
    return centred * inv, inv


def bounds_of(len_ref, row):
    out = []
    total = jnp.int32(0)
    for j in range(len_ref.shape[1] - 1):
        total = total + len_ref[row, j]
        out.append(total)
    return out


def qkv_body(heads, hd, meta, len_ref, *refs):
    xs = refs[:8]
    w_ref, g_ref, b_ref, gq_ref, gk_ref = refs[8:13]
    qt_ref, ka_ref, kt_ref, v_ref, vt_ref, x_ref = refs[13:]
    wid = heads * hd
    spot, row = meta[0], meta[1]
    bounds = bounds_of(len_ref, row)
    for s in range(8):
        c = jnp.bitwise_xor(spot, s)
        cols = pl.ds(pl.multiple_of(c * BLK, BLK), BLK)
        x = xs[s][...]
        x_ref[cols, :] = x
        hat, _ = norm_rows(x.astype(F32))
        first = (hat * g_ref[...] + b_ref[...]).astype(BF16)
        qkv = mm(w_ref[...], first, NT)
        place = c * BLK + lax.broadcasted_iota(jnp.int32, (8, BLK), 1)
        ident = jnp.zeros((8, BLK), jnp.int32)
        place_k = c * BLK + lax.broadcasted_iota(jnp.int32, (BLK, 128), 0)
        ident_k = jnp.zeros((BLK, 128), jnp.int32)
        for bound in bounds:
            ident = ident + (place >= bound).astype(jnp.int32)
            ident_k = ident_k + (place_k >= bound).astype(jnp.int32)
        which = lax.broadcasted_iota(jnp.int32, (8, BLK), 0)
        hot = jnp.where((ident == which) & (which < len(bounds)), 16.0, 0.0)
        hot = jnp.concatenate([hot, jnp.zeros((hd - 8, BLK), F32)], axis=0)
        lane = lax.broadcasted_iota(jnp.int32, (BLK, 128), 1) - hd
        hot_k = jnp.where((ident_k == lane) & (lane < len(bounds)), SHIFT / 16.0, 0.0)
        for h in range(heads):
            q, _ = norm_cols(qkv[h * hd : (h + 1) * hd])
            k, _ = norm_cols(qkv[wid + h * hd : wid + (h + 1) * hd])
            q = (q * gq_ref[...]).astype(BF16).astype(F32) * (hd**-0.5)
            k = k * gk_ref[...]
            v = qkv[2 * wid + h * hd : 2 * wid + (h + 1) * hd]
            qt_ref[h, :, cols] = jnp.concatenate([q, hot], axis=0).astype(BF16)
            kt_ref[h, :, cols] = k.astype(BF16)
            vt_ref[h, :, cols] = v.astype(BF16)
            both = jnp.transpose(jnp.concatenate([k, v], axis=0))
            ka_ref[h, cols, :] = jnp.where(lane < 0, both, hot_k).astype(BF16)
            v_ref[h, cols, :] = both[:, hd:].astype(BF16)


def make_qkv(meta, lengths, slots, w_t, gain, bias, gq, gk, heads, hd):
    length = 8 * slots[0].shape[0]
    width = slots[0].shape[1]
    smem = pl.BlockSpec(memory_space=pltpu.SMEM)
    vmem = pl.BlockSpec(memory_space=pltpu.VMEM)
    return pl.pallas_call(
        functools.partial(qkv_body, heads, hd),
        out_shape=(
            jax.ShapeDtypeStruct((heads, 2 * hd, length), BF16),
            jax.ShapeDtypeStruct((heads, length, 2 * hd), BF16),
            jax.ShapeDtypeStruct((heads, hd, length), BF16),
            jax.ShapeDtypeStruct((heads, length, hd), BF16),
            jax.ShapeDtypeStruct((heads, hd, length), BF16),
            jax.ShapeDtypeStruct((length, width), BF16),
        ),
        in_specs=[smem, smem] + [vmem] * 13,
        out_specs=(vmem,) * 6,
        compiler_params=params(),
        name="qkv_forward",
    )(meta, lengths, *slots, w_t, gain, bias, gq, gk)


def block_range(bounds, i):
    first = i * BLK
    last = first + BLK - 1
    lo = jnp.int32(0)
    hi = bounds[-1]
    for bound in bounds:
        lo = jnp.where(first >= bound, bound, lo)
    for bound in bounds[::-1]:
        hi = jnp.where(last < bound, bound, hi)
    lo_b = lo // BLK
    hi_b = (hi + BLK - 1) // BLK
    return lo_b, jnp.where(first >= bounds[-1], lo_b, hi_b)


def attend_body(heads, hd, meta, len_ref, qt_ref, ka_ref, vt_ref, o_ref, of_ref, ls_ref):
    i = pl.program_id(0)
    bounds = bounds_of(len_ref, meta[1])
    lo, hi = block_range(bounds, i)

    def step(b, carry):
        rows = pl.ds(pl.multiple_of(b * BLK, BLK), BLK)
        out = []
        for h in range(heads):
            acc, total = carry[h]
            scores = mm(ka_ref[h, rows, :], qt_ref[h])
            expo = jnp.exp2(scores * LOG2E - SHIFT * LOG2E)
            total = total + jnp.sum(expo.reshape(BLK // 8, 8, BLK), axis=0)
            acc = acc + mm(vt_ref[h, :, rows], expo.astype(BF16))
            out.append((acc, total))
        return tuple(out)

    init = tuple((jnp.zeros((hd, BLK), F32), jnp.zeros((8, BLK), F32)) for _ in range(heads))
    done = lax.fori_loop(lo, hi, step, init)
    for h in range(heads):
        acc, total = done[h]
        total = jnp.sum(total, axis=0, keepdims=True)
        live = total > 0.0
        safe = jnp.where(live, total, 1.0)
        out = jnp.where(live, acc * (1.0 / safe), 0.0)
        o_ref[0, h * hd : (h + 1) * hd, :] = out.astype(BF16)
        of_ref[h] = out
        ls_ref[h] = jnp.log2(safe) + SHIFT * LOG2E


def attend(meta, lengths, qt, ka, vt, heads, hd):
    length = qt.shape[2]
    blocks = length // BLK
    smem = pl.BlockSpec(memory_space=pltpu.SMEM)
    return pl.pallas_call(
        functools.partial(attend_body, heads, hd),
        grid=(blocks,),
        out_shape=(
            jax.ShapeDtypeStruct((blocks, heads * hd, BLK), BF16),
            jax.ShapeDtypeStruct((heads, hd, length), F32),
            jax.ShapeDtypeStruct((heads, 1, length), F32),
        ),
        in_specs=[
            smem,
            smem,
            pl.BlockSpec((heads, 2 * hd, BLK), lambda i: (0, 0, i)),
            pl.BlockSpec((heads, length, 2 * hd), lambda i: (0, 0, 0)),
            pl.BlockSpec((heads, hd, length), lambda i: (0, 0, 0)),
        ],
        out_specs=(
            pl.BlockSpec((1, heads * hd, BLK), lambda i: (i, 0, 0)),
            pl.BlockSpec((heads, hd, BLK), lambda i: (0, 0, i)),
            pl.BlockSpec((heads, 1, BLK), lambda i: (0, 0, i)),
        ),
        compiler_params=params(),
        name="attention_forward",
    )(meta, lengths, qt, ka, vt)


def attend_back_body(
    heads, hd, meta, len_ref, qt_ref, ka_ref, kt_ref, v_ref, of_ref, ls_ref, go_ref, dq_ref, dk_ref, dv_ref
):
    i = pl.program_id(0)
    bounds = bounds_of(len_ref, meta[1])
    lo, hi = block_range(bounds, i)

    @pl.when(i == 0)
    def _():
        dk_ref[...] = jnp.zeros_like(dk_ref)
        dv_ref[...] = jnp.zeros_like(dv_ref)

    inner = []
    for h in range(heads):
        go = go_ref[0, h * hd : (h + 1) * hd, :].astype(F32)
        inner.append(jnp.sum(go * of_ref[h], axis=0, keepdims=True))

    def step(b, carry):
        rows = pl.ds(pl.multiple_of(b * BLK, BLK), BLK)
        out = []
        for h in range(heads):
            go = go_ref[0, h * hd : (h + 1) * hd, :]
            qt = qt_ref[h]
            scores = mm(ka_ref[h, rows, :], qt)
            probs = jnp.exp2(scores * LOG2E - ls_ref[h])
            grad_probs = mm(v_ref[h, rows, :], go)
            grad_scores = (probs * (grad_probs - inner[h])).astype(BF16)
            dv_ref[h, :, rows] += mm(go, probs.astype(BF16), NT)
            dk_ref[h, :, rows] += mm(qt[:hd], grad_scores, NT)
            out.append(carry[h] + mm(kt_ref[h, :, rows], grad_scores))
        return tuple(out)

    done = lax.fori_loop(lo, hi, step, tuple(jnp.zeros((hd, BLK), F32) for _ in range(heads)))
    for h in range(heads):
        dq_ref[h] = done[h] * (hd**-0.5)


def attend_back(meta, lengths, qt, ka, kt, v, of, ls, go, heads, hd):
    length = qt.shape[2]
    blocks = length // BLK
    smem = pl.BlockSpec(memory_space=pltpu.SMEM)
    whole = lambda *shape: pl.BlockSpec(shape, lambda i: (0,) * len(shape))
    return pl.pallas_call(
        functools.partial(attend_back_body, heads, hd),
        grid=(blocks,),
        out_shape=tuple(jax.ShapeDtypeStruct((heads, hd, length), F32) for _ in range(3)),
        in_specs=[
            smem,
            smem,
            pl.BlockSpec((heads, 2 * hd, BLK), lambda i: (0, 0, i)),
            whole(heads, length, 2 * hd),
            whole(heads, hd, length),
            whole(heads, length, hd),
            pl.BlockSpec((heads, hd, BLK), lambda i: (0, 0, i)),
            pl.BlockSpec((heads, 1, BLK), lambda i: (0, 0, i)),
            pl.BlockSpec((1, heads * hd, BLK), lambda i: (i, 0, 0)),
        ],
        out_specs=(
            pl.BlockSpec((heads, hd, BLK), lambda i: (0, 0, i)),
            whole(heads, hd, length),
            whole(heads, hd, length),
        ),
        compiler_params=params(),
        name="attention_backward",
    )(meta, lengths, qt, ka, kt, v, of, ls, go)


def qkv_back_body(
    heads, hd, meta, x_ref, dq_ref, dk_ref, dv_ref, w_ref, g_ref, b_ref, gq_ref, gk_ref,
    da_ref, db_ref, dw_ref, vec_ref, gain_ref, acc_ref,
):
    i = pl.program_id(0)
    wid = heads * hd

    @pl.when(i == 0)
    def _():
        acc_ref[...] = jnp.zeros_like(acc_ref)
        vec_ref[...] = jnp.zeros_like(vec_ref)
        gain_ref[...] = jnp.zeros_like(gain_ref)

    hat, _ = norm_rows(x_ref[...].astype(F32))
    first = (hat * g_ref[...] + b_ref[...]).astype(BF16)
    qk = mm(w_ref[: 2 * wid, :], first, NT)
    pieces = []
    for at, gain, grad in ((0, gq_ref, dq_ref), (1, gk_ref, dk_ref)):
        for h in range(heads):
            unit, inv = norm_cols(qk[at * wid + h * hd : at * wid + (h + 1) * hd])
            gy = grad[h]
            gain_ref[at] += gy * unit
            e = gy * gain[...]
            pieces.append(
                inv
                * (
                    e
                    - jnp.mean(e, axis=0, keepdims=True)
                    - unit * jnp.mean(e * unit, axis=0, keepdims=True)
                )
            )
    for h in range(heads):
        pieces.append(dv_ref[h])
    grad = jnp.concatenate(pieces, axis=0).astype(BF16)
    acc_ref[...] += mm(grad, first)
    back = mm(grad, w_ref[...], TN)
    vec_ref[0] += jnp.sum((back * hat).reshape(BLK // 8, 8, -1), axis=0)
    vec_ref[1] += jnp.sum(back.reshape(BLK // 8, 8, -1), axis=0)
    half = back.shape[1] // 2
    da_ref[0] = back[:, :half].astype(BF16)
    db_ref[0] = back[:, half:].astype(BF16)

    @pl.when(i == pl.num_programs(0) - 1)
    def _():
        dw_ref[...] = acc_ref[...].astype(BF16)


def qkv_back(meta, x, dq, dk, dv, w_t, gain, bias, gq, gk, heads, hd):
    length, width = x.shape
    blocks = length // BLK
    whole = lambda *shape: pl.BlockSpec(shape, lambda i, m: (0,) * len(shape))
    part = pl.BlockSpec((heads, hd, BLK), lambda i, m: (0, 0, i))
    grads = pl.BlockSpec((1, BLK, width // 2), lambda i, m: (jnp.bitwise_xor(i, m[0]), 0, 0))
    return pl.pallas_call(
        functools.partial(qkv_back_body, heads, hd),
        grid_spec=pltpu.PrefetchScalarGridSpec(
            num_scalar_prefetch=1,
            grid=(blocks,),
            in_specs=[
                pl.BlockSpec((BLK, width), lambda i, m: (i, 0)),
                part,
                part,
                part,
                whole(*w_t.shape),
                whole(1, width),
                whole(1, width),
                whole(hd, 1),
                whole(hd, 1),
            ],
            out_specs=(
                grads,
                grads,
                whole(*w_t.shape),
                whole(2, 8, width),
                whole(2, hd, BLK),
            ),
            scratch_shapes=[pltpu.VMEM(w_t.shape, F32)],
        ),
        out_shape=(
            jax.ShapeDtypeStruct((blocks, BLK, width // 2), BF16),
            jax.ShapeDtypeStruct((blocks, BLK, width // 2), BF16),
            jax.ShapeDtypeStruct(w_t.shape, BF16),
            jax.ShapeDtypeStruct((2, 8, width), F32),
            jax.ShapeDtypeStruct((2, hd, BLK), F32),
        ),
        compiler_params=params(),
        name="qkv_backward",
    )(meta, x, dq, dk, dv, w_t, gain, bias, gq, gk)


def gelu_pair(u):
    a = jnp.abs(u)
    t = 1.0 / (1.0 + (0.3275911 * 0.7071067811865476) * a)
    poly = 1.061405429 * t - 1.453152027
    poly = poly * t + 1.421413741
    poly = poly * t - 0.284496736
    poly = poly * t + 0.254829592
    bell = jnp.exp(-0.5 * (u * u))
    tail = (0.5 * poly) * t * bell
    cdf = jnp.where(u >= 0.0, 1.0 - tail, tail)
    return u * cdf, cdf + u * (bell * 0.3989422804014327)


def ffn(meta, attn_t, x, dy, valid, gain, bias, wo, wo_p, up, up_p, dn, dn_p):
    tokens, width = x.shape
    hidden = up.shape[1]
    fc = 512
    steps = hidden // fc
    near = steps // 2
    packs, _, lanes = attn_t.shape
    whole = lambda *shape: pl.BlockSpec(shape, lambda i, m: (0,) * len(shape))
    ups = pl.BlockSpec((width // 2, fc), lambda i, m: (0, lax.rem(m[2] * near + i, steps)))
    acts = pl.BlockSpec((tokens, fc), lambda i, m: (0, lax.rem(m[2] * near + i, steps)))
    half = width // 2

    def body(meta, *refs):
        (at_ref, x_ref, dy_ref, valid_ref, g_ref, b_ref, wo_own, wo_peer, up_own, up_peer, dn_own, dn_peer) = refs[:12]
        (out_ref, gm_ref, gb_ref, h2_ref, act_ref, dup_ref, da_ref, vec_ref) = refs[12:20]
        (mid_s, acc_s, own_s, peer_s, gown_s, gpeer_s) = refs[20:]
        i = pl.program_id(0)
        core = meta[2]
        zero = core == 0

        @pl.when(i == 0)
        def _():
            for p in range(packs):
                rows = pl.ds(p * lanes, lanes)
                own = at_ref[p, pl.ds(pl.multiple_of(core * half, half), half), :]
                peer = at_ref[p, pl.ds(pl.multiple_of((1 - core) * half, half), half), :]
                mid = x_ref[rows, :].astype(F32) + mm(own, wo_own[...], TN) + mm(peer, wo_peer[...], TN)
                mid_s[rows, :] = mid
                acc_s[rows, :] = mid
                hat, _ = norm_rows(mid)
                second = (hat * g_ref[...] + b_ref[...]).astype(BF16)
                h2_ref[rows, :] = second
                lo, hi = second[:, :half], second[:, half:]
                own_s[rows, :] = jnp.where(zero, lo, hi)
                peer_s[rows, :] = jnp.where(zero, hi, lo)
            gown_s[...] = jnp.zeros_like(gown_s)
            gpeer_s[...] = jnp.zeros_like(gpeer_s)

        down = jnp.where(i < near, dn_own[...], dn_peer[...])
        upper = mm(own_s[...], up_own[...]) + mm(peer_s[...], up_peer[...])
        act, slope = gelu_pair(upper)
        act = act.astype(BF16)
        grad = (mm(dy_ref[...], down, NT) * slope).astype(BF16)
        act_ref[...] = act
        dup_ref[...] = grad
        acc_s[...] += mm(act, down)
        gown_s[...] += mm(grad, up_own[...], NT)
        gpeer_s[...] += mm(grad, up_peer[...], NT)

        @pl.when(i == steps - 1)
        def _():
            out_ref[...] = acc_s[...].astype(BF16)
            vec = [jnp.zeros((8, width), F32), jnp.zeros((8, width), F32)]
            for p in range(packs):
                rows = pl.ds(p * lanes, lanes)
                hat, inv = norm_rows(mid_s[rows, :])
                a, b = gown_s[rows, :], gpeer_s[rows, :]
                gy = jnp.concatenate([jnp.where(zero, a, b), jnp.where(zero, b, a)], axis=1)
                vec[0] = vec[0] + jnp.sum((gy * hat).reshape(lanes // 8, 8, width), axis=0)
                vec[1] = vec[1] + jnp.sum(gy.reshape(lanes // 8, 8, width), axis=0)
                e = gy * g_ref[...]
                gm = dy_ref[rows, :].astype(F32) + inv * (
                    e
                    - jnp.mean(e, axis=-1, keepdims=True)
                    - hat * jnp.mean(e * hat, axis=-1, keepdims=True)
                )
                gm_ref[rows, :] = gm
                gb = gm.astype(BF16)
                gb_ref[rows, :] = gb
                ok = valid_ref[p]
                da_ref[p, pl.ds(pl.multiple_of(core * half, half), half), :] = (
                    mm(wo_own[...], gb, NT) * ok
                ).astype(BF16)
                da_ref[p, pl.ds(pl.multiple_of((1 - core) * half, half), half), :] = (
                    mm(wo_peer[...], gb, NT) * ok
                ).astype(BF16)
            vec_ref[0] = vec[0]
            vec_ref[1] = vec[1]

    return pl.pallas_call(
        body,
        grid_spec=pltpu.PrefetchScalarGridSpec(
            num_scalar_prefetch=1,
            grid=(steps,),
            in_specs=[
                whole(*attn_t.shape),
                whole(tokens, width),
                whole(tokens, width),
                whole(*valid.shape),
                whole(1, width),
                whole(1, width),
                whole(half, width),
                whole(half, width),
                ups,
                ups,
                pl.BlockSpec((fc, width), lambda i, m: (jnp.minimum(i, near - 1), 0)),
                pl.BlockSpec((fc, width), lambda i, m: (jnp.maximum(i - near, 0), 0)),
            ],
            out_specs=(
                whole(tokens, width),
                whole(tokens, width),
                whole(tokens, width),
                whole(tokens, width),
                acts,
                acts,
                whole(*attn_t.shape),
                whole(2, 8, width),
            ),
            scratch_shapes=[
                pltpu.VMEM((tokens, width), F32),
                pltpu.VMEM((tokens, width), F32),
                pltpu.VMEM((tokens, half), BF16),
                pltpu.VMEM((tokens, half), BF16),
                pltpu.VMEM((tokens, half), F32),
                pltpu.VMEM((tokens, half), F32),
            ],
        ),
        out_shape=(
            jax.ShapeDtypeStruct((tokens, width), BF16),
            jax.ShapeDtypeStruct((tokens, width), F32),
            jax.ShapeDtypeStruct((tokens, width), BF16),
            jax.ShapeDtypeStruct((tokens, width), BF16),
            jax.ShapeDtypeStruct((tokens, hidden), BF16),
            jax.ShapeDtypeStruct((tokens, hidden), BF16),
            jax.ShapeDtypeStruct(attn_t.shape, BF16),
            jax.ShapeDtypeStruct((2, 8, width), F32),
        ),
        compiler_params=params(),
        name="ffn_both_ways",
    )(meta, attn_t, x, dy, valid, gain, bias, wo, wo_p, up, up_p, dn, dn_p)


def weight_grads(meta, attn_t, gb, h2, dup, act, dy):
    tokens, width = dy.shape
    hidden = act.shape[1]
    half = width // 2
    packs, _, lanes = attn_t.shape
    n_up = hidden // width
    n_dn = hidden // 2 // half
    per = 1 + n_up + n_dn

    def body(meta, at_ref, gb_ref, h2_ref, dup_ref, act_ref, dy_ref, out_ref):
        s, j = pl.program_id(0), pl.program_id(1)
        side = jnp.where(s == 0, 1 - meta[2], meta[2])

        @pl.when(j == 0)
        def _():
            rows = pl.ds(pl.multiple_of(side * half, half), half)
            total = jnp.zeros((half, width), F32)
            for p in range(packs):
                total = total + mm(at_ref[p, rows, :], gb_ref[p * lanes : (p + 1) * lanes, :])
            out_ref[0] = total.astype(BF16)

        @pl.when((j >= 1) & (j <= n_up))
        def _():
            part = jnp.where(side == 0, h2_ref[:, :half], h2_ref[:, half:])
            out_ref[0] = mm(part, dup_ref[...], TN).astype(BF16)

        @pl.when(j > n_up)
        def _():
            out_ref[0] = mm(act_ref[...], dy_ref[...], TN).astype(BF16)

    def act_at(s, j, m):
        side = jnp.where(s == 0, 1 - m[2], m[2])
        return (0, side * n_dn + jnp.clip(j - 1 - n_up, 0, n_dn - 1))

    whole = lambda *shape: pl.BlockSpec(shape, lambda s, j, m: (0,) * len(shape))
    return pl.pallas_call(
        body,
        grid_spec=pltpu.PrefetchScalarGridSpec(
            num_scalar_prefetch=1,
            grid=(2, per),
            in_specs=[
                whole(*attn_t.shape),
                whole(tokens, width),
                whole(tokens, width),
                pl.BlockSpec((tokens, width), lambda s, j, m: (0, jnp.clip(j - 1, 0, n_up - 1))),
                pl.BlockSpec((tokens, half), act_at),
                whole(tokens, width),
            ],
            out_specs=pl.BlockSpec((1, half, width), lambda s, j, m: (s, j, 0)),
        ),
        out_shape=jax.ShapeDtypeStruct((2, per * half, width), BF16),
        compiler_params=params(),
        name="weight_gradients",
    )(meta, attn_t, gb, h2, dup, act, dy)


def finish_body(x_ref, gm_ref, back_ref, g_ref, out_ref):
    hat, inv = norm_rows(x_ref[...].astype(F32))
    e = back_ref[...].astype(F32) * g_ref[...]
    out_ref[...] = gm_ref[...] + inv * (
        e - jnp.mean(e, axis=-1, keepdims=True) - hat * jnp.mean(e * hat, axis=-1, keepdims=True)
    )


def finish(x, gm, back, gain):
    tokens, width = x.shape
    rows = pl.BlockSpec((128, width), lambda i: (i, 0))
    return pl.pallas_call(
        finish_body,
        grid=(tokens // 128,),
        in_specs=[rows, rows, rows, pl.BlockSpec((1, width), lambda i: (0, 0))],
        out_specs=rows,
        out_shape=jax.ShapeDtypeStruct((tokens, width), F32),
        compiler_params=params(),
        name="first_norm_backward",
    )(x, gm, back, gain)


def flip(value, axis, mask):
    size = lax.axis_size(axis)
    return lax.ppermute(value, axis, [(i, i ^ mask) for i in range(size)])


def bit(axis, mask):
    return (lax.axis_index(axis) // mask) % 2


def halves(value, which, axis=0):
    n = value.shape[axis] // 2
    keep = lax.dynamic_slice_in_dim(value, which * n, n, axis)
    send = lax.dynamic_slice_in_dim(value, (1 - which) * n, n, axis)
    return keep, send


def join(own, other, which, axis=0):
    return jnp.where(
        which == 0,
        jnp.concatenate([own, other], axis=axis),
        jnp.concatenate([other, own], axis=axis),
    )


def add(a, b):
    return (a.astype(F32) + b.astype(F32)).astype(BF16)


def reduce_all(value, cuts, rest):
    for axis, mask in cuts:
        keep, send = halves(value, bit(axis, mask))
        value = add(keep, flip(send, axis, mask))
    for axis, mask in rest:
        value = add(value, flip(value, axis, mask))
    for axis, mask in cuts[::-1]:
        value = join(value, flip(value, axis, mask), bit(axis, mask))
    return value


def on_device(
    tokens, lengths, ln1_gain, ln1_bias, qkv_weight, q_gain, k_gain, out_weight,
    ln2_gain, ln2_bias, up_weight, down_weight, cotangent,
):
    micro, rows, local, width = tokens.shape
    n = lax.axis_size("seq")
    length = local * n
    every = micro * rows
    team = n // every
    heads = H // team
    hd = width // H
    half = width // 2
    idx = lax.axis_index("seq")
    core = lax.axis_index("fsdp")
    row, member = idx // team, idx % team
    direct = every == 2 and team == 4
    lengths = lengths.reshape(every, lengths.shape[-1])
    mine = tokens.reshape(every, local, width)

    def swap(value):
        return flip(value, "fsdp", 1)

    vec = jnp.concatenate([ln1_gain, ln1_bias, ln2_gain, ln2_bias, q_gain, k_gain])[None]
    vec_p = swap(vec)
    ordered = jnp.where(core == 0, jnp.concatenate([vec, vec_p]), jnp.concatenate([vec_p, vec])).astype(F32)
    g1, b1, g2, b2 = (ordered[:, k * half : (k + 1) * half].reshape(1, width) for k in range(4))
    gq = ordered[:, 4 * half : 4 * half + hd // 2].reshape(hd, 1)
    gk = ordered[:, 4 * half + hd // 2 :].reshape(hd, 1)

    w_own = lax.dynamic_slice_in_dim(
        qkv_weight.reshape(half, 3, width), member * heads * hd, heads * hd, 2
    ).reshape(half, 3 * heads * hd)
    w_t = jnp.transpose(join(w_own, swap(w_own), core))

    if direct:
        near = lax.dynamic_index_in_dim(mine, row, 0, keepdims=False)
        away = lax.dynamic_index_in_dim(mine, 1 - row, 0, keepdims=False)
        far = flip(away, "seq", 4)
        cut = local // 2

        def spread(own):
            one, two = flip(own, "seq", 1), flip(own, "seq", 2)
            three = jnp.concatenate([flip(two[:cut], "seq", 1), flip(one[cut:], "seq", 2)], axis=0)
            return [own, one, two, three]

        slots = spread(near) + spread(far)
        spot = idx
    else:
        same_member = [[q * team + p for q in range(every)] for p in range(team)]
        same_row = [[q * team + p for p in range(team)] for q in range(every)]
        got = lax.all_to_all(mine, "seq", 0, 0, axis_index_groups=same_member, tiled=True)
        got = lax.all_gather(got, "seq", axis_index_groups=same_row)
        whole = jnp.swapaxes(got, 0, 1).reshape(length, width)
        slots = [whole[s * (length // 8) : (s + 1) * (length // 8)] for s in range(8)]
        spot = jnp.int32(0)
    meta = jnp.stack([spot, row, core]).astype(jnp.int32)

    out_p, up_p, down_p = swap(out_weight), swap(up_weight), swap(down_weight)

    with jax.named_scope("forward_attention"):
        qt, ka, kt, v, vt, x_row = make_qkv(meta, lengths, slots, w_t, g1, b1, gq, gk, heads, hd)
        attn, attn_f, logsum = attend(meta, lengths, qt, ka, vt, heads, hd)

    def exchange(value):
        return lax.all_to_all(value, "seq", 0, 0, tiled=True)

    packs = every * local // BLK
    if direct:
        attn_t = exchange(attn).reshape(packs, width, BLK)
    else:
        cut = jnp.moveaxis(attn.reshape(BLK * 0 + 8, heads * hd, BLK // local, local), 2, 1)
        got = exchange(cut.reshape(n, heads * hd, local))
        got = got.reshape(packs, every // packs, width, local)
        attn_t = jnp.swapaxes(got, 1, 2).reshape(packs, width, BLK)

    total = jnp.sum(lengths[:, :-1], axis=-1)
    places = idx * local + jnp.arange(local, dtype=jnp.int32)
    valid = (places[None] < total[:, None]).astype(F32).reshape(packs, 1, BLK)
    x_home = tokens.reshape(every * local, width)
    dy = cotangent.reshape(every * local, width)

    with jax.named_scope("feed_forward"):
        output, grad_mid, grad_branch, h2, act, dup, grad_attn, vec2 = ffn(
            meta, attn_t, x_home, dy, valid, g2, b2, out_weight, out_p, up_weight, up_p, down_weight, down_p
        )
    if direct:
        grad_o = exchange(grad_attn.reshape(n, heads * hd, BLK))
    else:
        cut = jnp.swapaxes(grad_attn.reshape(packs, width, every // packs, local), 1, 2)
        got = exchange(cut.reshape(n, heads * hd, local))
        got = got.reshape(8, BLK // local, heads * hd, local)
        grad_o = jnp.swapaxes(got, 1, 2).reshape(8, heads * hd, BLK)

    with jax.named_scope("weight_gradients"):
        grads = weight_grads(meta, attn_t, grad_branch, h2, dup, act, dy)
        big = add(grads[1], swap(grads[0]))
        masks = [1 << k for k in range(n.bit_length() - 1)]
        left = reduce_all(
            big[:, :half],
            [("rep", 1), ("seq", masks[0]), ("seq", masks[1])],
            [("seq", m) for m in masks[2:]],
        )
        right = reduce_all(
            big[:, half:],
            [("seq", masks[0]), ("rep", 1), ("seq", masks[1])],
            [("seq", m) for m in masks[2:]],
        )
        big = jnp.concatenate([left, right], axis=1).astype(F32)
        grad_out = big[:half]
        hidden = up_weight.shape[1]
        n_up = hidden // width
        grad_up = jnp.concatenate([big[half * (1 + k) : half * (2 + k)] for k in range(n_up)], axis=1)
        grad_down = big[half * (1 + n_up) :]

    with jax.named_scope("backward_attention"):
        dq, dk, dv = attend_back(meta, lengths, qt, ka, kt, v, attn_f, logsum, grad_o, heads, hd)
        back_a, back_b, dw_t, vec1, gains = qkv_back(
            meta, x_row, dq, dk, dv, w_t, g1, b1, gq, gk, heads, hd
        )

    if direct:

        def gather(parts):
            a = parts[0].reshape(2, 2, 2, local, half)
            b = parts[1].reshape(2, 2, 2, local, half)
            out = []
            for kind in (1, 0):
                a1 = add(a[kind, :, 0], flip(a[kind, :, 1], "seq", 1))
                b1 = add(b[kind, 0], flip(b[kind, 1], "seq", 2))
                a2 = add(a1[0], flip(a1[1], "seq", 2))
                b2 = add(b1[0], flip(b1[1], "seq", 1))
                out.append(jnp.concatenate([a2, b2], axis=1))
            return out

        far_sum, near_sum = gather((back_a, back_b))
        other = flip(far_sum, "seq", 4)
        back = jnp.where(
            row == 0, jnp.stack([near_sum, other]), jnp.stack([other, near_sum])
        ).reshape(every * local, width)
    else:
        whole = jnp.concatenate([back_a, back_b], axis=-1).reshape(every, team, local, width)
        whole = lax.psum_scatter(whole, "seq", scatter_dimension=1, axis_index_groups=same_row, tiled=True)
        got = lax.all_to_all(whole[:, 0], "seq", 0, 0, axis_index_groups=same_member, tiled=True)
        back = got.reshape(every * local, width)
    grad_tokens = finish(x_home, grad_mid, back, g1)

    with jax.named_scope("first_projection_gradient"):
        n3 = 3 * heads * hd
        keep, send = halves(dw_t, core, 1)
        piece = add(keep, swap(send))
        step_rest = [("seq", m) for m in masks if m >= team]
        piece = reduce_all(piece, [("rep", 1)], step_rest)
        parts = lax.all_gather(piece, "seq", axis_index_groups=[[q * team + p for p in range(team)] for q in range(every)])
        parts = parts.reshape(team, 3, heads * hd, half)
        grad_qkv = jnp.transpose(parts, (3, 1, 0, 2)).reshape(half, 3 * width).astype(F32)

    small = jnp.concatenate(
        [
            jnp.sum(vec1, axis=1).reshape(-1),
            jnp.sum(vec2, axis=1).reshape(-1),
            jnp.sum(gains, axis=-1).reshape(-1),
        ]
    )
    small = lax.psum(small, ("rep", "fsdp", "seq"))
    cuts = [small[k * width : (k + 1) * width] for k in range(4)]
    cuts += [small[4 * width : 4 * width + hd], small[4 * width + hd :]]
    cuts = [lax.dynamic_slice_in_dim(c, core * (c.shape[0] // 2), c.shape[0] // 2, 0) for c in cuts]
    shape = tokens.shape
    return (
        output.reshape(shape), grad_tokens.reshape(shape), cuts[0], cuts[1], grad_qkv, cuts[4], cuts[5],
        grad_out, cuts[2], cuts[3], grad_up, grad_down,
    )


def solution(mesh):
    tok = P(None, ("rep", "fsdp"), "seq", None)
    one, two = P("fsdp"), P("fsdp", None)
    in_specs = (tok, P(None, ("rep", "fsdp"), None), one, one, two, one, one, two, one, one, two, two, tok)
    out_specs = (tok, tok, one, one, two, one, one, two, one, one, two, two)
    return jax.shard_map(on_device, mesh=mesh, in_specs=in_specs, out_specs=out_specs, check_vma=False)
```

```python
import functools

import jax
import jax.numpy as jnp
from jax import lax
from jax.experimental import pallas as pl
from jax.experimental.pallas import tpu as pltpu
from jax.sharding import PartitionSpec as P

H = 12
EPS = 1e-06
LOG2E = 1.4426950408889634
SHIFT = 512.0
BLK = 256
NN = (((1,), (0,)), ((), ()))
NT = (((1,), (1,)), ((), ()))
TN = (((0,), (0,)), ((), ()))
F32 = jnp.float32
BF16 = jnp.bfloat16


def mm(a, b, dims=NN):
    return lax.dot_general(a, b, dims, preferred_element_type=F32)


def params(**kw):
    return pltpu.CompilerParams(vmem_limit_bytes=60 * 1024 * 1024, **kw)


def cost(us):
    return pl.CostEstimate(flops=int(us * 1.1e9), bytes_accessed=1024, transcendentals=0)


def norm_rows(v):
    center = jnp.mean(v, axis=-1, keepdims=True)
    centred = v - center
    inv = lax.rsqrt(jnp.mean(centred * centred, axis=-1, keepdims=True) + EPS)
    return centred * inv, inv


def norm_cols(v):
    center = jnp.mean(v, axis=0, keepdims=True)
    centred = v - center
    inv = lax.rsqrt(jnp.mean(centred * centred, axis=0, keepdims=True) + EPS)
    return centred * inv, inv


def bounds_of(len_ref, row):
    out = []
    total = jnp.int32(0)
    for j in range(len_ref.shape[1] - 1):
        total = total + len_ref[row, j]
        out.append(total)
    return out


def qkv_body(heads, hd, meta, len_ref, *refs):
    xs = refs[:8]
    w_ref, g_ref, b_ref, gq_ref, gk_ref = refs[8:13]
    qt_ref, ka_ref, kt_ref, v_ref, vt_ref, x_ref = refs[13:]
    wid = heads * hd
    spot, row = meta[0], meta[1]
    bounds = bounds_of(len_ref, row)
    for s in range(8):
        c = jnp.bitwise_xor(spot, s)
        cols = pl.ds(pl.multiple_of(c * BLK, BLK), BLK)
        x = xs[s][...]
        x_ref[cols, :] = x
        hat, _ = norm_rows(x.astype(F32))
        first = (hat * g_ref[...] + b_ref[...]).astype(BF16)
        qkv = mm(w_ref[...], first, NT)
        place = c * BLK + lax.broadcasted_iota(jnp.int32, (8, BLK), 1)
        ident = jnp.zeros((8, BLK), jnp.int32)
        place_k = c * BLK + lax.broadcasted_iota(jnp.int32, (BLK, 128), 0)
        ident_k = jnp.zeros((BLK, 128), jnp.int32)
        for bound in bounds:
            ident = ident + (place >= bound).astype(jnp.int32)
            ident_k = ident_k + (place_k >= bound).astype(jnp.int32)
        which = lax.broadcasted_iota(jnp.int32, (8, BLK), 0)
        hot = jnp.where((ident == which) & (which < len(bounds)), 16.0, 0.0)
        hot = jnp.concatenate([hot, jnp.zeros((hd - 8, BLK), F32)], axis=0)
        lane = lax.broadcasted_iota(jnp.int32, (BLK, 128), 1) - hd
        hot_k = jnp.where((ident_k == lane) & (lane < len(bounds)), SHIFT / 16.0, 0.0)
        for h in range(heads):
            q, _ = norm_cols(qkv[h * hd : (h + 1) * hd])
            k, _ = norm_cols(qkv[wid + h * hd : wid + (h + 1) * hd])
            q = (q * gq_ref[...]).astype(BF16).astype(F32) * (hd**-0.5)
            k = k * gk_ref[...]
            v = qkv[2 * wid + h * hd : 2 * wid + (h + 1) * hd]
            qt_ref[h, :, cols] = jnp.concatenate([q, hot], axis=0).astype(BF16)
            kt_ref[h, :, cols] = k.astype(BF16)
            vt_ref[h, :, cols] = v.astype(BF16)
            both = jnp.transpose(jnp.concatenate([k, v], axis=0))
            ka_ref[h, cols, :] = jnp.where(lane < 0, both, hot_k).astype(BF16)
            v_ref[h, cols, :] = both[:, hd:].astype(BF16)


def make_qkv(meta, lengths, slots, w_t, gain, bias, gq, gk, heads, hd):
    length = 8 * slots[0].shape[0]
    width = slots[0].shape[1]
    smem = pl.BlockSpec(memory_space=pltpu.SMEM)
    vmem = pl.BlockSpec(memory_space=pltpu.VMEM)
    return pl.pallas_call(
        functools.partial(qkv_body, heads, hd),
        out_shape=(
            jax.ShapeDtypeStruct((heads, 2 * hd, length), BF16),
            jax.ShapeDtypeStruct((heads, length, 2 * hd), BF16),
            jax.ShapeDtypeStruct((heads, hd, length), BF16),
            jax.ShapeDtypeStruct((heads, length, hd), BF16),
            jax.ShapeDtypeStruct((heads, hd, length), BF16),
            jax.ShapeDtypeStruct((length, width), BF16),
        ),
        in_specs=[smem, smem] + [vmem] * 13,
        out_specs=(vmem,) * 6,
        compiler_params=params(),
        cost_estimate=cost(12),
        name="qkv_forward",
    )(meta, lengths, *slots, w_t, gain, bias, gq, gk)


def block_range(bounds, i):
    first = i * BLK
    last = first + BLK - 1
    lo = jnp.int32(0)
    hi = bounds[-1]
    for bound in bounds:
        lo = jnp.where(first >= bound, bound, lo)
    for bound in bounds[::-1]:
        hi = jnp.where(last < bound, bound, hi)
    lo_b = lo // BLK
    hi_b = (hi + BLK - 1) // BLK
    return lo_b, jnp.where(first >= bounds[-1], lo_b, hi_b)


def attend_body(heads, hd, meta, len_ref, qt_ref, ka_ref, vt_ref, o_ref, of_ref, ls_ref):
    i = pl.program_id(0)
    bounds = bounds_of(len_ref, meta[1])
    lo, hi = block_range(bounds, i)

    def step(b, carry):
        rows = pl.ds(pl.multiple_of(b * BLK, BLK), BLK)
        out = []
        for h in range(heads):
            acc, total = carry[h]
            scores = mm(ka_ref[h, rows, :], qt_ref[h])
            expo = jnp.exp2(scores * LOG2E - SHIFT * LOG2E)
            total = total + jnp.sum(expo.reshape(BLK // 8, 8, BLK), axis=0)
            acc = acc + mm(vt_ref[h, :, rows], expo.astype(BF16))
            out.append((acc, total))
        return tuple(out)

    init = tuple((jnp.zeros((hd, BLK), F32), jnp.zeros((8, BLK), F32)) for _ in range(heads))
    done = lax.fori_loop(lo, hi, step, init)
    for h in range(heads):
        acc, total = done[h]
        total = jnp.sum(total, axis=0, keepdims=True)
        live = total > 0.0
        safe = jnp.where(live, total, 1.0)
        out = jnp.where(live, acc * (1.0 / safe), 0.0)
        o_ref[0, h * hd : (h + 1) * hd, :] = out.astype(BF16)
        of_ref[h] = out
        ls_ref[h] = jnp.log2(safe) + SHIFT * LOG2E


def attend(meta, lengths, qt, ka, vt, heads, hd):
    length = qt.shape[2]
    blocks = length // BLK
    smem = pl.BlockSpec(memory_space=pltpu.SMEM)
    return pl.pallas_call(
        functools.partial(attend_body, heads, hd),
        grid=(blocks,),
        out_shape=(
            jax.ShapeDtypeStruct((blocks, heads * hd, BLK), BF16),
            jax.ShapeDtypeStruct((heads, hd, length), F32),
            jax.ShapeDtypeStruct((heads, 1, length), F32),
        ),
        in_specs=[
            smem,
            smem,
            pl.BlockSpec((heads, 2 * hd, BLK), lambda i: (0, 0, i)),
            pl.BlockSpec((heads, length, 2 * hd), lambda i: (0, 0, 0)),
            pl.BlockSpec((heads, hd, length), lambda i: (0, 0, 0)),
        ],
        out_specs=(
            pl.BlockSpec((1, heads * hd, BLK), lambda i: (i, 0, 0)),
            pl.BlockSpec((heads, hd, BLK), lambda i: (0, 0, i)),
            pl.BlockSpec((heads, 1, BLK), lambda i: (0, 0, i)),
        ),
        compiler_params=params(),
        cost_estimate=cost(25),
        name="attention_forward",
    )(meta, lengths, qt, ka, vt)


def attend_back_body(
    heads, hd, meta, len_ref, qt_ref, ka_ref, kt_ref, v_ref, of_ref, ls_ref, go_ref, dq_ref, dk_ref, dv_ref
):
    i = pl.program_id(0)
    bounds = bounds_of(len_ref, meta[1])
    lo, hi = block_range(bounds, i)

    @pl.when(i == 0)
    def _():
        dk_ref[...] = jnp.zeros_like(dk_ref)
        dv_ref[...] = jnp.zeros_like(dv_ref)

    inner = []
    for h in range(heads):
        go = go_ref[0, h * hd : (h + 1) * hd, :].astype(F32)
        inner.append(jnp.sum(go * of_ref[h], axis=0, keepdims=True))

    def step(b, carry):
        rows = pl.ds(pl.multiple_of(b * BLK, BLK), BLK)
        out = []
        for h in range(heads):
            go = go_ref[0, h * hd : (h + 1) * hd, :]
            qt = qt_ref[h]
            scores = mm(ka_ref[h, rows, :], qt)
            probs = jnp.exp2(scores * LOG2E - ls_ref[h])
            grad_probs = mm(v_ref[h, rows, :], go)
            grad_scores = (probs * (grad_probs - inner[h])).astype(BF16)
            dv_ref[h, :, rows] += mm(go, probs.astype(BF16), NT)
            dk_ref[h, :, rows] += mm(qt[:hd], grad_scores, NT)
            out.append(carry[h] + mm(kt_ref[h, :, rows], grad_scores))
        return tuple(out)

    done = lax.fori_loop(lo, hi, step, tuple(jnp.zeros((hd, BLK), F32) for _ in range(heads)))
    for h in range(heads):
        dq_ref[h] = done[h] * (hd**-0.5)


def attend_back(meta, lengths, qt, ka, kt, v, of, ls, go, at, heads, hd):
    length = qt.shape[2]
    blocks = length // BLK
    smem = pl.BlockSpec(memory_space=pltpu.SMEM)
    whole = lambda *shape: pl.BlockSpec(shape, lambda i: (at, 0, 0))
    all_out = lambda *shape: pl.BlockSpec(shape, lambda i: (0, 0, 0))
    return pl.pallas_call(
        functools.partial(attend_back_body, heads, hd),
        grid=(blocks,),
        out_shape=tuple(jax.ShapeDtypeStruct((heads, hd, length), F32) for _ in range(3)),
        in_specs=[
            smem,
            smem,
            pl.BlockSpec((heads, 2 * hd, BLK), lambda i: (at, 0, i)),
            whole(heads, length, 2 * hd),
            whole(heads, hd, length),
            whole(heads, length, hd),
            pl.BlockSpec((heads, hd, BLK), lambda i: (at, 0, i)),
            pl.BlockSpec((heads, 1, BLK), lambda i: (at, 0, i)),
            pl.BlockSpec((1, heads * hd, BLK), lambda i: (i, at, 0)),
        ],
        out_specs=(
            pl.BlockSpec((heads, hd, BLK), lambda i: (0, 0, i)),
            all_out(heads, hd, length),
            all_out(heads, hd, length),
        ),
        compiler_params=params(),
        cost_estimate=cost(11 * heads),
        name="attention_backward",
    )(meta, lengths, qt, ka, kt, v, of, ls, go)


def qkv_back_body(
    heads, hd, meta, x_ref, *refs
):
    dqs, dks, dvs = refs[:heads], refs[heads : 2 * heads], refs[2 * heads : 3 * heads]
    w_ref, g_ref, b_ref, gq_ref, gk_ref, da_ref, db_ref, dw_ref, vec_ref, gain_ref, acc_ref = refs[3 * heads :]
    i = pl.program_id(0)
    wid = heads * hd

    @pl.when(i == 0)
    def _():
        acc_ref[...] = jnp.zeros_like(acc_ref)
        vec_ref[...] = jnp.zeros_like(vec_ref)
        gain_ref[...] = jnp.zeros_like(gain_ref)

    hat, _ = norm_rows(x_ref[...].astype(F32))
    first = (hat * g_ref[...] + b_ref[...]).astype(BF16)
    qk = mm(w_ref[: 2 * wid, :], first, NT)
    pieces = []
    for at, gain, grad in ((0, gq_ref, dqs), (1, gk_ref, dks)):
        for h in range(heads):
            unit, inv = norm_cols(qk[at * wid + h * hd : at * wid + (h + 1) * hd])
            gy = grad[h][0]
            gain_ref[at] += gy * unit
            e = gy * gain[...]
            pieces.append(
                inv
                * (
                    e
                    - jnp.mean(e, axis=0, keepdims=True)
                    - unit * jnp.mean(e * unit, axis=0, keepdims=True)
                )
            )
    for h in range(heads):
        pieces.append(dvs[h][0])
    grad = jnp.concatenate(pieces, axis=0).astype(BF16)
    acc_ref[...] += mm(grad, first)
    back = mm(grad, w_ref[...], TN)
    vec_ref[0] += jnp.sum((back * hat).reshape(BLK // 8, 8, -1), axis=0)
    vec_ref[1] += jnp.sum(back.reshape(BLK // 8, 8, -1), axis=0)
    half = back.shape[1] // 2
    da_ref[0] = back[:, :half].astype(BF16)
    db_ref[0] = back[:, half:].astype(BF16)

    @pl.when(i == pl.num_programs(0) - 1)
    def _():
        dw_ref[...] = acc_ref[...].astype(BF16)


def qkv_back(meta, x, dq, dk, dv, w_t, gain, bias, gq, gk, heads, hd):
    length, width = x.shape
    blocks = length // BLK
    whole = lambda *shape: pl.BlockSpec(shape, lambda i, m: (0,) * len(shape))
    part = pl.BlockSpec((1, hd, BLK), lambda i, m: (0, 0, i))
    grads = pl.BlockSpec((1, BLK, width // 2), lambda i, m: (jnp.bitwise_xor(i, m[0]), 0, 0))
    return pl.pallas_call(
        functools.partial(qkv_back_body, heads, hd),
        grid_spec=pltpu.PrefetchScalarGridSpec(
            num_scalar_prefetch=1,
            grid=(blocks,),
            in_specs=[
                pl.BlockSpec((BLK, width), lambda i, m: (i, 0)),
                *([part] * (3 * heads)),
                whole(*w_t.shape),
                whole(1, width),
                whole(1, width),
                whole(hd, 1),
                whole(hd, 1),
            ],
            out_specs=(
                grads,
                grads,
                whole(*w_t.shape),
                whole(2, 8, width),
                whole(2, hd, BLK),
            ),
            scratch_shapes=[pltpu.VMEM(w_t.shape, F32)],
        ),
        out_shape=(
            jax.ShapeDtypeStruct((blocks, BLK, width // 2), BF16),
            jax.ShapeDtypeStruct((blocks, BLK, width // 2), BF16),
            jax.ShapeDtypeStruct(w_t.shape, BF16),
            jax.ShapeDtypeStruct((2, 8, width), F32),
            jax.ShapeDtypeStruct((2, hd, BLK), F32),
        ),
        compiler_params=params(),
        cost_estimate=cost(17),
        name="qkv_backward",
    )(meta, x, *dq, *dk, *dv, w_t, gain, bias, gq, gk)


def gelu_pair(u):
    a = jnp.abs(u)
    t = 1.0 / (1.0 + (0.3275911 * 0.7071067811865476) * a)
    poly = 1.061405429 * t - 1.453152027
    poly = poly * t + 1.421413741
    poly = poly * t - 0.284496736
    poly = poly * t + 0.254829592
    bell = jnp.exp(-0.5 * (u * u))
    tail = (0.5 * poly) * t * bell
    cdf = jnp.where(u >= 0.0, 1.0 - tail, tail)
    return u * cdf, cdf + u * (bell * 0.3989422804014327)


def ffn(meta, attn_t, x, dy, valid, gain, bias, wo, wo_p, up, up_p, dn, dn_p):
    tokens, width = x.shape
    hidden = up.shape[1]
    fc = 512
    steps = hidden // fc
    near = steps // 2
    packs, _, lanes = attn_t.shape
    whole = lambda *shape: pl.BlockSpec(shape, lambda i, m: (0,) * len(shape))
    ups = pl.BlockSpec((width // 2, fc), lambda i, m: (0, lax.rem(m[2] * near + i, steps)))
    acts = pl.BlockSpec((tokens, fc), lambda i, m: (0, lax.rem(m[2] * near + i, steps)))
    half = width // 2

    def body(meta, *refs):
        (at_ref, x_ref, dy_ref, valid_ref, g_ref, b_ref, wo_own, wo_peer, up_own, up_peer, dn_own, dn_peer) = refs[:12]
        (out_ref, gm_ref, gb_ref, h2_ref, act_ref, dup_ref, da_ref, vec_ref) = refs[12:20]
        (mid_s, acc_s, own_s, peer_s, gown_s, gpeer_s) = refs[20:]
        i = pl.program_id(0)
        core = meta[2]
        zero = core == 0

        @pl.when(i == 0)
        def _():
            for p in range(packs):
                rows = pl.ds(p * lanes, lanes)
                own = at_ref[p, pl.ds(pl.multiple_of(core * half, half), half), :]
                peer = at_ref[p, pl.ds(pl.multiple_of((1 - core) * half, half), half), :]
                mid = x_ref[rows, :].astype(F32) + mm(own, wo_own[...], TN) + mm(peer, wo_peer[...], TN)
                mid_s[rows, :] = mid
                acc_s[rows, :] = mid
                hat, _ = norm_rows(mid)
                second = (hat * g_ref[...] + b_ref[...]).astype(BF16)
                h2_ref[rows, :] = second
                lo, hi = second[:, :half], second[:, half:]
                own_s[rows, :] = jnp.where(zero, lo, hi)
                peer_s[rows, :] = jnp.where(zero, hi, lo)
            gown_s[...] = jnp.zeros_like(gown_s)
            gpeer_s[...] = jnp.zeros_like(gpeer_s)

        down = jnp.where(i < near, dn_own[...], dn_peer[...])
        upper = mm(own_s[...], up_own[...]) + mm(peer_s[...], up_peer[...])
        act, slope = gelu_pair(upper)
        act = act.astype(BF16)
        grad = (mm(dy_ref[...], down, NT) * slope).astype(BF16)
        act_ref[...] = act
        dup_ref[...] = grad
        acc_s[...] += mm(act, down)
        gown_s[...] += mm(grad, up_own[...], NT)
        gpeer_s[...] += mm(grad, up_peer[...], NT)

        @pl.when(i == steps - 1)
        def _():
            out_ref[...] = acc_s[...].astype(BF16)
            vec = [jnp.zeros((8, width), F32), jnp.zeros((8, width), F32)]
            for p in range(packs):
                rows = pl.ds(p * lanes, lanes)
                hat, inv = norm_rows(mid_s[rows, :])
                a, b = gown_s[rows, :], gpeer_s[rows, :]
                gy = jnp.concatenate([jnp.where(zero, a, b), jnp.where(zero, b, a)], axis=1)
                vec[0] = vec[0] + jnp.sum((gy * hat).reshape(lanes // 8, 8, width), axis=0)
                vec[1] = vec[1] + jnp.sum(gy.reshape(lanes // 8, 8, width), axis=0)
                e = gy * g_ref[...]
                gm = dy_ref[rows, :].astype(F32) + inv * (
                    e
                    - jnp.mean(e, axis=-1, keepdims=True)
                    - hat * jnp.mean(e * hat, axis=-1, keepdims=True)
                )
                gm_ref[rows, :] = gm
                gb = gm.astype(BF16)
                gb_ref[rows, :] = gb
                ok = valid_ref[p]
                da_ref[p, pl.ds(pl.multiple_of(core * half, half), half), :] = (
                    mm(wo_own[...], gb, NT) * ok
                ).astype(BF16)
                da_ref[p, pl.ds(pl.multiple_of((1 - core) * half, half), half), :] = (
                    mm(wo_peer[...], gb, NT) * ok
                ).astype(BF16)
            vec_ref[0] = vec[0]
            vec_ref[1] = vec[1]

    return pl.pallas_call(
        body,
        grid_spec=pltpu.PrefetchScalarGridSpec(
            num_scalar_prefetch=1,
            grid=(steps,),
            in_specs=[
                whole(*attn_t.shape),
                whole(tokens, width),
                whole(tokens, width),
                whole(*valid.shape),
                whole(1, width),
                whole(1, width),
                whole(half, width),
                whole(half, width),
                ups,
                ups,
                pl.BlockSpec((fc, width), lambda i, m: (jnp.minimum(i, near - 1), 0)),
                pl.BlockSpec((fc, width), lambda i, m: (jnp.maximum(i - near, 0), 0)),
            ],
            out_specs=(
                whole(tokens, width),
                whole(tokens, width),
                whole(tokens, width),
                whole(tokens, width),
                acts,
                acts,
                whole(*attn_t.shape),
                whole(2, 8, width),
            ),
            scratch_shapes=[
                pltpu.VMEM((tokens, width), F32),
                pltpu.VMEM((tokens, width), F32),
                pltpu.VMEM((tokens, half), BF16),
                pltpu.VMEM((tokens, half), BF16),
                pltpu.VMEM((tokens, half), F32),
                pltpu.VMEM((tokens, half), F32),
            ],
        ),
        out_shape=(
            jax.ShapeDtypeStruct((tokens, width), BF16),
            jax.ShapeDtypeStruct((tokens, width), F32),
            jax.ShapeDtypeStruct((tokens, width), BF16),
            jax.ShapeDtypeStruct((tokens, width), BF16),
            jax.ShapeDtypeStruct((tokens, hidden), BF16),
            jax.ShapeDtypeStruct((tokens, hidden), BF16),
            jax.ShapeDtypeStruct(attn_t.shape, BF16),
            jax.ShapeDtypeStruct((2, 8, width), F32),
        ),
        compiler_params=params(),
        cost_estimate=cost(25),
        name="ffn_both_ways",
    )(meta, attn_t, x, dy, valid, gain, bias, wo, wo_p, up, up_p, dn, dn_p)


def down_grads(meta, own, act, dy):
    tokens, width = dy.shape
    half = width // 2
    blocks = act.shape[1] // 2 // half

    def body(meta, act_ref, dy_ref, out_ref):
        out_ref[...] = mm(act_ref[...], dy_ref[...], TN).astype(BF16)

    side = (lambda m: m[2]) if own else (lambda m: 1 - m[2])
    return pl.pallas_call(
        body,
        grid_spec=pltpu.PrefetchScalarGridSpec(
            num_scalar_prefetch=1,
            grid=(blocks,),
            in_specs=[
                pl.BlockSpec((tokens, half), lambda j, m: (0, side(m) * blocks + j)),
                pl.BlockSpec((tokens, width), lambda j, m: (0, 0)),
            ],
            out_specs=pl.BlockSpec((half, width), lambda j, m: (j, 0)),
        ),
        out_shape=jax.ShapeDtypeStruct((blocks * half, width), BF16),
        compiler_params=params(),
        cost_estimate=cost(5),
        name="down_gradient",
    )(meta, act, dy)


def up_out_grads(meta, own, attn_t, gb, h2, dup):
    tokens, width = gb.shape
    hidden = dup.shape[1]
    half = width // 2
    packs, _, lanes = attn_t.shape
    blocks = hidden // width

    def body(meta, at_ref, gb_ref, h2_ref, dup_ref, out_ref):
        j = pl.program_id(0)
        side = meta[2] if own else 1 - meta[2]

        @pl.when(j < blocks)
        def _():
            part = jnp.where(side == 0, h2_ref[:, :half], h2_ref[:, half:])
            out_ref[...] = mm(part, dup_ref[...], TN).astype(BF16)

        @pl.when(j == blocks)
        def _():
            rows = pl.ds(pl.multiple_of(side * half, half), half)
            total = jnp.zeros((half, width), F32)
            for p in range(packs):
                total = total + mm(at_ref[p, rows, :], gb_ref[p * lanes : (p + 1) * lanes, :])
            out_ref[...] = total.astype(BF16)

    whole = lambda *shape: pl.BlockSpec(shape, lambda j, m: (0,) * len(shape))
    return pl.pallas_call(
        body,
        grid_spec=pltpu.PrefetchScalarGridSpec(
            num_scalar_prefetch=1,
            grid=(blocks + 1,),
            in_specs=[
                whole(*attn_t.shape),
                whole(tokens, width),
                whole(tokens, width),
                pl.BlockSpec((tokens, width), lambda j, m: (0, jnp.minimum(j, blocks - 1))),
            ],
            out_specs=pl.BlockSpec((half, width), lambda j, m: (j, 0)),
        ),
        out_shape=jax.ShapeDtypeStruct(((blocks + 1) * half, width), BF16),
        compiler_params=params(),
        cost_estimate=cost(5),
        name="up_out_gradient",
    )(meta, attn_t, gb, h2, dup)


def finish_body(x_ref, gm_ref, back_ref, g_ref, out_ref):
    hat, inv = norm_rows(x_ref[...].astype(F32))
    e = back_ref[...].astype(F32) * g_ref[...]
    out_ref[...] = gm_ref[...] + inv * (
        e - jnp.mean(e, axis=-1, keepdims=True) - hat * jnp.mean(e * hat, axis=-1, keepdims=True)
    )


def finish(x, gm, back, gain):
    tokens, width = x.shape
    rows = pl.BlockSpec((128, width), lambda i: (i, 0))
    return pl.pallas_call(
        finish_body,
        grid=(tokens // 128,),
        in_specs=[rows, rows, rows, pl.BlockSpec((1, width), lambda i: (0, 0))],
        out_specs=rows,
        out_shape=jax.ShapeDtypeStruct((tokens, width), F32),
        compiler_params=params(),
        cost_estimate=cost(4),
        name="first_norm_backward",
    )(x, gm, back, gain)


def flip(value, axis, mask):
    size = lax.axis_size(axis)
    return lax.ppermute(value, axis, [(i, i ^ mask) for i in range(size)])


def bit(axis, mask):
    return (lax.axis_index(axis) // mask) % 2


def halves(value, which, axis=0):
    n = value.shape[axis] // 2
    keep = lax.dynamic_slice_in_dim(value, which * n, n, axis)
    send = lax.dynamic_slice_in_dim(value, (1 - which) * n, n, axis)
    return keep, send


def join(own, other, which, axis=0):
    return jnp.where(
        which == 0,
        jnp.concatenate([own, other], axis=axis),
        jnp.concatenate([other, own], axis=axis),
    )


def add(a, b):
    return (a.astype(F32) + b.astype(F32)).astype(BF16)


def reduce_all(value, cuts, rest):
    for axis, mask in cuts:
        keep, send = halves(value, bit(axis, mask))
        value = add(keep, flip(send, axis, mask))
    for axis, mask in rest:
        value = add(value, flip(value, axis, mask))
    for axis, mask in cuts[::-1]:
        value = join(value, flip(value, axis, mask), bit(axis, mask))
    return value


def on_device(
    tokens, lengths, ln1_gain, ln1_bias, qkv_weight, q_gain, k_gain, out_weight,
    ln2_gain, ln2_bias, up_weight, down_weight, cotangent,
):
    micro, rows, local, width = tokens.shape
    n = lax.axis_size("seq")
    length = local * n
    every = micro * rows
    team = n // every
    heads = H // team
    hd = width // H
    half = width // 2
    idx = lax.axis_index("seq")
    core = lax.axis_index("fsdp")
    row, member = idx // team, idx % team
    direct = every == 2 and team == 4
    lengths = lengths.reshape(every, lengths.shape[-1])
    mine = tokens.reshape(every, local, width)

    def swap(value):
        return flip(value, "fsdp", 1)

    vec = jnp.concatenate([ln1_gain, ln1_bias, ln2_gain, ln2_bias, q_gain, k_gain])[None]
    vec_p = swap(vec)
    ordered = jnp.where(core == 0, jnp.concatenate([vec, vec_p]), jnp.concatenate([vec_p, vec])).astype(F32)
    g1, b1, g2, b2 = (ordered[:, k * half : (k + 1) * half].reshape(1, width) for k in range(4))
    gq = ordered[:, 4 * half : 4 * half + hd // 2].reshape(hd, 1)
    gk = ordered[:, 4 * half + hd // 2 :].reshape(hd, 1)

    w_own = lax.dynamic_slice_in_dim(
        qkv_weight.reshape(half, 3, width), member * heads * hd, heads * hd, 2
    ).reshape(half, 3 * heads * hd)
    w_t = jnp.transpose(join(w_own, swap(w_own), core))

    if direct:
        near = lax.dynamic_index_in_dim(mine, row, 0, keepdims=False)
        away = lax.dynamic_index_in_dim(mine, 1 - row, 0, keepdims=False)
        far = flip(away, "seq", 4)
        cut = local // 2

        def spread(own):
            one, two = flip(own, "seq", 1), flip(own, "seq", 2)
            three = jnp.concatenate([flip(two[:cut], "seq", 1), flip(one[cut:], "seq", 2)], axis=0)
            return [own, one, two, three]

        slots = spread(near) + spread(far)
        spot = idx
    else:
        same_member = [[q * team + p for q in range(every)] for p in range(team)]
        same_row = [[q * team + p for p in range(team)] for q in range(every)]
        got = lax.all_to_all(mine, "seq", 0, 0, axis_index_groups=same_member, tiled=True)
        got = lax.all_gather(got, "seq", axis_index_groups=same_row)
        whole = jnp.swapaxes(got, 0, 1).reshape(length, width)
        slots = [whole[s * (length // 8) : (s + 1) * (length // 8)] for s in range(8)]
        spot = jnp.int32(0)
    meta = jnp.stack([spot, row, core]).astype(jnp.int32)

    out_p, up_p, down_p = swap(out_weight), swap(up_weight), swap(down_weight)

    with jax.named_scope("forward_attention"):
        qt, ka, kt, v, vt, x_row = make_qkv(meta, lengths, slots, w_t, g1, b1, gq, gk, heads, hd)
        attn, attn_f, logsum = attend(meta, lengths, qt, ka, vt, heads, hd)

    def exchange(value):
        return lax.all_to_all(value, "seq", 0, 0, tiled=True)

    packs = every * local // BLK
    if direct:
        attn_t = exchange(attn).reshape(packs, width, BLK)
    else:
        cut = jnp.moveaxis(attn.reshape(BLK * 0 + 8, heads * hd, BLK // local, local), 2, 1)
        got = exchange(cut.reshape(n, heads * hd, local))
        got = got.reshape(packs, every // packs, width, local)
        attn_t = jnp.swapaxes(got, 1, 2).reshape(packs, width, BLK)

    total = jnp.sum(lengths[:, :-1], axis=-1)
    places = idx * local + jnp.arange(local, dtype=jnp.int32)
    valid = (places[None] < total[:, None]).astype(F32).reshape(packs, 1, BLK)
    x_home = tokens.reshape(every * local, width)
    dy = cotangent.reshape(every * local, width)

    with jax.named_scope("feed_forward"):
        output, grad_mid, grad_branch, h2, act, dup, grad_attn, vec2 = ffn(
            meta, attn_t, x_home, dy, valid, g2, b2, out_weight, out_p, up_weight, up_p, down_weight, down_p
        )
    if direct:
        grad_o = exchange(grad_attn.reshape(n, heads * hd, BLK))
    else:
        cut = jnp.swapaxes(grad_attn.reshape(packs, width, every // packs, local), 1, 2)
        got = exchange(cut.reshape(n, heads * hd, local))
        got = got.reshape(8, BLK // local, heads * hd, local)
        grad_o = jnp.swapaxes(got, 1, 2).reshape(8, heads * hd, BLK)

    masks = [1 << k for k in range(n.bit_length() - 1)]
    with jax.named_scope("weight_gradients"):
        far_d = swap(down_grads(meta, False, act, dy))
        grad_d = add(down_grads(meta, True, act, dy), far_d)
        far_u = swap(up_out_grads(meta, False, attn_t, grad_branch, h2, dup))
        grad_u = add(up_out_grads(meta, True, attn_t, grad_branch, h2, dup), far_u)
        rest = [("seq", m) for m in masks[2:]]
        grad_d = reduce_all(grad_d, [("rep", 1), ("seq", 1), ("seq", 2)], rest)
        grad_u = reduce_all(grad_u, [("seq", 1), ("rep", 1), ("seq", 2)], rest)
        hidden = up_weight.shape[1]
        n_up = hidden // width
        grad_down = grad_d.astype(F32)
        grad_up = jnp.concatenate([grad_u[half * k : half * (k + 1)] for k in range(n_up)], axis=1).astype(F32)
        grad_out = grad_u[half * n_up :].astype(F32)

    with jax.named_scope("backward_attention"):
        parts = [
            attend_back(meta, lengths, qt, ka, kt, v, attn_f, logsum, grad_o, h, 1, hd) for h in range(heads)
        ]
        dq, dk, dv = zip(*parts)
        back_a, back_b, dw_t, vec1, gains = qkv_back(
            meta, x_row, dq, dk, dv, w_t, g1, b1, gq, gk, heads, hd
        )

    if direct:

        def gather(parts):
            a = parts[0].reshape(2, 2, 2, local, half)
            b = parts[1].reshape(2, 2, 2, local, half)
            out = []
            for kind in (1, 0):
                a1 = add(a[kind, :, 0], flip(a[kind, :, 1], "seq", 1))
                b1 = add(b[kind, 0], flip(b[kind, 1], "seq", 2))
                a2 = add(a1[0], flip(a1[1], "seq", 2))
                b2 = add(b1[0], flip(b1[1], "seq", 1))
                out.append(jnp.concatenate([a2, b2], axis=1))
            return out

        far_sum, near_sum = gather((back_a, back_b))
        other = flip(far_sum, "seq", 4)
        back = jnp.where(
            row == 0, jnp.stack([near_sum, other]), jnp.stack([other, near_sum])
        ).reshape(every * local, width)
    else:
        whole = jnp.concatenate([back_a, back_b], axis=-1).reshape(every, team, local, width)
        whole = lax.psum_scatter(whole, "seq", scatter_dimension=1, axis_index_groups=same_row, tiled=True)
        got = lax.all_to_all(whole[:, 0], "seq", 0, 0, axis_index_groups=same_member, tiled=True)
        back = got.reshape(every * local, width)
    grad_tokens = finish(x_home, grad_mid, back, g1)

    with jax.named_scope("first_projection_gradient"):
        keep, send = halves(dw_t, core, 1)
        piece = add(keep, swap(send))
        keep, send = halves(piece, bit("rep", 1))
        piece = add(keep, flip(send, "rep", 1))
        for mask in masks:
            if mask >= team:
                piece = add(piece, flip(piece, "seq", mask))
        piece = piece[None]
        for mask in masks:
            if mask < team:
                piece = join(piece, flip(piece, "seq", mask), bit("seq", mask))
        piece = join(piece, flip(piece, "rep", 1), bit("rep", 1), 1)
        piece = piece.reshape(team, 3, heads * hd, half)
        grad_qkv = jnp.transpose(piece, (3, 1, 0, 2)).reshape(half, 3 * width).astype(F32)

    with jax.named_scope("vector_gradients"):
        small = jnp.concatenate([vec1, vec2]).sum(axis=1).reshape(4, 2, half)
        small = jnp.concatenate(
            [jnp.swapaxes(small, 0, 1).reshape(2, 4 * half)]
            + [gains[k].sum(axis=-1).reshape(2, hd // 2) for k in range(2)],
            axis=1,
        )
        keep, send = halves(small, core)
        small = keep + swap(send)
        for axis, mask in [("rep", 1)] + [("seq", m) for m in masks]:
            small = small + flip(small, axis, mask)
        small = small[0]
        cuts = [small[k * half : (k + 1) * half] for k in range(4)]
        cuts += [small[4 * half : 4 * half + hd // 2], small[4 * half + hd // 2 :]]
    shape = tokens.shape
    return (
        output.reshape(shape), grad_tokens.reshape(shape), cuts[0], cuts[1], grad_qkv, cuts[4], cuts[5],
        grad_out, cuts[2], cuts[3], grad_up, grad_down,
    )


def solution(mesh):
    tok = P(None, ("rep", "fsdp"), "seq", None)
    one, two = P("fsdp"), P("fsdp", None)
    in_specs = (tok, P(None, ("rep", "fsdp"), None), one, one, two, one, one, two, one, one, two, two, tok)
    out_specs = (tok, tok, one, one, two, one, one, two, one, one, two, two)
    return jax.shard_map(on_device, mesh=mesh, in_specs=in_specs, out_specs=out_specs, check_vma=False)
```

```python
import functools

import jax
import jax.numpy as jnp
from jax import lax
from jax.experimental import pallas as pl
from jax.experimental.pallas import tpu as pltpu
from jax.sharding import PartitionSpec as P

H = 12
EPS = 1e-06
LOG2E = 1.4426950408889634
SHIFT = 512.0
BLK = 256
NN = (((1,), (0,)), ((), ()))
NT = (((1,), (1,)), ((), ()))
TN = (((0,), (0,)), ((), ()))
F32 = jnp.float32
BF16 = jnp.bfloat16


def mm(a, b, dims=NN):
    return lax.dot_general(a, b, dims, preferred_element_type=F32)


def params(**kw):
    return pltpu.CompilerParams(vmem_limit_bytes=60 * 1024 * 1024, **kw)


def cost(us):
    return pl.CostEstimate(flops=int(us * 1.1e9), bytes_accessed=1024, transcendentals=0)


def norm_rows(v):
    center = jnp.mean(v, axis=-1, keepdims=True)
    centred = v - center
    inv = lax.rsqrt(jnp.mean(centred * centred, axis=-1, keepdims=True) + EPS)
    return centred * inv, inv


def norm_cols(v):
    center = jnp.mean(v, axis=0, keepdims=True)
    centred = v - center
    inv = lax.rsqrt(jnp.mean(centred * centred, axis=0, keepdims=True) + EPS)
    return centred * inv, inv


def bounds_of(len_ref, row):
    out = []
    total = jnp.int32(0)
    for j in range(len_ref.shape[1] - 1):
        total = total + len_ref[row, j]
        out.append(total)
    return out


def qkv_body(heads, hd, meta, len_ref, *refs):
    xs = refs[:8]
    w_ref, g_ref, b_ref, gq_ref, gk_ref = refs[8:13]
    qt_ref, ka_ref, kt_ref, v_ref, vt_ref, x_ref = refs[13:]
    wid = heads * hd
    spot, row = meta[0], meta[1]
    bounds = bounds_of(len_ref, row)
    for s in range(8):
        c = jnp.bitwise_xor(spot, s)
        cols = pl.ds(pl.multiple_of(c * BLK, BLK), BLK)
        x = xs[s][...]
        x_ref[cols, :] = x
        hat, _ = norm_rows(x.astype(F32))
        first = (hat * g_ref[...] + b_ref[...]).astype(BF16)
        qkv = mm(w_ref[...], first, NT)
        place = c * BLK + lax.broadcasted_iota(jnp.int32, (8, BLK), 1)
        ident = jnp.zeros((8, BLK), jnp.int32)
        place_k = c * BLK + lax.broadcasted_iota(jnp.int32, (BLK, 128), 0)
        ident_k = jnp.zeros((BLK, 128), jnp.int32)
        for bound in bounds:
            ident = ident + (place >= bound).astype(jnp.int32)
            ident_k = ident_k + (place_k >= bound).astype(jnp.int32)
        which = lax.broadcasted_iota(jnp.int32, (8, BLK), 0)
        hot = jnp.where((ident == which) & (which < len(bounds)), 16.0, 0.0)
        hot = jnp.concatenate([hot, jnp.zeros((hd - 8, BLK), F32)], axis=0)
        lane = lax.broadcasted_iota(jnp.int32, (BLK, 128), 1) - hd
        hot_k = jnp.where((ident_k == lane) & (lane < len(bounds)), SHIFT / 16.0, 0.0)
        for h in range(heads):
            q, _ = norm_cols(qkv[h * hd : (h + 1) * hd])
            k, _ = norm_cols(qkv[wid + h * hd : wid + (h + 1) * hd])
            q = (q * gq_ref[...]).astype(BF16).astype(F32) * (hd**-0.5)
            k = k * gk_ref[...]
            v = qkv[2 * wid + h * hd : 2 * wid + (h + 1) * hd]
            qt_ref[h, :, cols] = jnp.concatenate([q, hot], axis=0).astype(BF16)
            kt_ref[h, :, cols] = k.astype(BF16)
            vt_ref[h, :, cols] = v.astype(BF16)
            both = jnp.transpose(jnp.concatenate([k, v], axis=0))
            ka_ref[h, cols, :] = jnp.where(lane < 0, both, hot_k).astype(BF16)
            v_ref[h, cols, :] = both[:, hd:].astype(BF16)


def make_qkv(meta, lengths, slots, w_t, gain, bias, gq, gk, heads, hd):
    length = 8 * slots[0].shape[0]
    width = slots[0].shape[1]
    smem = pl.BlockSpec(memory_space=pltpu.SMEM)
    vmem = pl.BlockSpec(memory_space=pltpu.VMEM)
    return pl.pallas_call(
        functools.partial(qkv_body, heads, hd),
        out_shape=(
            jax.ShapeDtypeStruct((heads, 2 * hd, length), BF16),
            jax.ShapeDtypeStruct((heads, length, 2 * hd), BF16),
            jax.ShapeDtypeStruct((heads, hd, length), BF16),
            jax.ShapeDtypeStruct((heads, length, hd), BF16),
            jax.ShapeDtypeStruct((heads, hd, length), BF16),
            jax.ShapeDtypeStruct((length, width), BF16),
        ),
        in_specs=[smem, smem] + [vmem] * 13,
        out_specs=(vmem,) * 6,
        compiler_params=params(),
        cost_estimate=cost(12),
        name="qkv_forward",
    )(meta, lengths, *slots, w_t, gain, bias, gq, gk)


def block_range(bounds, i):
    first = i * BLK
    last = first + BLK - 1
    lo = jnp.int32(0)
    hi = bounds[-1]
    for bound in bounds:
        lo = jnp.where(first >= bound, bound, lo)
    for bound in bounds[::-1]:
        hi = jnp.where(last < bound, bound, hi)
    lo_b = lo // BLK
    hi_b = (hi + BLK - 1) // BLK
    return lo_b, jnp.where(first >= bounds[-1], lo_b, hi_b)


def attend_body(heads, hd, meta, len_ref, qt_ref, ka_ref, vt_ref, o_ref, of_ref, ls_ref):
    i = pl.program_id(0)
    bounds = bounds_of(len_ref, meta[1])
    lo, hi = block_range(bounds, i)

    def step(b, carry):
        rows = pl.ds(pl.multiple_of(b * BLK, BLK), BLK)
        out = []
        for h in range(heads):
            acc, total = carry[h]
            scores = mm(ka_ref[h, rows, :], qt_ref[h])
            expo = jnp.exp2(scores * LOG2E - SHIFT * LOG2E)
            total = total + jnp.sum(expo.reshape(BLK // 8, 8, BLK), axis=0)
            acc = acc + mm(vt_ref[h, :, rows], expo.astype(BF16))
            out.append((acc, total))
        return tuple(out)

    init = tuple((jnp.zeros((hd, BLK), F32), jnp.zeros((8, BLK), F32)) for _ in range(heads))
    done = lax.fori_loop(lo, hi, step, init)
    for h in range(heads):
        acc, total = done[h]
        total = jnp.sum(total, axis=0, keepdims=True)
        live = total > 0.0
        safe = jnp.where(live, total, 1.0)
        out = jnp.where(live, acc * (1.0 / safe), 0.0)
        o_ref[0, h * hd : (h + 1) * hd, :] = out.astype(BF16)
        of_ref[h] = out
        ls_ref[h] = jnp.log2(safe) + SHIFT * LOG2E


def attend(meta, lengths, qt, ka, vt, heads, hd):
    length = qt.shape[2]
    blocks = length // BLK
    smem = pl.BlockSpec(memory_space=pltpu.SMEM)
    return pl.pallas_call(
        functools.partial(attend_body, heads, hd),
        grid=(blocks,),
        out_shape=(
            jax.ShapeDtypeStruct((blocks, heads * hd, BLK), BF16),
            jax.ShapeDtypeStruct((heads, hd, length), F32),
            jax.ShapeDtypeStruct((heads, 1, length), F32),
        ),
        in_specs=[
            smem,
            smem,
            pl.BlockSpec((heads, 2 * hd, BLK), lambda i: (0, 0, i)),
            pl.BlockSpec((heads, length, 2 * hd), lambda i: (0, 0, 0)),
            pl.BlockSpec((heads, hd, length), lambda i: (0, 0, 0)),
        ],
        out_specs=(
            pl.BlockSpec((1, heads * hd, BLK), lambda i: (i, 0, 0)),
            pl.BlockSpec((heads, hd, BLK), lambda i: (0, 0, i)),
            pl.BlockSpec((heads, 1, BLK), lambda i: (0, 0, i)),
        ),
        compiler_params=params(),
        cost_estimate=cost(25),
        name="attention_forward",
    )(meta, lengths, qt, ka, vt)


def attend_back_body(
    heads, hd, meta, len_ref, qt_ref, ka_ref, kt_ref, v_ref, of_ref, ls_ref, go_ref, dq_ref, dk_ref, dv_ref
):
    i = pl.program_id(0)
    bounds = bounds_of(len_ref, meta[1])
    lo, hi = block_range(bounds, i)

    @pl.when(i == 0)
    def _():
        dk_ref[...] = jnp.zeros_like(dk_ref)
        dv_ref[...] = jnp.zeros_like(dv_ref)

    inner = []
    for h in range(heads):
        go = go_ref[0, h * hd : (h + 1) * hd, :].astype(F32)
        inner.append(jnp.sum(go * of_ref[h], axis=0, keepdims=True))

    def step(b, carry):
        rows = pl.ds(pl.multiple_of(b * BLK, BLK), BLK)
        out = []
        for h in range(heads):
            go = go_ref[0, h * hd : (h + 1) * hd, :]
            qt = qt_ref[h]
            scores = mm(ka_ref[h, rows, :], qt)
            probs = jnp.exp2(scores * LOG2E - ls_ref[h])
            grad_probs = mm(v_ref[h, rows, :], go)
            grad_scores = (probs * (grad_probs - inner[h])).astype(BF16)
            dv_ref[h, :, rows] += mm(go, probs.astype(BF16), NT)
            dk_ref[h, :, rows] += mm(qt[:hd], grad_scores, NT)
            out.append(carry[h] + mm(kt_ref[h, :, rows], grad_scores))
        return tuple(out)

    done = lax.fori_loop(lo, hi, step, tuple(jnp.zeros((hd, BLK), F32) for _ in range(heads)))
    for h in range(heads):
        dq_ref[h] = done[h] * (hd**-0.5)


def attend_back(meta, lengths, qt, ka, kt, v, of, ls, go, at, heads, hd):
    length = qt.shape[2]
    blocks = length // BLK
    smem = pl.BlockSpec(memory_space=pltpu.SMEM)
    whole = lambda *shape: pl.BlockSpec(shape, lambda i: (at, 0, 0))
    all_out = lambda *shape: pl.BlockSpec(shape, lambda i: (0, 0, 0))
    return pl.pallas_call(
        functools.partial(attend_back_body, heads, hd),
        grid=(blocks,),
        out_shape=tuple(jax.ShapeDtypeStruct((heads, hd, length), F32) for _ in range(3)),
        in_specs=[
            smem,
            smem,
            pl.BlockSpec((heads, 2 * hd, BLK), lambda i: (at, 0, i)),
            whole(heads, length, 2 * hd),
            whole(heads, hd, length),
            whole(heads, length, hd),
            pl.BlockSpec((heads, hd, BLK), lambda i: (at, 0, i)),
            pl.BlockSpec((heads, 1, BLK), lambda i: (at, 0, i)),
            pl.BlockSpec((1, heads * hd, BLK), lambda i: (i, at, 0)),
        ],
        out_specs=(
            pl.BlockSpec((heads, hd, BLK), lambda i: (0, 0, i)),
            all_out(heads, hd, length),
            all_out(heads, hd, length),
        ),
        compiler_params=params(),
        cost_estimate=cost(11 * heads),
        name="attention_backward",
    )(meta, lengths, qt, ka, kt, v, of, ls, go)


def qkv_back_body(
    heads, hd, meta, x_ref, *refs
):
    dqs, dks, dvs = refs[:heads], refs[heads : 2 * heads], refs[2 * heads : 3 * heads]
    w_ref, g_ref, b_ref, gq_ref, gk_ref, da_ref, db_ref, dw_ref, vec_ref, gain_ref, acc_ref = refs[3 * heads :]
    i = pl.program_id(0)
    wid = heads * hd

    @pl.when(i == 0)
    def _():
        acc_ref[...] = jnp.zeros_like(acc_ref)
        vec_ref[...] = jnp.zeros_like(vec_ref)
        gain_ref[...] = jnp.zeros_like(gain_ref)

    hat, _ = norm_rows(x_ref[...].astype(F32))
    first = (hat * g_ref[...] + b_ref[...]).astype(BF16)
    qk = mm(w_ref[: 2 * wid, :], first, NT)
    pieces = []
    for at, gain, grad in ((0, gq_ref, dqs), (1, gk_ref, dks)):
        for h in range(heads):
            unit, inv = norm_cols(qk[at * wid + h * hd : at * wid + (h + 1) * hd])
            gy = grad[h][0]
            gain_ref[at] += gy * unit
            e = gy * gain[...]
            pieces.append(
                inv
                * (
                    e
                    - jnp.mean(e, axis=0, keepdims=True)
                    - unit * jnp.mean(e * unit, axis=0, keepdims=True)
                )
            )
    for h in range(heads):
        pieces.append(dvs[h][0])
    grad = jnp.concatenate(pieces, axis=0).astype(BF16)
    acc_ref[...] += mm(grad, first)
    back = mm(grad, w_ref[...], TN)
    vec_ref[0] += jnp.sum((back * hat).reshape(BLK // 8, 8, -1), axis=0)
    vec_ref[1] += jnp.sum(back.reshape(BLK // 8, 8, -1), axis=0)
    half = back.shape[1] // 2
    da_ref[0] = back[:, :half].astype(BF16)
    db_ref[0] = back[:, half:].astype(BF16)

    @pl.when(i == pl.num_programs(0) - 1)
    def _():
        dw_ref[...] = acc_ref[...].astype(BF16)


def qkv_back(meta, x, dq, dk, dv, w_t, gain, bias, gq, gk, heads, hd):
    length, width = x.shape
    blocks = length // BLK
    whole = lambda *shape: pl.BlockSpec(shape, lambda i, m: (0,) * len(shape))
    part = pl.BlockSpec((1, hd, BLK), lambda i, m: (0, 0, i))
    grads = pl.BlockSpec((1, BLK, width // 2), lambda i, m: (jnp.bitwise_xor(i, m[0]), 0, 0))
    return pl.pallas_call(
        functools.partial(qkv_back_body, heads, hd),
        grid_spec=pltpu.PrefetchScalarGridSpec(
            num_scalar_prefetch=1,
            grid=(blocks,),
            in_specs=[
                pl.BlockSpec((BLK, width), lambda i, m: (i, 0)),
                *([part] * (3 * heads)),
                whole(*w_t.shape),
                whole(1, width),
                whole(1, width),
                whole(hd, 1),
                whole(hd, 1),
            ],
            out_specs=(
                grads,
                grads,
                whole(*w_t.shape),
                whole(2, 8, width),
                whole(2, hd, BLK),
            ),
            scratch_shapes=[pltpu.VMEM(w_t.shape, F32)],
        ),
        out_shape=(
            jax.ShapeDtypeStruct((blocks, BLK, width // 2), BF16),
            jax.ShapeDtypeStruct((blocks, BLK, width // 2), BF16),
            jax.ShapeDtypeStruct(w_t.shape, BF16),
            jax.ShapeDtypeStruct((2, 8, width), F32),
            jax.ShapeDtypeStruct((2, hd, BLK), F32),
        ),
        compiler_params=params(),
        cost_estimate=cost(17),
        name="qkv_backward",
    )(meta, x, *dq, *dk, *dv, w_t, gain, bias, gq, gk)


def gelu_pair(u):
    a = jnp.abs(u)
    t = 1.0 / (1.0 + (0.3275911 * 0.7071067811865476) * a)
    poly = 1.061405429 * t - 1.453152027
    poly = poly * t + 1.421413741
    poly = poly * t - 0.284496736
    poly = poly * t + 0.254829592
    bell = jnp.exp(-0.5 * (u * u))
    tail = (0.5 * poly) * t * bell
    cdf = jnp.where(u >= 0.0, 1.0 - tail, tail)
    return u * cdf, cdf + u * (bell * 0.3989422804014327)


def ffn(meta, attn_t, x, dy, valid, gain, bias, wo, wo_p, up, up_p, dn, dn_p):
    tokens, width = x.shape
    hidden = up.shape[1]
    fc = 512
    steps = hidden // fc
    near = steps // 2
    packs, _, lanes = attn_t.shape
    whole = lambda *shape: pl.BlockSpec(shape, lambda i, m: (0,) * len(shape))
    ups = pl.BlockSpec((width // 2, fc), lambda i, m: (0, lax.rem(m[2] * near + i, steps)))
    acts = pl.BlockSpec((tokens, fc), lambda i, m: (0, lax.rem(m[2] * near + i, steps)))
    half = width // 2

    def body(meta, *refs):
        (at_ref, x_ref, dy_ref, valid_ref, g_ref, b_ref, wo_own, wo_peer, up_own, up_peer, dn_own, dn_peer) = refs[:12]
        (out_ref, gm_ref, gb_ref, h2_ref, act_ref, dup_ref, da_ref, vec_ref) = refs[12:20]
        (mid_s, acc_s, own_s, peer_s, gown_s, gpeer_s) = refs[20:]
        i = pl.program_id(0)
        core = meta[2]
        zero = core == 0

        @pl.when(i == 0)
        def _():
            for p in range(packs):
                rows = pl.ds(p * lanes, lanes)
                own = at_ref[p, pl.ds(pl.multiple_of(core * half, half), half), :]
                peer = at_ref[p, pl.ds(pl.multiple_of((1 - core) * half, half), half), :]
                mid = x_ref[rows, :].astype(F32) + mm(own, wo_own[...], TN) + mm(peer, wo_peer[...], TN)
                mid_s[rows, :] = mid
                acc_s[rows, :] = mid
                hat, _ = norm_rows(mid)
                second = (hat * g_ref[...] + b_ref[...]).astype(BF16)
                h2_ref[rows, :] = second
                lo, hi = second[:, :half], second[:, half:]
                own_s[rows, :] = jnp.where(zero, lo, hi)
                peer_s[rows, :] = jnp.where(zero, hi, lo)
            gown_s[...] = jnp.zeros_like(gown_s)
            gpeer_s[...] = jnp.zeros_like(gpeer_s)

        down = jnp.where(i < near, dn_own[...], dn_peer[...])
        upper = mm(own_s[...], up_own[...]) + mm(peer_s[...], up_peer[...])
        act, slope = gelu_pair(upper)
        act = act.astype(BF16)
        grad = (mm(dy_ref[...], down, NT) * slope).astype(BF16)
        act_ref[...] = act
        dup_ref[...] = grad
        acc_s[...] += mm(act, down)
        gown_s[...] += mm(grad, up_own[...], NT)
        gpeer_s[...] += mm(grad, up_peer[...], NT)

        @pl.when(i == steps - 1)
        def _():
            out_ref[...] = acc_s[...].astype(BF16)
            vec = [jnp.zeros((8, width), F32), jnp.zeros((8, width), F32)]
            for p in range(packs):
                rows = pl.ds(p * lanes, lanes)
                hat, inv = norm_rows(mid_s[rows, :])
                a, b = gown_s[rows, :], gpeer_s[rows, :]
                gy = jnp.concatenate([jnp.where(zero, a, b), jnp.where(zero, b, a)], axis=1)
                vec[0] = vec[0] + jnp.sum((gy * hat).reshape(lanes // 8, 8, width), axis=0)
                vec[1] = vec[1] + jnp.sum(gy.reshape(lanes // 8, 8, width), axis=0)
                e = gy * g_ref[...]
                gm = dy_ref[rows, :].astype(F32) + inv * (
                    e
                    - jnp.mean(e, axis=-1, keepdims=True)
                    - hat * jnp.mean(e * hat, axis=-1, keepdims=True)
                )
                gm_ref[rows, :] = gm
                gb = gm.astype(BF16)
                gb_ref[rows, :] = gb
                ok = valid_ref[p]
                da_ref[p, pl.ds(pl.multiple_of(core * half, half), half), :] = (
                    mm(wo_own[...], gb, NT) * ok
                ).astype(BF16)
                da_ref[p, pl.ds(pl.multiple_of((1 - core) * half, half), half), :] = (
                    mm(wo_peer[...], gb, NT) * ok
                ).astype(BF16)
            vec_ref[0] = vec[0]
            vec_ref[1] = vec[1]

    return pl.pallas_call(
        body,
        grid_spec=pltpu.PrefetchScalarGridSpec(
            num_scalar_prefetch=1,
            grid=(steps,),
            in_specs=[
                whole(*attn_t.shape),
                whole(tokens, width),
                whole(tokens, width),
                whole(*valid.shape),
                whole(1, width),
                whole(1, width),
                whole(half, width),
                whole(half, width),
                ups,
                ups,
                pl.BlockSpec((fc, width), lambda i, m: (jnp.minimum(i, near - 1), 0)),
                pl.BlockSpec((fc, width), lambda i, m: (jnp.maximum(i - near, 0), 0)),
            ],
            out_specs=(
                whole(tokens, width),
                whole(tokens, width),
                whole(tokens, width),
                whole(tokens, width),
                acts,
                acts,
                whole(*attn_t.shape),
                whole(2, 8, width),
            ),
            scratch_shapes=[
                pltpu.VMEM((tokens, width), F32),
                pltpu.VMEM((tokens, width), F32),
                pltpu.VMEM((tokens, half), BF16),
                pltpu.VMEM((tokens, half), BF16),
                pltpu.VMEM((tokens, half), F32),
                pltpu.VMEM((tokens, half), F32),
            ],
        ),
        out_shape=(
            jax.ShapeDtypeStruct((tokens, width), BF16),
            jax.ShapeDtypeStruct((tokens, width), F32),
            jax.ShapeDtypeStruct((tokens, width), BF16),
            jax.ShapeDtypeStruct((tokens, width), BF16),
            jax.ShapeDtypeStruct((tokens, hidden), BF16),
            jax.ShapeDtypeStruct((tokens, hidden), BF16),
            jax.ShapeDtypeStruct(attn_t.shape, BF16),
            jax.ShapeDtypeStruct((2, 8, width), F32),
        ),
        compiler_params=params(),
        cost_estimate=cost(25),
        name="ffn_both_ways",
    )(meta, attn_t, x, dy, valid, gain, bias, wo, wo_p, up, up_p, dn, dn_p)


def up_out_grads(meta, attn_t, gb, h2, dup, far=None):
    tokens, width = gb.shape
    hidden = dup.shape[1]
    half = width // 2
    packs, _, lanes = attn_t.shape
    n = hidden // width
    own = far is not None

    def column(j, m):
        bit = jnp.where(j < n // 2, m[4], 1 - m[4])
        return bit * (n // 2) + lax.rem(jnp.minimum(j, n - 1), n // 2)

    def body(meta, at_ref, gb_ref, h2_ref, dup_ref, *rest):
        j = pl.program_id(0)
        side = meta[2] if own else 1 - meta[2]

        def up():
            part = jnp.where(side == 0, h2_ref[:, :half], h2_ref[:, half:])
            return mm(part, dup_ref[...], TN)

        def out():
            rows = pl.ds(pl.multiple_of(side * half, half), half)
            total = jnp.zeros((half, width), F32)
            for p in range(packs):
                total = total + mm(at_ref[p, rows, :], gb_ref[p * lanes : (p + 1) * lanes, :])
            lo, hi = total[: half // 2], total[half // 2 :]
            return jnp.where(meta[5] == 0, lo, hi), jnp.where(meta[5] == 0, hi, lo)

        if own:
            far_ref, uk_ref, us_ref, ok_ref, os_ref = rest

            @pl.when(j < n // 2)
            def _():
                uk_ref[...] = (up() + far_ref[...].astype(F32)).astype(BF16)

            @pl.when((j >= n // 2) & (j < n))
            def _():
                us_ref[...] = (up() + far_ref[...].astype(F32)).astype(BF16)

            @pl.when(j == n)
            def _():
                keep, send = out()
                ok_ref[...] = (keep + far_ref[: half // 2].astype(F32)).astype(BF16)
                os_ref[...] = (send + far_ref[half // 2 :].astype(F32)).astype(BF16)
        else:
            (out_ref,) = rest

            @pl.when(j < n)
            def _():
                out_ref[...] = up().astype(BF16)

            @pl.when(j == n)
            def _():
                keep, send = out()
                out_ref[: half // 2] = keep.astype(BF16)
                out_ref[half // 2 :] = send.astype(BF16)

    whole = lambda *shape: pl.BlockSpec(shape, lambda j, m: (0,) * len(shape))
    block = lambda index: pl.BlockSpec((half, width), index)
    if own:
        out_specs = (
            block(lambda j, m: (0, jnp.minimum(j, n // 2 - 1))),
            block(lambda j, m: (0, jnp.clip(j - n // 2, 0, n // 2 - 1))),
            whole(half // 2, width),
            whole(half // 2, width),
        )
        shapes = [(half, hidden // 2)] * 2 + [(half // 2, width)] * 2
        out_shape = tuple(jax.ShapeDtypeStruct(shape, BF16) for shape in shapes)
    else:
        out_specs = block(lambda j, m: (0, j))
        out_shape = jax.ShapeDtypeStruct((half, hidden + width), BF16)
    return pl.pallas_call(
        body,
        grid_spec=pltpu.PrefetchScalarGridSpec(
            num_scalar_prefetch=1,
            grid=(n + 1,),
            in_specs=[
                whole(*attn_t.shape),
                whole(tokens, width),
                whole(tokens, width),
                pl.BlockSpec((tokens, width), lambda j, m: (0, column(j, m))),
                *([block(lambda j, m: (0, j))] if own else []),
            ],
            out_specs=out_specs,
        ),
        out_shape=out_shape,
        compiler_params=params(),
        cost_estimate=cost(7),
        name="up_out_gradient",
    )(meta, attn_t, gb, h2, dup, *([far] if own else []))


def down_grads(meta, act, dy, far=None):
    tokens, width = dy.shape
    half = width // 2
    n = act.shape[1] // 2 // half
    own = far is not None

    def body(meta, act_ref, dy_ref, *rest):
        value = mm(act_ref[...], dy_ref[...], TN)
        if own:
            far_ref, keep_ref, send_ref = rest
            j = pl.program_id(0)
            value = (value + far_ref[...].astype(F32)).astype(BF16)

            @pl.when(j < n // 2)
            def _():
                keep_ref[...] = value

            @pl.when(j >= n // 2)
            def _():
                send_ref[...] = value
        else:
            (out_ref,) = rest
            out_ref[...] = value.astype(BF16)

    def column(j, m):
        side = m[2] if own else 1 - m[2]
        bit = jnp.where(j < n // 2, m[3], 1 - m[3])
        return side * n + bit * (n // 2) + lax.rem(j, n // 2)

    block = lambda index: pl.BlockSpec((half, width), index)
    if own:
        out_specs = (
            block(lambda j, m: (jnp.minimum(j, n // 2 - 1), 0)),
            block(lambda j, m: (jnp.maximum(j - n // 2, 0), 0)),
        )
        out_shape = (jax.ShapeDtypeStruct((n // 2 * half, width), BF16),) * 2
    else:
        out_specs = block(lambda j, m: (j, 0))
        out_shape = jax.ShapeDtypeStruct((n * half, width), BF16)
    return pl.pallas_call(
        body,
        grid_spec=pltpu.PrefetchScalarGridSpec(
            num_scalar_prefetch=1,
            grid=(n,),
            in_specs=[
                pl.BlockSpec((tokens, half), lambda j, m: (0, column(j, m))),
                pl.BlockSpec((tokens, width), lambda j, m: (0, 0)),
                *([block(lambda j, m: (j, 0))] if own else []),
            ],
            out_specs=out_specs,
        ),
        out_shape=out_shape,
        compiler_params=params(),
        cost_estimate=cost(6),
        name="down_gradient",
    )(meta, act, dy, *([far] if own else []))


def assemble(meta, downs, ups, outs):
    half, width = outs[0].shape[0] * 2, outs[0].shape[1]
    hidden = ups[0].shape[1] * 2
    cut = width // 2

    def body(meta, down_a, down_b, up_a, up_b, out_a, out_b, down_ref, up_ref, out_ref):
        i = pl.program_id(0)

        def place(ref, value, swapped):
            lo, hi = value[:, :cut].astype(F32), value[:, cut:].astype(F32)
            ref[:, :cut] = jnp.where(swapped == 0, lo, hi)
            ref[:, cut:] = jnp.where(swapped == 0, hi, lo)

        down_own = i // 2 == meta[3]
        place(down_ref, jnp.where(down_own, down_a[...], down_b[...]), meta[5])
        up_own = i // 2 == meta[4]
        place(up_ref, jnp.where(up_own, up_a[...], up_b[...]), meta[3])

        @pl.when(i == 0)
        def _():
            quarter = half // 4
            for z in range(2):
                for x in range(2):
                    rows = pl.ds(pl.multiple_of(jnp.bitwise_xor(meta[3], x) * quarter, quarter), quarter)
                    value = jnp.where(meta[5] == z, out_a[rows, :], out_b[rows, :])
                    place(out_ref.at[pl.ds((2 * z + x) * quarter, quarter)], value, meta[4])

    whole = lambda *shape: pl.BlockSpec(shape, lambda i, m: (0,) * len(shape))
    down = pl.BlockSpec((half, width), lambda i, m: (jnp.bitwise_xor(lax.rem(i, 2), m[4]), 0))
    up = pl.BlockSpec((half, width), lambda i, m: (0, jnp.bitwise_xor(lax.rem(i, 2), m[5])))
    return pl.pallas_call(
        body,
        grid_spec=pltpu.PrefetchScalarGridSpec(
            num_scalar_prefetch=1,
            grid=(4,),
            in_specs=[down, down, up, up, whole(*outs[0].shape), whole(*outs[0].shape)],
            out_specs=(
                pl.BlockSpec((half, width), lambda i, m: (i, 0)),
                pl.BlockSpec((half, width), lambda i, m: (0, i)),
                whole(half, width),
            ),
        ),
        out_shape=(
            jax.ShapeDtypeStruct((4 * half, width), F32),
            jax.ShapeDtypeStruct((half, hidden), F32),
            jax.ShapeDtypeStruct((half, width), F32),
        ),
        compiler_params=params(),
        cost_estimate=cost(7),
        name="weight_gradients",
    )(meta, *downs, *ups, *outs)


def finish_body(x_ref, gm_ref, back_ref, g_ref, out_ref):
    hat, inv = norm_rows(x_ref[...].astype(F32))
    e = back_ref[...].astype(F32) * g_ref[...]
    out_ref[...] = gm_ref[...] + inv * (
        e - jnp.mean(e, axis=-1, keepdims=True) - hat * jnp.mean(e * hat, axis=-1, keepdims=True)
    )


def finish(x, gm, back, gain):
    tokens, width = x.shape
    rows = pl.BlockSpec((128, width), lambda i: (i, 0))
    return pl.pallas_call(
        finish_body,
        grid=(tokens // 128,),
        in_specs=[rows, rows, rows, pl.BlockSpec((1, width), lambda i: (0, 0))],
        out_specs=rows,
        out_shape=jax.ShapeDtypeStruct((tokens, width), F32),
        compiler_params=params(),
        cost_estimate=cost(4),
        name="first_norm_backward",
    )(x, gm, back, gain)


def flip(value, axis, mask):
    size = lax.axis_size(axis)
    return lax.ppermute(value, axis, [(i, i ^ mask) for i in range(size)])


def bit(axis, mask):
    return (lax.axis_index(axis) // mask) % 2


def halves(value, which, axis=0):
    n = value.shape[axis] // 2
    keep = lax.dynamic_slice_in_dim(value, which * n, n, axis)
    send = lax.dynamic_slice_in_dim(value, (1 - which) * n, n, axis)
    return keep, send


def join(own, other, which, axis=0):
    return jnp.where(
        which == 0,
        jnp.concatenate([own, other], axis=axis),
        jnp.concatenate([other, own], axis=axis),
    )


def add(a, b):
    return (a.astype(F32) + b.astype(F32)).astype(BF16)


def on_device(
    tokens, lengths, ln1_gain, ln1_bias, qkv_weight, q_gain, k_gain, out_weight,
    ln2_gain, ln2_bias, up_weight, down_weight, cotangent,
):
    micro, rows, local, width = tokens.shape
    n = lax.axis_size("seq")
    length = local * n
    every = micro * rows
    team = n // every
    heads = H // team
    hd = width // H
    half = width // 2
    idx = lax.axis_index("seq")
    core = lax.axis_index("fsdp")
    row, member = idx // team, idx % team
    direct = every == 2 and team == 4
    lengths = lengths.reshape(every, lengths.shape[-1])
    mine = tokens.reshape(every, local, width)

    def swap(value):
        return flip(value, "fsdp", 1)

    vec = jnp.concatenate([ln1_gain, ln1_bias, ln2_gain, ln2_bias, q_gain, k_gain])[None]
    vec_p = swap(vec)
    ordered = jnp.where(core == 0, jnp.concatenate([vec, vec_p]), jnp.concatenate([vec_p, vec])).astype(F32)
    g1, b1, g2, b2 = (ordered[:, k * half : (k + 1) * half].reshape(1, width) for k in range(4))
    gq = ordered[:, 4 * half : 4 * half + hd // 2].reshape(hd, 1)
    gk = ordered[:, 4 * half + hd // 2 :].reshape(hd, 1)

    w_own = lax.dynamic_slice_in_dim(
        qkv_weight.reshape(half, 3, width), member * heads * hd, heads * hd, 2
    ).reshape(half, 3 * heads * hd)
    w_t = jnp.transpose(join(w_own, swap(w_own), core))

    if direct:
        near = lax.dynamic_index_in_dim(mine, row, 0, keepdims=False)
        away = lax.dynamic_index_in_dim(mine, 1 - row, 0, keepdims=False)
        far = flip(away, "seq", 4)
        cut = local // 2

        def spread(own):
            one, two = flip(own, "seq", 1), flip(own, "seq", 2)
            three = jnp.concatenate([flip(two[:cut], "seq", 1), flip(one[cut:], "seq", 2)], axis=0)
            return [own, one, two, three]

        slots = spread(near) + spread(far)
        spot = idx
    else:
        same_member = [[q * team + p for q in range(every)] for p in range(team)]
        same_row = [[q * team + p for p in range(team)] for q in range(every)]
        got = lax.all_to_all(mine, "seq", 0, 0, axis_index_groups=same_member, tiled=True)
        got = lax.all_gather(got, "seq", axis_index_groups=same_row)
        whole = jnp.swapaxes(got, 0, 1).reshape(length, width)
        slots = [whole[s * (length // 8) : (s + 1) * (length // 8)] for s in range(8)]
        spot = jnp.int32(0)
    meta = jnp.stack([spot, row, core, bit("rep", 1), bit("seq", 1), bit("seq", 2)]).astype(jnp.int32)

    out_p, up_p, down_p = swap(out_weight), swap(up_weight), swap(down_weight)

    with jax.named_scope("forward_attention"):
        qt, ka, kt, v, vt, x_row = make_qkv(meta, lengths, slots, w_t, g1, b1, gq, gk, heads, hd)
        attn, attn_f, logsum = attend(meta, lengths, qt, ka, vt, heads, hd)

    def exchange(value):
        return lax.all_to_all(value, "seq", 0, 0, tiled=True)

    packs = every * local // BLK
    if direct:
        attn_t = exchange(attn).reshape(packs, width, BLK)
    else:
        cut = jnp.moveaxis(attn.reshape(BLK * 0 + 8, heads * hd, BLK // local, local), 2, 1)
        got = exchange(cut.reshape(n, heads * hd, local))
        got = got.reshape(packs, every // packs, width, local)
        attn_t = jnp.swapaxes(got, 1, 2).reshape(packs, width, BLK)

    total = jnp.sum(lengths[:, :-1], axis=-1)
    places = idx * local + jnp.arange(local, dtype=jnp.int32)
    valid = (places[None] < total[:, None]).astype(F32).reshape(packs, 1, BLK)
    x_home = tokens.reshape(every * local, width)
    dy = cotangent.reshape(every * local, width)

    with jax.named_scope("feed_forward"):
        output, grad_mid, grad_branch, h2, act, dup, grad_attn, vec2 = ffn(
            meta, attn_t, x_home, dy, valid, g2, b2, out_weight, out_p, up_weight, up_p, down_weight, down_p
        )
    if direct:
        grad_o = exchange(grad_attn.reshape(n, heads * hd, BLK))
    else:
        cut = jnp.swapaxes(grad_attn.reshape(packs, width, every // packs, local), 1, 2)
        got = exchange(cut.reshape(n, heads * hd, local))
        got = got.reshape(8, BLK // local, heads * hd, local)
        grad_o = jnp.swapaxes(got, 1, 2).reshape(8, heads * hd, BLK)

    masks = [1 << k for k in range(n.bit_length() - 1)]
    with jax.named_scope("weight_gradients"):
        far_u = swap(up_out_grads(meta, attn_t, grad_branch, h2, dup))
        far_d = swap(down_grads(meta, act, dy))
        up_k, up_s, out_k, out_s = up_out_grads(meta, attn_t, grad_branch, h2, dup, far_u)
        down_k, down_s = down_grads(meta, act, dy, far_d)
        grad_o, up_k, up_s, out_k, out_s, down_k, down_s = lax.optimization_barrier(
            (grad_o, up_k, up_s, out_k, out_s, down_k, down_s)
        )
        x, y, z = ("rep", 1), ("seq", 1), ("seq", 2)

        def next_half(keep, got, way, axis):
            return halves(add(keep, got), bit(*way), axis)

        down_k, down_s = next_half(down_k, flip(down_s, *x), y, 0)
        up_k, up_s = next_half(up_k, flip(up_s, *y), z, 1)
        out_k, out_s = next_half(out_k, flip(out_s, *z), x, 0)
        down_k, down_s = next_half(down_k, flip(down_s, *y), z, 1)
        up_k, up_s = next_half(up_k, flip(up_s, *z), x, 1)
        out_k, out_s = next_half(out_k, flip(out_s, *x), y, 1)
        down = add(down_k, flip(down_s, *z))
        up = add(up_k, flip(up_s, *x))
        out = add(out_k, flip(out_s, *y))
        if masks[2:]:
            sizes = [down.shape[0], up.shape[0]]
            every_piece = jnp.concatenate([down, up, out])
            for mask in masks[2:]:
                every_piece = add(every_piece, flip(every_piece, "seq", mask))
            down, up, out = jnp.split(every_piece, [sizes[0], sizes[0] + sizes[1]])
        down = jnp.concatenate([down, flip(down, *z)], axis=1)
        up = jnp.concatenate([up, flip(up, *x)], axis=1)
        out = jnp.concatenate([out, flip(out, *y)], axis=1)
        down = jnp.concatenate([down, flip(down, *y)], axis=0)
        up = jnp.concatenate([up, flip(up, *z)], axis=1)
        out = jnp.concatenate([out, flip(out, *x)], axis=0)
        grad_down, grad_up, grad_out = assemble(
            meta, (down, flip(down, *x)), (up, flip(up, *y)), (out, flip(out, *z))
        )

    with jax.named_scope("backward_attention"):
        parts = [
            attend_back(meta, lengths, qt, ka, kt, v, attn_f, logsum, grad_o, h, 1, hd) for h in range(heads)
        ]
        dq, dk, dv = zip(*parts)
        back_a, back_b, dw_t, vec1, gains = qkv_back(
            meta, x_row, dq, dk, dv, w_t, g1, b1, gq, gk, heads, hd
        )

    if direct:

        def gather(parts):
            a = parts[0].reshape(2, 2, 2, local, half)
            b = parts[1].reshape(2, 2, 2, local, half)
            out = []
            for kind in (1, 0):
                a1 = add(a[kind, :, 0], flip(a[kind, :, 1], "seq", 1))
                b1 = add(b[kind, 0], flip(b[kind, 1], "seq", 2))
                a2 = add(a1[0], flip(a1[1], "seq", 2))
                b2 = add(b1[0], flip(b1[1], "seq", 1))
                out.append(jnp.concatenate([a2, b2], axis=1))
            return out

        far_sum, near_sum = gather((back_a, back_b))
        other = flip(far_sum, "seq", 4)
        back = jnp.where(
            row == 0, jnp.stack([near_sum, other]), jnp.stack([other, near_sum])
        ).reshape(every * local, width)
    else:
        whole = jnp.concatenate([back_a, back_b], axis=-1).reshape(every, team, local, width)
        whole = lax.psum_scatter(whole, "seq", scatter_dimension=1, axis_index_groups=same_row, tiled=True)
        got = lax.all_to_all(whole[:, 0], "seq", 0, 0, axis_index_groups=same_member, tiled=True)
        back = got.reshape(every * local, width)
    grad_tokens = finish(x_home, grad_mid, back, g1)

    with jax.named_scope("first_projection_gradient"):
        keep, send = halves(dw_t, core, 1)
        piece = add(keep, swap(send))
        keep, send = halves(piece, bit("rep", 1))
        piece = add(keep, flip(send, "rep", 1))
        for mask in masks:
            if mask >= team:
                piece = add(piece, flip(piece, "seq", mask))
        piece = piece[None]
        for mask in masks:
            if mask < team:
                piece = join(piece, flip(piece, "seq", mask), bit("seq", mask))
        piece = join(piece, flip(piece, "rep", 1), bit("rep", 1), 1)
        piece = piece.reshape(team, 3, heads * hd, half)
        grad_qkv = jnp.transpose(piece, (3, 1, 0, 2)).reshape(half, 3 * width).astype(F32)

    with jax.named_scope("vector_gradients"):
        small = jnp.concatenate([vec1, vec2]).sum(axis=1).reshape(4, 2, half)
        small = jnp.concatenate(
            [jnp.swapaxes(small, 0, 1).reshape(2, 4 * half)]
            + [gains[k].sum(axis=-1).reshape(2, hd // 2) for k in range(2)],
            axis=1,
        )
        small = lax.all_gather(small.reshape(-1), ("rep", "fsdp", "seq")).sum(axis=0).reshape(2, -1)
        small = jnp.where(core == 0, small[0], small[1])
        cuts = [small[k * half : (k + 1) * half] for k in range(4)]
        cuts += [small[4 * half : 4 * half + hd // 2], small[4 * half + hd // 2 :]]
    shape = tokens.shape
    return (
        output.reshape(shape), grad_tokens.reshape(shape), cuts[0], cuts[1], grad_qkv, cuts[4], cuts[5],
        grad_out, cuts[2], cuts[3], grad_up, grad_down,
    )


def solution(mesh):
    tok = P(None, ("rep", "fsdp"), "seq", None)
    one, two = P("fsdp"), P("fsdp", None)
    in_specs = (tok, P(None, ("rep", "fsdp"), None), one, one, two, one, one, two, one, one, two, two, tok)
    out_specs = (tok, tok, one, one, two, one, one, two, one, one, two, two)
    return jax.shard_map(on_device, mesh=mesh, in_specs=in_specs, out_specs=out_specs, check_vma=False)
```

```python
import functools

import jax
import jax.numpy as jnp
from jax import lax
from jax.experimental import pallas as pl
from jax.experimental.pallas import tpu as pltpu
from jax.sharding import PartitionSpec as P

H = 12
EPS = 1e-06
LOG2E = 1.4426950408889634
SHIFT = 512.0
BLK = 256
EXTRA = 32
NN = (((1,), (0,)), ((), ()))
NT = (((1,), (1,)), ((), ()))
TN = (((0,), (0,)), ((), ()))
F32 = jnp.float32
BF16 = jnp.bfloat16


def mm(a, b, dims=NN):
    return lax.dot_general(a, b, dims, preferred_element_type=F32)


def params(**kw):
    return pltpu.CompilerParams(vmem_limit_bytes=60 * 1024 * 1024, **kw)


def cost(us):
    return pl.CostEstimate(flops=int(us * 0.35e9), bytes_accessed=1024, transcendentals=0)


def norm_rows(v):
    center = jnp.mean(v, axis=-1, keepdims=True)
    centred = v - center
    inv = lax.rsqrt(jnp.mean(centred * centred, axis=-1, keepdims=True) + EPS)
    return centred * inv, inv


def norm_cols(v):
    center = jnp.mean(v, axis=0, keepdims=True)
    centred = v - center
    inv = lax.rsqrt(jnp.mean(centred * centred, axis=0, keepdims=True) + EPS)
    return centred * inv, inv


def bounds_of(len_ref, row):
    out = []
    total = jnp.int32(0)
    for j in range(len_ref.shape[1] - 1):
        total = total + len_ref[row, j]
        out.append(total)
    return out


def qkv_body(heads, hd, meta, len_ref, *refs):
    xs = refs[:8]
    w_ref, g_ref, b_ref, gq_ref, gk_ref = refs[8:13]
    qt_ref, ka_ref, kt_ref, v_ref, vt_ref, x_ref = refs[13:]
    wid = heads * hd
    spot, row = meta[0], meta[1]
    bounds = bounds_of(len_ref, row)
    for s in range(8):
        c = jnp.bitwise_xor(spot, s)
        cols = pl.ds(pl.multiple_of(c * BLK, BLK), BLK)
        x = xs[s][...]
        x_ref[cols, :] = x
        hat, _ = norm_rows(x.astype(F32))
        first = (hat * g_ref[...] + b_ref[...]).astype(BF16)
        qkv = mm(w_ref[...], first, NT)
        place = c * BLK + lax.broadcasted_iota(jnp.int32, (8, BLK), 1)
        ident = jnp.zeros((8, BLK), jnp.int32)
        place_k = c * BLK + lax.broadcasted_iota(jnp.int32, (BLK, 128), 0)
        ident_k = jnp.zeros((BLK, 128), jnp.int32)
        for bound in bounds:
            ident = ident + (place >= bound).astype(jnp.int32)
            ident_k = ident_k + (place_k >= bound).astype(jnp.int32)
        which = lax.broadcasted_iota(jnp.int32, (8, BLK), 0)
        hot = jnp.where((ident == which) & (which < len(bounds)), 16.0, 0.0)
        hot = jnp.concatenate([hot, jnp.zeros((hd - 8, BLK), F32)], axis=0)
        lane = lax.broadcasted_iota(jnp.int32, (BLK, 128), 1) - hd
        hot_k = jnp.where((ident_k == lane) & (lane < len(bounds)), SHIFT / 16.0, 0.0)
        for h in range(heads):
            q, _ = norm_cols(qkv[h * hd : (h + 1) * hd])
            k, _ = norm_cols(qkv[wid + h * hd : wid + (h + 1) * hd])
            q = (q * gq_ref[...]).astype(BF16).astype(F32) * (hd**-0.5)
            k = k * gk_ref[...]
            v = qkv[2 * wid + h * hd : 2 * wid + (h + 1) * hd]
            qt_ref[h, :, cols] = jnp.concatenate([q, hot], axis=0).astype(BF16)
            kt_ref[h, :, cols] = k.astype(BF16)
            vt_ref[h, :, cols] = v.astype(BF16)
            both = jnp.transpose(jnp.concatenate([k, v], axis=0))
            ka_ref[h, cols, :] = jnp.where(lane < 0, both, hot_k).astype(BF16)
            v_ref[h, cols, :] = both[:, hd:].astype(BF16)


def make_qkv(meta, lengths, slots, w_t, gain, bias, gq, gk, heads, hd):
    length = 8 * slots[0].shape[0]
    width = slots[0].shape[1]
    smem = pl.BlockSpec(memory_space=pltpu.SMEM)
    vmem = pl.BlockSpec(memory_space=pltpu.VMEM)
    return pl.pallas_call(
        functools.partial(qkv_body, heads, hd),
        out_shape=(
            jax.ShapeDtypeStruct((heads, 2 * hd, length), BF16),
            jax.ShapeDtypeStruct((heads, length, 2 * hd), BF16),
            jax.ShapeDtypeStruct((heads, hd, length), BF16),
            jax.ShapeDtypeStruct((heads, length, hd), BF16),
            jax.ShapeDtypeStruct((heads, hd, length), BF16),
            jax.ShapeDtypeStruct((length, width), BF16),
        ),
        in_specs=[smem, smem] + [vmem] * 13,
        out_specs=(vmem,) * 6,
        compiler_params=params(),
        cost_estimate=cost(12),
        name="qkv_forward",
    )(meta, lengths, *slots, w_t, gain, bias, gq, gk)


def block_range(bounds, i):
    first = i * BLK
    last = first + BLK - 1
    lo = jnp.int32(0)
    hi = bounds[-1]
    for bound in bounds:
        lo = jnp.where(first >= bound, bound, lo)
    for bound in bounds[::-1]:
        hi = jnp.where(last < bound, bound, hi)
    lo_b = lo // BLK
    hi_b = (hi + BLK - 1) // BLK
    return lo_b, jnp.where(first >= bounds[-1], lo_b, hi_b)


def attend_body(heads, hd, meta, len_ref, qt_ref, ka_ref, vt_ref, o_ref, of_ref, ls_ref):
    i = pl.program_id(0)
    bounds = bounds_of(len_ref, meta[1])
    lo, hi = block_range(bounds, i)

    def step(b, carry):
        rows = pl.ds(pl.multiple_of(b * BLK, BLK), BLK)
        out = []
        for h in range(heads):
            acc, total = carry[h]
            scores = mm(ka_ref[h, rows, :], qt_ref[h])
            expo = jnp.exp2(scores * LOG2E - SHIFT * LOG2E)
            total = total + jnp.sum(expo.reshape(BLK // 8, 8, BLK), axis=0)
            acc = acc + mm(vt_ref[h, :, rows], expo.astype(BF16))
            out.append((acc, total))
        return tuple(out)

    init = tuple((jnp.zeros((hd, BLK), F32), jnp.zeros((8, BLK), F32)) for _ in range(heads))
    done = lax.fori_loop(lo, hi, step, init)
    for h in range(heads):
        acc, total = done[h]
        total = jnp.sum(total, axis=0, keepdims=True)
        live = total > 0.0
        safe = jnp.where(live, total, 1.0)
        out = jnp.where(live, acc * (1.0 / safe), 0.0)
        o_ref[0, h * hd : (h + 1) * hd, :] = out.astype(BF16)
        of_ref[h] = out
        ls_ref[h] = jnp.log2(safe) + SHIFT * LOG2E


def attend(meta, lengths, qt, ka, vt, heads, hd):
    length = qt.shape[2]
    blocks = length // BLK
    smem = pl.BlockSpec(memory_space=pltpu.SMEM)
    return pl.pallas_call(
        functools.partial(attend_body, heads, hd),
        grid=(blocks,),
        out_shape=(
            jax.ShapeDtypeStruct((blocks, heads * hd, BLK), BF16),
            jax.ShapeDtypeStruct((heads, hd, length), F32),
            jax.ShapeDtypeStruct((heads, 1, length), F32),
        ),
        in_specs=[
            smem,
            smem,
            pl.BlockSpec((heads, 2 * hd, BLK), lambda i: (0, 0, i)),
            pl.BlockSpec((heads, length, 2 * hd), lambda i: (0, 0, 0)),
            pl.BlockSpec((heads, hd, length), lambda i: (0, 0, 0)),
        ],
        out_specs=(
            pl.BlockSpec((1, heads * hd, BLK), lambda i: (i, 0, 0)),
            pl.BlockSpec((heads, hd, BLK), lambda i: (0, 0, i)),
            pl.BlockSpec((heads, 1, BLK), lambda i: (0, 0, i)),
        ),
        compiler_params=params(),
        cost_estimate=cost(25),
        name="attention_forward",
    )(meta, lengths, qt, ka, vt)


def attend_back_body(
    heads, hd, meta, len_ref, qt_ref, ka_ref, kt_ref, v_ref, of_ref, ls_ref, go_ref, dq_ref, dk_ref, dv_ref
):
    i = pl.program_id(0)
    bounds = bounds_of(len_ref, meta[1])
    lo, hi = block_range(bounds, i)

    @pl.when(i == 0)
    def _():
        dk_ref[...] = jnp.zeros_like(dk_ref)
        dv_ref[...] = jnp.zeros_like(dv_ref)

    inner = []
    for h in range(heads):
        go = go_ref[0, h * hd : (h + 1) * hd, :].astype(F32)
        inner.append(jnp.sum(go * of_ref[h], axis=0, keepdims=True))

    def step(b, carry):
        rows = pl.ds(pl.multiple_of(b * BLK, BLK), BLK)
        out = []
        for h in range(heads):
            go = go_ref[0, h * hd : (h + 1) * hd, :]
            qt = qt_ref[h]
            scores = mm(ka_ref[h, rows, :], qt)
            probs = jnp.exp2(scores * LOG2E - ls_ref[h])
            grad_probs = mm(v_ref[h, rows, :], go)
            grad_scores = (probs * (grad_probs - inner[h])).astype(BF16)
            dv_ref[h, :, rows] += mm(go, probs.astype(BF16), NT)
            dk_ref[h, :, rows] += mm(qt[:hd], grad_scores, NT)
            out.append(carry[h] + mm(kt_ref[h, :, rows], grad_scores))
        return tuple(out)

    done = lax.fori_loop(lo, hi, step, tuple(jnp.zeros((hd, BLK), F32) for _ in range(heads)))
    for h in range(heads):
        dq_ref[h] = done[h] * (hd**-0.5)


def attend_back(meta, lengths, qt, ka, kt, v, of, ls, go, at, heads, hd):
    length = qt.shape[2]
    blocks = length // BLK
    smem = pl.BlockSpec(memory_space=pltpu.SMEM)
    whole = lambda *shape: pl.BlockSpec(shape, lambda i: (at, 0, 0))
    all_out = lambda *shape: pl.BlockSpec(shape, lambda i: (0, 0, 0))
    return pl.pallas_call(
        functools.partial(attend_back_body, heads, hd),
        grid=(blocks,),
        out_shape=tuple(jax.ShapeDtypeStruct((heads, hd, length), F32) for _ in range(3)),
        in_specs=[
            smem,
            smem,
            pl.BlockSpec((heads, 2 * hd, BLK), lambda i: (at, 0, i)),
            whole(heads, length, 2 * hd),
            whole(heads, hd, length),
            whole(heads, length, hd),
            pl.BlockSpec((heads, hd, BLK), lambda i: (at, 0, i)),
            pl.BlockSpec((heads, 1, BLK), lambda i: (at, 0, i)),
            pl.BlockSpec((1, heads * hd, BLK), lambda i: (i, at, 0)),
        ],
        out_specs=(
            pl.BlockSpec((heads, hd, BLK), lambda i: (0, 0, i)),
            all_out(heads, hd, length),
            all_out(heads, hd, length),
        ),
        compiler_params=params(),
        cost_estimate=cost(11 * heads),
        name="attention_backward",
    )(meta, lengths, qt, ka, kt, v, of, ls, go)


def qkv_back_body(
    heads, hd, meta, x_ref, *refs
):
    dqs, dks, dvs = refs[:heads], refs[heads : 2 * heads], refs[2 * heads : 3 * heads]
    w_ref, g_ref, b_ref, gq_ref, gk_ref, vec2_ref, da_ref, db_ref, dw_ref, acc_ref, vec_ref, gain_ref = refs[3 * heads :]
    i = pl.program_id(0)
    wid = heads * hd

    @pl.when(i == 0)
    def _():
        acc_ref[...] = jnp.zeros_like(acc_ref)
        vec_ref[...] = jnp.zeros_like(vec_ref)
        gain_ref[...] = jnp.zeros_like(gain_ref)

    hat, _ = norm_rows(x_ref[...].astype(F32))
    first = (hat * g_ref[...] + b_ref[...]).astype(BF16)
    qk = mm(w_ref[: 2 * wid, :], first, NT)
    pieces = []
    for at, gain, grad in ((0, gq_ref, dqs), (1, gk_ref, dks)):
        for h in range(heads):
            unit, inv = norm_cols(qk[at * wid + h * hd : at * wid + (h + 1) * hd])
            gy = grad[h][0]
            gain_ref[at] += gy * unit
            e = gy * gain[...]
            pieces.append(
                inv
                * (
                    e
                    - jnp.mean(e, axis=0, keepdims=True)
                    - unit * jnp.mean(e * unit, axis=0, keepdims=True)
                )
            )
    for h in range(heads):
        pieces.append(dvs[h][0])
    grad = jnp.concatenate(pieces, axis=0).astype(BF16)
    acc_ref[...] += mm(grad, first)
    back = mm(grad, w_ref[...], TN)
    vec_ref[0] += jnp.sum((back * hat).reshape(BLK // 8, 8, -1), axis=0)
    vec_ref[1] += jnp.sum(back.reshape(BLK // 8, 8, -1), axis=0)
    half = back.shape[1] // 2
    da_ref[0] = back[:, :half].astype(BF16)
    db_ref[0] = back[:, half:].astype(BF16)

    @pl.when(i == pl.num_programs(0) - 1)
    def _():
        dw_ref[: 3 * wid, :] = acc_ref[...].astype(BF16)
        lines = [jnp.sum(ref[k], axis=0, keepdims=True) for ref in (vec_ref, vec2_ref) for k in range(2)]
        width = dw_ref.shape[1]
        lane = lax.broadcasted_iota(jnp.int32, (hd, width), 1)
        item = lax.broadcasted_iota(jnp.int32, (hd, width), 0)
        spread = jnp.where(item < hd // 2, item, item - hd // 2 + width // 2)
        line = jnp.zeros((8, width), F32)
        for k in range(2):
            total = lax.dot_general(
                jnp.ones((8, BLK), F32), gain_ref[k], NT, precision=lax.Precision.HIGHEST, preferred_element_type=F32
            )
            pick = (lane == spread + k * (hd // 2)).astype(F32)
            line = line + lax.dot_general(
                total, pick, NN, precision=lax.Precision.HIGHEST, preferred_element_type=F32
            )
        lines.append(line[:1])
        place = lax.broadcasted_iota(jnp.int32, (EXTRA, width), 0)
        below = jnp.zeros((EXTRA, width), F32)
        for k, one in enumerate(lines):
            below = jnp.where(place == k, one, below)
        dw_ref[3 * wid :, :] = below.astype(BF16)


def qkv_back(meta, x, dq, dk, dv, w_t, gain, bias, gq, gk, vec2, heads, hd):
    length, width = x.shape
    blocks = length // BLK
    whole = lambda *shape: pl.BlockSpec(shape, lambda i, m: (0,) * len(shape))
    part = pl.BlockSpec((1, hd, BLK), lambda i, m: (0, 0, i))
    grads = pl.BlockSpec((1, BLK, width // 2), lambda i, m: (jnp.bitwise_xor(i, m[0]), 0, 0))
    return pl.pallas_call(
        functools.partial(qkv_back_body, heads, hd),
        grid_spec=pltpu.PrefetchScalarGridSpec(
            num_scalar_prefetch=1,
            grid=(blocks,),
            in_specs=[
                pl.BlockSpec((BLK, width), lambda i, m: (i, 0)),
                *([part] * (3 * heads)),
                whole(*w_t.shape),
                whole(1, width),
                whole(1, width),
                whole(hd, 1),
                whole(hd, 1),
                whole(2, 8, width),
            ],
            out_specs=(
                grads,
                grads,
                whole(w_t.shape[0] + EXTRA, width),
            ),
            scratch_shapes=[
                pltpu.VMEM(w_t.shape, F32),
                pltpu.VMEM((2, 8, width), F32),
                pltpu.VMEM((2, hd, BLK), F32),
            ],
        ),
        out_shape=(
            jax.ShapeDtypeStruct((blocks, BLK, width // 2), BF16),
            jax.ShapeDtypeStruct((blocks, BLK, width // 2), BF16),
            jax.ShapeDtypeStruct((w_t.shape[0] + EXTRA, width), BF16),
        ),
        compiler_params=params(),
        cost_estimate=cost(17),
        name="qkv_backward",
    )(meta, x, *dq, *dk, *dv, w_t, gain, bias, gq, gk, vec2)


def assemble_qkv(meta, own, other, heads, hd):
    team, part, half = own.shape
    wid = heads * hd
    turned = team * wid

    def body(meta, own_ref, other_ref, out_ref, vec_ref, all_s):
        t = pl.program_id(0)

        @pl.when(t == 0)
        def _():
            first = meta[3] == 0
            for y in range(2):
                for z in range(2):
                    at = 2 * jnp.bitwise_xor(meta[4], y) + jnp.bitwise_xor(meta[5], z)
                    a, b = own_ref[at], other_ref[at]
                    all_s[2 * z + y, :part, :] = jnp.where(first, a, b)
                    all_s[2 * z + y, part:, :] = jnp.where(first, b, a)
            total = jnp.zeros((EXTRA, half), F32)
            for p in range(team):
                total = total + all_s[p, 3 * wid :, :].astype(F32)
            vec_ref[...] = total

        rows = pl.ds(pl.multiple_of(t * wid, wid), wid)
        piece = jnp.concatenate([all_s[p, rows, :] for p in range(team)], axis=0)
        out_ref[...] = jnp.transpose(piece.astype(F32))

    whole = lambda *shape: pl.BlockSpec(shape, lambda i, m: (0,) * len(shape))
    return pl.pallas_call(
        body,
        grid_spec=pltpu.PrefetchScalarGridSpec(
            num_scalar_prefetch=1,
            grid=(3,),
            in_specs=[whole(team, part, half), whole(team, part, half)],
            out_specs=(pl.BlockSpec((half, turned), lambda i, m: (0, i)), whole(EXTRA, half)),
            scratch_shapes=[pltpu.VMEM((team, 2 * part, half), BF16)],
        ),
        out_shape=(jax.ShapeDtypeStruct((half, 3 * turned), F32), jax.ShapeDtypeStruct((EXTRA, half), F32)),
        compiler_params=params(),
        cost_estimate=cost(5),
        name="first_projection_gradient",
    )(meta, own, other)


def gelu_pair(u):
    a = jnp.abs(u)
    t = 1.0 / (1.0 + (0.3275911 * 0.7071067811865476) * a)
    poly = 1.061405429 * t - 1.453152027
    poly = poly * t + 1.421413741
    poly = poly * t - 0.284496736
    poly = poly * t + 0.254829592
    bell = jnp.exp(-0.5 * (u * u))
    tail = (0.5 * poly) * t * bell
    cdf = jnp.where(u >= 0.0, 1.0 - tail, tail)
    return u * cdf, cdf + u * (bell * 0.3989422804014327)


def ffn(meta, attn_t, x, dy, valid, gain, bias, wo, wo_p, up, up_p, dn, dn_p):
    tokens, width = x.shape
    hidden = up.shape[1]
    fc = 512
    steps = hidden // fc
    near = steps // 2
    packs, _, lanes = attn_t.shape
    whole = lambda *shape: pl.BlockSpec(shape, lambda i, m: (0,) * len(shape))
    ups = pl.BlockSpec((width // 2, fc), lambda i, m: (0, lax.rem(m[2] * near + i, steps)))
    acts = pl.BlockSpec((tokens, fc), lambda i, m: (0, lax.rem(m[2] * near + i, steps)))
    half = width // 2

    def body(meta, *refs):
        (at_ref, x_ref, dy_ref, valid_ref, g_ref, b_ref, wo_own, wo_peer, up_own, up_peer, dn_own, dn_peer) = refs[:12]
        (out_ref, gm_ref, gb_ref, h2_ref, act_ref, dup_ref, da_ref, vec_ref) = refs[12:20]
        (mid_s, acc_s, own_s, peer_s, gown_s, gpeer_s) = refs[20:]
        i = pl.program_id(0)
        core = meta[2]
        zero = core == 0

        @pl.when(i == 0)
        def _():
            for p in range(packs):
                rows = pl.ds(p * lanes, lanes)
                own = at_ref[p, pl.ds(pl.multiple_of(core * half, half), half), :]
                peer = at_ref[p, pl.ds(pl.multiple_of((1 - core) * half, half), half), :]
                mid = x_ref[rows, :].astype(F32) + mm(own, wo_own[...], TN) + mm(peer, wo_peer[...], TN)
                mid_s[rows, :] = mid
                acc_s[rows, :] = mid
                hat, _ = norm_rows(mid)
                second = (hat * g_ref[...] + b_ref[...]).astype(BF16)
                h2_ref[rows, :] = second
                lo, hi = second[:, :half], second[:, half:]
                own_s[rows, :] = jnp.where(zero, lo, hi)
                peer_s[rows, :] = jnp.where(zero, hi, lo)
            gown_s[...] = jnp.zeros_like(gown_s)
            gpeer_s[...] = jnp.zeros_like(gpeer_s)

        down = jnp.where(i < near, dn_own[...], dn_peer[...])
        upper = mm(own_s[...], up_own[...]) + mm(peer_s[...], up_peer[...])
        act, slope = gelu_pair(upper)
        act = act.astype(BF16)
        grad = (mm(dy_ref[...], down, NT) * slope).astype(BF16)
        act_ref[...] = act
        dup_ref[...] = grad
        acc_s[...] += mm(act, down)
        gown_s[...] += mm(grad, up_own[...], NT)
        gpeer_s[...] += mm(grad, up_peer[...], NT)

        @pl.when(i == steps - 1)
        def _():
            out_ref[...] = acc_s[...].astype(BF16)
            vec = [jnp.zeros((8, width), F32), jnp.zeros((8, width), F32)]
            for p in range(packs):
                rows = pl.ds(p * lanes, lanes)
                hat, inv = norm_rows(mid_s[rows, :])
                a, b = gown_s[rows, :], gpeer_s[rows, :]
                gy = jnp.concatenate([jnp.where(zero, a, b), jnp.where(zero, b, a)], axis=1)
                vec[0] = vec[0] + jnp.sum((gy * hat).reshape(lanes // 8, 8, width), axis=0)
                vec[1] = vec[1] + jnp.sum(gy.reshape(lanes // 8, 8, width), axis=0)
                e = gy * g_ref[...]
                gm = dy_ref[rows, :].astype(F32) + inv * (
                    e
                    - jnp.mean(e, axis=-1, keepdims=True)
                    - hat * jnp.mean(e * hat, axis=-1, keepdims=True)
                )
                gm_ref[rows, :] = gm
                gb = gm.astype(BF16)
                gb_ref[rows, :] = gb
                ok = valid_ref[p]
                da_ref[p, pl.ds(pl.multiple_of(core * half, half), half), :] = (
                    mm(wo_own[...], gb, NT) * ok
                ).astype(BF16)
                da_ref[p, pl.ds(pl.multiple_of((1 - core) * half, half), half), :] = (
                    mm(wo_peer[...], gb, NT) * ok
                ).astype(BF16)
            vec_ref[0] = vec[0]
            vec_ref[1] = vec[1]

    return pl.pallas_call(
        body,
        grid_spec=pltpu.PrefetchScalarGridSpec(
            num_scalar_prefetch=1,
            grid=(steps,),
            in_specs=[
                whole(*attn_t.shape),
                whole(tokens, width),
                whole(tokens, width),
                whole(*valid.shape),
                whole(1, width),
                whole(1, width),
                whole(half, width),
                whole(half, width),
                ups,
                ups,
                pl.BlockSpec((fc, width), lambda i, m: (jnp.minimum(i, near - 1), 0)),
                pl.BlockSpec((fc, width), lambda i, m: (jnp.maximum(i - near, 0), 0)),
            ],
            out_specs=(
                whole(tokens, width),
                whole(tokens, width),
                whole(tokens, width),
                whole(tokens, width),
                acts,
                acts,
                whole(*attn_t.shape),
                whole(2, 8, width),
            ),
            scratch_shapes=[
                pltpu.VMEM((tokens, width), F32),
                pltpu.VMEM((tokens, width), F32),
                pltpu.VMEM((tokens, half), BF16),
                pltpu.VMEM((tokens, half), BF16),
                pltpu.VMEM((tokens, half), F32),
                pltpu.VMEM((tokens, half), F32),
            ],
        ),
        out_shape=(
            jax.ShapeDtypeStruct((tokens, width), BF16),
            jax.ShapeDtypeStruct((tokens, width), F32),
            jax.ShapeDtypeStruct((tokens, width), BF16),
            jax.ShapeDtypeStruct((tokens, width), BF16),
            jax.ShapeDtypeStruct((tokens, hidden), BF16),
            jax.ShapeDtypeStruct((tokens, hidden), BF16),
            jax.ShapeDtypeStruct(attn_t.shape, BF16),
            jax.ShapeDtypeStruct((2, 8, width), F32),
        ),
        compiler_params=params(),
        cost_estimate=cost(25),
        name="ffn_both_ways",
    )(meta, attn_t, x, dy, valid, gain, bias, wo, wo_p, up, up_p, dn, dn_p)


def up_out_grads(meta, attn_t, gb, h2, dup, far=None):
    tokens, width = gb.shape
    hidden = dup.shape[1]
    half = width // 2
    packs, _, lanes = attn_t.shape
    n = hidden // width
    own = far is not None

    def column(j, m):
        bit = jnp.where(j < n // 2, m[4], 1 - m[4])
        return bit * (n // 2) + lax.rem(jnp.minimum(j, n - 1), n // 2)

    def body(meta, at_ref, gb_ref, h2_ref, dup_ref, *rest):
        j = pl.program_id(0)
        side = meta[2] if own else 1 - meta[2]

        def up():
            part = jnp.where(side == 0, h2_ref[:, :half], h2_ref[:, half:])
            return mm(part, dup_ref[...], TN)

        def out():
            rows = pl.ds(pl.multiple_of(side * half, half), half)
            total = jnp.zeros((half, width), F32)
            for p in range(packs):
                total = total + mm(at_ref[p, rows, :], gb_ref[p * lanes : (p + 1) * lanes, :])
            lo, hi = total[: half // 2], total[half // 2 :]
            return jnp.where(meta[5] == 0, lo, hi), jnp.where(meta[5] == 0, hi, lo)

        if own:
            far_ref, uk_ref, us_ref, ok_ref, os_ref = rest

            @pl.when(j < n // 2)
            def _():
                uk_ref[...] = (up() + far_ref[...].astype(F32)).astype(BF16)

            @pl.when((j >= n // 2) & (j < n))
            def _():
                us_ref[...] = (up() + far_ref[...].astype(F32)).astype(BF16)

            @pl.when(j == n)
            def _():
                keep, send = out()
                ok_ref[...] = (keep + far_ref[: half // 2].astype(F32)).astype(BF16)
                os_ref[...] = (send + far_ref[half // 2 :].astype(F32)).astype(BF16)
        else:
            (out_ref,) = rest

            @pl.when(j < n)
            def _():
                out_ref[...] = up().astype(BF16)

            @pl.when(j == n)
            def _():
                keep, send = out()
                out_ref[: half // 2] = keep.astype(BF16)
                out_ref[half // 2 :] = send.astype(BF16)

    whole = lambda *shape: pl.BlockSpec(shape, lambda j, m: (0,) * len(shape))
    block = lambda index: pl.BlockSpec((half, width), index)
    if own:
        out_specs = (
            block(lambda j, m: (0, jnp.minimum(j, n // 2 - 1))),
            block(lambda j, m: (0, jnp.clip(j - n // 2, 0, n // 2 - 1))),
            whole(half // 2, width),
            whole(half // 2, width),
        )
        shapes = [(half, hidden // 2)] * 2 + [(half // 2, width)] * 2
        out_shape = tuple(jax.ShapeDtypeStruct(shape, BF16) for shape in shapes)
    else:
        out_specs = block(lambda j, m: (0, j))
        out_shape = jax.ShapeDtypeStruct((half, hidden + width), BF16)
    return pl.pallas_call(
        body,
        grid_spec=pltpu.PrefetchScalarGridSpec(
            num_scalar_prefetch=1,
            grid=(n + 1,),
            in_specs=[
                whole(*attn_t.shape),
                whole(tokens, width),
                whole(tokens, width),
                pl.BlockSpec((tokens, width), lambda j, m: (0, column(j, m))),
                *([block(lambda j, m: (0, j))] if own else []),
            ],
            out_specs=out_specs,
        ),
        out_shape=out_shape,
        compiler_params=params(),
        cost_estimate=cost(7),
        name="up_out_gradient",
    )(meta, attn_t, gb, h2, dup, *([far] if own else []))


def down_grads(meta, act, dy, far=None):
    tokens, width = dy.shape
    half = width // 2
    n = act.shape[1] // 2 // half
    own = far is not None

    def body(meta, act_ref, dy_ref, *rest):
        value = mm(act_ref[...], dy_ref[...], TN)
        if own:
            far_ref, keep_ref, send_ref = rest
            j = pl.program_id(0)
            value = (value + far_ref[...].astype(F32)).astype(BF16)

            @pl.when(j < n // 2)
            def _():
                keep_ref[...] = value

            @pl.when(j >= n // 2)
            def _():
                send_ref[...] = value
        else:
            (out_ref,) = rest
            out_ref[...] = value.astype(BF16)

    def column(j, m):
        side = m[2] if own else 1 - m[2]
        bit = jnp.where(j < n // 2, m[3], 1 - m[3])
        return side * n + bit * (n // 2) + lax.rem(j, n // 2)

    block = lambda index: pl.BlockSpec((half, width), index)
    if own:
        out_specs = (
            block(lambda j, m: (jnp.minimum(j, n // 2 - 1), 0)),
            block(lambda j, m: (jnp.maximum(j - n // 2, 0), 0)),
        )
        out_shape = (jax.ShapeDtypeStruct((n // 2 * half, width), BF16),) * 2
    else:
        out_specs = block(lambda j, m: (j, 0))
        out_shape = jax.ShapeDtypeStruct((n * half, width), BF16)
    return pl.pallas_call(
        body,
        grid_spec=pltpu.PrefetchScalarGridSpec(
            num_scalar_prefetch=1,
            grid=(n,),
            in_specs=[
                pl.BlockSpec((tokens, half), lambda j, m: (0, column(j, m))),
                pl.BlockSpec((tokens, width), lambda j, m: (0, 0)),
                *([block(lambda j, m: (j, 0))] if own else []),
            ],
            out_specs=out_specs,
        ),
        out_shape=out_shape,
        compiler_params=params(),
        cost_estimate=cost(6),
        name="down_gradient",
    )(meta, act, dy, *([far] if own else []))


def assemble(meta, downs, ups, outs):
    half, width = outs[0].shape[0] * 2, outs[0].shape[1]
    hidden = ups[0].shape[1] * 2
    cut = width // 2

    def body(meta, down_a, down_b, up_a, up_b, out_a, out_b, down_ref, up_ref, out_ref):
        i = pl.program_id(0)

        def place(ref, value, swapped):
            lo, hi = value[:, :cut].astype(F32), value[:, cut:].astype(F32)
            ref[:, :cut] = jnp.where(swapped == 0, lo, hi)
            ref[:, cut:] = jnp.where(swapped == 0, hi, lo)

        down_own = i // 2 == meta[3]
        place(down_ref, jnp.where(down_own, down_a[...], down_b[...]), meta[5])
        up_own = i // 2 == meta[4]
        place(up_ref, jnp.where(up_own, up_a[...], up_b[...]), meta[3])

        @pl.when(i == 0)
        def _():
            quarter = half // 4
            for z in range(2):
                for x in range(2):
                    rows = pl.ds(pl.multiple_of(jnp.bitwise_xor(meta[3], x) * quarter, quarter), quarter)
                    value = jnp.where(meta[5] == z, out_a[rows, :], out_b[rows, :])
                    place(out_ref.at[pl.ds((2 * z + x) * quarter, quarter)], value, meta[4])

    whole = lambda *shape: pl.BlockSpec(shape, lambda i, m: (0,) * len(shape))
    down = pl.BlockSpec((half, width), lambda i, m: (jnp.bitwise_xor(lax.rem(i, 2), m[4]), 0))
    up = pl.BlockSpec((half, width), lambda i, m: (0, jnp.bitwise_xor(lax.rem(i, 2), m[5])))
    return pl.pallas_call(
        body,
        grid_spec=pltpu.PrefetchScalarGridSpec(
            num_scalar_prefetch=1,
            grid=(4,),
            in_specs=[down, down, up, up, whole(*outs[0].shape), whole(*outs[0].shape)],
            out_specs=(
                pl.BlockSpec((half, width), lambda i, m: (i, 0)),
                pl.BlockSpec((half, width), lambda i, m: (0, i)),
                whole(half, width),
            ),
        ),
        out_shape=(
            jax.ShapeDtypeStruct((4 * half, width), F32),
            jax.ShapeDtypeStruct((half, hidden), F32),
            jax.ShapeDtypeStruct((half, width), F32),
        ),
        compiler_params=params(),
        cost_estimate=cost(7),
        name="weight_gradients",
    )(meta, *downs, *ups, *outs)


def finish_body(x_ref, gm_ref, back_ref, g_ref, out_ref):
    hat, inv = norm_rows(x_ref[...].astype(F32))
    e = back_ref[...].astype(F32) * g_ref[...]
    out_ref[...] = gm_ref[...] + inv * (
        e - jnp.mean(e, axis=-1, keepdims=True) - hat * jnp.mean(e * hat, axis=-1, keepdims=True)
    )


def finish(x, gm, back, gain):
    tokens, width = x.shape
    rows = pl.BlockSpec((128, width), lambda i: (i, 0))
    return pl.pallas_call(
        finish_body,
        grid=(tokens // 128,),
        in_specs=[rows, rows, rows, pl.BlockSpec((1, width), lambda i: (0, 0))],
        out_specs=rows,
        out_shape=jax.ShapeDtypeStruct((tokens, width), F32),
        compiler_params=params(),
        cost_estimate=cost(4),
        name="first_norm_backward",
    )(x, gm, back, gain)


def flip(value, axis, mask):
    size = lax.axis_size(axis)
    return lax.ppermute(value, axis, [(i, i ^ mask) for i in range(size)])


def bit(axis, mask):
    return (lax.axis_index(axis) // mask) % 2


def halves(value, which, axis=0):
    n = value.shape[axis] // 2
    keep = lax.dynamic_slice_in_dim(value, which * n, n, axis)
    send = lax.dynamic_slice_in_dim(value, (1 - which) * n, n, axis)
    return keep, send


def join(own, other, which, axis=0):
    return jnp.where(
        which == 0,
        jnp.concatenate([own, other], axis=axis),
        jnp.concatenate([other, own], axis=axis),
    )


def add(a, b):
    return (a.astype(F32) + b.astype(F32)).astype(BF16)


def on_device(
    tokens, lengths, ln1_gain, ln1_bias, qkv_weight, q_gain, k_gain, out_weight,
    ln2_gain, ln2_bias, up_weight, down_weight, cotangent,
):
    micro, rows, local, width = tokens.shape
    n = lax.axis_size("seq")
    length = local * n
    every = micro * rows
    team = n // every
    heads = H // team
    hd = width // H
    half = width // 2
    idx = lax.axis_index("seq")
    core = lax.axis_index("fsdp")
    row, member = idx // team, idx % team
    direct = every == 2 and team == 4
    lengths = lengths.reshape(every, lengths.shape[-1])
    mine = tokens.reshape(every, local, width)

    def swap(value):
        return flip(value, "fsdp", 1)

    vec = jnp.concatenate([ln1_gain, ln1_bias, ln2_gain, ln2_bias, q_gain, k_gain])[None]
    vec_p = swap(vec)
    ordered = jnp.where(core == 0, jnp.concatenate([vec, vec_p]), jnp.concatenate([vec_p, vec])).astype(F32)
    g1, b1, g2, b2 = (ordered[:, k * half : (k + 1) * half].reshape(1, width) for k in range(4))
    gq = ordered[:, 4 * half : 4 * half + hd // 2].reshape(hd, 1)
    gk = ordered[:, 4 * half + hd // 2 :].reshape(hd, 1)

    w_own = lax.dynamic_slice_in_dim(
        qkv_weight.reshape(half, 3, width), member * heads * hd, heads * hd, 2
    ).reshape(half, 3 * heads * hd)
    w_t = jnp.transpose(join(w_own, swap(w_own), core))

    if direct:
        near = lax.dynamic_index_in_dim(mine, row, 0, keepdims=False)
        away = lax.dynamic_index_in_dim(mine, 1 - row, 0, keepdims=False)
        far = flip(away, "seq", 4)
        cut = local // 2

        def spread(own):
            one, two = flip(own, "seq", 1), flip(own, "seq", 2)
            three = jnp.concatenate([flip(two[:cut], "seq", 1), flip(one[cut:], "seq", 2)], axis=0)
            return [own, one, two, three]

        slots = spread(near) + spread(far)
        spot = idx
    else:
        same_member = [[q * team + p for q in range(every)] for p in range(team)]
        same_row = [[q * team + p for p in range(team)] for q in range(every)]
        got = lax.all_to_all(mine, "seq", 0, 0, axis_index_groups=same_member, tiled=True)
        got = lax.all_gather(got, "seq", axis_index_groups=same_row)
        whole = jnp.swapaxes(got, 0, 1).reshape(length, width)
        slots = [whole[s * (length // 8) : (s + 1) * (length // 8)] for s in range(8)]
        spot = jnp.int32(0)
    meta = jnp.stack([spot, row, core, bit("rep", 1), bit("seq", 1), bit("seq", 2)]).astype(jnp.int32)

    out_p, up_p, down_p = swap(out_weight), swap(up_weight), swap(down_weight)

    with jax.named_scope("forward_attention"):
        qt, ka, kt, v, vt, x_row = make_qkv(meta, lengths, slots, w_t, g1, b1, gq, gk, heads, hd)
        attn, attn_f, logsum = attend(meta, lengths, qt, ka, vt, heads, hd)

    def exchange(value):
        return lax.all_to_all(value, "seq", 0, 0, tiled=True)

    packs = every * local // BLK
    if direct:
        attn_t = exchange(attn).reshape(packs, width, BLK)
    else:
        cut = jnp.moveaxis(attn.reshape(BLK * 0 + 8, heads * hd, BLK // local, local), 2, 1)
        got = exchange(cut.reshape(n, heads * hd, local))
        got = got.reshape(packs, every // packs, width, local)
        attn_t = jnp.swapaxes(got, 1, 2).reshape(packs, width, BLK)

    total = jnp.sum(lengths[:, :-1], axis=-1)
    places = idx * local + jnp.arange(local, dtype=jnp.int32)
    valid = (places[None] < total[:, None]).astype(F32).reshape(packs, 1, BLK)
    x_home = tokens.reshape(every * local, width)
    dy = cotangent.reshape(every * local, width)

    with jax.named_scope("feed_forward"):
        output, grad_mid, grad_branch, h2, act, dup, grad_attn, vec2 = ffn(
            meta, attn_t, x_home, dy, valid, g2, b2, out_weight, out_p, up_weight, up_p, down_weight, down_p
        )
    if direct:
        grad_o = exchange(grad_attn.reshape(n, heads * hd, BLK))
    else:
        cut = jnp.swapaxes(grad_attn.reshape(packs, width, every // packs, local), 1, 2)
        got = exchange(cut.reshape(n, heads * hd, local))
        got = got.reshape(8, BLK // local, heads * hd, local)
        grad_o = jnp.swapaxes(got, 1, 2).reshape(8, heads * hd, BLK)

    masks = [1 << k for k in range(n.bit_length() - 1)]
    x, y, z = ("rep", 1), ("seq", 1), ("seq", 2)

    def next_half(keep, got, way, axis):
        return halves(add(keep, got), bit(*way), axis)

    with jax.named_scope("weight_gradients"):
        far_d = swap(down_grads(meta, act, dy))
        far_u = swap(up_out_grads(meta, attn_t, grad_branch, h2, dup))
        down_k, down_s = down_grads(meta, act, dy, far_d)
        up_k, up_s, out_k, out_s = up_out_grads(meta, attn_t, grad_branch, h2, dup, far_u)
        grad_o, up_k, up_s, out_k, out_s, down_k, down_s = lax.optimization_barrier(
            (grad_o, up_k, up_s, out_k, out_s, down_k, down_s)
        )
    got = flip(down_s, *x), flip(up_s, *y), flip(out_s, *z)
    back = lambda h, go: attend_back(meta, lengths, qt, ka, kt, v, attn_f, logsum, go, h, 1, hd)
    parts = [back(0, grad_o)]
    with jax.named_scope("weight_gradients"):
        grad_o, *got = lax.optimization_barrier((grad_o, *got))
        down_k, down_s = next_half(down_k, got[0], y, 0)
        up_k, up_s = next_half(up_k, got[1], z, 1)
        out_k, out_s = next_half(out_k, got[2], x, 0)
        got = flip(down_s, *y), flip(up_s, *z), flip(out_s, *x)
    for h in range(1, heads - 1):
        parts.append(back(h, grad_o))
    with jax.named_scope("weight_gradients"):
        grad_o, *got = lax.optimization_barrier((grad_o, *got))
        down_k, down_s = next_half(down_k, got[0], z, 1)
        up_k, up_s = next_half(up_k, got[1], x, 1)
        out_k, out_s = next_half(out_k, got[2], y, 1)
        got = flip(down_s, *z), flip(up_s, *x), flip(out_s, *y)
    parts.append(back(heads - 1, grad_o))
    x_row, *got = lax.optimization_barrier((x_row, *got))
    with jax.named_scope("weight_gradients"):
        down = add(down_k, got[0])
        up = add(up_k, got[1])
        out = add(out_k, got[2])
        if masks[2:]:
            sizes = [down.shape[0], up.shape[0]]
            every_piece = jnp.concatenate([down, up, out])
            for mask in masks[2:]:
                every_piece = add(every_piece, flip(every_piece, "seq", mask))
            down, up, out = jnp.split(every_piece, [sizes[0], sizes[0] + sizes[1]])
        down = jnp.concatenate([down, flip(down, *z)], axis=1)
        up = jnp.concatenate([up, flip(up, *x)], axis=1)
        out = jnp.concatenate([out, flip(out, *y)], axis=1)
        down = jnp.concatenate([down, flip(down, *y)], axis=0)
        up = jnp.concatenate([up, flip(up, *z)], axis=1)
        out = jnp.concatenate([out, flip(out, *x)], axis=0)
        grad_down, grad_up, grad_out = assemble(
            meta, (down, flip(down, *x)), (up, flip(up, *y)), (out, flip(out, *z))
        )

    with jax.named_scope("backward_attention"):
        dq, dk, dv = zip(*parts)
        back_a, back_b, dw_t = qkv_back(
            meta, x_row, dq, dk, dv, w_t, g1, b1, gq, gk, vec2, heads, hd
        )

    if direct:

        def gather(parts):
            a = parts[0].reshape(2, 2, 2, local, half)
            b = parts[1].reshape(2, 2, 2, local, half)
            out = []
            for kind in (1, 0):
                a1 = add(a[kind, :, 0], flip(a[kind, :, 1], "seq", 1))
                b1 = add(b[kind, 0], flip(b[kind, 1], "seq", 2))
                a2 = add(a1[0], flip(a1[1], "seq", 2))
                b2 = add(b1[0], flip(b1[1], "seq", 1))
                out.append(jnp.concatenate([a2, b2], axis=1))
            return out

        far_sum, near_sum = gather((back_a, back_b))
        other = flip(far_sum, "seq", 4)
        back = jnp.where(
            row == 0, jnp.stack([near_sum, other]), jnp.stack([other, near_sum])
        ).reshape(every * local, width)
    else:
        whole = jnp.concatenate([back_a, back_b], axis=-1).reshape(every, team, local, width)
        whole = lax.psum_scatter(whole, "seq", scatter_dimension=1, axis_index_groups=same_row, tiled=True)
        got = lax.all_to_all(whole[:, 0], "seq", 0, 0, axis_index_groups=same_member, tiled=True)
        back = got.reshape(every * local, width)
    grad_tokens = finish(x_home, grad_mid, back, g1)

    with jax.named_scope("first_projection_gradient"):
        keep, send = halves(dw_t, core, 1)
        piece, send = next_half(keep, swap(send), x, 0)
        piece = add(piece, flip(send, *x))
        for mask in masks:
            if mask >= team:
                piece = add(piece, flip(piece, "seq", mask))
        piece = jnp.stack([piece, flip(piece, *z)])
        piece = jnp.concatenate([piece, flip(piece, *y)], axis=0)
        grad_qkv, small = assemble_qkv(meta, piece, flip(piece, *x), heads, hd)
        cuts = [small[0], small[1], small[2], small[3], small[4, : hd // 2], small[4, hd // 2 : hd]]
    shape = tokens.shape
    return (
        output.reshape(shape), grad_tokens.reshape(shape), cuts[0], cuts[1], grad_qkv, cuts[4], cuts[5],
        grad_out, cuts[2], cuts[3], grad_up, grad_down,
    )


def solution(mesh):
    tok = P(None, ("rep", "fsdp"), "seq", None)
    one, two = P("fsdp"), P("fsdp", None)
    in_specs = (tok, P(None, ("rep", "fsdp"), None), one, one, two, one, one, two, one, one, two, two, tok)
    out_specs = (tok, tok, one, one, two, one, one, two, one, one, two, two)
    return jax.shard_map(on_device, mesh=mesh, in_specs=in_specs, out_specs=out_specs, check_vma=False)
```

```python
import functools

import jax
import jax.numpy as jnp
from jax import lax
from jax.experimental import pallas as pl
from jax.experimental.pallas import tpu as pltpu
from jax.sharding import PartitionSpec as P

H = 12
EPS = 1e-06
LOG2E = 1.4426950408889634
SHIFT = 512.0
BLK = 256
EXTRA = 32
NN = (((1,), (0,)), ((), ()))
NT = (((1,), (1,)), ((), ()))
TN = (((0,), (0,)), ((), ()))
F32 = jnp.float32
BF16 = jnp.bfloat16


def mm(a, b, dims=NN):
    return lax.dot_general(a, b, dims, preferred_element_type=F32)


def params(**kw):
    return pltpu.CompilerParams(vmem_limit_bytes=60 * 1024 * 1024, **kw)


def cost(us):
    return pl.CostEstimate(flops=int(us * 0.35e9), bytes_accessed=1024, transcendentals=0)


def norm_rows(v):
    center = jnp.mean(v, axis=-1, keepdims=True)
    centred = v - center
    inv = lax.rsqrt(jnp.mean(centred * centred, axis=-1, keepdims=True) + EPS)
    return centred * inv, inv


def norm_cols(v):
    center = jnp.mean(v, axis=0, keepdims=True)
    centred = v - center
    inv = lax.rsqrt(jnp.mean(centred * centred, axis=0, keepdims=True) + EPS)
    return centred * inv, inv


def bounds_of(len_ref, row):
    out = []
    total = jnp.int32(0)
    for j in range(len_ref.shape[1] - 1):
        total = total + len_ref[row, j]
        out.append(total)
    return out


def qkv_body(heads, hd, meta, len_ref, *refs):
    xs = refs[:8]
    w_ref, g_ref, b_ref, gq_ref, gk_ref = refs[8:13]
    qt_ref, ka_ref, kt_ref, v_ref, vt_ref, x_ref = refs[13:]
    wid = heads * hd
    spot, row = meta[0], meta[1]
    bounds = bounds_of(len_ref, row)
    for s in range(8):
        c = jnp.bitwise_xor(spot, s)
        cols = pl.ds(pl.multiple_of(c * BLK, BLK), BLK)
        x = xs[s][...]
        x_ref[cols, :] = x
        hat, _ = norm_rows(x.astype(F32))
        first = (hat * g_ref[...] + b_ref[...]).astype(BF16)
        qkv = mm(w_ref[...], first, NT)
        place = c * BLK + lax.broadcasted_iota(jnp.int32, (8, BLK), 1)
        ident = jnp.zeros((8, BLK), jnp.int32)
        place_k = c * BLK + lax.broadcasted_iota(jnp.int32, (BLK, 128), 0)
        ident_k = jnp.zeros((BLK, 128), jnp.int32)
        for bound in bounds:
            ident = ident + (place >= bound).astype(jnp.int32)
            ident_k = ident_k + (place_k >= bound).astype(jnp.int32)
        which = lax.broadcasted_iota(jnp.int32, (8, BLK), 0)
        hot = jnp.where((ident == which) & (which < len(bounds)), 16.0, 0.0)
        hot = jnp.concatenate([hot, jnp.zeros((hd - 8, BLK), F32)], axis=0)
        lane = lax.broadcasted_iota(jnp.int32, (BLK, 128), 1) - hd
        hot_k = jnp.where((ident_k == lane) & (lane < len(bounds)), SHIFT / 16.0, 0.0)
        for h in range(heads):
            q, _ = norm_cols(qkv[h * hd : (h + 1) * hd])
            k, _ = norm_cols(qkv[wid + h * hd : wid + (h + 1) * hd])
            q = (q * gq_ref[...]).astype(BF16).astype(F32) * (hd**-0.5)
            k = k * gk_ref[...]
            v = qkv[2 * wid + h * hd : 2 * wid + (h + 1) * hd]
            qt_ref[h, :, cols] = jnp.concatenate([q, hot], axis=0).astype(BF16)
            kt_ref[h, :, cols] = k.astype(BF16)
            vt_ref[h, :, cols] = v.astype(BF16)
            both = jnp.transpose(jnp.concatenate([k, v], axis=0))
            ka_ref[h, cols, :] = jnp.where(lane < 0, both, hot_k).astype(BF16)
            v_ref[h, cols, :] = both[:, hd:].astype(BF16)


def make_qkv(meta, lengths, slots, w_t, gain, bias, gq, gk, heads, hd):
    length = 8 * slots[0].shape[0]
    width = slots[0].shape[1]
    smem = pl.BlockSpec(memory_space=pltpu.SMEM)
    vmem = pl.BlockSpec(memory_space=pltpu.VMEM)
    return pl.pallas_call(
        functools.partial(qkv_body, heads, hd),
        out_shape=(
            jax.ShapeDtypeStruct((heads, 2 * hd, length), BF16),
            jax.ShapeDtypeStruct((heads, length, 2 * hd), BF16),
            jax.ShapeDtypeStruct((heads, hd, length), BF16),
            jax.ShapeDtypeStruct((heads, length, hd), BF16),
            jax.ShapeDtypeStruct((heads, hd, length), BF16),
            jax.ShapeDtypeStruct((length, width), BF16),
        ),
        in_specs=[smem, smem] + [vmem] * 13,
        out_specs=(vmem,) * 6,
        compiler_params=params(),
        cost_estimate=cost(12),
        name="qkv_forward",
    )(meta, lengths, *slots, w_t, gain, bias, gq, gk)


def block_range(bounds, i):
    first = i * BLK
    last = first + BLK - 1
    lo = jnp.int32(0)
    hi = bounds[-1]
    for bound in bounds:
        lo = jnp.where(first >= bound, bound, lo)
    for bound in bounds[::-1]:
        hi = jnp.where(last < bound, bound, hi)
    lo_b = lo // BLK
    hi_b = (hi + BLK - 1) // BLK
    return lo_b, jnp.where(first >= bounds[-1], lo_b, hi_b)


def attend_body(heads, hd, meta, len_ref, qt_ref, ka_ref, vt_ref, o_ref, of_ref, ls_ref):
    i = pl.program_id(0)
    bounds = bounds_of(len_ref, meta[1])
    lo, hi = block_range(bounds, i)

    def step(b, carry):
        rows = pl.ds(pl.multiple_of(b * BLK, BLK), BLK)
        out = []
        for h in range(heads):
            acc, total = carry[h]
            scores = mm(ka_ref[h, rows, :], qt_ref[h])
            expo = jnp.exp2(scores * LOG2E - SHIFT * LOG2E)
            total = total + jnp.sum(expo.reshape(BLK // 8, 8, BLK), axis=0)
            acc = acc + mm(vt_ref[h, :, rows], expo.astype(BF16))
            out.append((acc, total))
        return tuple(out)

    init = tuple((jnp.zeros((hd, BLK), F32), jnp.zeros((8, BLK), F32)) for _ in range(heads))
    done = lax.fori_loop(lo, hi, step, init)
    for h in range(heads):
        acc, total = done[h]
        total = jnp.sum(total, axis=0, keepdims=True)
        live = total > 0.0
        safe = jnp.where(live, total, 1.0)
        out = jnp.where(live, acc * (1.0 / safe), 0.0)
        o_ref[0, h * hd : (h + 1) * hd, :] = out.astype(BF16)
        of_ref[h] = out
        ls_ref[h] = jnp.log2(safe) + SHIFT * LOG2E


def attend(meta, lengths, qt, ka, vt, heads, hd):
    length = qt.shape[2]
    blocks = length // BLK
    smem = pl.BlockSpec(memory_space=pltpu.SMEM)
    return pl.pallas_call(
        functools.partial(attend_body, heads, hd),
        grid=(blocks,),
        out_shape=(
            jax.ShapeDtypeStruct((blocks, heads * hd, BLK), BF16),
            jax.ShapeDtypeStruct((heads, hd, length), F32),
            jax.ShapeDtypeStruct((heads, 1, length), F32),
        ),
        in_specs=[
            smem,
            smem,
            pl.BlockSpec((heads, 2 * hd, BLK), lambda i: (0, 0, i)),
            pl.BlockSpec((heads, length, 2 * hd), lambda i: (0, 0, 0)),
            pl.BlockSpec((heads, hd, length), lambda i: (0, 0, 0)),
        ],
        out_specs=(
            pl.BlockSpec((1, heads * hd, BLK), lambda i: (i, 0, 0)),
            pl.BlockSpec((heads, hd, BLK), lambda i: (0, 0, i)),
            pl.BlockSpec((heads, 1, BLK), lambda i: (0, 0, i)),
        ),
        compiler_params=params(),
        cost_estimate=cost(25),
        name="attention_forward",
    )(meta, lengths, qt, ka, vt)


def attend_back_body(
    heads, hd, meta, len_ref, qt_ref, ka_ref, kt_ref, v_ref, of_ref, ls_ref, go_ref, dq_ref, dk_ref, dv_ref
):
    i = pl.program_id(0)
    bounds = bounds_of(len_ref, meta[1])
    lo, hi = block_range(bounds, i)

    @pl.when(i == 0)
    def _():
        dk_ref[...] = jnp.zeros_like(dk_ref)
        dv_ref[...] = jnp.zeros_like(dv_ref)

    inner = []
    for h in range(heads):
        go = go_ref[0, h * hd : (h + 1) * hd, :].astype(F32)
        inner.append(jnp.sum(go * of_ref[h], axis=0, keepdims=True))

    def step(b, carry):
        rows = pl.ds(pl.multiple_of(b * BLK, BLK), BLK)
        out = []
        for h in range(heads):
            go = go_ref[0, h * hd : (h + 1) * hd, :]
            qt = qt_ref[h]
            scores = mm(ka_ref[h, rows, :], qt)
            probs = jnp.exp2(scores * LOG2E - ls_ref[h])
            grad_probs = mm(v_ref[h, rows, :], go)
            grad_scores = (probs * (grad_probs - inner[h])).astype(BF16)
            dv_ref[h, :, rows] += mm(go, probs.astype(BF16), NT)
            dk_ref[h, :, rows] += mm(qt[:hd], grad_scores, NT)
            out.append(carry[h] + mm(kt_ref[h, :, rows], grad_scores))
        return tuple(out)

    done = lax.fori_loop(lo, hi, step, tuple(jnp.zeros((hd, BLK), F32) for _ in range(heads)))
    for h in range(heads):
        dq_ref[h] = done[h] * (hd**-0.5)


def attend_back(meta, lengths, qt, ka, kt, v, of, ls, go, at, heads, hd):
    length = qt.shape[2]
    blocks = length // BLK
    smem = pl.BlockSpec(memory_space=pltpu.SMEM)
    whole = lambda *shape: pl.BlockSpec(shape, lambda i: (at, 0, 0))
    all_out = lambda *shape: pl.BlockSpec(shape, lambda i: (0, 0, 0))
    return pl.pallas_call(
        functools.partial(attend_back_body, heads, hd),
        grid=(blocks,),
        out_shape=tuple(jax.ShapeDtypeStruct((heads, hd, length), F32) for _ in range(3)),
        in_specs=[
            smem,
            smem,
            pl.BlockSpec((heads, 2 * hd, BLK), lambda i: (at, 0, i)),
            whole(heads, length, 2 * hd),
            whole(heads, hd, length),
            whole(heads, length, hd),
            pl.BlockSpec((heads, hd, BLK), lambda i: (at, 0, i)),
            pl.BlockSpec((heads, 1, BLK), lambda i: (at, 0, i)),
            pl.BlockSpec((1, heads * hd, BLK), lambda i: (i, at, 0)),
        ],
        out_specs=(
            pl.BlockSpec((heads, hd, BLK), lambda i: (0, 0, i)),
            all_out(heads, hd, length),
            all_out(heads, hd, length),
        ),
        compiler_params=params(),
        cost_estimate=cost(11 * heads),
        name="attention_backward",
    )(meta, lengths, qt, ka, kt, v, of, ls, go)


def qkv_back_body(
    heads, hd, meta, x_ref, *refs
):
    dqs, dks, dvs = refs[:heads], refs[heads : 2 * heads], refs[2 * heads : 3 * heads]
    w_ref, g_ref, b_ref, gq_ref, gk_ref, vec2_ref, da_ref, db_ref, dw_ref, acc_ref, vec_ref, gain_ref = refs[3 * heads :]
    i = pl.program_id(0)
    wid = heads * hd

    @pl.when(i == 0)
    def _():
        acc_ref[...] = jnp.zeros_like(acc_ref)
        vec_ref[...] = jnp.zeros_like(vec_ref)
        gain_ref[...] = jnp.zeros_like(gain_ref)

    hat, _ = norm_rows(x_ref[...].astype(F32))
    first = (hat * g_ref[...] + b_ref[...]).astype(BF16)
    qk = mm(w_ref[: 2 * wid, :], first, NT)
    pieces = []
    for at, gain, grad in ((0, gq_ref, dqs), (1, gk_ref, dks)):
        for h in range(heads):
            unit, inv = norm_cols(qk[at * wid + h * hd : at * wid + (h + 1) * hd])
            gy = grad[h][0]
            gain_ref[at] += gy * unit
            e = gy * gain[...]
            pieces.append(
                inv
                * (
                    e
                    - jnp.mean(e, axis=0, keepdims=True)
                    - unit * jnp.mean(e * unit, axis=0, keepdims=True)
                )
            )
    for h in range(heads):
        pieces.append(dvs[h][0])
    grad = jnp.concatenate(pieces, axis=0).astype(BF16)
    acc_ref[...] += mm(grad, first)
    back = mm(grad, w_ref[...], TN)
    vec_ref[0] += jnp.sum((back * hat).reshape(BLK // 8, 8, -1), axis=0)
    vec_ref[1] += jnp.sum(back.reshape(BLK // 8, 8, -1), axis=0)
    half = back.shape[1] // 2
    da_ref[0] = back[:, :half].astype(BF16)
    db_ref[0] = back[:, half:].astype(BF16)

    @pl.when(i == pl.num_programs(0) - 1)
    def _():
        dw_ref[: 3 * wid, :] = acc_ref[...].astype(BF16)
        lines = [jnp.sum(ref[k], axis=0, keepdims=True) for ref in (vec_ref, vec2_ref) for k in range(2)]
        width = dw_ref.shape[1]
        lane = lax.broadcasted_iota(jnp.int32, (hd, width), 1)
        item = lax.broadcasted_iota(jnp.int32, (hd, width), 0)
        spread = jnp.where(item < hd // 2, item, item - hd // 2 + width // 2)
        line = jnp.zeros((8, width), F32)
        for k in range(2):
            total = lax.dot_general(
                jnp.ones((8, BLK), F32), gain_ref[k], NT, precision=lax.Precision.HIGHEST, preferred_element_type=F32
            )
            pick = (lane == spread + k * (hd // 2)).astype(F32)
            line = line + lax.dot_general(
                total, pick, NN, precision=lax.Precision.HIGHEST, preferred_element_type=F32
            )
        lines.append(line[:1])
        place = lax.broadcasted_iota(jnp.int32, (EXTRA, width), 0)
        below = jnp.zeros((EXTRA, width), F32)
        for k, one in enumerate(lines):
            below = jnp.where(place == k, one, below)
        dw_ref[3 * wid :, :] = below.astype(BF16)


def qkv_back(meta, x, dq, dk, dv, w_t, gain, bias, gq, gk, vec2, heads, hd):
    length, width = x.shape
    blocks = length // BLK
    whole = lambda *shape: pl.BlockSpec(shape, lambda i, m: (0,) * len(shape))
    part = pl.BlockSpec((1, hd, BLK), lambda i, m: (0, 0, i))
    grads = pl.BlockSpec((1, BLK, width // 2), lambda i, m: (jnp.bitwise_xor(i, m[0]), 0, 0))
    return pl.pallas_call(
        functools.partial(qkv_back_body, heads, hd),
        grid_spec=pltpu.PrefetchScalarGridSpec(
            num_scalar_prefetch=1,
            grid=(blocks,),
            in_specs=[
                pl.BlockSpec((BLK, width), lambda i, m: (i, 0)),
                *([part] * (3 * heads)),
                whole(*w_t.shape),
                whole(1, width),
                whole(1, width),
                whole(hd, 1),
                whole(hd, 1),
                whole(2, 8, width),
            ],
            out_specs=(
                grads,
                grads,
                whole(w_t.shape[0] + EXTRA, width),
            ),
            scratch_shapes=[
                pltpu.VMEM(w_t.shape, F32),
                pltpu.VMEM((2, 8, width), F32),
                pltpu.VMEM((2, hd, BLK), F32),
            ],
        ),
        out_shape=(
            jax.ShapeDtypeStruct((blocks, BLK, width // 2), BF16),
            jax.ShapeDtypeStruct((blocks, BLK, width // 2), BF16),
            jax.ShapeDtypeStruct((w_t.shape[0] + EXTRA, width), BF16),
        ),
        compiler_params=params(),
        cost_estimate=cost(17),
        name="qkv_backward",
    )(meta, x, *dq, *dk, *dv, w_t, gain, bias, gq, gk, vec2)


def assemble_qkv(meta, own, other, heads, hd):
    team, part, half = own.shape
    wid = heads * hd
    turned = team * wid

    def body(meta, own_ref, other_ref, out_ref, vec_ref, all_s):
        t = pl.program_id(0)

        @pl.when(t == 0)
        def _():
            for y in range(2):
                for x in range(2):
                    at = 2 * jnp.bitwise_xor(meta[4], y) + jnp.bitwise_xor(meta[3], x)
                    a, b = own_ref[at], other_ref[at]
                    for z in range(2):
                        all_s[2 * z + y, x * part : (x + 1) * part, :] = jnp.where(meta[5] == z, a, b)
            total = jnp.zeros((EXTRA, half), F32)
            for p in range(team):
                total = total + all_s[p, 3 * wid :, :].astype(F32)
            vec_ref[...] = total

        rows = pl.ds(pl.multiple_of(t * wid, wid), wid)
        piece = jnp.concatenate([all_s[p, rows, :] for p in range(team)], axis=0)
        out_ref[...] = jnp.transpose(piece.astype(F32))

    whole = lambda *shape: pl.BlockSpec(shape, lambda i, m: (0,) * len(shape))
    return pl.pallas_call(
        body,
        grid_spec=pltpu.PrefetchScalarGridSpec(
            num_scalar_prefetch=1,
            grid=(3,),
            in_specs=[whole(team, part, half), whole(team, part, half)],
            out_specs=(pl.BlockSpec((half, turned), lambda i, m: (0, i)), whole(EXTRA, half)),
            scratch_shapes=[pltpu.VMEM((team, 2 * part, half), BF16)],
        ),
        out_shape=(jax.ShapeDtypeStruct((half, 3 * turned), F32), jax.ShapeDtypeStruct((EXTRA, half), F32)),
        compiler_params=params(),
        cost_estimate=cost(5),
        name="first_projection_gradient",
    )(meta, own, other)


def gelu_pair(u):
    a = jnp.abs(u)
    t = 1.0 / (1.0 + (0.3275911 * 0.7071067811865476) * a)
    poly = 1.061405429 * t - 1.453152027
    poly = poly * t + 1.421413741
    poly = poly * t - 0.284496736
    poly = poly * t + 0.254829592
    bell = jnp.exp(-0.5 * (u * u))
    tail = (0.5 * poly) * t * bell
    cdf = jnp.where(u >= 0.0, 1.0 - tail, tail)
    return u * cdf, cdf + u * (bell * 0.3989422804014327)


def ffn(meta, attn_t, x, dy, valid, gain, bias, wo, wo_p, up, up_p, dn, dn_p):
    tokens, width = x.shape
    hidden = up.shape[1]
    fc = 512
    steps = hidden // fc
    near = steps // 2
    packs, _, lanes = attn_t.shape
    whole = lambda *shape: pl.BlockSpec(shape, lambda i, m: (0,) * len(shape))
    ups = pl.BlockSpec((width // 2, fc), lambda i, m: (0, lax.rem(m[2] * near + i, steps)))
    acts = pl.BlockSpec((tokens, fc), lambda i, m: (0, lax.rem(m[2] * near + i, steps)))
    half = width // 2

    def body(meta, *refs):
        (at_ref, x_ref, dy_ref, valid_ref, g_ref, b_ref, wo_own, wo_peer, up_own, up_peer, dn_own, dn_peer) = refs[:12]
        (out_ref, gm_ref, gb_ref, h2_ref, act_ref, dup_ref, da_ref, vec_ref) = refs[12:20]
        (mid_s, acc_s, own_s, peer_s, gown_s, gpeer_s) = refs[20:]
        i = pl.program_id(0)
        core = meta[2]
        zero = core == 0

        @pl.when(i == 0)
        def _():
            for p in range(packs):
                rows = pl.ds(p * lanes, lanes)
                own = at_ref[p, pl.ds(pl.multiple_of(core * half, half), half), :]
                peer = at_ref[p, pl.ds(pl.multiple_of((1 - core) * half, half), half), :]
                mid = x_ref[rows, :].astype(F32) + mm(own, wo_own[...], TN) + mm(peer, wo_peer[...], TN)
                mid_s[rows, :] = mid
                acc_s[rows, :] = mid
                hat, _ = norm_rows(mid)
                second = (hat * g_ref[...] + b_ref[...]).astype(BF16)
                h2_ref[rows, :] = second
                lo, hi = second[:, :half], second[:, half:]
                own_s[rows, :] = jnp.where(zero, lo, hi)
                peer_s[rows, :] = jnp.where(zero, hi, lo)
            gown_s[...] = jnp.zeros_like(gown_s)
            gpeer_s[...] = jnp.zeros_like(gpeer_s)

        down = jnp.where(i < near, dn_own[...], dn_peer[...])
        upper = mm(own_s[...], up_own[...]) + mm(peer_s[...], up_peer[...])
        act, slope = gelu_pair(upper)
        act = act.astype(BF16)
        grad = (mm(dy_ref[...], down, NT) * slope).astype(BF16)
        act_ref[...] = act
        dup_ref[...] = grad
        acc_s[...] += mm(act, down)
        gown_s[...] += mm(grad, up_own[...], NT)
        gpeer_s[...] += mm(grad, up_peer[...], NT)

        @pl.when(i == steps - 1)
        def _():
            out_ref[...] = acc_s[...].astype(BF16)
            vec = [jnp.zeros((8, width), F32), jnp.zeros((8, width), F32)]
            for p in range(packs):
                rows = pl.ds(p * lanes, lanes)
                hat, inv = norm_rows(mid_s[rows, :])
                a, b = gown_s[rows, :], gpeer_s[rows, :]
                gy = jnp.concatenate([jnp.where(zero, a, b), jnp.where(zero, b, a)], axis=1)
                vec[0] = vec[0] + jnp.sum((gy * hat).reshape(lanes // 8, 8, width), axis=0)
                vec[1] = vec[1] + jnp.sum(gy.reshape(lanes // 8, 8, width), axis=0)
                e = gy * g_ref[...]
                gm = dy_ref[rows, :].astype(F32) + inv * (
                    e
                    - jnp.mean(e, axis=-1, keepdims=True)
                    - hat * jnp.mean(e * hat, axis=-1, keepdims=True)
                )
                gm_ref[rows, :] = gm
                gb = gm.astype(BF16)
                gb_ref[rows, :] = gb
                ok = valid_ref[p]
                da_ref[p, pl.ds(pl.multiple_of(core * half, half), half), :] = (
                    mm(wo_own[...], gb, NT) * ok
                ).astype(BF16)
                da_ref[p, pl.ds(pl.multiple_of((1 - core) * half, half), half), :] = (
                    mm(wo_peer[...], gb, NT) * ok
                ).astype(BF16)
            vec_ref[0] = vec[0]
            vec_ref[1] = vec[1]

    return pl.pallas_call(
        body,
        grid_spec=pltpu.PrefetchScalarGridSpec(
            num_scalar_prefetch=1,
            grid=(steps,),
            in_specs=[
                whole(*attn_t.shape),
                whole(tokens, width),
                whole(tokens, width),
                whole(*valid.shape),
                whole(1, width),
                whole(1, width),
                whole(half, width),
                whole(half, width),
                ups,
                ups,
                pl.BlockSpec((fc, width), lambda i, m: (jnp.minimum(i, near - 1), 0)),
                pl.BlockSpec((fc, width), lambda i, m: (jnp.maximum(i - near, 0), 0)),
            ],
            out_specs=(
                whole(tokens, width),
                whole(tokens, width),
                whole(tokens, width),
                whole(tokens, width),
                acts,
                acts,
                whole(*attn_t.shape),
                whole(2, 8, width),
            ),
            scratch_shapes=[
                pltpu.VMEM((tokens, width), F32),
                pltpu.VMEM((tokens, width), F32),
                pltpu.VMEM((tokens, half), BF16),
                pltpu.VMEM((tokens, half), BF16),
                pltpu.VMEM((tokens, half), F32),
                pltpu.VMEM((tokens, half), F32),
            ],
        ),
        out_shape=(
            jax.ShapeDtypeStruct((tokens, width), BF16),
            jax.ShapeDtypeStruct((tokens, width), F32),
            jax.ShapeDtypeStruct((tokens, width), BF16),
            jax.ShapeDtypeStruct((tokens, width), BF16),
            jax.ShapeDtypeStruct((tokens, hidden), BF16),
            jax.ShapeDtypeStruct((tokens, hidden), BF16),
            jax.ShapeDtypeStruct(attn_t.shape, BF16),
            jax.ShapeDtypeStruct((2, 8, width), F32),
        ),
        compiler_params=params(),
        cost_estimate=cost(25),
        name="ffn_both_ways",
    )(meta, attn_t, x, dy, valid, gain, bias, wo, wo_p, up, up_p, dn, dn_p)


def up_out_grads(meta, attn_t, gb, h2, dup, far=None):
    tokens, width = gb.shape
    hidden = dup.shape[1]
    half = width // 2
    packs, _, lanes = attn_t.shape
    n = hidden // width
    own = far is not None

    def column(j, m):
        bit = jnp.where(j < n // 2, m[4], 1 - m[4])
        return bit * (n // 2) + lax.rem(jnp.minimum(j, n - 1), n // 2)

    def body(meta, at_ref, gb_ref, h2_ref, dup_ref, *rest):
        j = pl.program_id(0)
        side = meta[2] if own else 1 - meta[2]

        def up():
            part = jnp.where(side == 0, h2_ref[:, :half], h2_ref[:, half:])
            return mm(part, dup_ref[...], TN)

        def out():
            rows = pl.ds(pl.multiple_of(side * half, half), half)
            total = jnp.zeros((half, width), F32)
            for p in range(packs):
                total = total + mm(at_ref[p, rows, :], gb_ref[p * lanes : (p + 1) * lanes, :])
            lo, hi = total[: half // 2], total[half // 2 :]
            return jnp.where(meta[5] == 0, lo, hi), jnp.where(meta[5] == 0, hi, lo)

        if own:
            far_ref, uk_ref, us_ref, ok_ref, os_ref = rest

            @pl.when(j < n // 2)
            def _():
                uk_ref[...] = (up() + far_ref[...].astype(F32)).astype(BF16)

            @pl.when((j >= n // 2) & (j < n))
            def _():
                us_ref[...] = (up() + far_ref[...].astype(F32)).astype(BF16)

            @pl.when(j == n)
            def _():
                keep, send = out()
                ok_ref[...] = (keep + far_ref[: half // 2].astype(F32)).astype(BF16)
                os_ref[...] = (send + far_ref[half // 2 :].astype(F32)).astype(BF16)
        else:
            (out_ref,) = rest

            @pl.when(j < n)
            def _():
                out_ref[...] = up().astype(BF16)

            @pl.when(j == n)
            def _():
                keep, send = out()
                out_ref[: half // 2] = keep.astype(BF16)
                out_ref[half // 2 :] = send.astype(BF16)

    whole = lambda *shape: pl.BlockSpec(shape, lambda j, m: (0,) * len(shape))
    block = lambda index: pl.BlockSpec((half, width), index)
    if own:
        out_specs = (
            block(lambda j, m: (0, jnp.minimum(j, n // 2 - 1))),
            block(lambda j, m: (0, jnp.clip(j - n // 2, 0, n // 2 - 1))),
            whole(half // 2, width),
            whole(half // 2, width),
        )
        shapes = [(half, hidden // 2)] * 2 + [(half // 2, width)] * 2
        out_shape = tuple(jax.ShapeDtypeStruct(shape, BF16) for shape in shapes)
    else:
        out_specs = block(lambda j, m: (0, j))
        out_shape = jax.ShapeDtypeStruct((half, hidden + width), BF16)
    return pl.pallas_call(
        body,
        grid_spec=pltpu.PrefetchScalarGridSpec(
            num_scalar_prefetch=1,
            grid=(n + 1,),
            in_specs=[
                whole(*attn_t.shape),
                whole(tokens, width),
                whole(tokens, width),
                pl.BlockSpec((tokens, width), lambda j, m: (0, column(j, m))),
                *([block(lambda j, m: (0, j))] if own else []),
            ],
            out_specs=out_specs,
        ),
        out_shape=out_shape,
        compiler_params=params(),
        cost_estimate=cost(7),
        name="up_out_gradient",
    )(meta, attn_t, gb, h2, dup, *([far] if own else []))


def down_grads(meta, act, dy, far=None):
    tokens, width = dy.shape
    half = width // 2
    n = act.shape[1] // 2 // half
    own = far is not None

    def body(meta, act_ref, dy_ref, *rest):
        value = mm(act_ref[...], dy_ref[...], TN)
        if own:
            far_ref, keep_ref, send_ref = rest
            j = pl.program_id(0)
            value = (value + far_ref[...].astype(F32)).astype(BF16)

            @pl.when(j < n // 2)
            def _():
                keep_ref[...] = value

            @pl.when(j >= n // 2)
            def _():
                send_ref[...] = value
        else:
            (out_ref,) = rest
            out_ref[...] = value.astype(BF16)

    def column(j, m):
        side = m[2] if own else 1 - m[2]
        bit = jnp.where(j < n // 2, m[3], 1 - m[3])
        return side * n + bit * (n // 2) + lax.rem(j, n // 2)

    block = lambda index: pl.BlockSpec((half, width), index)
    if own:
        out_specs = (
            block(lambda j, m: (jnp.minimum(j, n // 2 - 1), 0)),
            block(lambda j, m: (jnp.maximum(j - n // 2, 0), 0)),
        )
        out_shape = (jax.ShapeDtypeStruct((n // 2 * half, width), BF16),) * 2
    else:
        out_specs = block(lambda j, m: (j, 0))
        out_shape = jax.ShapeDtypeStruct((n * half, width), BF16)
    return pl.pallas_call(
        body,
        grid_spec=pltpu.PrefetchScalarGridSpec(
            num_scalar_prefetch=1,
            grid=(n,),
            in_specs=[
                pl.BlockSpec((tokens, half), lambda j, m: (0, column(j, m))),
                pl.BlockSpec((tokens, width), lambda j, m: (0, 0)),
                *([block(lambda j, m: (j, 0))] if own else []),
            ],
            out_specs=out_specs,
        ),
        out_shape=out_shape,
        compiler_params=params(),
        cost_estimate=cost(6),
        name="down_gradient",
    )(meta, act, dy, *([far] if own else []))


def assemble(meta, downs, ups, outs):
    half, width = outs[0].shape[0] * 2, outs[0].shape[1]
    hidden = ups[0].shape[1] * 2
    cut = width // 2

    def body(meta, down_a, down_b, up_a, up_b, out_a, out_b, down_ref, up_ref, out_ref):
        i = pl.program_id(0)

        def place(ref, value, swapped):
            lo, hi = value[:, :cut].astype(F32), value[:, cut:].astype(F32)
            ref[:, :cut] = jnp.where(swapped == 0, lo, hi)
            ref[:, cut:] = jnp.where(swapped == 0, hi, lo)

        down_own = i // 2 == meta[3]
        place(down_ref, jnp.where(down_own, down_a[...], down_b[...]), meta[5])
        up_own = i // 2 == meta[4]
        place(up_ref, jnp.where(up_own, up_a[...], up_b[...]), meta[3])

        @pl.when(i == 0)
        def _():
            quarter = half // 4
            for z in range(2):
                for x in range(2):
                    rows = pl.ds(pl.multiple_of(jnp.bitwise_xor(meta[3], x) * quarter, quarter), quarter)
                    value = jnp.where(meta[5] == z, out_a[rows, :], out_b[rows, :])
                    place(out_ref.at[pl.ds((2 * z + x) * quarter, quarter)], value, meta[4])

    whole = lambda *shape: pl.BlockSpec(shape, lambda i, m: (0,) * len(shape))
    down = pl.BlockSpec((half, width), lambda i, m: (jnp.bitwise_xor(lax.rem(i, 2), m[4]), 0))
    up = pl.BlockSpec((half, width), lambda i, m: (0, jnp.bitwise_xor(lax.rem(i, 2), m[5])))
    return pl.pallas_call(
        body,
        grid_spec=pltpu.PrefetchScalarGridSpec(
            num_scalar_prefetch=1,
            grid=(4,),
            in_specs=[down, down, up, up, whole(*outs[0].shape), whole(*outs[0].shape)],
            out_specs=(
                pl.BlockSpec((half, width), lambda i, m: (i, 0)),
                pl.BlockSpec((half, width), lambda i, m: (0, i)),
                whole(half, width),
            ),
        ),
        out_shape=(
            jax.ShapeDtypeStruct((4 * half, width), F32),
            jax.ShapeDtypeStruct((half, hidden), F32),
            jax.ShapeDtypeStruct((half, width), F32),
        ),
        compiler_params=params(),
        cost_estimate=cost(7),
        name="weight_gradients",
    )(meta, *downs, *ups, *outs)


def finish_body(x_ref, gm_ref, back_ref, g_ref, out_ref):
    hat, inv = norm_rows(x_ref[...].astype(F32))
    e = back_ref[...].astype(F32) * g_ref[...]
    out_ref[...] = gm_ref[...] + inv * (
        e - jnp.mean(e, axis=-1, keepdims=True) - hat * jnp.mean(e * hat, axis=-1, keepdims=True)
    )


def finish(x, gm, back, gain):
    tokens, width = x.shape
    rows = pl.BlockSpec((128, width), lambda i: (i, 0))
    return pl.pallas_call(
        finish_body,
        grid=(tokens // 128,),
        in_specs=[rows, rows, rows, pl.BlockSpec((1, width), lambda i: (0, 0))],
        out_specs=rows,
        out_shape=jax.ShapeDtypeStruct((tokens, width), F32),
        compiler_params=params(),
        cost_estimate=cost(4),
        name="first_norm_backward",
    )(x, gm, back, gain)


def flip(value, axis, mask):
    size = lax.axis_size(axis)
    return lax.ppermute(value, axis, [(i, i ^ mask) for i in range(size)])


def bit(axis, mask):
    return (lax.axis_index(axis) // mask) % 2


def halves(value, which, axis=0):
    n = value.shape[axis] // 2
    keep = lax.dynamic_slice_in_dim(value, which * n, n, axis)
    send = lax.dynamic_slice_in_dim(value, (1 - which) * n, n, axis)
    return keep, send


def join(own, other, which, axis=0):
    return jnp.where(
        which == 0,
        jnp.concatenate([own, other], axis=axis),
        jnp.concatenate([other, own], axis=axis),
    )


def add(a, b):
    return (a.astype(F32) + b.astype(F32)).astype(BF16)


def on_device(
    tokens, lengths, ln1_gain, ln1_bias, qkv_weight, q_gain, k_gain, out_weight,
    ln2_gain, ln2_bias, up_weight, down_weight, cotangent,
):
    micro, rows, local, width = tokens.shape
    n = lax.axis_size("seq")
    length = local * n
    every = micro * rows
    team = n // every
    heads = H // team
    hd = width // H
    half = width // 2
    idx = lax.axis_index("seq")
    core = lax.axis_index("fsdp")
    row, member = idx // team, idx % team
    direct = every == 2 and team == 4
    lengths = lengths.reshape(every, lengths.shape[-1])
    mine = tokens.reshape(every, local, width)

    def swap(value):
        return flip(value, "fsdp", 1)

    vec = jnp.concatenate([ln1_gain, ln1_bias, ln2_gain, ln2_bias, q_gain, k_gain])[None]
    vec_p = swap(vec)
    ordered = jnp.where(core == 0, jnp.concatenate([vec, vec_p]), jnp.concatenate([vec_p, vec])).astype(F32)
    g1, b1, g2, b2 = (ordered[:, k * half : (k + 1) * half].reshape(1, width) for k in range(4))
    gq = ordered[:, 4 * half : 4 * half + hd // 2].reshape(hd, 1)
    gk = ordered[:, 4 * half + hd // 2 :].reshape(hd, 1)

    w_own = lax.dynamic_slice_in_dim(
        qkv_weight.reshape(half, 3, width), member * heads * hd, heads * hd, 2
    ).reshape(half, 3 * heads * hd)
    w_t = jnp.transpose(join(w_own, swap(w_own), core))

    if direct:
        near = lax.dynamic_index_in_dim(mine, row, 0, keepdims=False)
        away = lax.dynamic_index_in_dim(mine, 1 - row, 0, keepdims=False)
        far = flip(away, "seq", 4)
        cut = local // 2

        def spread(own):
            one, two = flip(own, "seq", 1), flip(own, "seq", 2)
            three = jnp.concatenate([flip(two[:cut], "seq", 1), flip(one[cut:], "seq", 2)], axis=0)
            return [own, one, two, three]

        slots = spread(near) + spread(far)
        spot = idx
    else:
        same_member = [[q * team + p for q in range(every)] for p in range(team)]
        same_row = [[q * team + p for p in range(team)] for q in range(every)]
        got = lax.all_to_all(mine, "seq", 0, 0, axis_index_groups=same_member, tiled=True)
        got = lax.all_gather(got, "seq", axis_index_groups=same_row)
        whole = jnp.swapaxes(got, 0, 1).reshape(length, width)
        slots = [whole[s * (length // 8) : (s + 1) * (length // 8)] for s in range(8)]
        spot = jnp.int32(0)
    meta = jnp.stack([spot, row, core, bit("rep", 1), bit("seq", 1), bit("seq", 2)]).astype(jnp.int32)

    out_p, up_p, down_p = swap(out_weight), swap(up_weight), swap(down_weight)

    with jax.named_scope("forward_attention"):
        qt, ka, kt, v, vt, x_row = make_qkv(meta, lengths, slots, w_t, g1, b1, gq, gk, heads, hd)
        attn, attn_f, logsum = attend(meta, lengths, qt, ka, vt, heads, hd)

    def exchange(value):
        return lax.all_to_all(value, "seq", 0, 0, tiled=True)

    packs = every * local // BLK
    if direct:
        attn_t = exchange(attn).reshape(packs, width, BLK)
    else:
        cut = jnp.moveaxis(attn.reshape(BLK * 0 + 8, heads * hd, BLK // local, local), 2, 1)
        got = exchange(cut.reshape(n, heads * hd, local))
        got = got.reshape(packs, every // packs, width, local)
        attn_t = jnp.swapaxes(got, 1, 2).reshape(packs, width, BLK)

    total = jnp.sum(lengths[:, :-1], axis=-1)
    places = idx * local + jnp.arange(local, dtype=jnp.int32)
    valid = (places[None] < total[:, None]).astype(F32).reshape(packs, 1, BLK)
    x_home = tokens.reshape(every * local, width)
    dy = cotangent.reshape(every * local, width)

    with jax.named_scope("feed_forward"):
        output, grad_mid, grad_branch, h2, act, dup, grad_attn, vec2 = ffn(
            meta, attn_t, x_home, dy, valid, g2, b2, out_weight, out_p, up_weight, up_p, down_weight, down_p
        )
    if direct:
        grad_o = exchange(grad_attn.reshape(n, heads * hd, BLK))
    else:
        cut = jnp.swapaxes(grad_attn.reshape(packs, width, every // packs, local), 1, 2)
        got = exchange(cut.reshape(n, heads * hd, local))
        got = got.reshape(8, BLK // local, heads * hd, local)
        grad_o = jnp.swapaxes(got, 1, 2).reshape(8, heads * hd, BLK)

    masks = [1 << k for k in range(n.bit_length() - 1)]
    x, y, z = ("rep", 1), ("seq", 1), ("seq", 2)

    def next_half(keep, got, way, axis):
        return halves(add(keep, got), bit(*way), axis)

    with jax.named_scope("weight_gradients"):
        far_d = swap(down_grads(meta, act, dy))
        far_u = swap(up_out_grads(meta, attn_t, grad_branch, h2, dup))
        down_k, down_s = down_grads(meta, act, dy, far_d)
        up_k, up_s, out_k, out_s = up_out_grads(meta, attn_t, grad_branch, h2, dup, far_u)
        grad_o, up_k, up_s, out_k, out_s, down_k, down_s = lax.optimization_barrier(
            (grad_o, up_k, up_s, out_k, out_s, down_k, down_s)
        )
    got = flip(down_s, *x), flip(up_s, *y), flip(out_s, *z)
    back = lambda h, go: attend_back(meta, lengths, qt, ka, kt, v, attn_f, logsum, go, h, 1, hd)
    parts = [back(0, grad_o)]
    with jax.named_scope("weight_gradients"):
        grad_o, *got = lax.optimization_barrier((grad_o, *got))
        down_k, down_s = next_half(down_k, got[0], y, 0)
        up_k, up_s = next_half(up_k, got[1], z, 1)
        out_k, out_s = next_half(out_k, got[2], x, 0)
        got = flip(down_s, *y), flip(up_s, *z), flip(out_s, *x)
    for h in range(1, heads - 1):
        parts.append(back(h, grad_o))
    with jax.named_scope("weight_gradients"):
        grad_o, *got = lax.optimization_barrier((grad_o, *got))
        down_k, down_s = next_half(down_k, got[0], z, 1)
        up_k, up_s = next_half(up_k, got[1], x, 1)
        out_k, out_s = next_half(out_k, got[2], y, 1)
        got = flip(down_s, *z), flip(up_s, *x), flip(out_s, *y)
    parts.append(back(heads - 1, grad_o))
    x_row, *got = lax.optimization_barrier((x_row, *got))
    with jax.named_scope("weight_gradients"):
        down = add(down_k, got[0])
        up = add(up_k, got[1])
        out = add(out_k, got[2])
        if masks[2:]:
            sizes = [down.shape[0], up.shape[0]]
            every_piece = jnp.concatenate([down, up, out])
            for mask in masks[2:]:
                every_piece = add(every_piece, flip(every_piece, "seq", mask))
            down, up, out = jnp.split(every_piece, [sizes[0], sizes[0] + sizes[1]])

    with jax.named_scope("backward_attention"):
        dq, dk, dv = zip(*parts)
        back_a, back_b, dw_t = qkv_back(
            meta, x_row, dq, dk, dv, w_t, g1, b1, gq, gk, vec2, heads, hd
        )
    back_a, back_b, dw_t, down, up, out = lax.optimization_barrier((back_a, back_b, dw_t, down, up, out))
    with jax.named_scope("weight_gradients"):
        down = jnp.concatenate([down, flip(down, *z)], axis=1)
        up = jnp.concatenate([up, flip(up, *x)], axis=1)
        out = jnp.concatenate([out, flip(out, *y)], axis=1)
        down = jnp.concatenate([down, flip(down, *y)], axis=0)
        up = jnp.concatenate([up, flip(up, *z)], axis=1)
        out = jnp.concatenate([out, flip(out, *x)], axis=0)
        grad_down, grad_up, grad_out = assemble(
            meta, (down, flip(down, *x)), (up, flip(up, *y)), (out, flip(out, *z))
        )

    if direct:

        def gather(parts):
            a = parts[0].reshape(2, 2, 2, local, half)
            b = parts[1].reshape(2, 2, 2, local, half)
            out = []
            for kind in (1, 0):
                a1 = add(a[kind, :, 0], flip(a[kind, :, 1], "seq", 1))
                b1 = add(b[kind, 0], flip(b[kind, 1], "seq", 2))
                a2 = add(a1[0], flip(a1[1], "seq", 2))
                b2 = add(b1[0], flip(b1[1], "seq", 1))
                out.append(jnp.concatenate([a2, b2], axis=1))
            return out

        far_sum, near_sum = gather((back_a, back_b))
        other = flip(far_sum, "seq", 4)
        back = jnp.where(
            row == 0, jnp.stack([near_sum, other]), jnp.stack([other, near_sum])
        ).reshape(every * local, width)
    else:
        whole = jnp.concatenate([back_a, back_b], axis=-1).reshape(every, team, local, width)
        whole = lax.psum_scatter(whole, "seq", scatter_dimension=1, axis_index_groups=same_row, tiled=True)
        got = lax.all_to_all(whole[:, 0], "seq", 0, 0, axis_index_groups=same_member, tiled=True)
        back = got.reshape(every * local, width)
    grad_tokens = finish(x_home, grad_mid, back, g1)

    with jax.named_scope("first_projection_gradient"):
        keep, send = halves(dw_t, core, 1)
        piece, send = next_half(keep, swap(send), x, 0)
        piece = add(piece, flip(send, *x))
        for mask in masks:
            if mask >= team:
                piece = add(piece, flip(piece, "seq", mask))
        piece = jnp.stack([piece, flip(piece, *x)])
        piece = jnp.concatenate([piece, flip(piece, *y)], axis=0)
        grad_qkv, small = assemble_qkv(meta, piece, flip(piece, *z), heads, hd)
        cuts = [small[0], small[1], small[2], small[3], small[4, : hd // 2], small[4, hd // 2 : hd]]
    shape = tokens.shape
    return (
        output.reshape(shape), grad_tokens.reshape(shape), cuts[0], cuts[1], grad_qkv, cuts[4], cuts[5],
        grad_out, cuts[2], cuts[3], grad_up, grad_down,
    )


def solution(mesh):
    tok = P(None, ("rep", "fsdp"), "seq", None)
    one, two = P("fsdp"), P("fsdp", None)
    in_specs = (tok, P(None, ("rep", "fsdp"), None), one, one, two, one, one, two, one, one, two, two, tok)
    out_specs = (tok, tok, one, one, two, one, one, two, one, one, two, two)
    return jax.shard_map(on_device, mesh=mesh, in_specs=in_specs, out_specs=out_specs, check_vma=False)
```

```python
import functools

import jax
import jax.numpy as jnp
from jax import lax
from jax.experimental import pallas as pl
from jax.experimental.pallas import tpu as pltpu
from jax.sharding import PartitionSpec as P

H = 12
EPS = 1e-06
LOG2E = 1.4426950408889634
SHIFT = 512.0
BLK = 256
EXTRA = 32
NN = (((1,), (0,)), ((), ()))
NT = (((1,), (1,)), ((), ()))
TN = (((0,), (0,)), ((), ()))
F32 = jnp.float32
BF16 = jnp.bfloat16


def mm(a, b, dims=NN):
    return lax.dot_general(a, b, dims, preferred_element_type=F32)


def params(**kw):
    return pltpu.CompilerParams(vmem_limit_bytes=60 * 1024 * 1024, **kw)


def cost(us):
    return pl.CostEstimate(flops=int(us * 0.35e9), bytes_accessed=1024, transcendentals=0)


def norm_rows(v):
    center = jnp.mean(v, axis=-1, keepdims=True)
    centred = v - center
    inv = lax.rsqrt(jnp.mean(centred * centred, axis=-1, keepdims=True) + EPS)
    return centred * inv, inv


def norm_cols(v):
    center = jnp.mean(v, axis=0, keepdims=True)
    centred = v - center
    inv = lax.rsqrt(jnp.mean(centred * centred, axis=0, keepdims=True) + EPS)
    return centred * inv, inv


def bounds_of(len_ref, row):
    out = []
    total = jnp.int32(0)
    for j in range(len_ref.shape[1] - 1):
        total = total + len_ref[row, j]
        out.append(total)
    return out


def qkv_body(heads, hd, meta, len_ref, *refs):
    xs = refs[:8]
    w_ref, g_ref, b_ref, gq_ref, gk_ref = refs[8:13]
    qt_ref, ka_ref, kt_ref, v_ref, vt_ref, x_ref = refs[13:]
    wid = heads * hd
    spot, row = meta[0], meta[1]
    bounds = bounds_of(len_ref, row)
    for s in range(8):
        c = jnp.bitwise_xor(spot, s)
        cols = pl.ds(pl.multiple_of(c * BLK, BLK), BLK)
        x = xs[s][...]
        x_ref[cols, :] = x
        hat, _ = norm_rows(x.astype(F32))
        first = (hat * g_ref[...] + b_ref[...]).astype(BF16)
        qkv = mm(w_ref[...], first, NT)
        place = c * BLK + lax.broadcasted_iota(jnp.int32, (8, BLK), 1)
        ident = jnp.zeros((8, BLK), jnp.int32)
        place_k = c * BLK + lax.broadcasted_iota(jnp.int32, (BLK, 128), 0)
        ident_k = jnp.zeros((BLK, 128), jnp.int32)
        for bound in bounds:
            ident = ident + (place >= bound).astype(jnp.int32)
            ident_k = ident_k + (place_k >= bound).astype(jnp.int32)
        which = lax.broadcasted_iota(jnp.int32, (8, BLK), 0)
        hot = jnp.where((ident == which) & (which < len(bounds)), 16.0, 0.0)
        hot = jnp.concatenate([hot, jnp.zeros((hd - 8, BLK), F32)], axis=0)
        lane = lax.broadcasted_iota(jnp.int32, (BLK, 128), 1) - hd
        hot_k = jnp.where((ident_k == lane) & (lane < len(bounds)), SHIFT / 16.0, 0.0)
        for h in range(heads):
            q, _ = norm_cols(qkv[h * hd : (h + 1) * hd])
            k, _ = norm_cols(qkv[wid + h * hd : wid + (h + 1) * hd])
            q = (q * gq_ref[...]).astype(BF16).astype(F32) * (hd**-0.5)
            k = k * gk_ref[...]
            v = qkv[2 * wid + h * hd : 2 * wid + (h + 1) * hd]
            qt_ref[h, :, cols] = jnp.concatenate([q, hot], axis=0).astype(BF16)
            kt_ref[h, :, cols] = k.astype(BF16)
            vt_ref[h, :, cols] = v.astype(BF16)
            both = jnp.transpose(jnp.concatenate([k, v], axis=0))
            ka_ref[h, cols, :] = jnp.where(lane < 0, both, hot_k).astype(BF16)
            v_ref[h, cols, :] = both[:, hd:].astype(BF16)


def make_qkv(meta, lengths, slots, w_t, gain, bias, gq, gk, heads, hd):
    length = 8 * slots[0].shape[0]
    width = slots[0].shape[1]
    smem = pl.BlockSpec(memory_space=pltpu.SMEM)
    vmem = pl.BlockSpec(memory_space=pltpu.VMEM)
    return pl.pallas_call(
        functools.partial(qkv_body, heads, hd),
        out_shape=(
            jax.ShapeDtypeStruct((heads, 2 * hd, length), BF16),
            jax.ShapeDtypeStruct((heads, length, 2 * hd), BF16),
            jax.ShapeDtypeStruct((heads, hd, length), BF16),
            jax.ShapeDtypeStruct((heads, length, hd), BF16),
            jax.ShapeDtypeStruct((heads, hd, length), BF16),
            jax.ShapeDtypeStruct((length, width), BF16),
        ),
        in_specs=[smem, smem] + [vmem] * 13,
        out_specs=(vmem,) * 6,
        compiler_params=params(),
        cost_estimate=cost(12),
        name="qkv_forward",
    )(meta, lengths, *slots, w_t, gain, bias, gq, gk)


def block_range(bounds, i):
    first = i * BLK
    last = first + BLK - 1
    lo = jnp.int32(0)
    hi = bounds[-1]
    for bound in bounds:
        lo = jnp.where(first >= bound, bound, lo)
    for bound in bounds[::-1]:
        hi = jnp.where(last < bound, bound, hi)
    lo_b = lo // BLK
    hi_b = (hi + BLK - 1) // BLK
    return lo_b, jnp.where(first >= bounds[-1], lo_b, hi_b)


def attend_body(heads, hd, meta, len_ref, qt_ref, ka_ref, vt_ref, o_ref, of_ref, ls_ref):
    i = pl.program_id(0)
    bounds = bounds_of(len_ref, meta[1])
    lo, hi = block_range(bounds, i)

    def step(b, carry):
        rows = pl.ds(pl.multiple_of(b * BLK, BLK), BLK)
        out = []
        for h in range(heads):
            acc, total = carry[h]
            scores = mm(ka_ref[h, rows, :], qt_ref[h])
            expo = jnp.exp2(scores * LOG2E - SHIFT * LOG2E)
            total = total + jnp.sum(expo.reshape(BLK // 8, 8, BLK), axis=0)
            acc = acc + mm(vt_ref[h, :, rows], expo.astype(BF16))
            out.append((acc, total))
        return tuple(out)

    init = tuple((jnp.zeros((hd, BLK), F32), jnp.zeros((8, BLK), F32)) for _ in range(heads))
    done = lax.fori_loop(lo, hi, step, init)
    for h in range(heads):
        acc, total = done[h]
        total = jnp.sum(total, axis=0, keepdims=True)
        live = total > 0.0
        safe = jnp.where(live, total, 1.0)
        out = jnp.where(live, acc * (1.0 / safe), 0.0)
        o_ref[0, h * hd : (h + 1) * hd, :] = out.astype(BF16)
        of_ref[h] = out
        ls_ref[h] = jnp.log2(safe) + SHIFT * LOG2E


def attend(meta, lengths, qt, ka, vt, heads, hd):
    length = qt.shape[2]
    blocks = length // BLK
    smem = pl.BlockSpec(memory_space=pltpu.SMEM)
    return pl.pallas_call(
        functools.partial(attend_body, heads, hd),
        grid=(blocks,),
        out_shape=(
            jax.ShapeDtypeStruct((blocks, heads * hd, BLK), BF16),
            jax.ShapeDtypeStruct((heads, hd, length), F32),
            jax.ShapeDtypeStruct((heads, 1, length), F32),
        ),
        in_specs=[
            smem,
            smem,
            pl.BlockSpec((heads, 2 * hd, BLK), lambda i: (0, 0, i)),
            pl.BlockSpec((heads, length, 2 * hd), lambda i: (0, 0, 0)),
            pl.BlockSpec((heads, hd, length), lambda i: (0, 0, 0)),
        ],
        out_specs=(
            pl.BlockSpec((1, heads * hd, BLK), lambda i: (i, 0, 0)),
            pl.BlockSpec((heads, hd, BLK), lambda i: (0, 0, i)),
            pl.BlockSpec((heads, 1, BLK), lambda i: (0, 0, i)),
        ),
        compiler_params=params(),
        cost_estimate=cost(25),
        name="attention_forward",
    )(meta, lengths, qt, ka, vt)


def attend_back_body(
    heads, hd, meta, len_ref, qt_ref, ka_ref, kt_ref, v_ref, of_ref, ls_ref, go_ref, dq_ref, dk_ref, dv_ref
):
    i = pl.program_id(0)
    bounds = bounds_of(len_ref, meta[1])
    lo, hi = block_range(bounds, i)

    @pl.when(i == 0)
    def _():
        dk_ref[...] = jnp.zeros_like(dk_ref)
        dv_ref[...] = jnp.zeros_like(dv_ref)

    inner = []
    for h in range(heads):
        go = go_ref[0, h * hd : (h + 1) * hd, :].astype(F32)
        inner.append(jnp.sum(go * of_ref[h], axis=0, keepdims=True))

    def step(b, carry):
        rows = pl.ds(pl.multiple_of(b * BLK, BLK), BLK)
        out = []
        for h in range(heads):
            go = go_ref[0, h * hd : (h + 1) * hd, :]
            qt = qt_ref[h]
            scores = mm(ka_ref[h, rows, :], qt)
            probs = jnp.exp2(scores * LOG2E - ls_ref[h])
            grad_probs = mm(v_ref[h, rows, :], go)
            grad_scores = (probs * (grad_probs - inner[h])).astype(BF16)
            dv_ref[h, :, rows] += mm(go, probs.astype(BF16), NT)
            dk_ref[h, :, rows] += mm(qt[:hd], grad_scores, NT)
            out.append(carry[h] + mm(kt_ref[h, :, rows], grad_scores))
        return tuple(out)

    done = lax.fori_loop(lo, hi, step, tuple(jnp.zeros((hd, BLK), F32) for _ in range(heads)))
    for h in range(heads):
        dq_ref[h] = done[h] * (hd**-0.5)


def attend_back(meta, lengths, qt, ka, kt, v, of, ls, go, at, heads, hd):
    length = qt.shape[2]
    blocks = length // BLK
    smem = pl.BlockSpec(memory_space=pltpu.SMEM)
    whole = lambda *shape: pl.BlockSpec(shape, lambda i: (at, 0, 0))
    all_out = lambda *shape: pl.BlockSpec(shape, lambda i: (0, 0, 0))
    return pl.pallas_call(
        functools.partial(attend_back_body, heads, hd),
        grid=(blocks,),
        out_shape=tuple(jax.ShapeDtypeStruct((heads, hd, length), F32) for _ in range(3)),
        in_specs=[
            smem,
            smem,
            pl.BlockSpec((heads, 2 * hd, BLK), lambda i: (at, 0, i)),
            whole(heads, length, 2 * hd),
            whole(heads, hd, length),
            whole(heads, length, hd),
            pl.BlockSpec((heads, hd, BLK), lambda i: (at, 0, i)),
            pl.BlockSpec((heads, 1, BLK), lambda i: (at, 0, i)),
            pl.BlockSpec((1, heads * hd, BLK), lambda i: (i, at, 0)),
        ],
        out_specs=(
            pl.BlockSpec((heads, hd, BLK), lambda i: (0, 0, i)),
            all_out(heads, hd, length),
            all_out(heads, hd, length),
        ),
        compiler_params=params(),
        cost_estimate=cost(11 * heads),
        name="attention_backward",
    )(meta, lengths, qt, ka, kt, v, of, ls, go)


def qkv_back_body(
    heads, hd, meta, x_ref, *refs
):
    dqs, dks, dvs = refs[:heads], refs[heads : 2 * heads], refs[2 * heads : 3 * heads]
    w_ref, g_ref, b_ref, gq_ref, gk_ref, vec2_ref, da_ref, db_ref, dw_ref, acc_ref, vec_ref, gain_ref = refs[3 * heads :]
    i = pl.program_id(0)
    wid = heads * hd

    @pl.when(i == 0)
    def _():
        acc_ref[...] = jnp.zeros_like(acc_ref)
        vec_ref[...] = jnp.zeros_like(vec_ref)
        gain_ref[...] = jnp.zeros_like(gain_ref)

    hat, _ = norm_rows(x_ref[...].astype(F32))
    first = (hat * g_ref[...] + b_ref[...]).astype(BF16)
    qk = mm(w_ref[: 2 * wid, :], first, NT)
    pieces = []
    for at, gain, grad in ((0, gq_ref, dqs), (1, gk_ref, dks)):
        for h in range(heads):
            unit, inv = norm_cols(qk[at * wid + h * hd : at * wid + (h + 1) * hd])
            gy = grad[h][0]
            gain_ref[at] += gy * unit
            e = gy * gain[...]
            pieces.append(
                inv
                * (
                    e
                    - jnp.mean(e, axis=0, keepdims=True)
                    - unit * jnp.mean(e * unit, axis=0, keepdims=True)
                )
            )
    for h in range(heads):
        pieces.append(dvs[h][0])
    grad = jnp.concatenate(pieces, axis=0).astype(BF16)
    acc_ref[...] += mm(grad, first)
    back = mm(grad, w_ref[...], TN)
    vec_ref[0] += jnp.sum((back * hat).reshape(BLK // 8, 8, -1), axis=0)
    vec_ref[1] += jnp.sum(back.reshape(BLK // 8, 8, -1), axis=0)
    half = back.shape[1] // 2
    da_ref[0] = back[:, :half].astype(BF16)
    db_ref[0] = back[:, half:].astype(BF16)

    @pl.when(i == pl.num_programs(0) - 1)
    def _():
        dw_ref[: 3 * wid, :] = acc_ref[...].astype(BF16)
        lines = [jnp.sum(ref[k], axis=0, keepdims=True) for ref in (vec_ref, vec2_ref) for k in range(2)]
        width = dw_ref.shape[1]
        lane = lax.broadcasted_iota(jnp.int32, (hd, width), 1)
        item = lax.broadcasted_iota(jnp.int32, (hd, width), 0)
        spread = jnp.where(item < hd // 2, item, item - hd // 2 + width // 2)
        line = jnp.zeros((8, width), F32)
        for k in range(2):
            total = lax.dot_general(
                jnp.ones((8, BLK), F32), gain_ref[k], NT, precision=lax.Precision.HIGHEST, preferred_element_type=F32
            )
            pick = (lane == spread + k * (hd // 2)).astype(F32)
            line = line + lax.dot_general(
                total, pick, NN, precision=lax.Precision.HIGHEST, preferred_element_type=F32
            )
        lines.append(line[:1])
        place = lax.broadcasted_iota(jnp.int32, (EXTRA, width), 0)
        below = jnp.zeros((EXTRA, width), F32)
        for k, one in enumerate(lines):
            below = jnp.where(place == k, one, below)
        dw_ref[3 * wid :, :] = below.astype(BF16)


def qkv_back(meta, x, dq, dk, dv, w_t, gain, bias, gq, gk, vec2, heads, hd):
    length, width = x.shape
    blocks = length // BLK
    whole = lambda *shape: pl.BlockSpec(shape, lambda i, m: (0,) * len(shape))
    part = pl.BlockSpec((1, hd, BLK), lambda i, m: (0, 0, i))
    grads = pl.BlockSpec((1, BLK, width // 2), lambda i, m: (jnp.bitwise_xor(i, m[0]), 0, 0))
    return pl.pallas_call(
        functools.partial(qkv_back_body, heads, hd),
        grid_spec=pltpu.PrefetchScalarGridSpec(
            num_scalar_prefetch=1,
            grid=(blocks,),
            in_specs=[
                pl.BlockSpec((BLK, width), lambda i, m: (i, 0)),
                *([part] * (3 * heads)),
                whole(*w_t.shape),
                whole(1, width),
                whole(1, width),
                whole(hd, 1),
                whole(hd, 1),
                whole(2, 8, width),
            ],
            out_specs=(
                grads,
                grads,
                whole(w_t.shape[0] + EXTRA, width),
            ),
            scratch_shapes=[
                pltpu.VMEM(w_t.shape, F32),
                pltpu.VMEM((2, 8, width), F32),
                pltpu.VMEM((2, hd, BLK), F32),
            ],
        ),
        out_shape=(
            jax.ShapeDtypeStruct((blocks, BLK, width // 2), BF16),
            jax.ShapeDtypeStruct((blocks, BLK, width // 2), BF16),
            jax.ShapeDtypeStruct((w_t.shape[0] + EXTRA, width), BF16),
        ),
        compiler_params=params(),
        cost_estimate=cost(17),
        name="qkv_backward",
    )(meta, x, *dq, *dk, *dv, w_t, gain, bias, gq, gk, vec2)


def assemble_qkv(meta, pieces, heads, hd):
    _, part, half = pieces[0].shape
    team = 4
    wid = heads * hd
    turned = team * wid

    def body(meta, p00, p01, p10, p11, out_ref, vec_ref, all_s):
        t = pl.program_id(0)

        @pl.when(t == 0)
        def _():
            for y in range(2):
                at = jnp.bitwise_xor(meta[4], y)
                for z in range(2):
                    own_z = meta[5] == z
                    near, away = jnp.where(own_z, p00[at], p01[at]), jnp.where(own_z, p10[at], p11[at])
                    for x in range(2):
                        all_s[2 * z + y, x * part : (x + 1) * part, :] = jnp.where(meta[3] == x, near, away)
            total = jnp.zeros((EXTRA, half), F32)
            for p in range(team):
                total = total + all_s[p, 3 * wid :, :].astype(F32)
            vec_ref[...] = total

        rows = pl.ds(pl.multiple_of(t * wid, wid), wid)
        piece = jnp.concatenate([all_s[p, rows, :] for p in range(team)], axis=0)
        out_ref[...] = jnp.transpose(piece.astype(F32))

    whole = lambda *shape: pl.BlockSpec(shape, lambda i, m: (0,) * len(shape))
    return pl.pallas_call(
        body,
        grid_spec=pltpu.PrefetchScalarGridSpec(
            num_scalar_prefetch=1,
            grid=(3,),
            in_specs=[whole(2, part, half)] * 4,
            out_specs=(pl.BlockSpec((half, turned), lambda i, m: (0, i)), whole(EXTRA, half)),
            scratch_shapes=[pltpu.VMEM((team, 2 * part, half), BF16)],
        ),
        out_shape=(jax.ShapeDtypeStruct((half, 3 * turned), F32), jax.ShapeDtypeStruct((EXTRA, half), F32)),
        compiler_params=params(),
        cost_estimate=cost(5),
        name="first_projection_gradient",
    )(meta, *pieces)


def gelu_pair(u):
    a = jnp.abs(u)
    t = 1.0 / (1.0 + (0.3275911 * 0.7071067811865476) * a)
    poly = 1.061405429 * t - 1.453152027
    poly = poly * t + 1.421413741
    poly = poly * t - 0.284496736
    poly = poly * t + 0.254829592
    bell = jnp.exp(-0.5 * (u * u))
    tail = (0.5 * poly) * t * bell
    cdf = jnp.where(u >= 0.0, 1.0 - tail, tail)
    return u * cdf, cdf + u * (bell * 0.3989422804014327)


def ffn(meta, attn_t, x, dy, valid, gain, bias, wo, wo_p, up, up_p, dn, dn_p):
    tokens, width = x.shape
    hidden = up.shape[1]
    fc = 512
    steps = hidden // fc
    near = steps // 2
    packs, _, lanes = attn_t.shape
    whole = lambda *shape: pl.BlockSpec(shape, lambda i, m: (0,) * len(shape))
    ups = pl.BlockSpec((width // 2, fc), lambda i, m: (0, lax.rem(m[2] * near + i, steps)))
    acts = pl.BlockSpec((tokens, fc), lambda i, m: (0, lax.rem(m[2] * near + i, steps)))
    half = width // 2

    def body(meta, *refs):
        (at_ref, x_ref, dy_ref, valid_ref, g_ref, b_ref, wo_own, wo_peer, up_own, up_peer, dn_own, dn_peer) = refs[:12]
        (out_ref, gm_ref, gb_ref, h2_ref, act_ref, dup_ref, da_ref, vec_ref) = refs[12:20]
        (mid_s, acc_s, own_s, peer_s, gown_s, gpeer_s) = refs[20:]
        i = pl.program_id(0)
        core = meta[2]
        zero = core == 0

        @pl.when(i == 0)
        def _():
            for p in range(packs):
                rows = pl.ds(p * lanes, lanes)
                own = at_ref[p, pl.ds(pl.multiple_of(core * half, half), half), :]
                peer = at_ref[p, pl.ds(pl.multiple_of((1 - core) * half, half), half), :]
                mid = x_ref[rows, :].astype(F32) + mm(own, wo_own[...], TN) + mm(peer, wo_peer[...], TN)
                mid_s[rows, :] = mid
                acc_s[rows, :] = mid
                hat, _ = norm_rows(mid)
                second = (hat * g_ref[...] + b_ref[...]).astype(BF16)
                h2_ref[rows, :] = second
                lo, hi = second[:, :half], second[:, half:]
                own_s[rows, :] = jnp.where(zero, lo, hi)
                peer_s[rows, :] = jnp.where(zero, hi, lo)
            gown_s[...] = jnp.zeros_like(gown_s)
            gpeer_s[...] = jnp.zeros_like(gpeer_s)

        down = jnp.where(i < near, dn_own[...], dn_peer[...])
        upper = mm(own_s[...], up_own[...]) + mm(peer_s[...], up_peer[...])
        act, slope = gelu_pair(upper)
        act = act.astype(BF16)
        grad = (mm(dy_ref[...], down, NT) * slope).astype(BF16)
        act_ref[...] = act
        dup_ref[...] = grad
        acc_s[...] += mm(act, down)
        gown_s[...] += mm(grad, up_own[...], NT)
        gpeer_s[...] += mm(grad, up_peer[...], NT)

        @pl.when(i == steps - 1)
        def _():
            out_ref[...] = acc_s[...].astype(BF16)
            vec = [jnp.zeros((8, width), F32), jnp.zeros((8, width), F32)]
            for p in range(packs):
                rows = pl.ds(p * lanes, lanes)
                hat, inv = norm_rows(mid_s[rows, :])
                a, b = gown_s[rows, :], gpeer_s[rows, :]
                gy = jnp.concatenate([jnp.where(zero, a, b), jnp.where(zero, b, a)], axis=1)
                vec[0] = vec[0] + jnp.sum((gy * hat).reshape(lanes // 8, 8, width), axis=0)
                vec[1] = vec[1] + jnp.sum(gy.reshape(lanes // 8, 8, width), axis=0)
                e = gy * g_ref[...]
                gm = dy_ref[rows, :].astype(F32) + inv * (
                    e
                    - jnp.mean(e, axis=-1, keepdims=True)
                    - hat * jnp.mean(e * hat, axis=-1, keepdims=True)
                )
                gm_ref[rows, :] = gm
                gb = gm.astype(BF16)
                gb_ref[rows, :] = gb
                ok = valid_ref[p]
                da_ref[p, pl.ds(pl.multiple_of(core * half, half), half), :] = (
                    mm(wo_own[...], gb, NT) * ok
                ).astype(BF16)
                da_ref[p, pl.ds(pl.multiple_of((1 - core) * half, half), half), :] = (
                    mm(wo_peer[...], gb, NT) * ok
                ).astype(BF16)
            vec_ref[0] = vec[0]
            vec_ref[1] = vec[1]

    return pl.pallas_call(
        body,
        grid_spec=pltpu.PrefetchScalarGridSpec(
            num_scalar_prefetch=1,
            grid=(steps,),
            in_specs=[
                whole(*attn_t.shape),
                whole(tokens, width),
                whole(tokens, width),
                whole(*valid.shape),
                whole(1, width),
                whole(1, width),
                whole(half, width),
                whole(half, width),
                ups,
                ups,
                pl.BlockSpec((fc, width), lambda i, m: (jnp.minimum(i, near - 1), 0)),
                pl.BlockSpec((fc, width), lambda i, m: (jnp.maximum(i - near, 0), 0)),
            ],
            out_specs=(
                whole(tokens, width),
                whole(tokens, width),
                whole(tokens, width),
                whole(tokens, width),
                acts,
                acts,
                whole(*attn_t.shape),
                whole(2, 8, width),
            ),
            scratch_shapes=[
                pltpu.VMEM((tokens, width), F32),
                pltpu.VMEM((tokens, width), F32),
                pltpu.VMEM((tokens, half), BF16),
                pltpu.VMEM((tokens, half), BF16),
                pltpu.VMEM((tokens, half), F32),
                pltpu.VMEM((tokens, half), F32),
            ],
        ),
        out_shape=(
            jax.ShapeDtypeStruct((tokens, width), BF16),
            jax.ShapeDtypeStruct((tokens, width), F32),
            jax.ShapeDtypeStruct((tokens, width), BF16),
            jax.ShapeDtypeStruct((tokens, width), BF16),
            jax.ShapeDtypeStruct((tokens, hidden), BF16),
            jax.ShapeDtypeStruct((tokens, hidden), BF16),
            jax.ShapeDtypeStruct(attn_t.shape, BF16),
            jax.ShapeDtypeStruct((2, 8, width), F32),
        ),
        compiler_params=params(),
        cost_estimate=cost(25),
        name="ffn_both_ways",
    )(meta, attn_t, x, dy, valid, gain, bias, wo, wo_p, up, up_p, dn, dn_p)


def up_out_grads(meta, attn_t, gb, h2, dup, far=None):
    tokens, width = gb.shape
    hidden = dup.shape[1]
    half = width // 2
    packs, _, lanes = attn_t.shape
    n = hidden // width
    own = far is not None

    def column(j, m):
        bit = jnp.where(j < n // 2, m[4], 1 - m[4])
        return bit * (n // 2) + lax.rem(jnp.minimum(j, n - 1), n // 2)

    def body(meta, at_ref, gb_ref, h2_ref, dup_ref, *rest):
        j = pl.program_id(0)
        side = meta[2] if own else 1 - meta[2]

        def up():
            part = jnp.where(side == 0, h2_ref[:, :half], h2_ref[:, half:])
            return mm(part, dup_ref[...], TN)

        def out():
            rows = pl.ds(pl.multiple_of(side * half, half), half)
            total = jnp.zeros((half, width), F32)
            for p in range(packs):
                total = total + mm(at_ref[p, rows, :], gb_ref[p * lanes : (p + 1) * lanes, :])
            lo, hi = total[: half // 2], total[half // 2 :]
            return jnp.where(meta[5] == 0, lo, hi), jnp.where(meta[5] == 0, hi, lo)

        if own:
            far_ref, uk_ref, us_ref, ok_ref, os_ref = rest

            @pl.when(j < n // 2)
            def _():
                uk_ref[...] = (up() + far_ref[...].astype(F32)).astype(BF16)

            @pl.when((j >= n // 2) & (j < n))
            def _():
                us_ref[...] = (up() + far_ref[...].astype(F32)).astype(BF16)

            @pl.when(j == n)
            def _():
                keep, send = out()
                ok_ref[...] = (keep + far_ref[: half // 2].astype(F32)).astype(BF16)
                os_ref[...] = (send + far_ref[half // 2 :].astype(F32)).astype(BF16)
        else:
            (out_ref,) = rest

            @pl.when(j < n)
            def _():
                out_ref[...] = up().astype(BF16)

            @pl.when(j == n)
            def _():
                keep, send = out()
                out_ref[: half // 2] = keep.astype(BF16)
                out_ref[half // 2 :] = send.astype(BF16)

    whole = lambda *shape: pl.BlockSpec(shape, lambda j, m: (0,) * len(shape))
    block = lambda index: pl.BlockSpec((half, width), index)
    if own:
        out_specs = (
            block(lambda j, m: (0, jnp.minimum(j, n // 2 - 1))),
            block(lambda j, m: (0, jnp.clip(j - n // 2, 0, n // 2 - 1))),
            whole(half // 2, width),
            whole(half // 2, width),
        )
        shapes = [(half, hidden // 2)] * 2 + [(half // 2, width)] * 2
        out_shape = tuple(jax.ShapeDtypeStruct(shape, BF16) for shape in shapes)
    else:
        out_specs = block(lambda j, m: (0, j))
        out_shape = jax.ShapeDtypeStruct((half, hidden + width), BF16)
    return pl.pallas_call(
        body,
        grid_spec=pltpu.PrefetchScalarGridSpec(
            num_scalar_prefetch=1,
            grid=(n + 1,),
            in_specs=[
                whole(*attn_t.shape),
                whole(tokens, width),
                whole(tokens, width),
                pl.BlockSpec((tokens, width), lambda j, m: (0, column(j, m))),
                *([block(lambda j, m: (0, j))] if own else []),
            ],
            out_specs=out_specs,
        ),
        out_shape=out_shape,
        compiler_params=params(),
        cost_estimate=cost(7),
        name="up_out_gradient",
    )(meta, attn_t, gb, h2, dup, *([far] if own else []))


def down_grads(meta, act, dy, far=None):
    tokens, width = dy.shape
    half = width // 2
    n = act.shape[1] // 2 // half
    own = far is not None

    def body(meta, act_ref, dy_ref, *rest):
        value = mm(act_ref[...], dy_ref[...], TN)
        if own:
            far_ref, keep_ref, send_ref = rest
            j = pl.program_id(0)
            value = (value + far_ref[...].astype(F32)).astype(BF16)

            @pl.when(j < n // 2)
            def _():
                keep_ref[...] = value

            @pl.when(j >= n // 2)
            def _():
                send_ref[...] = value
        else:
            (out_ref,) = rest
            out_ref[...] = value.astype(BF16)

    def column(j, m):
        side = m[2] if own else 1 - m[2]
        bit = jnp.where(j < n // 2, m[3], 1 - m[3])
        return side * n + bit * (n // 2) + lax.rem(j, n // 2)

    block = lambda index: pl.BlockSpec((half, width), index)
    if own:
        out_specs = (
            block(lambda j, m: (jnp.minimum(j, n // 2 - 1), 0)),
            block(lambda j, m: (jnp.maximum(j - n // 2, 0), 0)),
        )
        out_shape = (jax.ShapeDtypeStruct((n // 2 * half, width), BF16),) * 2
    else:
        out_specs = block(lambda j, m: (j, 0))
        out_shape = jax.ShapeDtypeStruct((n * half, width), BF16)
    return pl.pallas_call(
        body,
        grid_spec=pltpu.PrefetchScalarGridSpec(
            num_scalar_prefetch=1,
            grid=(n,),
            in_specs=[
                pl.BlockSpec((tokens, half), lambda j, m: (0, column(j, m))),
                pl.BlockSpec((tokens, width), lambda j, m: (0, 0)),
                *([block(lambda j, m: (j, 0))] if own else []),
            ],
            out_specs=out_specs,
        ),
        out_shape=out_shape,
        compiler_params=params(),
        cost_estimate=cost(6),
        name="down_gradient",
    )(meta, act, dy, *([far] if own else []))


def assemble(meta, downs, ups, outs):
    half, width = outs[0].shape[0] * 2, outs[0].shape[1]
    hidden = ups[0].shape[1] * 2
    cut = width // 2

    def body(meta, down_aa, down_ab, down_ba, down_bb, up_a, up_b, out_a, out_b, down_ref, up_ref, out_ref):
        i = pl.program_id(0)

        def place(ref, value, swapped):
            lo, hi = value[:, :cut].astype(F32), value[:, cut:].astype(F32)
            ref[:, :cut] = jnp.where(swapped == 0, lo, hi)
            ref[:, cut:] = jnp.where(swapped == 0, hi, lo)

        down_x, down_y = i // 2 == meta[3], lax.rem(i, 2) == meta[4]
        own_x = jnp.where(down_y, down_aa[...], down_ab[...])
        place(down_ref, jnp.where(down_x, own_x, jnp.where(down_y, down_ba[...], down_bb[...])), meta[5])
        up_own = i // 2 == meta[4]
        place(up_ref, jnp.where(up_own, up_a[...], up_b[...]), meta[3])

        @pl.when(i == 0)
        def _():
            quarter = half // 4
            for z in range(2):
                for x in range(2):
                    rows = pl.ds(pl.multiple_of(jnp.bitwise_xor(meta[3], x) * quarter, quarter), quarter)
                    value = jnp.where(meta[5] == z, out_a[rows, :], out_b[rows, :])
                    place(out_ref.at[pl.ds((2 * z + x) * quarter, quarter)], value, meta[4])

    whole = lambda *shape: pl.BlockSpec(shape, lambda i, m: (0,) * len(shape))
    down = whole(half, width)
    up = pl.BlockSpec((half, width), lambda i, m: (0, jnp.bitwise_xor(lax.rem(i, 2), m[5])))
    return pl.pallas_call(
        body,
        grid_spec=pltpu.PrefetchScalarGridSpec(
            num_scalar_prefetch=1,
            grid=(4,),
            in_specs=[down, down, down, down, up, up, whole(*outs[0].shape), whole(*outs[0].shape)],
            out_specs=(
                pl.BlockSpec((half, width), lambda i, m: (i, 0)),
                pl.BlockSpec((half, width), lambda i, m: (0, i)),
                whole(half, width),
            ),
        ),
        out_shape=(
            jax.ShapeDtypeStruct((4 * half, width), F32),
            jax.ShapeDtypeStruct((half, hidden), F32),
            jax.ShapeDtypeStruct((half, width), F32),
        ),
        compiler_params=params(),
        cost_estimate=cost(7),
        name="weight_gradients",
    )(meta, *downs, *ups, *outs)


def finish_body(x_ref, gm_ref, back_ref, g_ref, out_ref):
    hat, inv = norm_rows(x_ref[...].astype(F32))
    e = back_ref[...].astype(F32) * g_ref[...]
    out_ref[...] = gm_ref[...] + inv * (
        e - jnp.mean(e, axis=-1, keepdims=True) - hat * jnp.mean(e * hat, axis=-1, keepdims=True)
    )


def finish(x, gm, back, gain):
    tokens, width = x.shape
    rows = pl.BlockSpec((128, width), lambda i: (i, 0))
    return pl.pallas_call(
        finish_body,
        grid=(tokens // 128,),
        in_specs=[rows, rows, rows, pl.BlockSpec((1, width), lambda i: (0, 0))],
        out_specs=rows,
        out_shape=jax.ShapeDtypeStruct((tokens, width), F32),
        compiler_params=params(),
        cost_estimate=cost(4),
        name="first_norm_backward",
    )(x, gm, back, gain)


def flip(value, axis, mask):
    size = lax.axis_size(axis)
    return lax.ppermute(value, axis, [(i, i ^ mask) for i in range(size)])


def bit(axis, mask):
    return (lax.axis_index(axis) // mask) % 2


def halves(value, which, axis=0):
    n = value.shape[axis] // 2
    keep = lax.dynamic_slice_in_dim(value, which * n, n, axis)
    send = lax.dynamic_slice_in_dim(value, (1 - which) * n, n, axis)
    return keep, send


def join(own, other, which, axis=0):
    return jnp.where(
        which == 0,
        jnp.concatenate([own, other], axis=axis),
        jnp.concatenate([other, own], axis=axis),
    )


def add(a, b):
    return (a.astype(F32) + b.astype(F32)).astype(BF16)


def on_device(
    tokens, lengths, ln1_gain, ln1_bias, qkv_weight, q_gain, k_gain, out_weight,
    ln2_gain, ln2_bias, up_weight, down_weight, cotangent,
):
    micro, rows, local, width = tokens.shape
    n = lax.axis_size("seq")
    length = local * n
    every = micro * rows
    team = n // every
    heads = H // team
    hd = width // H
    half = width // 2
    idx = lax.axis_index("seq")
    core = lax.axis_index("fsdp")
    row, member = idx // team, idx % team
    direct = every == 2 and team == 4
    lengths = lengths.reshape(every, lengths.shape[-1])
    mine = tokens.reshape(every, local, width)

    def swap(value):
        return flip(value, "fsdp", 1)

    vec = jnp.concatenate([ln1_gain, ln1_bias, ln2_gain, ln2_bias, q_gain, k_gain])[None]
    vec_p = swap(vec)
    ordered = jnp.where(core == 0, jnp.concatenate([vec, vec_p]), jnp.concatenate([vec_p, vec])).astype(F32)
    g1, b1, g2, b2 = (ordered[:, k * half : (k + 1) * half].reshape(1, width) for k in range(4))
    gq = ordered[:, 4 * half : 4 * half + hd // 2].reshape(hd, 1)
    gk = ordered[:, 4 * half + hd // 2 :].reshape(hd, 1)

    w_own = lax.dynamic_slice_in_dim(
        qkv_weight.reshape(half, 3, width), member * heads * hd, heads * hd, 2
    ).reshape(half, 3 * heads * hd)
    w_t = jnp.transpose(join(w_own, swap(w_own), core))

    if direct:
        near = lax.dynamic_index_in_dim(mine, row, 0, keepdims=False)
        away = lax.dynamic_index_in_dim(mine, 1 - row, 0, keepdims=False)
        far = flip(away, "seq", 4)
        cut = local // 2

        def spread(own):
            one, two = flip(own, "seq", 1), flip(own, "seq", 2)
            three = jnp.concatenate([flip(two[:cut], "seq", 1), flip(one[cut:], "seq", 2)], axis=0)
            return [own, one, two, three]

        slots = spread(near) + spread(far)
        spot = idx
    else:
        same_member = [[q * team + p for q in range(every)] for p in range(team)]
        same_row = [[q * team + p for p in range(team)] for q in range(every)]
        got = lax.all_to_all(mine, "seq", 0, 0, axis_index_groups=same_member, tiled=True)
        got = lax.all_gather(got, "seq", axis_index_groups=same_row)
        whole = jnp.swapaxes(got, 0, 1).reshape(length, width)
        slots = [whole[s * (length // 8) : (s + 1) * (length // 8)] for s in range(8)]
        spot = jnp.int32(0)
    meta = jnp.stack([spot, row, core, bit("rep", 1), bit("seq", 1), bit("seq", 2)]).astype(jnp.int32)

    out_p, up_p, down_p = swap(out_weight), swap(up_weight), swap(down_weight)

    with jax.named_scope("forward_attention"):
        qt, ka, kt, v, vt, x_row = make_qkv(meta, lengths, slots, w_t, g1, b1, gq, gk, heads, hd)
        attn, attn_f, logsum = attend(meta, lengths, qt, ka, vt, heads, hd)

    def exchange(value):
        return lax.all_to_all(value, "seq", 0, 0, tiled=True)

    packs = every * local // BLK
    if direct:
        attn_t = exchange(attn).reshape(packs, width, BLK)
    else:
        cut = jnp.moveaxis(attn.reshape(BLK * 0 + 8, heads * hd, BLK // local, local), 2, 1)
        got = exchange(cut.reshape(n, heads * hd, local))
        got = got.reshape(packs, every // packs, width, local)
        attn_t = jnp.swapaxes(got, 1, 2).reshape(packs, width, BLK)

    total = jnp.sum(lengths[:, :-1], axis=-1)
    places = idx * local + jnp.arange(local, dtype=jnp.int32)
    valid = (places[None] < total[:, None]).astype(F32).reshape(packs, 1, BLK)
    x_home = tokens.reshape(every * local, width)
    dy = cotangent.reshape(every * local, width)

    with jax.named_scope("feed_forward"):
        output, grad_mid, grad_branch, h2, act, dup, grad_attn, vec2 = ffn(
            meta, attn_t, x_home, dy, valid, g2, b2, out_weight, out_p, up_weight, up_p, down_weight, down_p
        )
    if direct:
        grad_o = exchange(grad_attn.reshape(n, heads * hd, BLK))
    else:
        cut = jnp.swapaxes(grad_attn.reshape(packs, width, every // packs, local), 1, 2)
        got = exchange(cut.reshape(n, heads * hd, local))
        got = got.reshape(8, BLK // local, heads * hd, local)
        grad_o = jnp.swapaxes(got, 1, 2).reshape(8, heads * hd, BLK)

    masks = [1 << k for k in range(n.bit_length() - 1)]
    x, y, z = ("rep", 1), ("seq", 1), ("seq", 2)

    def next_half(keep, got, way, axis):
        return halves(add(keep, got), bit(*way), axis)

    tie = lambda *values: lax.optimization_barrier(values)
    with jax.named_scope("weight_gradients"):
        far_u = swap(up_out_grads(meta, attn_t, grad_branch, h2, dup))
        far_d = swap(down_grads(meta, act, dy))
        up_k, up_s, out_k, out_s = up_out_grads(meta, attn_t, grad_branch, h2, dup, far_u)
        down_k, down_s = down_grads(meta, act, dy, far_d)
        got = flip(down_s, *x), flip(up_s, *y), flip(out_s, *z)
    grad_o = tie(grad_o, up_k, up_s, out_k, out_s, down_k, down_s)[0]
    head = lambda h, go: attend_back(meta, lengths, qt, ka, kt, v, attn_f, logsum, go, h, 1, hd)
    parts = [None] * heads
    parts[0] = head(0, grad_o)
    grad_o, parts[0], *got = tie(grad_o, parts[0], *got)
    with jax.named_scope("weight_gradients"):
        down_k, down_s = next_half(down_k, got[0], y, 0)
        up_k, up_s = next_half(up_k, got[1], z, 1)
        out_k, out_s = next_half(out_k, got[2], x, 0)
        got = flip(down_s, *y), flip(up_s, *z), flip(out_s, *x)
    for h in range(1, heads - 1):
        parts[h] = head(h, grad_o)
    grad_o, parts[1:-1], *got = tie(grad_o, parts[1:-1], *got)
    with jax.named_scope("weight_gradients"):
        down_k, down_s = next_half(down_k, got[0], z, 1)
        up_k, up_s = next_half(up_k, got[1], x, 1)
        out_k, out_s = next_half(out_k, got[2], y, 1)
        got = flip(down_s, *z), flip(up_s, *x), flip(out_s, *y)
    parts[-1] = head(heads - 1, grad_o)
    parts[-1], *got = tie(parts[-1], *got)
    with jax.named_scope("weight_gradients"):
        down, up, out = add(down_k, got[0]), add(up_k, got[1]), add(out_k, got[2])
        sizes = [down.shape[0], up.shape[0]]
        pieces = jnp.concatenate([down, up, out])
        for mask in masks[2:]:
            pieces = add(pieces, flip(pieces, "seq", mask))
        down, up, out = jnp.split(pieces, [sizes[0], sizes[0] + sizes[1]])

    with jax.named_scope("backward_attention"):
        dq, dk, dv = zip(*parts)
        back_a, back_b, dw_t = qkv_back(meta, x_row, dq, dk, dv, w_t, g1, b1, gq, gk, vec2, heads, hd)
    back_a, back_b, dw_t, down, up, out = tie(back_a, back_b, dw_t, down, up, out)

    with jax.named_scope("first_round"):
        keep, send = halves(dw_t, core, 1)
        q_keep, q_send = next_half(keep, swap(send), x, 0)
        got = [flip(down, *z), flip(up, *x), flip(out, *y), flip(q_send, *x)]
        if direct:
            a = back_a.reshape(2, 2, 2, local, half)
            b = back_b.reshape(2, 2, 2, local, half)
            got += [flip(a[:, :, 1], *y), flip(b[:, 1], *z)]
        got = tie(*got)
        down = jnp.concatenate([down, got[0]], axis=1)
        up = jnp.concatenate([up, got[1]], axis=1)
        out = jnp.concatenate([out, got[2]], axis=1)
        piece = add(q_keep, got[3])
        if direct:
            a, b = add(a[:, :, 0], got[4]), add(b[:, 0], got[5])
    with jax.named_scope("second_round"):
        rows_at = [mask for mask in masks if mask >= team]
        got = [flip(down, *y), flip(down, *x), flip(up, *z), flip(out, *x)]
        got += [flip(piece, "seq", mask) for mask in rows_at[:1]]
        if direct:
            got += [flip(a[:, 1], *z), flip(b[:, 1], *y)]
        got = tie(*got)
        downs = [down, got[0], got[1]]
        up = jnp.concatenate([up, got[2]], axis=1)
        out = jnp.concatenate([out, got[3]], axis=0)
        if rows_at:
            piece = add(piece, got[4])
        for mask in rows_at[1:]:
            piece = add(piece, flip(piece, "seq", mask))
        if direct:
            a, b = add(a[:, 0], got[-2]), add(b[:, 0], got[-1])
    with jax.named_scope("third_round"):
        piece_y, up = tie(flip(piece, *y), up)
        piece = jnp.stack([piece, piece_y])
        if direct:
            mixed = jnp.concatenate([a, b], axis=-1)
            near, far = mixed[0], flip(mixed[1], "seq", 4)
            back = jnp.where(row == 0, jnp.stack([near, far]), jnp.stack([far, near])).reshape(every * local, width)
        else:
            whole = jnp.concatenate([back_a, back_b], axis=-1).reshape(every, team, local, width)
            whole = lax.psum_scatter(whole, "seq", scatter_dimension=1, axis_index_groups=same_row, tiled=True)
            back = lax.all_to_all(
                whole[:, 0], "seq", 0, 0, axis_index_groups=same_member, tiled=True
            ).reshape(every * local, width)
        downs.append(flip(downs[1], *x))
        piece_z = flip(piece, *z)
        pieces = [piece, piece_z, flip(piece, *x), flip(piece_z, *x)]
        ups, outs = (up, flip(up, *y)), (out, flip(out, *z))
    grad_tokens = finish(x_home, grad_mid, back, g1)
    grad_qkv, small = assemble_qkv(meta, pieces, heads, hd)
    grad_down, grad_up, grad_out = assemble(meta, downs, ups, outs)
    cuts = [small[0], small[1], small[2], small[3], small[4, : hd // 2], small[4, hd // 2 : hd]]
    shape = tokens.shape
    return (
        output.reshape(shape), grad_tokens.reshape(shape), cuts[0], cuts[1], grad_qkv, cuts[4], cuts[5],
        grad_out, cuts[2], cuts[3], grad_up, grad_down,
    )


def solution(mesh):
    tok = P(None, ("rep", "fsdp"), "seq", None)
    one, two = P("fsdp"), P("fsdp", None)
    in_specs = (tok, P(None, ("rep", "fsdp"), None), one, one, two, one, one, two, one, one, two, two, tok)
    out_specs = (tok, tok, one, one, two, one, one, two, one, one, two, two)
    return jax.shard_map(on_device, mesh=mesh, in_specs=in_specs, out_specs=out_specs, check_vma=False)
```

```python
import functools

import jax
import jax.numpy as jnp
from jax import lax
from jax.experimental import pallas as pl
from jax.experimental.pallas import tpu as pltpu
from jax.sharding import PartitionSpec as P

H = 12
EPS = 1e-06
LOG2E = 1.4426950408889634
SHIFT = 512.0
BLK = 256
EXTRA = 32
NN = (((1,), (0,)), ((), ()))
NT = (((1,), (1,)), ((), ()))
TN = (((0,), (0,)), ((), ()))
F32 = jnp.float32
BF16 = jnp.bfloat16


def mm(a, b, dims=NN):
    return lax.dot_general(a, b, dims, preferred_element_type=F32)


def params(**kw):
    return pltpu.CompilerParams(vmem_limit_bytes=60 * 1024 * 1024, **kw)


def cost(us):
    return pl.CostEstimate(flops=int(us * 0.35e9), bytes_accessed=1024, transcendentals=0)


def norm_rows(v):
    center = jnp.mean(v, axis=-1, keepdims=True)
    centred = v - center
    inv = lax.rsqrt(jnp.mean(centred * centred, axis=-1, keepdims=True) + EPS)
    return centred * inv, inv


def norm_cols(v):
    center = jnp.mean(v, axis=0, keepdims=True)
    centred = v - center
    inv = lax.rsqrt(jnp.mean(centred * centred, axis=0, keepdims=True) + EPS)
    return centred * inv, inv


def bounds_of(len_ref, row):
    out = []
    total = jnp.int32(0)
    for j in range(len_ref.shape[1] - 1):
        total = total + len_ref[row, j]
        out.append(total)
    return out


def qkv_body(heads, hd, meta, len_ref, *refs):
    xs = refs[:8]
    w_ref, g_ref, b_ref, gq_ref, gk_ref = refs[8:13]
    qt_ref, ka_ref, kt_ref, v_ref, vt_ref, x_ref = refs[13:]
    wid = heads * hd
    spot, row = meta[0], meta[1]
    bounds = bounds_of(len_ref, row)
    for s in range(8):
        c = jnp.bitwise_xor(spot, s)
        cols = pl.ds(pl.multiple_of(c * BLK, BLK), BLK)
        x = xs[s][...]
        x_ref[cols, :] = x
        hat, _ = norm_rows(x.astype(F32))
        first = (hat * g_ref[...] + b_ref[...]).astype(BF16)
        qkv = mm(w_ref[...], first, NT)
        place = c * BLK + lax.broadcasted_iota(jnp.int32, (8, BLK), 1)
        ident = jnp.zeros((8, BLK), jnp.int32)
        place_k = c * BLK + lax.broadcasted_iota(jnp.int32, (BLK, 128), 0)
        ident_k = jnp.zeros((BLK, 128), jnp.int32)
        for bound in bounds:
            ident = ident + (place >= bound).astype(jnp.int32)
            ident_k = ident_k + (place_k >= bound).astype(jnp.int32)
        which = lax.broadcasted_iota(jnp.int32, (8, BLK), 0)
        hot = jnp.where((ident == which) & (which < len(bounds)), 16.0, 0.0)
        hot = jnp.concatenate([hot, jnp.zeros((hd - 8, BLK), F32)], axis=0)
        lane = lax.broadcasted_iota(jnp.int32, (BLK, 128), 1) - hd
        hot_k = jnp.where((ident_k == lane) & (lane < len(bounds)), SHIFT / 16.0, 0.0)
        for h in range(heads):
            q, _ = norm_cols(qkv[h * hd : (h + 1) * hd])
            k, _ = norm_cols(qkv[wid + h * hd : wid + (h + 1) * hd])
            q = (q * gq_ref[...]).astype(BF16).astype(F32) * (hd**-0.5)
            k = k * gk_ref[...]
            v = qkv[2 * wid + h * hd : 2 * wid + (h + 1) * hd]
            qt_ref[h, :, cols] = jnp.concatenate([q, hot], axis=0).astype(BF16)
            kt_ref[h, :, cols] = k.astype(BF16)
            vt_ref[h, :, cols] = v.astype(BF16)
            both = jnp.transpose(jnp.concatenate([k, v], axis=0))
            ka_ref[h, cols, :] = jnp.where(lane < 0, both, hot_k).astype(BF16)
            v_ref[h, cols, :] = both[:, hd:].astype(BF16)


def make_qkv(meta, lengths, slots, w_t, gain, bias, gq, gk, heads, hd):
    length = 8 * slots[0].shape[0]
    width = slots[0].shape[1]
    smem = pl.BlockSpec(memory_space=pltpu.SMEM)
    vmem = pl.BlockSpec(memory_space=pltpu.VMEM)
    return pl.pallas_call(
        functools.partial(qkv_body, heads, hd),
        out_shape=(
            jax.ShapeDtypeStruct((heads, 2 * hd, length), BF16),
            jax.ShapeDtypeStruct((heads, length, 2 * hd), BF16),
            jax.ShapeDtypeStruct((heads, hd, length), BF16),
            jax.ShapeDtypeStruct((heads, length, hd), BF16),
            jax.ShapeDtypeStruct((heads, hd, length), BF16),
            jax.ShapeDtypeStruct((length, width), BF16),
        ),
        in_specs=[smem, smem] + [vmem] * 13,
        out_specs=(vmem,) * 6,
        compiler_params=params(),
        cost_estimate=cost(12),
        name="qkv_forward",
    )(meta, lengths, *slots, w_t, gain, bias, gq, gk)


def block_range(bounds, i):
    first = i * BLK
    last = first + BLK - 1
    lo = jnp.int32(0)
    hi = bounds[-1]
    for bound in bounds:
        lo = jnp.where(first >= bound, bound, lo)
    for bound in bounds[::-1]:
        hi = jnp.where(last < bound, bound, hi)
    lo_b = lo // BLK
    hi_b = (hi + BLK - 1) // BLK
    return lo_b, jnp.where(first >= bounds[-1], lo_b, hi_b)


def in_pairs(lo, hi, step, carry):
    pairs = (hi - lo) // 2
    carry = lax.fori_loop(0, pairs, lambda k, c: step([lo + 2 * k, lo + 2 * k + 1], c), carry)
    return lax.fori_loop(lo + 2 * pairs, hi, lambda b, c: step([b], c), carry)


def attend_body(heads, hd, meta, len_ref, qt_ref, ka_ref, vt_ref, o_ref, of_ref, ls_ref):
    i = pl.program_id(0)
    bounds = bounds_of(len_ref, meta[1])
    lo, hi = block_range(bounds, i)

    def step(blocks, carry):
        rows = [pl.ds(pl.multiple_of(b * BLK, BLK), BLK) for b in blocks]
        items = [(h, r) for r in rows for h in range(heads)]
        scores = [mm(ka_ref[h, r, :], qt_ref[h]) for h, r in items]
        expos = [jnp.exp2(one * LOG2E - SHIFT * LOG2E) for one in scores]
        out = list(carry)
        for expo, (h, r) in zip(expos, items):
            acc, total = out[h]
            total = total + jnp.sum(expo.reshape(BLK // 8, 8, BLK), axis=0)
            out[h] = (acc + mm(vt_ref[h, :, r], expo.astype(BF16)), total)
        return tuple(out)

    init = tuple((jnp.zeros((hd, BLK), F32), jnp.zeros((8, BLK), F32)) for _ in range(heads))
    done = in_pairs(lo, hi, step, init)
    for h in range(heads):
        acc, total = done[h]
        total = jnp.sum(total, axis=0, keepdims=True)
        live = total > 0.0
        safe = jnp.where(live, total, 1.0)
        out = jnp.where(live, acc * (1.0 / safe), 0.0)
        o_ref[0, h * hd : (h + 1) * hd, :] = out.astype(BF16)
        of_ref[h] = out
        ls_ref[h] = jnp.log2(safe) + SHIFT * LOG2E


def attend(meta, lengths, qt, ka, vt, heads, hd):
    length = qt.shape[2]
    blocks = length // BLK
    smem = pl.BlockSpec(memory_space=pltpu.SMEM)
    return pl.pallas_call(
        functools.partial(attend_body, heads, hd),
        grid=(blocks,),
        out_shape=(
            jax.ShapeDtypeStruct((blocks, heads * hd, BLK), BF16),
            jax.ShapeDtypeStruct((heads, hd, length), F32),
            jax.ShapeDtypeStruct((heads, 1, length), F32),
        ),
        in_specs=[
            smem,
            smem,
            pl.BlockSpec((heads, 2 * hd, BLK), lambda i: (0, 0, i)),
            pl.BlockSpec((heads, length, 2 * hd), lambda i: (0, 0, 0)),
            pl.BlockSpec((heads, hd, length), lambda i: (0, 0, 0)),
        ],
        out_specs=(
            pl.BlockSpec((1, heads * hd, BLK), lambda i: (i, 0, 0)),
            pl.BlockSpec((heads, hd, BLK), lambda i: (0, 0, i)),
            pl.BlockSpec((heads, 1, BLK), lambda i: (0, 0, i)),
        ),
        compiler_params=params(),
        cost_estimate=cost(25),
        name="attention_forward",
    )(meta, lengths, qt, ka, vt)


def attend_back_body(first, heads, hd, meta, len_ref, *refs):
    qt_ref, ka_ref, kt_ref, v_ref, of_ref, ls_ref, go_ref = refs[:7]
    dq_ref, dk_ref, dv_ref = refs[-3:]
    i = pl.program_id(0)
    bounds = bounds_of(len_ref, meta[1])
    lo, hi = block_range(bounds, i + first)

    @pl.when(i == 0)
    def _():
        if first:
            dk_ref[...] = refs[8][...]
            dv_ref[...] = refs[9][...]
        else:
            dk_ref[...] = jnp.zeros_like(dk_ref)
            dv_ref[...] = jnp.zeros_like(dv_ref)

    inner = []
    for h in range(heads):
        go = go_ref[0, h * hd : (h + 1) * hd, :].astype(F32)
        inner.append(jnp.sum(go * of_ref[h], axis=0, keepdims=True))

    def step(blocks, carry):
        rows = [pl.ds(pl.multiple_of(b * BLK, BLK), BLK) for b in blocks]
        items = [(h, r) for r in rows for h in range(heads)]
        gos = [go_ref[0, h * hd : (h + 1) * hd, :] for h in range(heads)]
        scores = [mm(ka_ref[h, r, :], qt_ref[h]) for h, r in items]
        grad_probs = [mm(v_ref[h, r, :], gos[h]) for h, r in items]
        probs = [jnp.exp2(one * LOG2E - ls_ref[h]) for one, (h, _) in zip(scores, items)]
        grads = [(p * (g - inner[h])).astype(BF16) for p, g, (h, _) in zip(probs, grad_probs, items)]
        out = list(carry)
        for p, g, (h, r) in zip(probs, grads, items):
            dv_ref[h, :, r] += mm(gos[h], p.astype(BF16), NT)
            dk_ref[h, :, r] += mm(qt_ref[h][:hd], g, NT)
            out[h] = out[h] + mm(kt_ref[h, :, r], g)
        return tuple(out)

    done = in_pairs(lo, hi, step, tuple(jnp.zeros((hd, BLK), F32) for _ in range(heads)))
    for h in range(heads):
        dq_ref[h] = done[h] * (hd**-0.5)


def attend_back(meta, lengths, qt, ka, kt, v, of, ls, go, heads, hd, before=None):
    length = qt.shape[2]
    count = length // BLK // 2
    first = count if before else 0
    smem = pl.BlockSpec(memory_space=pltpu.SMEM)
    whole = lambda *shape: pl.BlockSpec(shape, lambda i: (0, 0, 0))
    part = lambda *shape: pl.BlockSpec(shape, lambda i: (0, 0, first + i))
    more = [pl.BlockSpec(memory_space=pl.ANY), whole(heads, hd, length), whole(heads, hd, length)]
    return pl.pallas_call(
        functools.partial(attend_back_body, first, heads, hd),
        grid=(count,),
        out_shape=tuple(jax.ShapeDtypeStruct((heads, hd, length), F32) for _ in range(3)),
        in_specs=[
            smem,
            smem,
            part(heads, 2 * hd, BLK),
            whole(heads, length, 2 * hd),
            whole(heads, hd, length),
            whole(heads, length, hd),
            part(heads, hd, BLK),
            part(heads, 1, BLK),
            pl.BlockSpec((1, heads * hd, BLK), lambda i: (first + i, 0, 0)),
            *(more if before else []),
        ],
        out_specs=(part(heads, hd, BLK), whole(heads, hd, length), whole(heads, hd, length)),
        input_output_aliases={9: 0} if before else {},
        compiler_params=params(),
        cost_estimate=cost(15),
        name="attention_backward",
    )(meta, lengths, qt, ka, kt, v, of, ls, go, *(before or ()))


def qkv_back_body(
    heads, hd, meta, x_ref, *refs
):
    dq_ref, dk_ref, dv_ref, w_ref, g_ref, b_ref, gq_ref, gk_ref, vec2_ref = refs[:9]
    da_ref, db_ref, dw_ref, acc_ref, vec_ref, gain_ref = refs[9:]
    i = pl.program_id(0)
    wid = heads * hd

    @pl.when(i == 0)
    def _():
        acc_ref[...] = jnp.zeros_like(acc_ref)
        vec_ref[...] = jnp.zeros_like(vec_ref)
        gain_ref[...] = jnp.zeros_like(gain_ref)

    hat, _ = norm_rows(x_ref[...].astype(F32))
    first = (hat * g_ref[...] + b_ref[...]).astype(BF16)
    qk = mm(w_ref[: 2 * wid, :], first, NT)
    pieces = []
    for at, gain, grad in ((0, gq_ref, dq_ref), (1, gk_ref, dk_ref)):
        for h in range(heads):
            unit, inv = norm_cols(qk[at * wid + h * hd : at * wid + (h + 1) * hd])
            gy = grad[h]
            gain_ref[at] += gy * unit
            e = gy * gain[...]
            pieces.append(
                inv
                * (
                    e
                    - jnp.mean(e, axis=0, keepdims=True)
                    - unit * jnp.mean(e * unit, axis=0, keepdims=True)
                )
            )
    for h in range(heads):
        pieces.append(dv_ref[h])
    grad = jnp.concatenate(pieces, axis=0).astype(BF16)
    acc_ref[...] += mm(grad, first)
    back = mm(grad, w_ref[...], TN)
    vec_ref[0] += jnp.sum((back * hat).reshape(BLK // 8, 8, -1), axis=0)
    vec_ref[1] += jnp.sum(back.reshape(BLK // 8, 8, -1), axis=0)
    half = back.shape[1] // 2
    da_ref[0] = back[:, :half].astype(BF16)
    db_ref[0] = back[:, half:].astype(BF16)

    @pl.when(i == pl.num_programs(0) - 1)
    def _():
        dw_ref[: 3 * wid, :] = acc_ref[...].astype(BF16)
        lines = [jnp.sum(ref[k], axis=0, keepdims=True) for ref in (vec_ref, vec2_ref) for k in range(2)]
        width = dw_ref.shape[1]
        lane = lax.broadcasted_iota(jnp.int32, (hd, width), 1)
        item = lax.broadcasted_iota(jnp.int32, (hd, width), 0)
        spread = jnp.where(item < hd // 2, item, item - hd // 2 + width // 2)
        line = jnp.zeros((8, width), F32)
        for k in range(2):
            total = lax.dot_general(
                jnp.ones((8, BLK), F32), gain_ref[k], NT, precision=lax.Precision.HIGHEST, preferred_element_type=F32
            )
            pick = (lane == spread + k * (hd // 2)).astype(F32)
            line = line + lax.dot_general(
                total, pick, NN, precision=lax.Precision.HIGHEST, preferred_element_type=F32
            )
        lines.append(line[:1])
        place = lax.broadcasted_iota(jnp.int32, (EXTRA, width), 0)
        below = jnp.zeros((EXTRA, width), F32)
        for k, one in enumerate(lines):
            below = jnp.where(place == k, one, below)
        dw_ref[3 * wid :, :] = below.astype(BF16)


def qkv_back(meta, x, dq, dk, dv, w_t, gain, bias, gq, gk, vec2, heads, hd):
    length, width = x.shape
    blocks = length // BLK
    whole = lambda *shape: pl.BlockSpec(shape, lambda i, m: (0,) * len(shape))
    part = pl.BlockSpec((heads, hd, BLK), lambda i, m: (0, 0, i))
    grads = pl.BlockSpec((1, BLK, width // 2), lambda i, m: (jnp.bitwise_xor(i, m[0]), 0, 0))
    return pl.pallas_call(
        functools.partial(qkv_back_body, heads, hd),
        grid_spec=pltpu.PrefetchScalarGridSpec(
            num_scalar_prefetch=1,
            grid=(blocks,),
            in_specs=[
                pl.BlockSpec((BLK, width), lambda i, m: (i, 0)),
                part,
                part,
                part,
                whole(*w_t.shape),
                whole(1, width),
                whole(1, width),
                whole(hd, 1),
                whole(hd, 1),
                whole(2, 8, width),
            ],
            out_specs=(
                grads,
                grads,
                whole(w_t.shape[0] + EXTRA, width),
            ),
            scratch_shapes=[
                pltpu.VMEM(w_t.shape, F32),
                pltpu.VMEM((2, 8, width), F32),
                pltpu.VMEM((2, hd, BLK), F32),
            ],
        ),
        out_shape=(
            jax.ShapeDtypeStruct((blocks, BLK, width // 2), BF16),
            jax.ShapeDtypeStruct((blocks, BLK, width // 2), BF16),
            jax.ShapeDtypeStruct((w_t.shape[0] + EXTRA, width), BF16),
        ),
        compiler_params=params(),
        cost_estimate=cost(17),
        name="qkv_backward",
    )(meta, x, dq, dk, dv, w_t, gain, bias, gq, gk, vec2)


def assemble_qkv(meta, pieces, heads, hd):
    _, part, half = pieces[0].shape
    team = 4
    wid = heads * hd
    turned = team * wid

    def body(meta, p00, p01, p10, p11, out_ref, vec_ref, all_s):
        t = pl.program_id(0)

        @pl.when(t == 0)
        def _():
            for y in range(2):
                at = jnp.bitwise_xor(meta[4], y)
                for z in range(2):
                    own_z = meta[5] == z
                    near, away = jnp.where(own_z, p00[at], p01[at]), jnp.where(own_z, p10[at], p11[at])
                    for x in range(2):
                        all_s[2 * z + y, x * part : (x + 1) * part, :] = jnp.where(meta[3] == x, near, away)
            total = jnp.zeros((EXTRA, half), F32)
            for p in range(team):
                total = total + all_s[p, 3 * wid :, :].astype(F32)
            vec_ref[...] = total

        rows = pl.ds(pl.multiple_of(t * wid, wid), wid)
        piece = jnp.concatenate([all_s[p, rows, :] for p in range(team)], axis=0)
        out_ref[...] = jnp.transpose(piece.astype(F32))

    whole = lambda *shape: pl.BlockSpec(shape, lambda i, m: (0,) * len(shape))
    return pl.pallas_call(
        body,
        grid_spec=pltpu.PrefetchScalarGridSpec(
            num_scalar_prefetch=1,
            grid=(3,),
            in_specs=[whole(2, part, half)] * 4,
            out_specs=(pl.BlockSpec((half, turned), lambda i, m: (0, i)), whole(EXTRA, half)),
            scratch_shapes=[pltpu.VMEM((team, 2 * part, half), BF16)],
        ),
        out_shape=(jax.ShapeDtypeStruct((half, 3 * turned), F32), jax.ShapeDtypeStruct((EXTRA, half), F32)),
        compiler_params=params(),
        cost_estimate=cost(5),
        name="first_projection_gradient",
    )(meta, *pieces)


def gelu_pair(u):
    a = jnp.abs(u)
    t = 1.0 / (1.0 + (0.3275911 * 0.7071067811865476) * a)
    poly = 1.061405429 * t - 1.453152027
    poly = poly * t + 1.421413741
    poly = poly * t - 0.284496736
    poly = poly * t + 0.254829592
    bell = jnp.exp(-0.5 * (u * u))
    tail = (0.5 * poly) * t * bell
    cdf = jnp.where(u >= 0.0, 1.0 - tail, tail)
    return u * cdf, cdf + u * (bell * 0.3989422804014327)


def ffn(meta, attn_t, x, dy, valid, gain, bias, wo, wo_p, up, up_p, dn, dn_p):
    tokens, width = x.shape
    hidden = up.shape[1]
    fc = 512
    steps = hidden // fc
    near = steps // 2
    packs, _, lanes = attn_t.shape
    whole = lambda *shape: pl.BlockSpec(shape, lambda i, m: (0,) * len(shape))
    ups = pl.BlockSpec((width // 2, fc), lambda i, m: (0, lax.rem(m[2] * near + i, steps)))
    acts = pl.BlockSpec((tokens, fc), lambda i, m: (0, lax.rem(m[2] * near + i, steps)))
    half = width // 2

    def body(meta, *refs):
        (at_ref, x_ref, dy_ref, valid_ref, g_ref, b_ref, wo_own, wo_peer, up_own, up_peer, dn_own, dn_peer) = refs[:12]
        (out_ref, gm_ref, gb_ref, h2_ref, act_ref, dup_ref, da_ref, vec_ref) = refs[12:20]
        (mid_s, acc_s, own_s, peer_s, gown_s, gpeer_s) = refs[20:]
        i = pl.program_id(0)
        core = meta[2]
        zero = core == 0

        @pl.when(i == 0)
        def _():
            for p in range(packs):
                rows = pl.ds(p * lanes, lanes)
                own = at_ref[p, pl.ds(pl.multiple_of(core * half, half), half), :]
                peer = at_ref[p, pl.ds(pl.multiple_of((1 - core) * half, half), half), :]
                mid = x_ref[rows, :].astype(F32) + mm(own, wo_own[...], TN) + mm(peer, wo_peer[...], TN)
                mid_s[rows, :] = mid
                acc_s[rows, :] = mid
                hat, _ = norm_rows(mid)
                second = (hat * g_ref[...] + b_ref[...]).astype(BF16)
                h2_ref[rows, :] = second
                lo, hi = second[:, :half], second[:, half:]
                own_s[rows, :] = jnp.where(zero, lo, hi)
                peer_s[rows, :] = jnp.where(zero, hi, lo)
            gown_s[...] = jnp.zeros_like(gown_s)
            gpeer_s[...] = jnp.zeros_like(gpeer_s)

        down = jnp.where(i < near, dn_own[...], dn_peer[...])
        upper = mm(own_s[...], up_own[...]) + mm(peer_s[...], up_peer[...])
        act, slope = gelu_pair(upper)
        act = act.astype(BF16)
        grad = (mm(dy_ref[...], down, NT) * slope).astype(BF16)
        act_ref[...] = act
        dup_ref[...] = grad
        acc_s[...] += mm(act, down)
        gown_s[...] += mm(grad, up_own[...], NT)
        gpeer_s[...] += mm(grad, up_peer[...], NT)

        @pl.when(i == steps - 1)
        def _():
            out_ref[...] = acc_s[...].astype(BF16)
            vec = [jnp.zeros((8, width), F32), jnp.zeros((8, width), F32)]
            for p in range(packs):
                rows = pl.ds(p * lanes, lanes)
                hat, inv = norm_rows(mid_s[rows, :])
                a, b = gown_s[rows, :], gpeer_s[rows, :]
                gy = jnp.concatenate([jnp.where(zero, a, b), jnp.where(zero, b, a)], axis=1)
                vec[0] = vec[0] + jnp.sum((gy * hat).reshape(lanes // 8, 8, width), axis=0)
                vec[1] = vec[1] + jnp.sum(gy.reshape(lanes // 8, 8, width), axis=0)
                e = gy * g_ref[...]
                gm = dy_ref[rows, :].astype(F32) + inv * (
                    e
                    - jnp.mean(e, axis=-1, keepdims=True)
                    - hat * jnp.mean(e * hat, axis=-1, keepdims=True)
                )
                gm_ref[rows, :] = gm
                gb = gm.astype(BF16)
                gb_ref[rows, :] = gb
                ok = valid_ref[p]
                da_ref[p, pl.ds(pl.multiple_of(core * half, half), half), :] = (
                    mm(wo_own[...], gb, NT) * ok
                ).astype(BF16)
                da_ref[p, pl.ds(pl.multiple_of((1 - core) * half, half), half), :] = (
                    mm(wo_peer[...], gb, NT) * ok
                ).astype(BF16)
            vec_ref[0] = vec[0]
            vec_ref[1] = vec[1]

    return pl.pallas_call(
        body,
        grid_spec=pltpu.PrefetchScalarGridSpec(
            num_scalar_prefetch=1,
            grid=(steps,),
            in_specs=[
                whole(*attn_t.shape),
                whole(tokens, width),
                whole(tokens, width),
                whole(*valid.shape),
                whole(1, width),
                whole(1, width),
                whole(half, width),
                whole(half, width),
                ups,
                ups,
                pl.BlockSpec((fc, width), lambda i, m: (jnp.minimum(i, near - 1), 0)),
                pl.BlockSpec((fc, width), lambda i, m: (jnp.maximum(i - near, 0), 0)),
            ],
            out_specs=(
                whole(tokens, width),
                whole(tokens, width),
                whole(tokens, width),
                whole(tokens, width),
                acts,
                acts,
                whole(*attn_t.shape),
                whole(2, 8, width),
            ),
            scratch_shapes=[
                pltpu.VMEM((tokens, width), F32),
                pltpu.VMEM((tokens, width), F32),
                pltpu.VMEM((tokens, half), BF16),
                pltpu.VMEM((tokens, half), BF16),
                pltpu.VMEM((tokens, half), F32),
                pltpu.VMEM((tokens, half), F32),
            ],
        ),
        out_shape=(
            jax.ShapeDtypeStruct((tokens, width), BF16),
            jax.ShapeDtypeStruct((tokens, width), F32),
            jax.ShapeDtypeStruct((tokens, width), BF16),
            jax.ShapeDtypeStruct((tokens, width), BF16),
            jax.ShapeDtypeStruct((tokens, hidden), BF16),
            jax.ShapeDtypeStruct((tokens, hidden), BF16),
            jax.ShapeDtypeStruct(attn_t.shape, BF16),
            jax.ShapeDtypeStruct((2, 8, width), F32),
        ),
        compiler_params=params(),
        cost_estimate=cost(25),
        name="ffn_both_ways",
    )(meta, attn_t, x, dy, valid, gain, bias, wo, wo_p, up, up_p, dn, dn_p)


def up_out_grads(meta, attn_t, gb, h2, dup, far=None):
    tokens, width = gb.shape
    hidden = dup.shape[1]
    half = width // 2
    packs, _, lanes = attn_t.shape
    n = hidden // width
    own = far is not None

    def column(j, m):
        bit = jnp.where(j < n // 2, m[4], 1 - m[4])
        return bit * (n // 2) + lax.rem(jnp.minimum(j, n - 1), n // 2)

    def body(meta, at_ref, gb_ref, h2_ref, dup_ref, *rest):
        j = pl.program_id(0)
        side = meta[2] if own else 1 - meta[2]

        def up():
            part = jnp.where(side == 0, h2_ref[:, :half], h2_ref[:, half:])
            return mm(part, dup_ref[...], TN)

        def out():
            rows = pl.ds(pl.multiple_of(side * half, half), half)
            total = jnp.zeros((half, width), F32)
            for p in range(packs):
                total = total + mm(at_ref[p, rows, :], gb_ref[p * lanes : (p + 1) * lanes, :])
            lo, hi = total[: half // 2], total[half // 2 :]
            return jnp.where(meta[5] == 0, lo, hi), jnp.where(meta[5] == 0, hi, lo)

        if own:
            far_ref, uk_ref, us_ref, ok_ref, os_ref = rest

            @pl.when(j < n // 2)
            def _():
                uk_ref[...] = (up() + far_ref[...].astype(F32)).astype(BF16)

            @pl.when((j >= n // 2) & (j < n))
            def _():
                us_ref[...] = (up() + far_ref[...].astype(F32)).astype(BF16)

            @pl.when(j == n)
            def _():
                keep, send = out()
                ok_ref[...] = (keep + far_ref[: half // 2].astype(F32)).astype(BF16)
                os_ref[...] = (send + far_ref[half // 2 :].astype(F32)).astype(BF16)
        else:
            (out_ref,) = rest

            @pl.when(j < n)
            def _():
                out_ref[...] = up().astype(BF16)

            @pl.when(j == n)
            def _():
                keep, send = out()
                out_ref[: half // 2] = keep.astype(BF16)
                out_ref[half // 2 :] = send.astype(BF16)

    whole = lambda *shape: pl.BlockSpec(shape, lambda j, m: (0,) * len(shape))
    block = lambda index: pl.BlockSpec((half, width), index)
    if own:
        out_specs = (
            block(lambda j, m: (0, jnp.minimum(j, n // 2 - 1))),
            block(lambda j, m: (0, jnp.clip(j - n // 2, 0, n // 2 - 1))),
            whole(half // 2, width),
            whole(half // 2, width),
        )
        shapes = [(half, hidden // 2)] * 2 + [(half // 2, width)] * 2
        out_shape = tuple(jax.ShapeDtypeStruct(shape, BF16) for shape in shapes)
    else:
        out_specs = block(lambda j, m: (0, j))
        out_shape = jax.ShapeDtypeStruct((half, hidden + width), BF16)
    return pl.pallas_call(
        body,
        grid_spec=pltpu.PrefetchScalarGridSpec(
            num_scalar_prefetch=1,
            grid=(n + 1,),
            in_specs=[
                whole(*attn_t.shape),
                whole(tokens, width),
                whole(tokens, width),
                pl.BlockSpec((tokens, width), lambda j, m: (0, column(j, m))),
                *([block(lambda j, m: (0, j))] if own else []),
            ],
            out_specs=out_specs,
        ),
        out_shape=out_shape,
        compiler_params=params(),
        cost_estimate=cost(7),
        name="up_out_gradient",
    )(meta, attn_t, gb, h2, dup, *([far] if own else []))


def down_grads(meta, act, dy, far=None):
    tokens, width = dy.shape
    half = width // 2
    n = act.shape[1] // 2 // half
    own = far is not None

    def body(meta, act_ref, dy_ref, *rest):
        value = mm(act_ref[...], dy_ref[...], TN)
        if own:
            far_ref, keep_ref, send_ref = rest
            j = pl.program_id(0)
            value = (value + far_ref[...].astype(F32)).astype(BF16)

            @pl.when(j < n // 2)
            def _():
                keep_ref[...] = value

            @pl.when(j >= n // 2)
            def _():
                send_ref[...] = value
        else:
            (out_ref,) = rest
            out_ref[...] = value.astype(BF16)

    def column(j, m):
        side = m[2] if own else 1 - m[2]
        bit = jnp.where(j < n // 2, m[3], 1 - m[3])
        return side * n + bit * (n // 2) + lax.rem(j, n // 2)

    block = lambda index: pl.BlockSpec((half, width), index)
    if own:
        out_specs = (
            block(lambda j, m: (jnp.minimum(j, n // 2 - 1), 0)),
            block(lambda j, m: (jnp.maximum(j - n // 2, 0), 0)),
        )
        out_shape = (jax.ShapeDtypeStruct((n // 2 * half, width), BF16),) * 2
    else:
        out_specs = block(lambda j, m: (j, 0))
        out_shape = jax.ShapeDtypeStruct((n * half, width), BF16)
    return pl.pallas_call(
        body,
        grid_spec=pltpu.PrefetchScalarGridSpec(
            num_scalar_prefetch=1,
            grid=(n,),
            in_specs=[
                pl.BlockSpec((tokens, half), lambda j, m: (0, column(j, m))),
                pl.BlockSpec((tokens, width), lambda j, m: (0, 0)),
                *([block(lambda j, m: (j, 0))] if own else []),
            ],
            out_specs=out_specs,
        ),
        out_shape=out_shape,
        compiler_params=params(),
        cost_estimate=cost(6),
        name="down_gradient",
    )(meta, act, dy, *([far] if own else []))


def assemble(meta, downs, ups, outs):
    half, width = outs[0].shape[0] * 2, outs[0].shape[1]
    hidden = ups[0].shape[1] * 2
    cut = width // 2

    def body(meta, down_aa, down_ab, down_ba, down_bb, up_a, up_b, out_a, out_b, down_ref, up_ref, out_ref):
        i = pl.program_id(0)

        def place(ref, value, swapped):
            lo, hi = value[:, :cut].astype(F32), value[:, cut:].astype(F32)
            ref[:, :cut] = jnp.where(swapped == 0, lo, hi)
            ref[:, cut:] = jnp.where(swapped == 0, hi, lo)

        down_x, down_y = i // 2 == meta[3], lax.rem(i, 2) == meta[4]
        own_x = jnp.where(down_y, down_aa[...], down_ab[...])
        place(down_ref, jnp.where(down_x, own_x, jnp.where(down_y, down_ba[...], down_bb[...])), meta[5])
        up_own = i // 2 == meta[4]
        place(up_ref, jnp.where(up_own, up_a[...], up_b[...]), meta[3])

        @pl.when(i == 0)
        def _():
            quarter = half // 4
            for z in range(2):
                for x in range(2):
                    rows = pl.ds(pl.multiple_of(jnp.bitwise_xor(meta[3], x) * quarter, quarter), quarter)
                    value = jnp.where(meta[5] == z, out_a[rows, :], out_b[rows, :])
                    place(out_ref.at[pl.ds((2 * z + x) * quarter, quarter)], value, meta[4])

    whole = lambda *shape: pl.BlockSpec(shape, lambda i, m: (0,) * len(shape))
    down = whole(half, width)
    up = pl.BlockSpec((half, width), lambda i, m: (0, jnp.bitwise_xor(lax.rem(i, 2), m[5])))
    return pl.pallas_call(
        body,
        grid_spec=pltpu.PrefetchScalarGridSpec(
            num_scalar_prefetch=1,
            grid=(4,),
            in_specs=[down, down, down, down, up, up, whole(*outs[0].shape), whole(*outs[0].shape)],
            out_specs=(
                pl.BlockSpec((half, width), lambda i, m: (i, 0)),
                pl.BlockSpec((half, width), lambda i, m: (0, i)),
                whole(half, width),
            ),
        ),
        out_shape=(
            jax.ShapeDtypeStruct((4 * half, width), F32),
            jax.ShapeDtypeStruct((half, hidden), F32),
            jax.ShapeDtypeStruct((half, width), F32),
        ),
        compiler_params=params(),
        cost_estimate=cost(7),
        name="weight_gradients",
    )(meta, *downs, *ups, *outs)


def finish_body(x_ref, gm_ref, back_ref, g_ref, out_ref):
    hat, inv = norm_rows(x_ref[...].astype(F32))
    e = back_ref[...].astype(F32) * g_ref[...]
    out_ref[...] = gm_ref[...] + inv * (
        e - jnp.mean(e, axis=-1, keepdims=True) - hat * jnp.mean(e * hat, axis=-1, keepdims=True)
    )


def finish(x, gm, back, gain):
    tokens, width = x.shape
    rows = pl.BlockSpec((128, width), lambda i: (i, 0))
    return pl.pallas_call(
        finish_body,
        grid=(tokens // 128,),
        in_specs=[rows, rows, rows, pl.BlockSpec((1, width), lambda i: (0, 0))],
        out_specs=rows,
        out_shape=jax.ShapeDtypeStruct((tokens, width), F32),
        compiler_params=params(),
        cost_estimate=cost(4),
        name="first_norm_backward",
    )(x, gm, back, gain)


def flip(value, axis, mask):
    size = lax.axis_size(axis)
    return lax.ppermute(value, axis, [(i, i ^ mask) for i in range(size)])


def bit(axis, mask):
    return (lax.axis_index(axis) // mask) % 2


def halves(value, which, axis=0):
    n = value.shape[axis] // 2
    keep = lax.dynamic_slice_in_dim(value, which * n, n, axis)
    send = lax.dynamic_slice_in_dim(value, (1 - which) * n, n, axis)
    return keep, send


def join(own, other, which, axis=0):
    return jnp.where(
        which == 0,
        jnp.concatenate([own, other], axis=axis),
        jnp.concatenate([other, own], axis=axis),
    )


def add(a, b):
    return (a.astype(F32) + b.astype(F32)).astype(BF16)


def on_device(
    tokens, lengths, ln1_gain, ln1_bias, qkv_weight, q_gain, k_gain, out_weight,
    ln2_gain, ln2_bias, up_weight, down_weight, cotangent,
):
    micro, rows, local, width = tokens.shape
    n = lax.axis_size("seq")
    length = local * n
    every = micro * rows
    team = n // every
    heads = H // team
    hd = width // H
    half = width // 2
    idx = lax.axis_index("seq")
    core = lax.axis_index("fsdp")
    row, member = idx // team, idx % team
    direct = every == 2 and team == 4
    lengths = lengths.reshape(every, lengths.shape[-1])
    mine = tokens.reshape(every, local, width)

    def swap(value):
        return flip(value, "fsdp", 1)

    vec = jnp.concatenate([ln1_gain, ln1_bias, ln2_gain, ln2_bias, q_gain, k_gain])[None]
    vec_p = swap(vec)
    ordered = jnp.where(core == 0, jnp.concatenate([vec, vec_p]), jnp.concatenate([vec_p, vec])).astype(F32)
    g1, b1, g2, b2 = (ordered[:, k * half : (k + 1) * half].reshape(1, width) for k in range(4))
    gq = ordered[:, 4 * half : 4 * half + hd // 2].reshape(hd, 1)
    gk = ordered[:, 4 * half + hd // 2 :].reshape(hd, 1)

    w_own = lax.dynamic_slice_in_dim(
        qkv_weight.reshape(half, 3, width), member * heads * hd, heads * hd, 2
    ).reshape(half, 3 * heads * hd)
    w_t = jnp.transpose(join(w_own, swap(w_own), core))

    if direct:
        near = lax.dynamic_index_in_dim(mine, row, 0, keepdims=False)
        away = lax.dynamic_index_in_dim(mine, 1 - row, 0, keepdims=False)
        far = flip(away, "seq", 4)
        cut = local // 2

        def spread(own):
            one, two = flip(own, "seq", 1), flip(own, "seq", 2)
            three = jnp.concatenate([flip(two[:cut], "seq", 1), flip(one[cut:], "seq", 2)], axis=0)
            return [own, one, two, three]

        slots = spread(near) + spread(far)
        spot = idx
    else:
        same_member = [[q * team + p for q in range(every)] for p in range(team)]
        same_row = [[q * team + p for p in range(team)] for q in range(every)]
        got = lax.all_to_all(mine, "seq", 0, 0, axis_index_groups=same_member, tiled=True)
        got = lax.all_gather(got, "seq", axis_index_groups=same_row)
        whole = jnp.swapaxes(got, 0, 1).reshape(length, width)
        slots = [whole[s * (length // 8) : (s + 1) * (length // 8)] for s in range(8)]
        spot = jnp.int32(0)
    meta = jnp.stack([spot, row, core, bit("rep", 1), bit("seq", 1), bit("seq", 2)]).astype(jnp.int32)

    out_p, up_p, down_p = swap(out_weight), swap(up_weight), swap(down_weight)

    with jax.named_scope("forward_attention"):
        qt, ka, kt, v, vt, x_row = make_qkv(meta, lengths, slots, w_t, g1, b1, gq, gk, heads, hd)
        attn, attn_f, logsum = attend(meta, lengths, qt, ka, vt, heads, hd)

    def exchange(value):
        return lax.all_to_all(value, "seq", 0, 0, tiled=True)

    packs = every * local // BLK
    if direct:
        attn_t = exchange(attn).reshape(packs, width, BLK)
    else:
        cut = jnp.moveaxis(attn.reshape(BLK * 0 + 8, heads * hd, BLK // local, local), 2, 1)
        got = exchange(cut.reshape(n, heads * hd, local))
        got = got.reshape(packs, every // packs, width, local)
        attn_t = jnp.swapaxes(got, 1, 2).reshape(packs, width, BLK)

    total = jnp.sum(lengths[:, :-1], axis=-1)
    places = idx * local + jnp.arange(local, dtype=jnp.int32)
    valid = (places[None] < total[:, None]).astype(F32).reshape(packs, 1, BLK)
    x_home = tokens.reshape(every * local, width)
    dy = cotangent.reshape(every * local, width)

    with jax.named_scope("feed_forward"):
        output, grad_mid, grad_branch, h2, act, dup, grad_attn, vec2 = ffn(
            meta, attn_t, x_home, dy, valid, g2, b2, out_weight, out_p, up_weight, up_p, down_weight, down_p
        )
    if direct:
        grad_o = exchange(grad_attn.reshape(n, heads * hd, BLK))
    else:
        cut = jnp.swapaxes(grad_attn.reshape(packs, width, every // packs, local), 1, 2)
        got = exchange(cut.reshape(n, heads * hd, local))
        got = got.reshape(8, BLK // local, heads * hd, local)
        grad_o = jnp.swapaxes(got, 1, 2).reshape(8, heads * hd, BLK)

    masks = [1 << k for k in range(n.bit_length() - 1)]
    x, y, z = ("rep", 1), ("seq", 1), ("seq", 2)

    def next_half(keep, got, way, axis):
        return halves(add(keep, got), bit(*way), axis)

    tie = lambda *values: lax.optimization_barrier(values)
    with jax.named_scope("weight_gradients"):
        far_u = swap(up_out_grads(meta, attn_t, grad_branch, h2, dup))
        far_d = swap(down_grads(meta, act, dy))
        up_k, up_s, out_k, out_s = up_out_grads(meta, attn_t, grad_branch, h2, dup, far_u)
        down_k, down_s = down_grads(meta, act, dy, far_d)
        got = flip(down_s, *x), flip(up_s, *y), flip(out_s, *z)
    grad_o = tie(grad_o, up_k, up_s, out_k, out_s, down_k, down_s)[0]
    go_back = lambda go, before: attend_back(
        meta, lengths, qt, ka, kt, v, attn_f, logsum, go, heads, hd, before
    )
    with jax.named_scope("backward_attention"):
        parts = go_back(grad_o, None)
    parts, *got = tie(parts, *got)
    with jax.named_scope("weight_gradients"):
        down_k, down_s = next_half(down_k, got[0], y, 0)
        up_k, up_s = next_half(up_k, got[1], z, 1)
        out_k, out_s = next_half(out_k, got[2], x, 0)
        got = flip(down_s, *y), flip(up_s, *z), flip(out_s, *x)
    with jax.named_scope("backward_attention"):
        parts = go_back(grad_o, parts)
    parts, *got = tie(parts, *got)
    with jax.named_scope("weight_gradients"):
        down_k, down_s = next_half(down_k, got[0], z, 1)
        up_k, up_s = next_half(up_k, got[1], x, 1)
        out_k, out_s = next_half(out_k, got[2], y, 1)
        got = flip(down_s, *z), flip(up_s, *x), flip(out_s, *y)
    with jax.named_scope("backward_attention"):
        dq, dk, dv = parts
        back_a, back_b, dw_t = qkv_back(meta, x_row, dq, dk, dv, w_t, g1, b1, gq, gk, vec2, heads, hd)
    back_a, back_b, dw_t, *got = tie(back_a, back_b, dw_t, *got)
    with jax.named_scope("weight_gradients"):
        down, up, out = add(down_k, got[0]), add(up_k, got[1]), add(out_k, got[2])
        sizes = [down.shape[0], up.shape[0]]
        pieces = jnp.concatenate([down, up, out])
        for mask in masks[2:]:
            pieces = add(pieces, flip(pieces, "seq", mask))
        down, up, out = jnp.split(pieces, [sizes[0], sizes[0] + sizes[1]])

    with jax.named_scope("first_round"):
        keep, send = halves(dw_t, core, 1)
        q_keep, q_send = next_half(keep, swap(send), x, 0)
        got = [flip(down, *z), flip(up, *x), flip(out, *y), flip(q_send, *x)]
        if direct:
            a = back_a.reshape(2, 2, 2, local, half)
            b = back_b.reshape(2, 2, 2, local, half)
            got += [flip(a[:, :, 1], *y), flip(b[:, 1], *z)]
        got = tie(*got)
        down = jnp.concatenate([down, got[0]], axis=1)
        up = jnp.concatenate([up, got[1]], axis=1)
        out = jnp.concatenate([out, got[2]], axis=1)
        piece = add(q_keep, got[3])
        if direct:
            a, b = add(a[:, :, 0], got[4]), add(b[:, 0], got[5])
    with jax.named_scope("second_round"):
        rows_at = [mask for mask in masks if mask >= team]
        got = [flip(down, *y), flip(down, *x), flip(up, *z), flip(out, *x)]
        got += [flip(piece, "seq", mask) for mask in rows_at[:1]]
        if direct:
            got += [flip(a[:, 1], *z), flip(b[:, 1], *y)]
        got = tie(*got)
        downs = [down, got[0], got[1]]
        up = jnp.concatenate([up, got[2]], axis=1)
        out = jnp.concatenate([out, got[3]], axis=0)
        if rows_at:
            piece = add(piece, got[4])
        for mask in rows_at[1:]:
            piece = add(piece, flip(piece, "seq", mask))
        if direct:
            a, b = add(a[:, 0], got[-2]), add(b[:, 0], got[-1])
    with jax.named_scope("third_round"):
        piece_y, up = tie(flip(piece, *y), up)
        piece = jnp.stack([piece, piece_y])
        if direct:
            mixed = jnp.concatenate([a, b], axis=-1)
            near, far = mixed[0], flip(mixed[1], "seq", 4)
            back = jnp.where(row == 0, jnp.stack([near, far]), jnp.stack([far, near])).reshape(every * local, width)
        else:
            whole = jnp.concatenate([back_a, back_b], axis=-1).reshape(every, team, local, width)
            whole = lax.psum_scatter(whole, "seq", scatter_dimension=1, axis_index_groups=same_row, tiled=True)
            back = lax.all_to_all(
                whole[:, 0], "seq", 0, 0, axis_index_groups=same_member, tiled=True
            ).reshape(every * local, width)
        downs.append(flip(downs[1], *x))
        piece_z = flip(piece, *z)
        pieces = [piece, piece_z, flip(piece, *x), flip(piece_z, *x)]
        ups, outs = (up, flip(up, *y)), (out, flip(out, *z))
    grad_tokens = finish(x_home, grad_mid, back, g1)
    grad_qkv, small = assemble_qkv(meta, pieces, heads, hd)
    grad_down, grad_up, grad_out = assemble(meta, downs, ups, outs)
    cuts = [small[0], small[1], small[2], small[3], small[4, : hd // 2], small[4, hd // 2 : hd]]
    shape = tokens.shape
    return (
        output.reshape(shape), grad_tokens.reshape(shape), cuts[0], cuts[1], grad_qkv, cuts[4], cuts[5],
        grad_out, cuts[2], cuts[3], grad_up, grad_down,
    )


def solution(mesh):
    tok = P(None, ("rep", "fsdp"), "seq", None)
    one, two = P("fsdp"), P("fsdp", None)
    in_specs = (tok, P(None, ("rep", "fsdp"), None), one, one, two, one, one, two, one, one, two, two, tok)
    out_specs = (tok, tok, one, one, two, one, one, two, one, one, two, two)
    return jax.shard_map(on_device, mesh=mesh, in_specs=in_specs, out_specs=out_specs, check_vma=False)
```

```python
import functools

import jax
import jax.numpy as jnp
from jax import lax
from jax.experimental import pallas as pl
from jax.experimental.pallas import tpu as pltpu
from jax.sharding import PartitionSpec as P

H = 12
EPS = 1e-06
LOG2E = 1.4426950408889634
SHIFT = 512.0
BLK = 256
EXTRA = 32
NN = (((1,), (0,)), ((), ()))
NT = (((1,), (1,)), ((), ()))
TN = (((0,), (0,)), ((), ()))
F32 = jnp.float32
BF16 = jnp.bfloat16


def mm(a, b, dims=NN):
    return lax.dot_general(a, b, dims, preferred_element_type=F32)


def params(**kw):
    return pltpu.CompilerParams(vmem_limit_bytes=60 * 1024 * 1024, **kw)


def cost(us):
    return pl.CostEstimate(flops=int(us * 0.35e9), bytes_accessed=1024, transcendentals=0)


def norm_rows(v):
    center = jnp.mean(v, axis=-1, keepdims=True)
    centred = v - center
    inv = lax.rsqrt(jnp.mean(centred * centred, axis=-1, keepdims=True) + EPS)
    return centred * inv, inv


def norm_cols(v):
    center = jnp.mean(v, axis=0, keepdims=True)
    centred = v - center
    inv = lax.rsqrt(jnp.mean(centred * centred, axis=0, keepdims=True) + EPS)
    return centred * inv, inv


def bounds_of(len_ref, row):
    out = []
    total = jnp.int32(0)
    for j in range(len_ref.shape[1] - 1):
        total = total + len_ref[row, j]
        out.append(total)
    return out


def qkv_body(heads, hd, cuts, meta, len_ref, *refs):
    xs = []
    for count in cuts:
        xs.append(refs[:count])
        refs = refs[count:]
    w_ref, g_ref, b_ref, gq_ref, gk_ref = refs[:5]
    qt_ref, ka_ref, kt_ref, v_ref, vt_ref, x_ref = refs[5:]
    wid = heads * hd
    spot, row = meta[0], meta[1]
    bounds = bounds_of(len_ref, row)
    for s in range(8):
        c = jnp.bitwise_xor(spot, s)
        cols = pl.ds(pl.multiple_of(c * BLK, BLK), BLK)
        x = jnp.concatenate([ref[...] for ref in xs[s]], axis=0) if len(xs[s]) > 1 else xs[s][0][...]
        x_ref[cols, :] = x
        hat, _ = norm_rows(x.astype(F32))
        first = (hat * g_ref[...] + b_ref[...]).astype(BF16)
        qkv = mm(w_ref[...], first, NT)
        place = c * BLK + lax.broadcasted_iota(jnp.int32, (8, BLK), 1)
        ident = jnp.zeros((8, BLK), jnp.int32)
        place_k = c * BLK + lax.broadcasted_iota(jnp.int32, (BLK, 128), 0)
        ident_k = jnp.zeros((BLK, 128), jnp.int32)
        for bound in bounds:
            ident = ident + (place >= bound).astype(jnp.int32)
            ident_k = ident_k + (place_k >= bound).astype(jnp.int32)
        which = lax.broadcasted_iota(jnp.int32, (8, BLK), 0)
        hot = jnp.where((ident == which) & (which < len(bounds)), 16.0, 0.0)
        hot = jnp.concatenate([hot, jnp.zeros((hd - 8, BLK), F32)], axis=0)
        lane = lax.broadcasted_iota(jnp.int32, (BLK, 128), 1) - hd
        hot_k = jnp.where((ident_k == lane) & (lane < len(bounds)), SHIFT / 16.0, 0.0)
        for h in range(heads):
            q, _ = norm_cols(qkv[h * hd : (h + 1) * hd])
            k, _ = norm_cols(qkv[wid + h * hd : wid + (h + 1) * hd])
            q = (q * gq_ref[...]).astype(BF16).astype(F32) * (hd**-0.5)
            k = k * gk_ref[...]
            v = qkv[2 * wid + h * hd : 2 * wid + (h + 1) * hd]
            qt_ref[h, :, cols] = jnp.concatenate([q, hot], axis=0).astype(BF16)
            kt_ref[h, :, cols] = k.astype(BF16)
            vt_ref[h, :, cols] = v.astype(BF16)
            both = jnp.transpose(jnp.concatenate([k, v], axis=0))
            ka_ref[h, cols, :] = jnp.where(lane < 0, both, hot_k).astype(BF16)
            v_ref[h, cols, :] = both[:, hd:].astype(BF16)


def make_qkv(meta, lengths, slots, w_t, gain, bias, gq, gk, heads, hd):
    length = 8 * sum(one.shape[0] for one in slots[0])
    width = slots[0][0].shape[1]
    cuts = tuple(len(one) for one in slots)
    smem = pl.BlockSpec(memory_space=pltpu.SMEM)
    vmem = pl.BlockSpec(memory_space=pltpu.VMEM)
    return pl.pallas_call(
        functools.partial(qkv_body, heads, hd, cuts),
        out_shape=(
            jax.ShapeDtypeStruct((heads, 2 * hd, length), BF16),
            jax.ShapeDtypeStruct((heads, length, 2 * hd), BF16),
            jax.ShapeDtypeStruct((heads, hd, length), BF16),
            jax.ShapeDtypeStruct((heads, length, hd), BF16),
            jax.ShapeDtypeStruct((heads, hd, length), BF16),
            jax.ShapeDtypeStruct((length, width), BF16),
        ),
        in_specs=[smem, smem] + [vmem] * (sum(cuts) + 5),
        out_specs=(vmem,) * 6,
        compiler_params=params(),
        cost_estimate=cost(12),
        name="qkv_forward",
    )(meta, lengths, *sum(slots, ()), w_t, gain, bias, gq, gk)


def block_range(bounds, i):
    first = i * BLK
    last = first + BLK - 1
    lo = jnp.int32(0)
    hi = bounds[-1]
    for bound in bounds:
        lo = jnp.where(first >= bound, bound, lo)
    for bound in bounds[::-1]:
        hi = jnp.where(last < bound, bound, hi)
    lo_b = lo // BLK
    hi_b = (hi + BLK - 1) // BLK
    return lo_b, jnp.where(first >= bounds[-1], lo_b, hi_b)


def in_pairs(lo, hi, step, carry):
    pairs = (hi - lo) // 2
    carry = lax.fori_loop(0, pairs, lambda k, c: step([lo + 2 * k, lo + 2 * k + 1], c), carry)
    return lax.fori_loop(lo + 2 * pairs, hi, lambda b, c: step([b], c), carry)


def attend_body(heads, hd, meta, len_ref, qt_ref, ka_ref, vt_ref, o_ref, of_ref, ls_ref):
    i = pl.program_id(0)
    bounds = bounds_of(len_ref, meta[1])
    lo, hi = block_range(bounds, i)

    def step(blocks, carry):
        rows = [pl.ds(pl.multiple_of(b * BLK, BLK), BLK) for b in blocks]
        items = [(h, r) for r in rows for h in range(heads)]
        scores = [mm(ka_ref[h, r, :], qt_ref[h]) for h, r in items]
        expos = [jnp.exp2(one * LOG2E - SHIFT * LOG2E) for one in scores]
        out = list(carry)
        for expo, (h, r) in zip(expos, items):
            acc, total = out[h]
            total = total + jnp.sum(expo.reshape(BLK // 8, 8, BLK), axis=0)
            out[h] = (acc + mm(vt_ref[h, :, r], expo.astype(BF16)), total)
        return tuple(out)

    init = tuple((jnp.zeros((hd, BLK), F32), jnp.zeros((8, BLK), F32)) for _ in range(heads))
    done = in_pairs(lo, hi, step, init)
    for h in range(heads):
        acc, total = done[h]
        total = jnp.sum(total, axis=0, keepdims=True)
        live = total > 0.0
        safe = jnp.where(live, total, 1.0)
        out = jnp.where(live, acc * (1.0 / safe), 0.0)
        o_ref[0, h * hd : (h + 1) * hd, :] = out.astype(BF16)
        of_ref[h] = out
        ls_ref[h] = jnp.log2(safe) + SHIFT * LOG2E


def attend(meta, lengths, qt, ka, vt, heads, hd):
    length = qt.shape[2]
    blocks = length // BLK
    smem = pl.BlockSpec(memory_space=pltpu.SMEM)
    return pl.pallas_call(
        functools.partial(attend_body, heads, hd),
        grid=(blocks,),
        out_shape=(
            jax.ShapeDtypeStruct((blocks, heads * hd, BLK), BF16),
            jax.ShapeDtypeStruct((heads, hd, length), F32),
            jax.ShapeDtypeStruct((heads, 1, length), F32),
        ),
        in_specs=[
            smem,
            smem,
            pl.BlockSpec((heads, 2 * hd, BLK), lambda i: (0, 0, i)),
            pl.BlockSpec((heads, length, 2 * hd), lambda i: (0, 0, 0)),
            pl.BlockSpec((heads, hd, length), lambda i: (0, 0, 0)),
        ],
        out_specs=(
            pl.BlockSpec((1, heads * hd, BLK), lambda i: (i, 0, 0)),
            pl.BlockSpec((heads, hd, BLK), lambda i: (0, 0, i)),
            pl.BlockSpec((heads, 1, BLK), lambda i: (0, 0, i)),
        ),
        compiler_params=params(),
        cost_estimate=cost(25),
        name="attention_forward",
    )(meta, lengths, qt, ka, vt)


def attend_back_body(first, heads, hd, meta, len_ref, *refs):
    qt_ref, ka_ref, kt_ref, v_ref, of_ref, ls_ref, go_ref = refs[:7]
    dq_ref, dk_ref, dv_ref = refs[-3:]
    i = pl.program_id(0)
    bounds = bounds_of(len_ref, meta[1])
    lo, hi = block_range(bounds, i + first)

    @pl.when(i == 0)
    def _():
        if first:
            dk_ref[...] = refs[8][...]
            dv_ref[...] = refs[9][...]
        else:
            dk_ref[...] = jnp.zeros_like(dk_ref)
            dv_ref[...] = jnp.zeros_like(dv_ref)

    inner = []
    for h in range(heads):
        go = go_ref[0, h * hd : (h + 1) * hd, :].astype(F32)
        inner.append(jnp.sum(go * of_ref[h], axis=0, keepdims=True))

    def step(blocks, carry):
        rows = [pl.ds(pl.multiple_of(b * BLK, BLK), BLK) for b in blocks]
        items = [(h, r) for r in rows for h in range(heads)]
        gos = [go_ref[0, h * hd : (h + 1) * hd, :] for h in range(heads)]
        scores = [mm(ka_ref[h, r, :], qt_ref[h]) for h, r in items]
        grad_probs = [mm(v_ref[h, r, :], gos[h]) for h, r in items]
        probs = [jnp.exp2(one * LOG2E - ls_ref[h]) for one, (h, _) in zip(scores, items)]
        grads = [(p * (g - inner[h])).astype(BF16) for p, g, (h, _) in zip(probs, grad_probs, items)]
        out = list(carry)
        for p, g, (h, r) in zip(probs, grads, items):
            dv_ref[h, :, r] += mm(gos[h], p.astype(BF16), NT)
            dk_ref[h, :, r] += mm(qt_ref[h][:hd], g, NT)
            out[h] = out[h] + mm(kt_ref[h, :, r], g)
        return tuple(out)

    done = in_pairs(lo, hi, step, tuple(jnp.zeros((hd, BLK), F32) for _ in range(heads)))
    for h in range(heads):
        dq_ref[h] = done[h] * (hd**-0.5)


def attend_back(meta, lengths, qt, ka, kt, v, of, ls, go, heads, hd, before=None):
    length = qt.shape[2]
    count = length // BLK // 2
    first = count if before else 0
    smem = pl.BlockSpec(memory_space=pltpu.SMEM)
    whole = lambda *shape: pl.BlockSpec(shape, lambda i: (0, 0, 0))
    part = lambda *shape: pl.BlockSpec(shape, lambda i: (0, 0, first + i))
    more = [pl.BlockSpec(memory_space=pl.ANY), whole(heads, hd, length), whole(heads, hd, length)]
    return pl.pallas_call(
        functools.partial(attend_back_body, first, heads, hd),
        grid=(count,),
        out_shape=tuple(jax.ShapeDtypeStruct((heads, hd, length), F32) for _ in range(3)),
        in_specs=[
            smem,
            smem,
            part(heads, 2 * hd, BLK),
            whole(heads, length, 2 * hd),
            whole(heads, hd, length),
            whole(heads, length, hd),
            part(heads, hd, BLK),
            part(heads, 1, BLK),
            pl.BlockSpec((1, heads * hd, BLK), lambda i: (first + i, 0, 0)),
            *(more if before else []),
        ],
        out_specs=(part(heads, hd, BLK), whole(heads, hd, length), whole(heads, hd, length)),
        input_output_aliases={9: 0} if before else {},
        compiler_params=params(),
        cost_estimate=cost(15),
        name="attention_backward",
    )(meta, lengths, qt, ka, kt, v, of, ls, go, *(before or ()))


def qkv_back_body(
    heads, hd, meta, x_ref, *refs
):
    dq_ref, dk_ref, dv_ref, w_ref, g_ref, b_ref, gq_ref, gk_ref, vec2_ref = refs[:9]
    da_ref, db_ref, dw_ref, acc_ref, vec_ref, gain_ref = refs[9:]
    i = pl.program_id(0)
    wid = heads * hd

    @pl.when(i == 0)
    def _():
        acc_ref[...] = jnp.zeros_like(acc_ref)
        vec_ref[...] = jnp.zeros_like(vec_ref)
        gain_ref[...] = jnp.zeros_like(gain_ref)

    hat, _ = norm_rows(x_ref[...].astype(F32))
    first = (hat * g_ref[...] + b_ref[...]).astype(BF16)
    qk = mm(w_ref[: 2 * wid, :], first, NT)
    pieces = []
    for at, gain, grad in ((0, gq_ref, dq_ref), (1, gk_ref, dk_ref)):
        for h in range(heads):
            unit, inv = norm_cols(qk[at * wid + h * hd : at * wid + (h + 1) * hd])
            gy = grad[h]
            gain_ref[at] += gy * unit
            e = gy * gain[...]
            pieces.append(
                inv
                * (
                    e
                    - jnp.mean(e, axis=0, keepdims=True)
                    - unit * jnp.mean(e * unit, axis=0, keepdims=True)
                )
            )
    for h in range(heads):
        pieces.append(dv_ref[h])
    grad = jnp.concatenate(pieces, axis=0).astype(BF16)
    acc_ref[...] += mm(grad, first)
    back = mm(grad, w_ref[...], TN)
    vec_ref[0] += jnp.sum((back * hat).reshape(BLK // 8, 8, -1), axis=0)
    vec_ref[1] += jnp.sum(back.reshape(BLK // 8, 8, -1), axis=0)
    half = back.shape[1] // 2
    da_ref[0] = back[:, :half].astype(BF16)
    db_ref[0] = back[:, half:].astype(BF16)

    @pl.when(i == pl.num_programs(0) - 1)
    def _():
        dw_ref[: 3 * wid, :] = acc_ref[...].astype(BF16)
        lines = [jnp.sum(ref[k], axis=0, keepdims=True) for ref in (vec_ref, vec2_ref) for k in range(2)]
        width = dw_ref.shape[1]
        lane = lax.broadcasted_iota(jnp.int32, (hd, width), 1)
        item = lax.broadcasted_iota(jnp.int32, (hd, width), 0)
        spread = jnp.where(item < hd // 2, item, item - hd // 2 + width // 2)
        for k in range(2):
            total = lax.dot_general(
                jnp.ones((8, BLK), F32), gain_ref[k], NT, precision=lax.Precision.HIGHEST, preferred_element_type=F32
            )
            pick = (lane == spread).astype(F32)
            line = lax.dot_general(total, pick, NN, precision=lax.Precision.HIGHEST, preferred_element_type=F32)
            lines.append(line[:1])
        place = lax.broadcasted_iota(jnp.int32, (EXTRA, width), 0)
        below = jnp.zeros((EXTRA, width), F32)
        for k, one in enumerate(lines):
            below = jnp.where(place == k, one, below)
        dw_ref[3 * wid :, :] = below.astype(BF16)


def qkv_back(meta, x, dq, dk, dv, w_t, gain, bias, gq, gk, vec2, heads, hd):
    length, width = x.shape
    blocks = length // BLK
    whole = lambda *shape: pl.BlockSpec(shape, lambda i, m: (0,) * len(shape))
    part = pl.BlockSpec((heads, hd, BLK), lambda i, m: (0, 0, i))
    grads = pl.BlockSpec((1, BLK, width // 2), lambda i, m: (jnp.bitwise_xor(i, m[0]), 0, 0))
    return pl.pallas_call(
        functools.partial(qkv_back_body, heads, hd),
        grid_spec=pltpu.PrefetchScalarGridSpec(
            num_scalar_prefetch=1,
            grid=(blocks,),
            in_specs=[
                pl.BlockSpec((BLK, width), lambda i, m: (i, 0)),
                part,
                part,
                part,
                whole(*w_t.shape),
                whole(1, width),
                whole(1, width),
                whole(hd, 1),
                whole(hd, 1),
                whole(2, 8, width),
            ],
            out_specs=(
                grads,
                grads,
                whole(w_t.shape[0] + EXTRA, width),
            ),
            scratch_shapes=[
                pltpu.VMEM(w_t.shape, F32),
                pltpu.VMEM((2, 8, width), F32),
                pltpu.VMEM((2, hd, BLK), F32),
            ],
        ),
        out_shape=(
            jax.ShapeDtypeStruct((blocks, BLK, width // 2), BF16),
            jax.ShapeDtypeStruct((blocks, BLK, width // 2), BF16),
            jax.ShapeDtypeStruct((w_t.shape[0] + EXTRA, width), BF16),
        ),
        compiler_params=params(),
        cost_estimate=cost(17),
        name="qkv_backward",
    )(meta, x, dq, dk, dv, w_t, gain, bias, gq, gk, vec2)


def assemble_qkv(meta, pieces, heads, hd):
    _, part, half = pieces[0].shape
    team = 4
    wid = heads * hd
    sizes = [half] * 4 + [hd // 2] * 2
    turned = team * wid

    def body(meta, p00, p01, p10, p11, out_ref, *refs):
        vec_refs, all_s = refs[:-1], refs[-1]
        t = pl.program_id(0)

        @pl.when(t == 0)
        def _():
            for y in range(2):
                at = jnp.bitwise_xor(meta[4], y)
                for z in range(2):
                    own_z = meta[5] == z
                    near, away = jnp.where(own_z, p00[at], p01[at]), jnp.where(own_z, p10[at], p11[at])
                    for x in range(2):
                        all_s[2 * z + y, x * part : (x + 1) * part, :] = jnp.where(meta[3] == x, near, away)
            total = jnp.zeros((EXTRA, half), F32)
            for p in range(team):
                total = total + all_s[p, 3 * wid :, :].astype(F32)
            for k, ref in enumerate(vec_refs):
                ref[...] = total[k : k + 1, : ref.shape[1]]

        rows = pl.ds(pl.multiple_of(t * wid, wid), wid)
        piece = jnp.concatenate([all_s[p, rows, :] for p in range(team)], axis=0)
        out_ref[...] = jnp.transpose(piece.astype(F32))

    whole = lambda *shape: pl.BlockSpec(shape, lambda i, m: (0,) * len(shape))
    return pl.pallas_call(
        body,
        grid_spec=pltpu.PrefetchScalarGridSpec(
            num_scalar_prefetch=1,
            grid=(3,),
            in_specs=[whole(2, part, half)] * 4,
            out_specs=(pl.BlockSpec((half, turned), lambda i, m: (0, i)), *(whole(1, k) for k in sizes)),
            scratch_shapes=[pltpu.VMEM((team, 2 * part, half), BF16)],
        ),
        out_shape=(
            jax.ShapeDtypeStruct((half, 3 * turned), F32),
            *(jax.ShapeDtypeStruct((1, k), F32) for k in sizes),
        ),
        compiler_params=params(),
        cost_estimate=cost(5),
        name="first_projection_gradient",
    )(meta, *pieces)


def gelu_pair(u):
    a = jnp.abs(u)
    t = 1.0 / (1.0 + (0.3275911 * 0.7071067811865476) * a)
    poly = 1.061405429 * t - 1.453152027
    poly = poly * t + 1.421413741
    poly = poly * t - 0.284496736
    poly = poly * t + 0.254829592
    bell = jnp.exp(-0.5 * (u * u))
    tail = (0.5 * poly) * t * bell
    cdf = jnp.where(u >= 0.0, 1.0 - tail, tail)
    return u * cdf, cdf + u * (bell * 0.3989422804014327)


def ffn(meta, attn_t, x, dy, valid, gain, bias, wo, wo_p, up, up_p, dn, dn_p):
    tokens, width = x.shape
    hidden = up.shape[1]
    fc = 512
    steps = hidden // fc
    near = steps // 2
    packs, _, lanes = attn_t.shape
    whole = lambda *shape: pl.BlockSpec(shape, lambda i, m: (0,) * len(shape))
    ups = pl.BlockSpec((width // 2, fc), lambda i, m: (0, lax.rem(m[2] * near + i, steps)))
    acts = pl.BlockSpec((tokens, fc), lambda i, m: (0, lax.rem(m[2] * near + i, steps)))
    half = width // 2

    def body(meta, *refs):
        (at_ref, x_ref, dy_ref, valid_ref, g_ref, b_ref, wo_own, wo_peer, up_own, up_peer, dn_own, dn_peer) = refs[:12]
        (out_ref, gm_ref, gb_ref, h2_ref, act_ref, dup_ref, da_ref, vec_ref) = refs[12:20]
        (mid_s, acc_s, own_s, peer_s, gown_s, gpeer_s) = refs[20:]
        i = pl.program_id(0)
        core = meta[2]
        zero = core == 0

        @pl.when(i == 0)
        def _():
            for p in range(packs):
                rows = pl.ds(p * lanes, lanes)
                own = at_ref[p, pl.ds(pl.multiple_of(core * half, half), half), :]
                peer = at_ref[p, pl.ds(pl.multiple_of((1 - core) * half, half), half), :]
                mid = x_ref[rows, :].astype(F32) + mm(own, wo_own[...], TN) + mm(peer, wo_peer[...], TN)
                mid_s[rows, :] = mid
                acc_s[rows, :] = mid
                hat, _ = norm_rows(mid)
                second = (hat * g_ref[...] + b_ref[...]).astype(BF16)
                h2_ref[:, rows] = jnp.transpose(hat * g_ref[...] + b_ref[...]).astype(BF16)
                lo, hi = second[:, :half], second[:, half:]
                own_s[rows, :] = jnp.where(zero, lo, hi)
                peer_s[rows, :] = jnp.where(zero, hi, lo)
            gown_s[...] = jnp.zeros_like(gown_s)
            gpeer_s[...] = jnp.zeros_like(gpeer_s)

        down = jnp.where(i < near, dn_own[...], dn_peer[...])
        upper = mm(own_s[...], up_own[...]) + mm(peer_s[...], up_peer[...])
        act, slope = gelu_pair(upper)
        act = act.astype(BF16)
        grad = (mm(dy_ref[...], down, NT) * slope).astype(BF16)
        act_ref[...] = act
        dup_ref[...] = grad
        acc_s[...] += mm(act, down)
        gown_s[...] += mm(grad, up_own[...], NT)
        gpeer_s[...] += mm(grad, up_peer[...], NT)

        @pl.when(i == steps - 1)
        def _():
            out_ref[...] = acc_s[...].astype(BF16)
            vec = [jnp.zeros((8, width), F32), jnp.zeros((8, width), F32)]
            for p in range(packs):
                rows = pl.ds(p * lanes, lanes)
                hat, inv = norm_rows(mid_s[rows, :])
                a, b = gown_s[rows, :], gpeer_s[rows, :]
                gy = jnp.concatenate([jnp.where(zero, a, b), jnp.where(zero, b, a)], axis=1)
                vec[0] = vec[0] + jnp.sum((gy * hat).reshape(lanes // 8, 8, width), axis=0)
                vec[1] = vec[1] + jnp.sum(gy.reshape(lanes // 8, 8, width), axis=0)
                e = gy * g_ref[...]
                gm = dy_ref[rows, :].astype(F32) + inv * (
                    e
                    - jnp.mean(e, axis=-1, keepdims=True)
                    - hat * jnp.mean(e * hat, axis=-1, keepdims=True)
                )
                gm_ref[rows, :] = gm
                gb = gm.astype(BF16)
                gb_ref[rows, :] = gb
                ok = valid_ref[p]
                da_ref[p, pl.ds(pl.multiple_of(core * half, half), half), :] = (
                    mm(wo_own[...], gb, NT) * ok
                ).astype(BF16)
                da_ref[p, pl.ds(pl.multiple_of((1 - core) * half, half), half), :] = (
                    mm(wo_peer[...], gb, NT) * ok
                ).astype(BF16)
            vec_ref[0] = vec[0]
            vec_ref[1] = vec[1]

    return pl.pallas_call(
        body,
        grid_spec=pltpu.PrefetchScalarGridSpec(
            num_scalar_prefetch=1,
            grid=(steps,),
            in_specs=[
                whole(*attn_t.shape),
                whole(tokens, width),
                whole(tokens, width),
                whole(*valid.shape),
                whole(1, width),
                whole(1, width),
                whole(half, width),
                whole(half, width),
                ups,
                ups,
                pl.BlockSpec((fc, width), lambda i, m: (jnp.minimum(i, near - 1), 0)),
                pl.BlockSpec((fc, width), lambda i, m: (jnp.maximum(i - near, 0), 0)),
            ],
            out_specs=(
                whole(tokens, width),
                whole(tokens, width),
                whole(tokens, width),
                whole(width, tokens),
                acts,
                acts,
                whole(*attn_t.shape),
                whole(2, 8, width),
            ),
            scratch_shapes=[
                pltpu.VMEM((tokens, width), F32),
                pltpu.VMEM((tokens, width), F32),
                pltpu.VMEM((tokens, half), BF16),
                pltpu.VMEM((tokens, half), BF16),
                pltpu.VMEM((tokens, half), F32),
                pltpu.VMEM((tokens, half), F32),
            ],
        ),
        out_shape=(
            jax.ShapeDtypeStruct((tokens, width), BF16),
            jax.ShapeDtypeStruct((tokens, width), F32),
            jax.ShapeDtypeStruct((tokens, width), BF16),
            jax.ShapeDtypeStruct((width, tokens), BF16),
            jax.ShapeDtypeStruct((tokens, hidden), BF16),
            jax.ShapeDtypeStruct((tokens, hidden), BF16),
            jax.ShapeDtypeStruct(attn_t.shape, BF16),
            jax.ShapeDtypeStruct((2, 8, width), F32),
        ),
        compiler_params=params(),
        cost_estimate=cost(25),
        name="ffn_both_ways",
    )(meta, attn_t, x, dy, valid, gain, bias, wo, wo_p, up, up_p, dn, dn_p)


def up_out_grads(meta, attn_t, gb, h2, dup, far=None):
    tokens, width = gb.shape
    hidden = dup.shape[1]
    half = width // 2
    packs, _, lanes = attn_t.shape
    n = hidden // width
    own = far is not None

    def column(j, m):
        bit = jnp.where(j < n // 2, m[4], 1 - m[4])
        return bit * (n // 2) + lax.rem(jnp.minimum(j, n - 1), n // 2)

    def body(meta, at_ref, gb_ref, h2_ref, dup_ref, *rest):
        j = pl.program_id(0)
        side = meta[2] if own else 1 - meta[2]

        def up():
            return mm(h2_ref[pl.ds(pl.multiple_of(side * half, half), half), :], dup_ref[...])

        def out():
            rows = pl.ds(pl.multiple_of(side * half, half), half)
            total = jnp.zeros((half, width), F32)
            for p in range(packs):
                total = total + mm(at_ref[p, rows, :], gb_ref[p * lanes : (p + 1) * lanes, :])
            lo, hi = total[: half // 2], total[half // 2 :]
            return jnp.where(meta[5] == 0, lo, hi), jnp.where(meta[5] == 0, hi, lo)

        if own:
            far_ref, uk_ref, us_ref, ok_ref, os_ref = rest

            @pl.when(j < n // 2)
            def _():
                uk_ref[...] = (up() + far_ref[...].astype(F32)).astype(BF16)

            @pl.when((j >= n // 2) & (j < n))
            def _():
                us_ref[...] = (up() + far_ref[...].astype(F32)).astype(BF16)

            @pl.when(j == n)
            def _():
                keep, send = out()
                ok_ref[...] = (keep + far_ref[: half // 2].astype(F32)).astype(BF16)
                os_ref[...] = (send + far_ref[half // 2 :].astype(F32)).astype(BF16)
        else:
            (out_ref,) = rest

            @pl.when(j < n)
            def _():
                out_ref[...] = up().astype(BF16)

            @pl.when(j == n)
            def _():
                keep, send = out()
                out_ref[: half // 2] = keep.astype(BF16)
                out_ref[half // 2 :] = send.astype(BF16)

    whole = lambda *shape: pl.BlockSpec(shape, lambda j, m: (0,) * len(shape))
    block = lambda index: pl.BlockSpec((half, width), index)
    if own:
        out_specs = (
            block(lambda j, m: (0, jnp.minimum(j, n // 2 - 1))),
            block(lambda j, m: (0, jnp.clip(j - n // 2, 0, n // 2 - 1))),
            whole(half // 2, width),
            whole(half // 2, width),
        )
        shapes = [(half, hidden // 2)] * 2 + [(half // 2, width)] * 2
        out_shape = tuple(jax.ShapeDtypeStruct(shape, BF16) for shape in shapes)
    else:
        out_specs = block(lambda j, m: (0, j))
        out_shape = jax.ShapeDtypeStruct((half, hidden + width), BF16)
    return pl.pallas_call(
        body,
        grid_spec=pltpu.PrefetchScalarGridSpec(
            num_scalar_prefetch=1,
            grid=(n + 1,),
            in_specs=[
                whole(*attn_t.shape),
                whole(tokens, width),
                whole(width, tokens),
                pl.BlockSpec((tokens, width), lambda j, m: (0, column(j, m))),
                *([block(lambda j, m: (0, j))] if own else []),
            ],
            out_specs=out_specs,
        ),
        out_shape=out_shape,
        compiler_params=params(),
        cost_estimate=cost(0.2),
        name="up_out_gradient",
    )(meta, attn_t, gb, h2, dup, *([far] if own else []))


def down_grads(meta, act, dy, far=None):
    tokens, width = dy.shape
    half = width // 2
    n = act.shape[1] // 2 // half
    own = far is not None

    def body(meta, act_ref, dy_ref, *rest):
        value = mm(act_ref[...], dy_ref[...], TN)
        if own:
            far_ref, keep_ref, send_ref = rest
            j = pl.program_id(0)
            value = (value + far_ref[...].astype(F32)).astype(BF16)

            @pl.when(j < n // 2)
            def _():
                keep_ref[...] = value

            @pl.when(j >= n // 2)
            def _():
                send_ref[...] = value
        else:
            (out_ref,) = rest
            out_ref[...] = value.astype(BF16)

    def column(j, m):
        side = m[2] if own else 1 - m[2]
        bit = jnp.where(j < n // 2, m[3], 1 - m[3])
        return side * n + bit * (n // 2) + lax.rem(j, n // 2)

    block = lambda index: pl.BlockSpec((half, width), index)
    if own:
        out_specs = (
            block(lambda j, m: (jnp.minimum(j, n // 2 - 1), 0)),
            block(lambda j, m: (jnp.maximum(j - n // 2, 0), 0)),
        )
        out_shape = (jax.ShapeDtypeStruct((n // 2 * half, width), BF16),) * 2
    else:
        out_specs = block(lambda j, m: (j, 0))
        out_shape = jax.ShapeDtypeStruct((n * half, width), BF16)
    return pl.pallas_call(
        body,
        grid_spec=pltpu.PrefetchScalarGridSpec(
            num_scalar_prefetch=1,
            grid=(n,),
            in_specs=[
                pl.BlockSpec((tokens, half), lambda j, m: (0, column(j, m))),
                pl.BlockSpec((tokens, width), lambda j, m: (0, 0)),
                *([block(lambda j, m: (j, 0))] if own else []),
            ],
            out_specs=out_specs,
        ),
        out_shape=out_shape,
        compiler_params=params(),
        cost_estimate=cost(0.2),
        name="down_gradient",
    )(meta, act, dy, *([far] if own else []))


def assemble(meta, downs, ups, outs):
    half, width = outs[0].shape[0] * 2, outs[0].shape[1]
    hidden = ups[0].shape[1] * 2
    cut = width // 2

    def body(meta, down_aa, down_ab, down_ba, down_bb, up_a, up_b, out_a, out_b, down_ref, up_ref, out_ref):
        i = pl.program_id(0)

        def place(ref, value, swapped):
            lo, hi = value[:, :cut].astype(F32), value[:, cut:].astype(F32)
            ref[:, :cut] = jnp.where(swapped == 0, lo, hi)
            ref[:, cut:] = jnp.where(swapped == 0, hi, lo)

        down_x, down_y = i // 2 == meta[3], lax.rem(i, 2) == meta[4]
        own_x = jnp.where(down_y, down_aa[...], down_ab[...])
        place(down_ref, jnp.where(down_x, own_x, jnp.where(down_y, down_ba[...], down_bb[...])), meta[5])
        up_own = i // 2 == meta[4]
        place(up_ref, jnp.where(up_own, up_a[...], up_b[...]), meta[3])

        @pl.when(i == 0)
        def _():
            quarter = half // 4
            for z in range(2):
                for x in range(2):
                    rows = pl.ds(pl.multiple_of(jnp.bitwise_xor(meta[3], x) * quarter, quarter), quarter)
                    value = jnp.where(meta[5] == z, out_a[rows, :], out_b[rows, :])
                    place(out_ref.at[pl.ds((2 * z + x) * quarter, quarter)], value, meta[4])

    whole = lambda *shape: pl.BlockSpec(shape, lambda i, m: (0,) * len(shape))
    down = whole(half, width)
    up = pl.BlockSpec((half, width), lambda i, m: (0, jnp.bitwise_xor(lax.rem(i, 2), m[5])))
    return pl.pallas_call(
        body,
        grid_spec=pltpu.PrefetchScalarGridSpec(
            num_scalar_prefetch=1,
            grid=(4,),
            in_specs=[down, down, down, down, up, up, whole(*outs[0].shape), whole(*outs[0].shape)],
            out_specs=(
                pl.BlockSpec((half, width), lambda i, m: (i, 0)),
                pl.BlockSpec((half, width), lambda i, m: (0, i)),
                whole(half, width),
            ),
        ),
        out_shape=(
            jax.ShapeDtypeStruct((4 * half, width), F32),
            jax.ShapeDtypeStruct((half, hidden), F32),
            jax.ShapeDtypeStruct((half, width), F32),
        ),
        compiler_params=params(),
        cost_estimate=cost(7),
        name="weight_gradients",
    )(meta, *downs, *ups, *outs)


def finish_body(x_ref, gm_ref, back_ref, g_ref, out_ref):
    hat, inv = norm_rows(x_ref[...].astype(F32))
    e = back_ref[...].astype(F32) * g_ref[...]
    out_ref[...] = gm_ref[...] + inv * (
        e - jnp.mean(e, axis=-1, keepdims=True) - hat * jnp.mean(e * hat, axis=-1, keepdims=True)
    )


def finish(x, gm, back, gain):
    tokens, width = x.shape
    rows = pl.BlockSpec((128, width), lambda i: (i, 0))
    return pl.pallas_call(
        finish_body,
        grid=(tokens // 128,),
        in_specs=[rows, rows, rows, pl.BlockSpec((1, width), lambda i: (0, 0))],
        out_specs=rows,
        out_shape=jax.ShapeDtypeStruct((tokens, width), F32),
        compiler_params=params(),
        cost_estimate=cost(4),
        name="first_norm_backward",
    )(x, gm, back, gain)


def flip(value, axis, mask):
    size = lax.axis_size(axis)
    return lax.ppermute(value, axis, [(i, i ^ mask) for i in range(size)])


def bit(axis, mask):
    return (lax.axis_index(axis) // mask) % 2


def halves(value, which, axis=0):
    n = value.shape[axis] // 2
    keep = lax.dynamic_slice_in_dim(value, which * n, n, axis)
    send = lax.dynamic_slice_in_dim(value, (1 - which) * n, n, axis)
    return keep, send


def join(own, other, which, axis=0):
    return jnp.where(
        which == 0,
        jnp.concatenate([own, other], axis=axis),
        jnp.concatenate([other, own], axis=axis),
    )


def add(a, b):
    return (a.astype(F32) + b.astype(F32)).astype(BF16)


def on_device(
    tokens, lengths, ln1_gain, ln1_bias, qkv_weight, q_gain, k_gain, out_weight,
    ln2_gain, ln2_bias, up_weight, down_weight, cotangent,
):
    micro, rows, local, width = tokens.shape
    n = lax.axis_size("seq")
    length = local * n
    every = micro * rows
    team = n // every
    heads = H // team
    hd = width // H
    half = width // 2
    idx = lax.axis_index("seq")
    core = lax.axis_index("fsdp")
    row, member = idx // team, idx % team
    direct = every == 2 and team == 4
    lengths = lengths.reshape(every, lengths.shape[-1])
    mine = tokens.reshape(every, local, width)

    def swap(value):
        return flip(value, "fsdp", 1)

    vec = jnp.concatenate([ln1_gain, ln1_bias, ln2_gain, ln2_bias, q_gain, k_gain])[None]
    vec_p = swap(vec)
    ordered = jnp.where(core == 0, jnp.concatenate([vec, vec_p]), jnp.concatenate([vec_p, vec])).astype(F32)
    g1, b1, g2, b2 = (ordered[:, k * half : (k + 1) * half].reshape(1, width) for k in range(4))
    gq = ordered[:, 4 * half : 4 * half + hd // 2].reshape(hd, 1)
    gk = ordered[:, 4 * half + hd // 2 :].reshape(hd, 1)

    w_own = lax.dynamic_slice_in_dim(
        qkv_weight.reshape(half, 3, width), member * heads * hd, heads * hd, 2
    ).reshape(half, 3 * heads * hd)
    w_t = jnp.transpose(join(w_own, swap(w_own), core))

    if direct:
        near = lax.dynamic_index_in_dim(mine, row, 0, keepdims=False)
        away = lax.dynamic_index_in_dim(mine, 1 - row, 0, keepdims=False)
        cut = local // 2
        far = flip(away[:cut], "seq", 4), flip(away[cut:], "seq", 4)
        one, two = flip(near, "seq", 1), flip(near, "seq", 2)
        three = flip(two[:cut], "seq", 1), flip(one[cut:], "seq", 2)
        slots = [(near,), (one,), (two,), three]
        one = tuple(flip(part, "seq", 1) for part in far)
        two = tuple(flip(part, "seq", 2) for part in far)
        three = flip(two[0], "seq", 1), flip(one[1], "seq", 2)
        slots += [far, one, two, three]
        spot = idx
    else:
        same_member = [[q * team + p for q in range(every)] for p in range(team)]
        same_row = [[q * team + p for p in range(team)] for q in range(every)]
        got = lax.all_to_all(mine, "seq", 0, 0, axis_index_groups=same_member, tiled=True)
        got = lax.all_gather(got, "seq", axis_index_groups=same_row)
        whole = jnp.swapaxes(got, 0, 1).reshape(length, width)
        slots = [(whole[s * (length // 8) : (s + 1) * (length // 8)],) for s in range(8)]
        spot = jnp.int32(0)
    meta = jnp.stack([spot, row, core, bit("rep", 1), bit("seq", 1), bit("seq", 2)]).astype(jnp.int32)

    out_p, up_p, down_p = swap(out_weight), swap(up_weight), swap(down_weight)

    with jax.named_scope("forward_attention"):
        qt, ka, kt, v, vt, x_row = make_qkv(meta, lengths, slots, w_t, g1, b1, gq, gk, heads, hd)
        attn, attn_f, logsum = attend(meta, lengths, qt, ka, vt, heads, hd)

    def exchange(value):
        return lax.all_to_all(value, "seq", 0, 0, tiled=True)

    packs = every * local // BLK
    if direct:
        attn_t = exchange(attn).reshape(packs, width, BLK)
    else:
        cut = jnp.moveaxis(attn.reshape(BLK * 0 + 8, heads * hd, BLK // local, local), 2, 1)
        got = exchange(cut.reshape(n, heads * hd, local))
        got = got.reshape(packs, every // packs, width, local)
        attn_t = jnp.swapaxes(got, 1, 2).reshape(packs, width, BLK)

    total = jnp.sum(lengths[:, :-1], axis=-1)
    places = idx * local + jnp.arange(local, dtype=jnp.int32)
    valid = (places[None] < total[:, None]).astype(F32).reshape(packs, 1, BLK)
    x_home = tokens.reshape(every * local, width)
    dy = cotangent.reshape(every * local, width)

    with jax.named_scope("feed_forward"):
        output, grad_mid, grad_branch, h2, act, dup, grad_attn, vec2 = ffn(
            meta, attn_t, x_home, dy, valid, g2, b2, out_weight, out_p, up_weight, up_p, down_weight, down_p
        )
    if direct:
        grad_o = exchange(grad_attn.reshape(n, heads * hd, BLK))
    else:
        cut = jnp.swapaxes(grad_attn.reshape(packs, width, every // packs, local), 1, 2)
        got = exchange(cut.reshape(n, heads * hd, local))
        got = got.reshape(8, BLK // local, heads * hd, local)
        grad_o = jnp.swapaxes(got, 1, 2).reshape(8, heads * hd, BLK)

    masks = [1 << k for k in range(n.bit_length() - 1)]
    x, y, z = ("rep", 1), ("seq", 1), ("seq", 2)

    def next_half(keep, got, way, axis):
        return halves(add(keep, got), bit(*way), axis)

    tie = lambda *values: lax.optimization_barrier(values)
    with jax.named_scope("weight_gradients"):
        far_u = swap(up_out_grads(meta, attn_t, grad_branch, h2, dup))
        far_d = swap(down_grads(meta, act, dy))
        up_k, up_s, out_k, out_s = up_out_grads(meta, attn_t, grad_branch, h2, dup, far_u)
        down_k, down_s = down_grads(meta, act, dy, far_d)
        got = flip(down_s, *x), flip(up_s, *y), flip(out_s, *z)
    grad_o = tie(grad_o, up_k, up_s, out_k, out_s, down_k, down_s)[0]
    go_back = lambda go, before: attend_back(
        meta, lengths, qt, ka, kt, v, attn_f, logsum, go, heads, hd, before
    )
    with jax.named_scope("backward_attention"):
        parts = go_back(grad_o, None)
    parts, *got = tie(parts, *got)
    with jax.named_scope("weight_gradients"):
        down_k, down_s = next_half(down_k, got[0], y, 0)
        up_k, up_s = next_half(up_k, got[1], z, 1)
        out_k, out_s = next_half(out_k, got[2], x, 0)
        got = flip(down_s, *y), flip(up_s, *z), flip(out_s, *x)
    with jax.named_scope("backward_attention"):
        parts = go_back(grad_o, parts)
    parts, *got = tie(parts, *got)
    with jax.named_scope("weight_gradients"):
        down_k, down_s = next_half(down_k, got[0], z, 1)
        up_k, up_s = next_half(up_k, got[1], x, 1)
        out_k, out_s = next_half(out_k, got[2], y, 1)
        got = flip(down_s, *z), flip(up_s, *x), flip(out_s, *y)
    parts, *got = tie(parts, *got)
    with jax.named_scope("weight_gradients"):
        down, up, out = add(down_k, got[0]), add(up_k, got[1]), add(out_k, got[2])
        sizes = [down.shape[0], up.shape[0]]
        pieces = jnp.concatenate([down, up, out])
        for mask in masks[2:]:
            pieces = add(pieces, flip(pieces, "seq", mask))
    with jax.named_scope("backward_attention"):
        dq, dk, dv = parts
        back_a, back_b, dw_t = qkv_back(meta, x_row, dq, dk, dv, w_t, g1, b1, gq, gk, vec2, heads, hd)
    dw_t, pieces = tie(dw_t, pieces)
    down, up, out = jnp.split(pieces, [sizes[0], sizes[0] + sizes[1]])

    with jax.named_scope("first_round"):
        keep, send = halves(dw_t, core, 1)
        q_keep, q_send = next_half(keep, swap(send), x, 0)
        got = [flip(down, *z), flip(up, *x), flip(out, *y), flip(q_send, *x)]
        if direct:
            a = back_a.reshape(2, 2, 2, local, half)
            b = back_b.reshape(2, 2, 2, local, half)
            got += [flip(a[:, :, 1], *y), flip(b[:, 1], *z)]
        got = tie(*got)
        down = jnp.concatenate([down, got[0]], axis=1)
        up = jnp.concatenate([up, got[1]], axis=1)
        out = jnp.concatenate([out, got[2]], axis=1)
        piece = add(q_keep, got[3])
        if direct:
            a, b = add(a[:, :, 0], got[4]), add(b[:, 0], got[5])
    with jax.named_scope("second_round"):
        rows_at = [mask for mask in masks if mask >= team]
        got = [flip(down, *y), flip(down, *x), flip(up, *z), flip(out, *x)]
        got += [flip(piece, "seq", mask) for mask in rows_at[:1]]
        if direct:
            got += [flip(a[:, 1], *z), flip(b[:, 1], *y)]
        got = tie(*got)
        downs = [down, got[0], got[1]]
        up = jnp.concatenate([up, got[2]], axis=1)
        out = jnp.concatenate([out, got[3]], axis=0)
        if rows_at:
            piece = add(piece, got[4])
        for mask in rows_at[1:]:
            piece = add(piece, flip(piece, "seq", mask))
        if direct:
            a, b = add(a[:, 0], got[-2]), add(b[:, 0], got[-1])
    with jax.named_scope("third_round"):
        piece_y, up = tie(flip(piece, *y), up)
        piece = jnp.stack([piece, piece_y])
        if direct:
            mixed = jnp.concatenate([a, b], axis=-1)
            near, far = mixed[0], flip(mixed[1], "seq", 4)
            back = jnp.where(row == 0, jnp.stack([near, far]), jnp.stack([far, near])).reshape(every * local, width)
        else:
            whole = jnp.concatenate([back_a, back_b], axis=-1).reshape(every, team, local, width)
            whole = lax.psum_scatter(whole, "seq", scatter_dimension=1, axis_index_groups=same_row, tiled=True)
            back = lax.all_to_all(
                whole[:, 0], "seq", 0, 0, axis_index_groups=same_member, tiled=True
            ).reshape(every * local, width)
        downs.append(flip(downs[1], *x))
        piece_z = flip(piece, *z)
        pieces = [piece, piece_z, flip(piece, *x), flip(piece_z, *x)]
        ups, outs = (up, flip(up, *y)), (out, flip(out, *z))
    grad_tokens = finish(x_home, grad_mid, back, g1)
    grad_qkv, *cuts = assemble_qkv(meta, pieces, heads, hd)
    grad_down, grad_up, grad_out = assemble(meta, downs, ups, outs)
    cuts = [one.reshape(-1) for one in cuts]
    shape = tokens.shape
    return (
        output.reshape(shape), grad_tokens.reshape(shape), cuts[0], cuts[1], grad_qkv, cuts[4], cuts[5],
        grad_out, cuts[2], cuts[3], grad_up, grad_down,
    )


def solution(mesh):
    tok = P(None, ("rep", "fsdp"), "seq", None)
    one, two = P("fsdp"), P("fsdp", None)
    in_specs = (tok, P(None, ("rep", "fsdp"), None), one, one, two, one, one, two, one, one, two, two, tok)
    out_specs = (tok, tok, one, one, two, one, one, two, one, one, two, two)
    return jax.shard_map(on_device, mesh=mesh, in_specs=in_specs, out_specs=out_specs, check_vma=False)
```

```python
import functools

import jax
import jax.numpy as jnp
from jax import lax
from jax.experimental import pallas as pl
from jax.experimental.pallas import tpu as pltpu
from jax.sharding import PartitionSpec as P

H = 12
EPS = 1e-06
LOG2E = 1.4426950408889634
SHIFT = 512.0
BLK = 256
EXTRA = 32
NN = (((1,), (0,)), ((), ()))
NT = (((1,), (1,)), ((), ()))
TN = (((0,), (0,)), ((), ()))
F32 = jnp.float32
BF16 = jnp.bfloat16


def mm(a, b, dims=NN):
    return lax.dot_general(a, b, dims, preferred_element_type=F32)


def params(**kw):
    return pltpu.CompilerParams(vmem_limit_bytes=60 * 1024 * 1024, **kw)


def cost(us):
    return pl.CostEstimate(flops=int(us * 0.35e9), bytes_accessed=1024, transcendentals=0)


def norm_rows(v):
    center = jnp.mean(v, axis=-1, keepdims=True)
    centred = v - center
    inv = lax.rsqrt(jnp.mean(centred * centred, axis=-1, keepdims=True) + EPS)
    return centred * inv, inv


def norm_cols(v):
    center = jnp.mean(v, axis=0, keepdims=True)
    centred = v - center
    inv = lax.rsqrt(jnp.mean(centred * centred, axis=0, keepdims=True) + EPS)
    return centred * inv, inv


def bounds_of(len_ref, row):
    out = []
    total = jnp.int32(0)
    for j in range(len_ref.shape[1] - 1):
        total = total + len_ref[row, j]
        out.append(total)
    return out


def qkv_body(heads, hd, cuts, meta, len_ref, *refs):
    xs = []
    for count in cuts:
        xs.append(refs[:count])
        refs = refs[count:]
    w_ref, g_ref, b_ref, gq_ref, gk_ref = refs[:5]
    qt_ref, ka_ref, kt_ref, v_ref, vt_ref, x_ref = refs[5:]
    wid = heads * hd
    spot, row = meta[0], meta[1]
    bounds = bounds_of(len_ref, row)
    for s in range(8):
        c = jnp.bitwise_xor(spot, s)
        cols = pl.ds(pl.multiple_of(c * BLK, BLK), BLK)
        x = jnp.concatenate([ref[...] for ref in xs[s]], axis=0) if len(xs[s]) > 1 else xs[s][0][...]
        x_ref[cols, :] = x
        hat, _ = norm_rows(x.astype(F32))
        first = (hat * g_ref[...] + b_ref[...]).astype(BF16)
        qkv = mm(w_ref[...], first, NT)
        place = c * BLK + lax.broadcasted_iota(jnp.int32, (8, BLK), 1)
        ident = jnp.zeros((8, BLK), jnp.int32)
        place_k = c * BLK + lax.broadcasted_iota(jnp.int32, (BLK, 128), 0)
        ident_k = jnp.zeros((BLK, 128), jnp.int32)
        for bound in bounds:
            ident = ident + (place >= bound).astype(jnp.int32)
            ident_k = ident_k + (place_k >= bound).astype(jnp.int32)
        which = lax.broadcasted_iota(jnp.int32, (8, BLK), 0)
        hot = jnp.where((ident == which) & (which < len(bounds)), 16.0, 0.0)
        hot = jnp.concatenate([hot, jnp.zeros((hd - 8, BLK), F32)], axis=0)
        lane = lax.broadcasted_iota(jnp.int32, (BLK, 128), 1) - hd
        hot_k = jnp.where((ident_k == lane) & (lane < len(bounds)), SHIFT / 16.0, 0.0)
        for h in range(heads):
            q, _ = norm_cols(qkv[h * hd : (h + 1) * hd])
            k, _ = norm_cols(qkv[wid + h * hd : wid + (h + 1) * hd])
            q = (q * gq_ref[...]).astype(BF16).astype(F32) * (hd**-0.5)
            k = k * gk_ref[...]
            v = qkv[2 * wid + h * hd : 2 * wid + (h + 1) * hd]
            qt_ref[h, :, cols] = jnp.concatenate([q, hot], axis=0).astype(BF16)
            kt_ref[h, :, cols] = k.astype(BF16)
            vt_ref[h, :, cols] = v.astype(BF16)
            both = jnp.transpose(jnp.concatenate([k, v], axis=0))
            ka_ref[h, cols, :] = jnp.where(lane < 0, both, hot_k).astype(BF16)
            v_ref[h, cols, :] = both[:, hd:].astype(BF16)


def make_qkv(meta, lengths, slots, w_t, gain, bias, gq, gk, heads, hd):
    length = 8 * sum(one.shape[0] for one in slots[0])
    width = slots[0][0].shape[1]
    cuts = tuple(len(one) for one in slots)
    smem = pl.BlockSpec(memory_space=pltpu.SMEM)
    vmem = pl.BlockSpec(memory_space=pltpu.VMEM)
    return pl.pallas_call(
        functools.partial(qkv_body, heads, hd, cuts),
        out_shape=(
            jax.ShapeDtypeStruct((heads, 2 * hd, length), BF16),
            jax.ShapeDtypeStruct((heads, length, 2 * hd), BF16),
            jax.ShapeDtypeStruct((heads, hd, length), BF16),
            jax.ShapeDtypeStruct((heads, length, hd), BF16),
            jax.ShapeDtypeStruct((heads, hd, length), BF16),
            jax.ShapeDtypeStruct((length, width), BF16),
        ),
        in_specs=[smem, smem] + [vmem] * (sum(cuts) + 5),
        out_specs=(vmem,) * 6,
        compiler_params=params(),
        cost_estimate=cost(12),
        name="qkv_forward",
    )(meta, lengths, *sum(slots, ()), w_t, gain, bias, gq, gk)


def block_range(bounds, i):
    first = i * BLK
    last = first + BLK - 1
    lo = jnp.int32(0)
    hi = bounds[-1]
    for bound in bounds:
        lo = jnp.where(first >= bound, bound, lo)
    for bound in bounds[::-1]:
        hi = jnp.where(last < bound, bound, hi)
    lo_b = lo // BLK
    hi_b = (hi + BLK - 1) // BLK
    return lo_b, jnp.where(first >= bounds[-1], lo_b, hi_b)


def in_pairs(lo, hi, step, carry):
    pairs = (hi - lo) // 2
    carry = lax.fori_loop(0, pairs, lambda k, c: step([lo + 2 * k, lo + 2 * k + 1], c), carry)
    return lax.fori_loop(lo + 2 * pairs, hi, lambda b, c: step([b], c), carry)


def attend_body(heads, hd, meta, len_ref, qt_ref, ka_ref, vt_ref, o_ref, of_ref, ls_ref):
    i = pl.program_id(0)
    bounds = bounds_of(len_ref, meta[1])
    lo, hi = block_range(bounds, i)

    def step(blocks, carry):
        rows = [pl.ds(pl.multiple_of(b * BLK, BLK), BLK) for b in blocks]
        items = [(h, r) for r in rows for h in range(heads)]
        scores = [mm(ka_ref[h, r, :], qt_ref[h]) for h, r in items]
        expos = [jnp.exp2(one * LOG2E - SHIFT * LOG2E) for one in scores]
        out = list(carry)
        for expo, (h, r) in zip(expos, items):
            acc, total = out[h]
            total = total + jnp.sum(expo.reshape(BLK // 8, 8, BLK), axis=0)
            out[h] = (acc + mm(vt_ref[h, :, r], expo.astype(BF16)), total)
        return tuple(out)

    init = tuple((jnp.zeros((hd, BLK), F32), jnp.zeros((8, BLK), F32)) for _ in range(heads))
    done = in_pairs(lo, hi, step, init)
    for h in range(heads):
        acc, total = done[h]
        total = jnp.sum(total, axis=0, keepdims=True)
        live = total > 0.0
        safe = jnp.where(live, total, 1.0)
        out = jnp.where(live, acc * (1.0 / safe), 0.0)
        o_ref[0, h * hd : (h + 1) * hd, :] = out.astype(BF16)
        of_ref[h] = out
        ls_ref[h] = jnp.log2(safe) + SHIFT * LOG2E


def attend(meta, lengths, qt, ka, vt, heads, hd):
    length = qt.shape[2]
    blocks = length // BLK
    smem = pl.BlockSpec(memory_space=pltpu.SMEM)
    return pl.pallas_call(
        functools.partial(attend_body, heads, hd),
        grid=(blocks,),
        out_shape=(
            jax.ShapeDtypeStruct((blocks, heads * hd, BLK), BF16),
            jax.ShapeDtypeStruct((heads, hd, length), F32),
            jax.ShapeDtypeStruct((heads, 1, length), F32),
        ),
        in_specs=[
            smem,
            smem,
            pl.BlockSpec((heads, 2 * hd, BLK), lambda i: (0, 0, i)),
            pl.BlockSpec((heads, length, 2 * hd), lambda i: (0, 0, 0)),
            pl.BlockSpec((heads, hd, length), lambda i: (0, 0, 0)),
        ],
        out_specs=(
            pl.BlockSpec((1, heads * hd, BLK), lambda i: (i, 0, 0)),
            pl.BlockSpec((heads, hd, BLK), lambda i: (0, 0, i)),
            pl.BlockSpec((heads, 1, BLK), lambda i: (0, 0, i)),
        ),
        compiler_params=params(),
        cost_estimate=cost(25),
        name="attention_forward",
    )(meta, lengths, qt, ka, vt)


def attend_back_body(first, heads, hd, meta, len_ref, *refs):
    qt_ref, ka_ref, kt_ref, v_ref, of_ref, ls_ref, go_ref = refs[:7]
    dq_ref, dk_ref, dv_ref = refs[-3:]
    i = pl.program_id(0)
    bounds = bounds_of(len_ref, meta[1])
    lo, hi = block_range(bounds, i + first)

    @pl.when(i == 0)
    def _():
        if first:
            dk_ref[...] = refs[8][...]
            dv_ref[...] = refs[9][...]
        else:
            dk_ref[...] = jnp.zeros_like(dk_ref)
            dv_ref[...] = jnp.zeros_like(dv_ref)

    inner = []
    for h in range(heads):
        go = go_ref[0, h * hd : (h + 1) * hd, :].astype(F32)
        inner.append(jnp.sum(go * of_ref[h], axis=0, keepdims=True))

    def step(blocks, carry):
        rows = [pl.ds(pl.multiple_of(b * BLK, BLK), BLK) for b in blocks]
        items = [(h, r) for r in rows for h in range(heads)]
        gos = [go_ref[0, h * hd : (h + 1) * hd, :] for h in range(heads)]
        scores = [mm(ka_ref[h, r, :], qt_ref[h]) for h, r in items]
        grad_probs = [mm(v_ref[h, r, :], gos[h]) for h, r in items]
        probs = [jnp.exp2(one * LOG2E - ls_ref[h]) for one, (h, _) in zip(scores, items)]
        grads = [(p * (g - inner[h])).astype(BF16) for p, g, (h, _) in zip(probs, grad_probs, items)]
        out = list(carry)
        for p, g, (h, r) in zip(probs, grads, items):
            dv_ref[h, :, r] += mm(gos[h], p.astype(BF16), NT)
            dk_ref[h, :, r] += mm(qt_ref[h][:hd], g, NT)
            out[h] = out[h] + mm(kt_ref[h, :, r], g)
        return tuple(out)

    done = in_pairs(lo, hi, step, tuple(jnp.zeros((hd, BLK), F32) for _ in range(heads)))
    for h in range(heads):
        dq_ref[h] = done[h] * (hd**-0.5)


def attend_back(meta, lengths, qt, ka, kt, v, of, ls, go, heads, hd, before=None):
    length = qt.shape[2]
    count = length // BLK // 2
    first = count if before else 0
    smem = pl.BlockSpec(memory_space=pltpu.SMEM)
    whole = lambda *shape: pl.BlockSpec(shape, lambda i: (0, 0, 0))
    part = lambda *shape: pl.BlockSpec(shape, lambda i: (0, 0, first + i))
    more = [pl.BlockSpec(memory_space=pl.ANY), whole(heads, hd, length), whole(heads, hd, length)]
    return pl.pallas_call(
        functools.partial(attend_back_body, first, heads, hd),
        grid=(count,),
        out_shape=tuple(jax.ShapeDtypeStruct((heads, hd, length), F32) for _ in range(3)),
        in_specs=[
            smem,
            smem,
            part(heads, 2 * hd, BLK),
            whole(heads, length, 2 * hd),
            whole(heads, hd, length),
            whole(heads, length, hd),
            part(heads, hd, BLK),
            part(heads, 1, BLK),
            pl.BlockSpec((1, heads * hd, BLK), lambda i: (first + i, 0, 0)),
            *(more if before else []),
        ],
        out_specs=(part(heads, hd, BLK), whole(heads, hd, length), whole(heads, hd, length)),
        input_output_aliases={9: 0} if before else {},
        compiler_params=params(),
        cost_estimate=cost(15),
        name="attention_backward",
    )(meta, lengths, qt, ka, kt, v, of, ls, go, *(before or ()))


def qkv_back_body(
    heads, hd, meta, x_ref, *refs
):
    dq_ref, dk_ref, dv_ref, w_ref, g_ref, b_ref, gq_ref, gk_ref, vec2_ref = refs[:9]
    da_ref, db_ref, dw_ref, acc_ref, vec_ref, gain_ref = refs[9:]
    i = pl.program_id(0)
    wid = heads * hd

    @pl.when(i == 0)
    def _():
        acc_ref[...] = jnp.zeros_like(acc_ref)
        vec_ref[...] = jnp.zeros_like(vec_ref)
        gain_ref[...] = jnp.zeros_like(gain_ref)

    hat, _ = norm_rows(x_ref[...].astype(F32))
    first = (hat * g_ref[...] + b_ref[...]).astype(BF16)
    qk = mm(w_ref[: 2 * wid, :], first, NT)
    pieces = []
    for at, gain, grad in ((0, gq_ref, dq_ref), (1, gk_ref, dk_ref)):
        for h in range(heads):
            unit, inv = norm_cols(qk[at * wid + h * hd : at * wid + (h + 1) * hd])
            gy = grad[h]
            gain_ref[at] += gy * unit
            e = gy * gain[...]
            pieces.append(
                inv
                * (
                    e
                    - jnp.mean(e, axis=0, keepdims=True)
                    - unit * jnp.mean(e * unit, axis=0, keepdims=True)
                )
            )
    for h in range(heads):
        pieces.append(dv_ref[h])
    grad = jnp.concatenate(pieces, axis=0).astype(BF16)
    acc_ref[...] += mm(grad, first)
    back = mm(grad, w_ref[...], TN)
    vec_ref[0] += jnp.sum((back * hat).reshape(BLK // 8, 8, -1), axis=0)
    vec_ref[1] += jnp.sum(back.reshape(BLK // 8, 8, -1), axis=0)
    half = back.shape[1] // 2
    da_ref[0] = back[:, :half].astype(BF16)
    db_ref[0] = back[:, half:].astype(BF16)

    @pl.when(i == pl.num_programs(0) - 1)
    def _():
        dw_ref[: 3 * wid, :] = acc_ref[...].astype(BF16)
        lines = [jnp.sum(ref[k], axis=0, keepdims=True) for ref in (vec_ref, vec2_ref) for k in range(2)]
        width = dw_ref.shape[1]
        lane = lax.broadcasted_iota(jnp.int32, (hd, width), 1)
        item = lax.broadcasted_iota(jnp.int32, (hd, width), 0)
        spread = jnp.where(item < hd // 2, item, item - hd // 2 + width // 2)
        for k in range(2):
            total = lax.dot_general(
                jnp.ones((8, BLK), F32), gain_ref[k], NT, precision=lax.Precision.HIGHEST, preferred_element_type=F32
            )
            pick = (lane == spread).astype(F32)
            line = lax.dot_general(total, pick, NN, precision=lax.Precision.HIGHEST, preferred_element_type=F32)
            lines.append(line[:1])
        place = lax.broadcasted_iota(jnp.int32, (EXTRA, width), 0)
        below = jnp.zeros((EXTRA, width), F32)
        for k, one in enumerate(lines):
            below = jnp.where(place == k, one, below)
        dw_ref[3 * wid :, :] = below.astype(BF16)


def qkv_back(meta, x, dq, dk, dv, w_t, gain, bias, gq, gk, vec2, heads, hd):
    length, width = x.shape
    blocks = length // BLK
    whole = lambda *shape: pl.BlockSpec(shape, lambda i, m: (0,) * len(shape))
    part = pl.BlockSpec((heads, hd, BLK), lambda i, m: (0, 0, i))
    grads = pl.BlockSpec((1, BLK, width // 2), lambda i, m: (jnp.bitwise_xor(i, m[0]), 0, 0))
    return pl.pallas_call(
        functools.partial(qkv_back_body, heads, hd),
        grid_spec=pltpu.PrefetchScalarGridSpec(
            num_scalar_prefetch=1,
            grid=(blocks,),
            in_specs=[
                pl.BlockSpec((BLK, width), lambda i, m: (i, 0)),
                part,
                part,
                part,
                whole(*w_t.shape),
                whole(1, width),
                whole(1, width),
                whole(hd, 1),
                whole(hd, 1),
                whole(2, 8, width),
            ],
            out_specs=(
                grads,
                grads,
                whole(w_t.shape[0] + EXTRA, width),
            ),
            scratch_shapes=[
                pltpu.VMEM(w_t.shape, F32),
                pltpu.VMEM((2, 8, width), F32),
                pltpu.VMEM((2, hd, BLK), F32),
            ],
        ),
        out_shape=(
            jax.ShapeDtypeStruct((blocks, BLK, width // 2), BF16),
            jax.ShapeDtypeStruct((blocks, BLK, width // 2), BF16),
            jax.ShapeDtypeStruct((w_t.shape[0] + EXTRA, width), BF16),
        ),
        compiler_params=params(),
        cost_estimate=cost(17),
        name="qkv_backward",
    )(meta, x, dq, dk, dv, w_t, gain, bias, gq, gk, vec2)


def assemble_qkv(meta, pieces, heads, hd):
    _, part, half = pieces[0].shape
    team = 4
    wid = heads * hd
    turned = team * wid

    def body(meta, p00, p01, p10, p11, out_ref, vec_ref, all_s):
        t = pl.program_id(0)

        @pl.when(t == 0)
        def _():
            for y in range(2):
                at = jnp.bitwise_xor(meta[4], y)
                for z in range(2):
                    own_z = meta[5] == z
                    near, away = jnp.where(own_z, p00[at], p01[at]), jnp.where(own_z, p10[at], p11[at])
                    for x in range(2):
                        all_s[2 * z + y, x * part : (x + 1) * part, :] = jnp.where(meta[3] == x, near, away)
            total = jnp.zeros((EXTRA, half), F32)
            for p in range(team):
                total = total + all_s[p, 3 * wid :, :].astype(F32)
            vec_ref[...] = total

        rows = pl.ds(pl.multiple_of(t * wid, wid), wid)
        piece = jnp.concatenate([all_s[p, rows, :] for p in range(team)], axis=0)
        out_ref[...] = jnp.transpose(piece.astype(F32))

    whole = lambda *shape: pl.BlockSpec(shape, lambda i, m: (0,) * len(shape))
    return pl.pallas_call(
        body,
        grid_spec=pltpu.PrefetchScalarGridSpec(
            num_scalar_prefetch=1,
            grid=(3,),
            in_specs=[whole(2, part, half)] * 4,
            out_specs=(pl.BlockSpec((half, turned), lambda i, m: (0, i)), whole(EXTRA, half)),
            scratch_shapes=[pltpu.VMEM((team, 2 * part, half), BF16)],
        ),
        out_shape=(jax.ShapeDtypeStruct((half, 3 * turned), F32), jax.ShapeDtypeStruct((EXTRA, half), F32)),
        compiler_params=params(),
        cost_estimate=cost(5),
        name="first_projection_gradient",
    )(meta, *pieces)


def gelu_pair(u):
    a = jnp.abs(u)
    t = 1.0 / (1.0 + (0.3275911 * 0.7071067811865476) * a)
    poly = 1.061405429 * t - 1.453152027
    poly = poly * t + 1.421413741
    poly = poly * t - 0.284496736
    poly = poly * t + 0.254829592
    bell = jnp.exp(-0.5 * (u * u))
    tail = (0.5 * poly) * t * bell
    cdf = jnp.where(u >= 0.0, 1.0 - tail, tail)
    return u * cdf, cdf + u * (bell * 0.3989422804014327)


def ffn(meta, attn_t, x, dy, valid, gain, bias, wo, wo_p, up, up_p, dn, dn_p):
    tokens, width = x.shape
    hidden = up.shape[1]
    fc = 512
    steps = hidden // fc
    near = steps // 2
    packs, _, lanes = attn_t.shape
    whole = lambda *shape: pl.BlockSpec(shape, lambda i, m: (0,) * len(shape))
    ups = pl.BlockSpec((width // 2, fc), lambda i, m: (0, lax.rem(m[2] * near + i, steps)))
    acts = pl.BlockSpec((tokens, fc), lambda i, m: (0, lax.rem(m[2] * near + i, steps)))
    half = width // 2

    def body(meta, *refs):
        (at_ref, x_ref, dy_ref, valid_ref, g_ref, b_ref, wo_own, wo_peer, up_own, up_peer, dn_own, dn_peer) = refs[:12]
        (out_ref, gm_ref, gb_ref, h2_ref, act_ref, dup_ref, da_ref, vec_ref) = refs[12:20]
        (mid_s, acc_s, own_s, peer_s, gown_s, gpeer_s) = refs[20:]
        i = pl.program_id(0)
        core = meta[2]
        zero = core == 0

        @pl.when(i == 0)
        def _():
            for p in range(packs):
                rows = pl.ds(p * lanes, lanes)
                own = at_ref[p, pl.ds(pl.multiple_of(core * half, half), half), :]
                peer = at_ref[p, pl.ds(pl.multiple_of((1 - core) * half, half), half), :]
                mid = x_ref[rows, :].astype(F32) + mm(own, wo_own[...], TN) + mm(peer, wo_peer[...], TN)
                mid_s[rows, :] = mid
                acc_s[rows, :] = mid
                hat, _ = norm_rows(mid)
                second = (hat * g_ref[...] + b_ref[...]).astype(BF16)
                h2_ref[:, rows] = jnp.transpose(hat * g_ref[...] + b_ref[...]).astype(BF16)
                lo, hi = second[:, :half], second[:, half:]
                own_s[rows, :] = jnp.where(zero, lo, hi)
                peer_s[rows, :] = jnp.where(zero, hi, lo)
            gown_s[...] = jnp.zeros_like(gown_s)
            gpeer_s[...] = jnp.zeros_like(gpeer_s)

        down = jnp.where(i < near, dn_own[...], dn_peer[...])
        upper = mm(own_s[...], up_own[...]) + mm(peer_s[...], up_peer[...])
        act, slope = gelu_pair(upper)
        act = act.astype(BF16)
        grad = (mm(dy_ref[...], down, NT) * slope).astype(BF16)
        act_ref[...] = act
        dup_ref[...] = grad
        acc_s[...] += mm(act, down)
        gown_s[...] += mm(grad, up_own[...], NT)
        gpeer_s[...] += mm(grad, up_peer[...], NT)

        @pl.when(i == steps - 1)
        def _():
            out_ref[...] = acc_s[...].astype(BF16)
            vec = [jnp.zeros((8, width), F32), jnp.zeros((8, width), F32)]
            for p in range(packs):
                rows = pl.ds(p * lanes, lanes)
                hat, inv = norm_rows(mid_s[rows, :])
                a, b = gown_s[rows, :], gpeer_s[rows, :]
                gy = jnp.concatenate([jnp.where(zero, a, b), jnp.where(zero, b, a)], axis=1)
                vec[0] = vec[0] + jnp.sum((gy * hat).reshape(lanes // 8, 8, width), axis=0)
                vec[1] = vec[1] + jnp.sum(gy.reshape(lanes // 8, 8, width), axis=0)
                e = gy * g_ref[...]
                gm = dy_ref[rows, :].astype(F32) + inv * (
                    e
                    - jnp.mean(e, axis=-1, keepdims=True)
                    - hat * jnp.mean(e * hat, axis=-1, keepdims=True)
                )
                gm_ref[rows, :] = gm
                gb = gm.astype(BF16)
                gb_ref[rows, :] = gb
                ok = valid_ref[p]
                da_ref[p, pl.ds(pl.multiple_of(core * half, half), half), :] = (
                    mm(wo_own[...], gb, NT) * ok
                ).astype(BF16)
                da_ref[p, pl.ds(pl.multiple_of((1 - core) * half, half), half), :] = (
                    mm(wo_peer[...], gb, NT) * ok
                ).astype(BF16)
            vec_ref[0] = vec[0]
            vec_ref[1] = vec[1]

    return pl.pallas_call(
        body,
        grid_spec=pltpu.PrefetchScalarGridSpec(
            num_scalar_prefetch=1,
            grid=(steps,),
            in_specs=[
                whole(*attn_t.shape),
                whole(tokens, width),
                whole(tokens, width),
                whole(*valid.shape),
                whole(1, width),
                whole(1, width),
                whole(half, width),
                whole(half, width),
                ups,
                ups,
                pl.BlockSpec((fc, width), lambda i, m: (jnp.minimum(i, near - 1), 0)),
                pl.BlockSpec((fc, width), lambda i, m: (jnp.maximum(i - near, 0), 0)),
            ],
            out_specs=(
                whole(tokens, width),
                whole(tokens, width),
                whole(tokens, width),
                whole(width, tokens),
                acts,
                acts,
                whole(*attn_t.shape),
                whole(2, 8, width),
            ),
            scratch_shapes=[
                pltpu.VMEM((tokens, width), F32),
                pltpu.VMEM((tokens, width), F32),
                pltpu.VMEM((tokens, half), BF16),
                pltpu.VMEM((tokens, half), BF16),
                pltpu.VMEM((tokens, half), F32),
                pltpu.VMEM((tokens, half), F32),
            ],
        ),
        out_shape=(
            jax.ShapeDtypeStruct((tokens, width), BF16),
            jax.ShapeDtypeStruct((tokens, width), F32),
            jax.ShapeDtypeStruct((tokens, width), BF16),
            jax.ShapeDtypeStruct((width, tokens), BF16),
            jax.ShapeDtypeStruct((tokens, hidden), BF16),
            jax.ShapeDtypeStruct((tokens, hidden), BF16),
            jax.ShapeDtypeStruct(attn_t.shape, BF16),
            jax.ShapeDtypeStruct((2, 8, width), F32),
        ),
        compiler_params=params(),
        cost_estimate=cost(25),
        name="ffn_both_ways",
    )(meta, attn_t, x, dy, valid, gain, bias, wo, wo_p, up, up_p, dn, dn_p)


def up_grads(meta, h2, dup, far=None):
    width, tokens = h2.shape
    hidden = dup.shape[1]
    half = width // 2
    n = hidden // width
    own = far is not None

    def body(meta, h2_ref, dup_ref, *rest):
        j = pl.program_id(0)
        side = meta[2] if own else 1 - meta[2]
        value = mm(h2_ref[pl.ds(pl.multiple_of(side * half, half), half), :], dup_ref[...])
        if own:
            store_halves(j, n, value, *rest)
        else:
            rest[0][...] = value.astype(BF16)

    def column(j, m):
        return jnp.where(j < n // 2, m[4], 1 - m[4]) * (n // 2) + lax.rem(j, n // 2)

    block = lambda index: pl.BlockSpec((half, width), index)
    if own:
        out_specs = (
            block(lambda j, m: (0, jnp.minimum(j, n // 2 - 1))),
            block(lambda j, m: (0, jnp.maximum(j - n // 2, 0))),
        )
        out_shape = (jax.ShapeDtypeStruct((half, hidden // 2), BF16),) * 2
    else:
        out_specs = block(lambda j, m: (0, j))
        out_shape = jax.ShapeDtypeStruct((half, hidden), BF16)
    return pl.pallas_call(
        body,
        grid_spec=pltpu.PrefetchScalarGridSpec(
            num_scalar_prefetch=1,
            grid=(n,),
            in_specs=[
                pl.BlockSpec((width, tokens), lambda j, m: (0, 0)),
                pl.BlockSpec((tokens, width), lambda j, m: (0, column(j, m))),
                *([block(lambda j, m: (0, j))] if own else []),
            ],
            out_specs=out_specs,
        ),
        out_shape=out_shape,
        compiler_params=params(),
        cost_estimate=cost(0.2),
        name="up_gradient",
    )(meta, h2, dup, *([far] if own else []))


def store_halves(j, n, value, far_ref, keep_ref, send_ref):
    value = (value + far_ref[...].astype(F32)).astype(BF16)

    @pl.when(j < n // 2)
    def _():
        keep_ref[...] = value

    @pl.when(j >= n // 2)
    def _():
        send_ref[...] = value


def down_out_grads(meta, act, dy, attn_t, gb, far=None):
    tokens, width = dy.shape
    half = width // 2
    packs, _, lanes = attn_t.shape
    n = act.shape[1] // 2 // half
    quarter = half // n
    rows = half + quarter
    own = far is not None

    def block_at(j, m):
        return jnp.where(j < n // 2, m[3], 1 - m[3]) * (n // 2) + lax.rem(j, n // 2)

    def body(meta, act_ref, dy_ref, at_ref, gb_ref, *rest):
        j = pl.program_id(0)
        side = meta[2] if own else 1 - meta[2]
        at = pl.ds(pl.multiple_of(side * half + block_at(j, meta) * quarter, quarter), quarter)
        total = jnp.zeros((quarter, width), F32)
        for p in range(packs):
            total = total + mm(at_ref[p, at, :], gb_ref[p * lanes : (p + 1) * lanes, :])
        value = jnp.concatenate([mm(act_ref[...], dy_ref[...], TN), total], axis=0)
        if own:
            store_halves(j, n, value, *rest)
        else:
            rest[0][...] = value.astype(BF16)

    def column(j, m):
        return (m[2] if own else 1 - m[2]) * n + block_at(j, m)

    whole = lambda *shape: pl.BlockSpec(shape, lambda j, m: (0,) * len(shape))
    block = lambda index: pl.BlockSpec((rows, width), index)
    if own:
        out_specs = (
            block(lambda j, m: (jnp.minimum(j, n // 2 - 1), 0)),
            block(lambda j, m: (jnp.maximum(j - n // 2, 0), 0)),
        )
        out_shape = (jax.ShapeDtypeStruct((n // 2 * rows, width), BF16),) * 2
    else:
        out_specs = block(lambda j, m: (j, 0))
        out_shape = jax.ShapeDtypeStruct((n * rows, width), BF16)
    return pl.pallas_call(
        body,
        grid_spec=pltpu.PrefetchScalarGridSpec(
            num_scalar_prefetch=1,
            grid=(n,),
            in_specs=[
                pl.BlockSpec((tokens, half), lambda j, m: (0, column(j, m))),
                whole(tokens, width),
                whole(*attn_t.shape),
                whole(tokens, width),
                *([block(lambda j, m: (j, 0))] if own else []),
            ],
            out_specs=out_specs,
        ),
        out_shape=out_shape,
        compiler_params=params(),
        cost_estimate=cost(0.2),
        name="down_out_gradient",
    )(meta, act, dy, attn_t, gb, *([far] if own else []))


def assemble(meta, downs, ups):
    rows, width = downs[0].shape
    half = width // 2
    quarter = rows - half
    hidden = ups[0].shape[1] * 2

    def body(meta, down_aa, down_ab, down_ba, down_bb, up_a, up_b, down_ref, up_ref, out_ref):
        i = pl.program_id(0)

        def place(ref, value, swapped):
            lo, hi = value[:, :half].astype(F32), value[:, half:].astype(F32)
            ref[:, :half] = jnp.where(swapped == 0, lo, hi)
            ref[:, half:] = jnp.where(swapped == 0, hi, lo)

        down_x, down_y = i // 2 == meta[3], lax.rem(i, 2) == meta[4]
        own_x = jnp.where(down_y, down_aa[...], down_ab[...])
        down = jnp.where(down_x, own_x, jnp.where(down_y, down_ba[...], down_bb[...]))
        place(down_ref, down[:half], meta[5])
        place(out_ref, down[half:], meta[5])
        place(up_ref, jnp.where(i // 2 == meta[4], up_a[...], up_b[...]), meta[3])

    down = pl.BlockSpec((rows, width), lambda i, m: (0, 0))
    up = pl.BlockSpec((half, width), lambda i, m: (0, jnp.bitwise_xor(lax.rem(i, 2), m[5])))
    return pl.pallas_call(
        body,
        grid_spec=pltpu.PrefetchScalarGridSpec(
            num_scalar_prefetch=1,
            grid=(4,),
            in_specs=[down, down, down, down, up, up],
            out_specs=(
                pl.BlockSpec((half, width), lambda i, m: (i, 0)),
                pl.BlockSpec((half, width), lambda i, m: (0, i)),
                pl.BlockSpec((quarter, width), lambda i, m: (i, 0)),
            ),
        ),
        out_shape=(
            jax.ShapeDtypeStruct((4 * half, width), F32),
            jax.ShapeDtypeStruct((half, hidden), F32),
            jax.ShapeDtypeStruct((half, width), F32),
        ),
        compiler_params=params(),
        cost_estimate=cost(7),
        name="weight_gradients",
    )(meta, *downs, *ups)


def finish_body(x_ref, gm_ref, back_ref, g_ref, out_ref):
    hat, inv = norm_rows(x_ref[...].astype(F32))
    e = back_ref[...].astype(F32) * g_ref[...]
    out_ref[...] = gm_ref[...] + inv * (
        e - jnp.mean(e, axis=-1, keepdims=True) - hat * jnp.mean(e * hat, axis=-1, keepdims=True)
    )


def finish(x, gm, back, gain):
    tokens, width = x.shape
    rows = pl.BlockSpec((128, width), lambda i: (i, 0))
    return pl.pallas_call(
        finish_body,
        grid=(tokens // 128,),
        in_specs=[rows, rows, rows, pl.BlockSpec((1, width), lambda i: (0, 0))],
        out_specs=rows,
        out_shape=jax.ShapeDtypeStruct((tokens, width), F32),
        compiler_params=params(),
        cost_estimate=cost(4),
        name="first_norm_backward",
    )(x, gm, back, gain)


def flip(value, axis, mask):
    size = lax.axis_size(axis)
    return lax.ppermute(value, axis, [(i, i ^ mask) for i in range(size)])


def bit(axis, mask):
    return (lax.axis_index(axis) // mask) % 2


def halves(value, which, axis=0):
    n = value.shape[axis] // 2
    keep = lax.dynamic_slice_in_dim(value, which * n, n, axis)
    send = lax.dynamic_slice_in_dim(value, (1 - which) * n, n, axis)
    return keep, send


def join(own, other, which, axis=0):
    return jnp.where(
        which == 0,
        jnp.concatenate([own, other], axis=axis),
        jnp.concatenate([other, own], axis=axis),
    )


def add(a, b):
    return (a.astype(F32) + b.astype(F32)).astype(BF16)


def on_device(
    tokens, lengths, ln1_gain, ln1_bias, qkv_weight, q_gain, k_gain, out_weight,
    ln2_gain, ln2_bias, up_weight, down_weight, cotangent,
):
    micro, rows, local, width = tokens.shape
    n = lax.axis_size("seq")
    length = local * n
    every = micro * rows
    team = n // every
    heads = H // team
    hd = width // H
    half = width // 2
    idx = lax.axis_index("seq")
    core = lax.axis_index("fsdp")
    row, member = idx // team, idx % team
    direct = every == 2 and team == 4
    lengths = lengths.reshape(every, lengths.shape[-1])
    mine = tokens.reshape(every, local, width)

    def swap(value):
        return flip(value, "fsdp", 1)

    vec = jnp.concatenate([ln1_gain, ln1_bias, ln2_gain, ln2_bias, q_gain, k_gain])[None]
    vec_p = swap(vec)
    ordered = jnp.where(core == 0, jnp.concatenate([vec, vec_p]), jnp.concatenate([vec_p, vec])).astype(F32)
    g1, b1, g2, b2 = (ordered[:, k * half : (k + 1) * half].reshape(1, width) for k in range(4))
    gq = ordered[:, 4 * half : 4 * half + hd // 2].reshape(hd, 1)
    gk = ordered[:, 4 * half + hd // 2 :].reshape(hd, 1)

    w_own = lax.dynamic_slice_in_dim(
        qkv_weight.reshape(half, 3, width), member * heads * hd, heads * hd, 2
    ).reshape(half, 3 * heads * hd)
    w_t = jnp.transpose(join(w_own, swap(w_own), core))

    if direct:
        near = lax.dynamic_index_in_dim(mine, row, 0, keepdims=False)
        away = lax.dynamic_index_in_dim(mine, 1 - row, 0, keepdims=False)
        cut = local // 2
        far = flip(away[:cut], "seq", 4), flip(away[cut:], "seq", 4)
        one = flip(near, "seq", 1)
        later, start = lax.optimization_barrier((near, far[0]))
        far = start, far[1]
        two = flip(later, "seq", 2)
        slots = [(near,), (one,), (two,), (flip(two, "seq", 1),)]
        one = tuple(flip(part, "seq", 1) for part in far)
        two = tuple(flip(part, "seq", 2) for part in far)
        three = flip(two[0], "seq", 1), flip(one[1], "seq", 2)
        slots += [far, one, two, three]
        spot = idx
    else:
        same_member = [[q * team + p for q in range(every)] for p in range(team)]
        same_row = [[q * team + p for p in range(team)] for q in range(every)]
        got = lax.all_to_all(mine, "seq", 0, 0, axis_index_groups=same_member, tiled=True)
        got = lax.all_gather(got, "seq", axis_index_groups=same_row)
        whole = jnp.swapaxes(got, 0, 1).reshape(length, width)
        slots = [(whole[s * (length // 8) : (s + 1) * (length // 8)],) for s in range(8)]
        spot = jnp.int32(0)
    meta = jnp.stack([spot, row, core, bit("rep", 1), bit("seq", 1), bit("seq", 2)]).astype(jnp.int32)

    out_p, up_p, down_p = swap(out_weight), swap(up_weight), swap(down_weight)

    with jax.named_scope("forward_attention"):
        qt, ka, kt, v, vt, x_row = make_qkv(meta, lengths, slots, w_t, g1, b1, gq, gk, heads, hd)
        attn, attn_f, logsum = attend(meta, lengths, qt, ka, vt, heads, hd)

    def exchange(value):
        return lax.all_to_all(value, "seq", 0, 0, tiled=True)

    packs = every * local // BLK
    if direct:
        attn_t = exchange(attn).reshape(packs, width, BLK)
    else:
        cut = jnp.moveaxis(attn.reshape(BLK * 0 + 8, heads * hd, BLK // local, local), 2, 1)
        got = exchange(cut.reshape(n, heads * hd, local))
        got = got.reshape(packs, every // packs, width, local)
        attn_t = jnp.swapaxes(got, 1, 2).reshape(packs, width, BLK)

    total = jnp.sum(lengths[:, :-1], axis=-1)
    places = idx * local + jnp.arange(local, dtype=jnp.int32)
    valid = (places[None] < total[:, None]).astype(F32).reshape(packs, 1, BLK)
    x_home = tokens.reshape(every * local, width)
    dy = cotangent.reshape(every * local, width)

    with jax.named_scope("feed_forward"):
        output, grad_mid, grad_branch, h2, act, dup, grad_attn, vec2 = ffn(
            meta, attn_t, x_home, dy, valid, g2, b2, out_weight, out_p, up_weight, up_p, down_weight, down_p
        )
    if direct:
        grad_o = exchange(grad_attn.reshape(n, heads * hd, BLK))
    else:
        cut = jnp.swapaxes(grad_attn.reshape(packs, width, every // packs, local), 1, 2)
        got = exchange(cut.reshape(n, heads * hd, local))
        got = got.reshape(8, BLK // local, heads * hd, local)
        grad_o = jnp.swapaxes(got, 1, 2).reshape(8, heads * hd, BLK)

    masks = [1 << k for k in range(n.bit_length() - 1)]
    x, y, z = ("rep", 1), ("seq", 1), ("seq", 2)

    def next_half(keep, got, way, axis):
        return halves(add(keep, got), bit(*way), axis)

    tie = lambda *values: lax.optimization_barrier(values)
    with jax.named_scope("weight_gradients"):
        far_d = swap(down_out_grads(meta, act, dy, attn_t, grad_branch))
        far_u = swap(up_grads(meta, h2, dup))
        down_k, down_s = down_out_grads(meta, act, dy, attn_t, grad_branch, far_d)
        up_k, up_s = up_grads(meta, h2, dup, far_u)
        got = flip(down_s, *x), flip(up_s, *y)
    grad_o = tie(grad_o, up_k, up_s, down_k, down_s)[0]
    go_back = lambda go, before: attend_back(
        meta, lengths, qt, ka, kt, v, attn_f, logsum, go, heads, hd, before
    )
    with jax.named_scope("backward_attention"):
        parts = go_back(grad_o, None)
    parts, *got = tie(parts, *got)
    with jax.named_scope("weight_gradients"):
        down_k, down_s = next_half(down_k, got[0], y, 0)
        up_k, up_s = next_half(up_k, got[1], z, 1)
        got = flip(down_s, *y), flip(up_s, *z)
    with jax.named_scope("backward_attention"):
        parts = go_back(grad_o, parts)
    parts, *got = tie(parts, *got)
    with jax.named_scope("weight_gradients"):
        down_k, down_s = next_half(down_k, got[0], z, 1)
        up_k, up_s = next_half(up_k, got[1], x, 1)
        got = flip(down_s, *z), flip(up_s, *x)
    parts, *got = tie(parts, *got)
    with jax.named_scope("weight_gradients"):
        down, up = add(down_k, got[0]), add(up_k, got[1])
        pieces = jnp.concatenate([down, up])
        for mask in masks[2:]:
            pieces = add(pieces, flip(pieces, "seq", mask))
    with jax.named_scope("backward_attention"):
        dq, dk, dv = parts
        back_a, back_b, dw_t = qkv_back(meta, x_row, dq, dk, dv, w_t, g1, b1, gq, gk, vec2, heads, hd)
    dw_t, pieces = tie(dw_t, pieces)
    down, up = jnp.split(pieces, [down.shape[0]])

    with jax.named_scope("first_round"):
        keep, send = halves(dw_t, core, 1)
        q_keep, q_send = next_half(keep, swap(send), x, 0)
        got = [flip(down, *z), flip(up, *x), flip(q_send, *x)]
        if direct:
            a = back_a.reshape(2, 2, 2, local, half)
            b = back_b.reshape(2, 2, 2, local, half)
            got += [flip(a[:, :, 1], *y), flip(b[:, 1], *z)]
        got = tie(*got)
        down = jnp.concatenate([down, got[0]], axis=1)
        up = jnp.concatenate([up, got[1]], axis=1)
        piece = add(q_keep, got[2])
        if direct:
            a, b = add(a[:, :, 0], got[3]), add(b[:, 0], got[4])
    with jax.named_scope("second_round"):
        rows_at = [mask for mask in masks if mask >= team]
        got = [flip(down, *y), flip(down, *x), flip(up, *z)]
        got += [flip(piece, "seq", mask) for mask in rows_at[:1]]
        if direct:
            got += [flip(a[:, 1], *z), flip(b[:, 1], *y)]
        got = tie(*got)
        downs = [down, got[0], got[1]]
        up = jnp.concatenate([up, got[2]], axis=1)
        if rows_at:
            piece = add(piece, got[3])
        for mask in rows_at[1:]:
            piece = add(piece, flip(piece, "seq", mask))
        if direct:
            a, b = add(a[:, 0], got[-2]), add(b[:, 0], got[-1])
    with jax.named_scope("third_round"):
        piece_y, up = tie(flip(piece, *y), up)
        piece = jnp.stack([piece, piece_y])
        if direct:
            mixed = jnp.concatenate([a, b], axis=-1)
            near, far = mixed[0], flip(mixed[1], "seq", 4)
            back = jnp.where(row == 0, jnp.stack([near, far]), jnp.stack([far, near])).reshape(every * local, width)
        else:
            whole = jnp.concatenate([back_a, back_b], axis=-1).reshape(every, team, local, width)
            whole = lax.psum_scatter(whole, "seq", scatter_dimension=1, axis_index_groups=same_row, tiled=True)
            back = lax.all_to_all(
                whole[:, 0], "seq", 0, 0, axis_index_groups=same_member, tiled=True
            ).reshape(every * local, width)
        downs.append(flip(downs[1], *x))
        piece_z = flip(piece, *z)
        pieces = [piece, piece_z, flip(piece, *x), flip(piece_z, *x)]
        ups = (up, flip(up, *y))
    grad_tokens = finish(x_home, grad_mid, back, g1)
    grad_qkv, small = assemble_qkv(meta, pieces, heads, hd)
    grad_down, grad_up, grad_out = assemble(meta, downs, ups)
    cuts = [small[k] for k in range(4)] + [small[4, : hd // 2], small[5, : hd // 2]]
    shape = tokens.shape
    return (
        output.reshape(shape), grad_tokens.reshape(shape), cuts[0], cuts[1], grad_qkv, cuts[4], cuts[5],
        grad_out, cuts[2], cuts[3], grad_up, grad_down,
    )


def solution(mesh):
    tok = P(None, ("rep", "fsdp"), "seq", None)
    one, two = P("fsdp"), P("fsdp", None)
    in_specs = (tok, P(None, ("rep", "fsdp"), None), one, one, two, one, one, two, one, one, two, two, tok)
    out_specs = (tok, tok, one, one, two, one, one, two, one, one, two, two)
    return jax.shard_map(on_device, mesh=mesh, in_specs=in_specs, out_specs=out_specs, check_vma=False)
```

```python
import functools

import jax
import jax.numpy as jnp
from jax import lax
from jax.experimental import pallas as pl
from jax.experimental.pallas import tpu as pltpu
from jax.sharding import PartitionSpec as P

H = 12
EPS = 1e-06
LOG2E = 1.4426950408889634
SHIFT = 512.0
BLK = 256
EXTRA = 32
NN = (((1,), (0,)), ((), ()))
NT = (((1,), (1,)), ((), ()))
TN = (((0,), (0,)), ((), ()))
F32 = jnp.float32
BF16 = jnp.bfloat16


def mm(a, b, dims=NN):
    return lax.dot_general(a, b, dims, preferred_element_type=F32)


def params(**kw):
    return pltpu.CompilerParams(vmem_limit_bytes=60 * 1024 * 1024, **kw)


def cost(us):
    return pl.CostEstimate(flops=int(us * 0.35e9), bytes_accessed=1024, transcendentals=0)


def norm_rows(v):
    center = jnp.mean(v, axis=-1, keepdims=True)
    centred = v - center
    inv = lax.rsqrt(jnp.mean(centred * centred, axis=-1, keepdims=True) + EPS)
    return centred * inv, inv


def norm_cols(v):
    center = jnp.mean(v, axis=0, keepdims=True)
    centred = v - center
    inv = lax.rsqrt(jnp.mean(centred * centred, axis=0, keepdims=True) + EPS)
    return centred * inv, inv


def bounds_of(len_ref, row):
    out = []
    total = jnp.int32(0)
    for j in range(len_ref.shape[1] - 1):
        total = total + len_ref[row, j]
        out.append(total)
    return out


def qkv_body(heads, hd, cuts, meta, len_ref, *refs):
    xs = []
    for count in cuts:
        xs.append(refs[:count])
        refs = refs[count:]
    w_ref, g_ref, b_ref, gq_ref, gk_ref = refs[:5]
    qt_ref, ka_ref, kt_ref, v_ref, vt_ref, x_ref = refs[5:]
    wid = heads * hd
    spot, row = meta[0], meta[1]
    bounds = bounds_of(len_ref, row)
    for s in range(8):
        c = jnp.bitwise_xor(spot, s)
        cols = pl.ds(pl.multiple_of(c * BLK, BLK), BLK)
        x = jnp.concatenate([ref[...] for ref in xs[s]], axis=0) if len(xs[s]) > 1 else xs[s][0][...]
        x_ref[cols, :] = x
        hat, _ = norm_rows(x.astype(F32))
        first = (hat * g_ref[...] + b_ref[...]).astype(BF16)
        qkv = mm(w_ref[...], first, NT)
        place = c * BLK + lax.broadcasted_iota(jnp.int32, (8, BLK), 1)
        ident = jnp.zeros((8, BLK), jnp.int32)
        place_k = c * BLK + lax.broadcasted_iota(jnp.int32, (BLK, 128), 0)
        ident_k = jnp.zeros((BLK, 128), jnp.int32)
        for bound in bounds:
            ident = ident + (place >= bound).astype(jnp.int32)
            ident_k = ident_k + (place_k >= bound).astype(jnp.int32)
        which = lax.broadcasted_iota(jnp.int32, (8, BLK), 0)
        hot = jnp.where((ident == which) & (which < len(bounds)), 16.0, 0.0)
        hot = jnp.concatenate([hot, jnp.zeros((hd - 8, BLK), F32)], axis=0)
        lane = lax.broadcasted_iota(jnp.int32, (BLK, 128), 1) - hd
        hot_k = jnp.where((ident_k == lane) & (lane < len(bounds)), SHIFT / 16.0, 0.0)
        for h in range(heads):
            q, _ = norm_cols(qkv[h * hd : (h + 1) * hd])
            k, _ = norm_cols(qkv[wid + h * hd : wid + (h + 1) * hd])
            q = (q * gq_ref[...]).astype(BF16).astype(F32) * (hd**-0.5)
            k = k * gk_ref[...]
            v = qkv[2 * wid + h * hd : 2 * wid + (h + 1) * hd]
            qt_ref[h, :, cols] = jnp.concatenate([q, hot], axis=0).astype(BF16)
            kt_ref[h, :, cols] = k.astype(BF16)
            vt_ref[h, :, cols] = v.astype(BF16)
            both = jnp.transpose(jnp.concatenate([k, v], axis=0))
            ka_ref[h, cols, :] = jnp.where(lane < 0, both, hot_k).astype(BF16)
            v_ref[h, cols, :] = both[:, hd:].astype(BF16)


def make_qkv(meta, lengths, slots, w_t, gain, bias, gq, gk, heads, hd):
    length = 8 * sum(one.shape[0] for one in slots[0])
    width = slots[0][0].shape[1]
    cuts = tuple(len(one) for one in slots)
    smem = pl.BlockSpec(memory_space=pltpu.SMEM)
    vmem = pl.BlockSpec(memory_space=pltpu.VMEM)
    return pl.pallas_call(
        functools.partial(qkv_body, heads, hd, cuts),
        out_shape=(
            jax.ShapeDtypeStruct((heads, 2 * hd, length), BF16),
            jax.ShapeDtypeStruct((heads, length, 2 * hd), BF16),
            jax.ShapeDtypeStruct((heads, hd, length), BF16),
            jax.ShapeDtypeStruct((heads, length, hd), BF16),
            jax.ShapeDtypeStruct((heads, hd, length), BF16),
            jax.ShapeDtypeStruct((length, width), BF16),
        ),
        in_specs=[smem, smem] + [vmem] * (sum(cuts) + 5),
        out_specs=(vmem,) * 6,
        compiler_params=params(),
        cost_estimate=cost(12),
        name="qkv_forward",
    )(meta, lengths, *sum(slots, ()), w_t, gain, bias, gq, gk)


def block_range(bounds, i):
    first = i * BLK
    last = first + BLK - 1
    lo = jnp.int32(0)
    hi = bounds[-1]
    for bound in bounds:
        lo = jnp.where(first >= bound, bound, lo)
    for bound in bounds[::-1]:
        hi = jnp.where(last < bound, bound, hi)
    lo_b = lo // BLK
    hi_b = (hi + BLK - 1) // BLK
    return lo_b, jnp.where(first >= bounds[-1], lo_b, hi_b)


def in_pairs(lo, hi, step, carry):
    pairs = (hi - lo) // 2
    carry = lax.fori_loop(0, pairs, lambda k, c: step([lo + 2 * k, lo + 2 * k + 1], c), carry)
    return lax.fori_loop(lo + 2 * pairs, hi, lambda b, c: step([b], c), carry)


def attend_body(heads, hd, meta, len_ref, qt_ref, ka_ref, vt_ref, o_ref, of_ref, ls_ref):
    i = pl.program_id(0)
    bounds = bounds_of(len_ref, meta[1])
    lo, hi = block_range(bounds, i)

    def step(blocks, carry):
        rows = [pl.ds(pl.multiple_of(b * BLK, BLK), BLK) for b in blocks]
        items = [(h, r) for r in rows for h in range(heads)]
        scores = [mm(ka_ref[h, r, :], qt_ref[h]) for h, r in items]
        expos = [jnp.exp2(one * LOG2E - SHIFT * LOG2E) for one in scores]
        out = list(carry)
        for expo, (h, r) in zip(expos, items):
            acc, total = out[h]
            total = total + jnp.sum(expo.reshape(BLK // 8, 8, BLK), axis=0)
            out[h] = (acc + mm(vt_ref[h, :, r], expo.astype(BF16)), total)
        return tuple(out)

    init = tuple((jnp.zeros((hd, BLK), F32), jnp.zeros((8, BLK), F32)) for _ in range(heads))
    done = in_pairs(lo, hi, step, init)
    for h in range(heads):
        acc, total = done[h]
        total = jnp.sum(total, axis=0, keepdims=True)
        live = total > 0.0
        safe = jnp.where(live, total, 1.0)
        out = jnp.where(live, acc * (1.0 / safe), 0.0)
        o_ref[0, h * hd : (h + 1) * hd, :] = out.astype(BF16)
        of_ref[h] = out
        ls_ref[h] = jnp.log2(safe) + SHIFT * LOG2E


def attend(meta, lengths, qt, ka, vt, heads, hd):
    length = qt.shape[2]
    blocks = length // BLK
    smem = pl.BlockSpec(memory_space=pltpu.SMEM)
    return pl.pallas_call(
        functools.partial(attend_body, heads, hd),
        grid=(blocks,),
        out_shape=(
            jax.ShapeDtypeStruct((blocks, heads * hd, BLK), BF16),
            jax.ShapeDtypeStruct((heads, hd, length), F32),
            jax.ShapeDtypeStruct((heads, 1, length), F32),
        ),
        in_specs=[
            smem,
            smem,
            pl.BlockSpec((heads, 2 * hd, BLK), lambda i: (0, 0, i)),
            pl.BlockSpec((heads, length, 2 * hd), lambda i: (0, 0, 0)),
            pl.BlockSpec((heads, hd, length), lambda i: (0, 0, 0)),
        ],
        out_specs=(
            pl.BlockSpec((1, heads * hd, BLK), lambda i: (i, 0, 0)),
            pl.BlockSpec((heads, hd, BLK), lambda i: (0, 0, i)),
            pl.BlockSpec((heads, 1, BLK), lambda i: (0, 0, i)),
        ),
        compiler_params=params(),
        cost_estimate=cost(25),
        name="attention_forward",
    )(meta, lengths, qt, ka, vt)


def attend_back_body(first, heads, hd, meta, len_ref, *refs):
    qt_ref, ka_ref, kt_ref, v_ref, of_ref, ls_ref, go_ref = refs[:7]
    dq_ref, dk_ref, dv_ref = refs[-3:]
    i = pl.program_id(0)
    bounds = bounds_of(len_ref, meta[1])
    lo, hi = block_range(bounds, i + first)

    @pl.when(i == 0)
    def _():
        if first:
            dk_ref[...] = refs[8][...]
            dv_ref[...] = refs[9][...]
        else:
            dk_ref[...] = jnp.zeros_like(dk_ref)
            dv_ref[...] = jnp.zeros_like(dv_ref)

    inner = []
    for h in range(heads):
        go = go_ref[0, h * hd : (h + 1) * hd, :].astype(F32)
        inner.append(jnp.sum(go * of_ref[h], axis=0, keepdims=True))

    def step(blocks, carry):
        rows = [pl.ds(pl.multiple_of(b * BLK, BLK), BLK) for b in blocks]
        items = [(h, r) for r in rows for h in range(heads)]
        gos = [go_ref[0, h * hd : (h + 1) * hd, :] for h in range(heads)]
        scores = [mm(ka_ref[h, r, :], qt_ref[h]) for h, r in items]
        grad_probs = [mm(v_ref[h, r, :], gos[h]) for h, r in items]
        probs = [jnp.exp2(one * LOG2E - ls_ref[h]) for one, (h, _) in zip(scores, items)]
        grads = [(p * (g - inner[h])).astype(BF16) for p, g, (h, _) in zip(probs, grad_probs, items)]
        out = list(carry)
        for p, g, (h, r) in zip(probs, grads, items):
            dv_ref[h, :, r] += mm(gos[h], p.astype(BF16), NT)
            dk_ref[h, :, r] += mm(qt_ref[h][:hd], g, NT)
            out[h] = out[h] + mm(kt_ref[h, :, r], g)
        return tuple(out)

    done = in_pairs(lo, hi, step, tuple(jnp.zeros((hd, BLK), F32) for _ in range(heads)))
    for h in range(heads):
        dq_ref[h] = done[h] * (hd**-0.5)


def attend_back(meta, lengths, qt, ka, kt, v, of, ls, go, heads, hd, before=None):
    length = qt.shape[2]
    count = length // BLK // 2
    first = count if before else 0
    smem = pl.BlockSpec(memory_space=pltpu.SMEM)
    whole = lambda *shape: pl.BlockSpec(shape, lambda i: (0, 0, 0))
    part = lambda *shape: pl.BlockSpec(shape, lambda i: (0, 0, first + i))
    more = [pl.BlockSpec(memory_space=pl.ANY), whole(heads, hd, length), whole(heads, hd, length)]
    return pl.pallas_call(
        functools.partial(attend_back_body, first, heads, hd),
        grid=(count,),
        out_shape=tuple(jax.ShapeDtypeStruct((heads, hd, length), F32) for _ in range(3)),
        in_specs=[
            smem,
            smem,
            part(heads, 2 * hd, BLK),
            whole(heads, length, 2 * hd),
            whole(heads, hd, length),
            whole(heads, length, hd),
            part(heads, hd, BLK),
            part(heads, 1, BLK),
            pl.BlockSpec((1, heads * hd, BLK), lambda i: (first + i, 0, 0)),
            *(more if before else []),
        ],
        out_specs=(part(heads, hd, BLK), whole(heads, hd, length), whole(heads, hd, length)),
        input_output_aliases={9: 0} if before else {},
        compiler_params=params(),
        cost_estimate=cost(15),
        name="attention_backward",
    )(meta, lengths, qt, ka, kt, v, of, ls, go, *(before or ()))


def qkv_back_body(
    heads, hd, meta, x_ref, *refs
):
    dq_ref, dk_ref, dv_ref, w_ref, g_ref, b_ref, gq_ref, gk_ref, vec2_ref = refs[:9]
    da_ref, db_ref, dw_ref, acc_ref, vec_ref, gain_ref = refs[9:]
    i = pl.program_id(0)
    wid = heads * hd

    @pl.when(i == 0)
    def _():
        acc_ref[...] = jnp.zeros_like(acc_ref)
        vec_ref[...] = jnp.zeros_like(vec_ref)
        gain_ref[...] = jnp.zeros_like(gain_ref)

    hat, _ = norm_rows(x_ref[...].astype(F32))
    first = (hat * g_ref[...] + b_ref[...]).astype(BF16)
    qk = mm(w_ref[: 2 * wid, :], first, NT)
    pieces = []
    for at, gain, grad in ((0, gq_ref, dq_ref), (1, gk_ref, dk_ref)):
        for h in range(heads):
            unit, inv = norm_cols(qk[at * wid + h * hd : at * wid + (h + 1) * hd])
            gy = grad[h]
            gain_ref[at] += gy * unit
            e = gy * gain[...]
            pieces.append(
                inv
                * (
                    e
                    - jnp.mean(e, axis=0, keepdims=True)
                    - unit * jnp.mean(e * unit, axis=0, keepdims=True)
                )
            )
    for h in range(heads):
        pieces.append(dv_ref[h])
    grad = jnp.concatenate(pieces, axis=0).astype(BF16)
    acc_ref[...] += mm(grad, first)
    back = mm(grad, w_ref[...], TN)
    vec_ref[0] += jnp.sum((back * hat).reshape(BLK // 8, 8, -1), axis=0)
    vec_ref[1] += jnp.sum(back.reshape(BLK // 8, 8, -1), axis=0)
    half = back.shape[1] // 2
    da_ref[0] = back[:, :half].astype(BF16)
    db_ref[0] = back[:, half:].astype(BF16)

    @pl.when(i == pl.num_programs(0) - 1)
    def _():
        dw_ref[: 3 * wid, :] = acc_ref[...].astype(BF16)
        lines = [jnp.sum(ref[k], axis=0, keepdims=True) for ref in (vec_ref, vec2_ref) for k in range(2)]
        width = dw_ref.shape[1]
        lane = lax.broadcasted_iota(jnp.int32, (hd, width), 1)
        item = lax.broadcasted_iota(jnp.int32, (hd, width), 0)
        spread = jnp.where(item < hd // 2, item, item - hd // 2 + width // 2)
        for k in range(2):
            total = lax.dot_general(
                jnp.ones((8, BLK), F32), gain_ref[k], NT, precision=lax.Precision.HIGHEST, preferred_element_type=F32
            )
            pick = (lane == spread).astype(F32)
            line = lax.dot_general(total, pick, NN, precision=lax.Precision.HIGHEST, preferred_element_type=F32)
            lines.append(line[:1])
        place = lax.broadcasted_iota(jnp.int32, (EXTRA, width), 0)
        below = jnp.zeros((EXTRA, width), F32)
        for k, one in enumerate(lines):
            below = jnp.where(place == k, one, below)
        dw_ref[3 * wid :, :] = below.astype(BF16)


def qkv_back(meta, x, dq, dk, dv, w_t, gain, bias, gq, gk, vec2, heads, hd):
    length, width = x.shape
    blocks = length // BLK
    whole = lambda *shape: pl.BlockSpec(shape, lambda i, m: (0,) * len(shape))
    part = pl.BlockSpec((heads, hd, BLK), lambda i, m: (0, 0, i))
    grads = pl.BlockSpec((1, BLK, width // 2), lambda i, m: (jnp.bitwise_xor(i, m[0]), 0, 0))
    return pl.pallas_call(
        functools.partial(qkv_back_body, heads, hd),
        grid_spec=pltpu.PrefetchScalarGridSpec(
            num_scalar_prefetch=1,
            grid=(blocks,),
            in_specs=[
                pl.BlockSpec((BLK, width), lambda i, m: (i, 0)),
                part,
                part,
                part,
                whole(*w_t.shape),
                whole(1, width),
                whole(1, width),
                whole(hd, 1),
                whole(hd, 1),
                whole(2, 8, width),
            ],
            out_specs=(
                grads,
                grads,
                whole(w_t.shape[0] + EXTRA, width),
            ),
            scratch_shapes=[
                pltpu.VMEM(w_t.shape, F32),
                pltpu.VMEM((2, 8, width), F32),
                pltpu.VMEM((2, hd, BLK), F32),
            ],
        ),
        out_shape=(
            jax.ShapeDtypeStruct((blocks, BLK, width // 2), BF16),
            jax.ShapeDtypeStruct((blocks, BLK, width // 2), BF16),
            jax.ShapeDtypeStruct((w_t.shape[0] + EXTRA, width), BF16),
        ),
        compiler_params=params(),
        cost_estimate=cost(17),
        name="qkv_backward",
    )(meta, x, dq, dk, dv, w_t, gain, bias, gq, gk, vec2)


def assemble_qkv(meta, pieces, heads, hd):
    _, part, half = pieces[0].shape
    team = 4
    wid = heads * hd
    turned = team * wid

    def body(meta, p00, p01, p10, p11, out_ref, vec_ref, all_s):
        t = pl.program_id(0)

        @pl.when(t == 0)
        def _():
            for y in range(2):
                at = jnp.bitwise_xor(meta[4], y)
                for z in range(2):
                    own_z = meta[5] == z
                    near, away = jnp.where(own_z, p00[at], p01[at]), jnp.where(own_z, p10[at], p11[at])
                    for x in range(2):
                        all_s[2 * z + y, x * part : (x + 1) * part, :] = jnp.where(meta[3] == x, near, away)
            total = jnp.zeros((EXTRA, half), F32)
            for p in range(team):
                total = total + all_s[p, 3 * wid :, :].astype(F32)
            vec_ref[...] = total

        rows = pl.ds(pl.multiple_of(t * wid, wid), wid)
        piece = jnp.concatenate([all_s[p, rows, :] for p in range(team)], axis=0)
        out_ref[...] = jnp.transpose(piece.astype(F32))

    whole = lambda *shape: pl.BlockSpec(shape, lambda i, m: (0,) * len(shape))
    return pl.pallas_call(
        body,
        grid_spec=pltpu.PrefetchScalarGridSpec(
            num_scalar_prefetch=1,
            grid=(3,),
            in_specs=[whole(2, part, half)] * 4,
            out_specs=(pl.BlockSpec((half, turned), lambda i, m: (0, i)), whole(EXTRA, half)),
            scratch_shapes=[pltpu.VMEM((team, 2 * part, half), BF16)],
        ),
        out_shape=(jax.ShapeDtypeStruct((half, 3 * turned), F32), jax.ShapeDtypeStruct((EXTRA, half), F32)),
        compiler_params=params(),
        cost_estimate=cost(5),
        name="first_projection_gradient",
    )(meta, *pieces)


def gelu_pair(u):
    a = jnp.abs(u)
    t = 1.0 / (1.0 + (0.3275911 * 0.7071067811865476) * a)
    poly = 1.061405429 * t - 1.453152027
    poly = poly * t + 1.421413741
    poly = poly * t - 0.284496736
    poly = poly * t + 0.254829592
    bell = jnp.exp(-0.5 * (u * u))
    tail = (0.5 * poly) * t * bell
    cdf = jnp.where(u >= 0.0, 1.0 - tail, tail)
    return u * cdf, cdf + u * (bell * 0.3989422804014327)


def ffn(meta, attn_t, x, dy, valid, gain, bias, wo, wo_p, up, up_p, dn, dn_p):
    tokens, width = x.shape
    hidden = up.shape[1]
    fc = 512
    steps = hidden // fc
    near = steps // 2
    packs, _, lanes = attn_t.shape
    whole = lambda *shape: pl.BlockSpec(shape, lambda i, m: (0,) * len(shape))
    ups = pl.BlockSpec((width // 2, fc), lambda i, m: (0, lax.rem(m[2] * near + i, steps)))
    acts = pl.BlockSpec((tokens, fc), lambda i, m: (0, lax.rem(m[2] * near + i, steps)))
    half = width // 2

    def body(meta, *refs):
        (at_ref, x_ref, dy_ref, valid_ref, g_ref, b_ref, wo_own, wo_peer, up_own, up_peer, dn_own, dn_peer) = refs[:12]
        (out_ref, gm_ref, gb_ref, h2_ref, act_ref, dup_ref, da_ref, vec_ref) = refs[12:20]
        (mid_s, acc_s, own_s, peer_s, gown_s, gpeer_s) = refs[20:]
        i = pl.program_id(0)
        core = meta[2]
        zero = core == 0

        @pl.when(i == 0)
        def _():
            for p in range(packs):
                rows = pl.ds(p * lanes, lanes)
                own = at_ref[p, pl.ds(pl.multiple_of(core * half, half), half), :]
                peer = at_ref[p, pl.ds(pl.multiple_of((1 - core) * half, half), half), :]
                mid = x_ref[rows, :].astype(F32) + mm(own, wo_own[...], TN) + mm(peer, wo_peer[...], TN)
                mid_s[rows, :] = mid
                acc_s[rows, :] = mid
                hat, _ = norm_rows(mid)
                second = (hat * g_ref[...] + b_ref[...]).astype(BF16)
                h2_ref[:, rows] = jnp.transpose(hat * g_ref[...] + b_ref[...]).astype(BF16)
                lo, hi = second[:, :half], second[:, half:]
                own_s[rows, :] = jnp.where(zero, lo, hi)
                peer_s[rows, :] = jnp.where(zero, hi, lo)
            gown_s[...] = jnp.zeros_like(gown_s)
            gpeer_s[...] = jnp.zeros_like(gpeer_s)

        down = jnp.where(i < near, dn_own[...], dn_peer[...])
        upper = mm(own_s[...], up_own[...]) + mm(peer_s[...], up_peer[...])
        act, slope = gelu_pair(upper)
        act = act.astype(BF16)
        grad = (mm(dy_ref[...], down, NT) * slope).astype(BF16)
        act_ref[...] = act
        dup_ref[...] = grad
        acc_s[...] += mm(act, down)
        gown_s[...] += mm(grad, up_own[...], NT)
        gpeer_s[...] += mm(grad, up_peer[...], NT)

        @pl.when(i == steps - 1)
        def _():
            out_ref[...] = acc_s[...].astype(BF16)
            vec = [jnp.zeros((8, width), F32), jnp.zeros((8, width), F32)]
            for p in range(packs):
                rows = pl.ds(p * lanes, lanes)
                hat, inv = norm_rows(mid_s[rows, :])
                a, b = gown_s[rows, :], gpeer_s[rows, :]
                gy = jnp.concatenate([jnp.where(zero, a, b), jnp.where(zero, b, a)], axis=1)
                vec[0] = vec[0] + jnp.sum((gy * hat).reshape(lanes // 8, 8, width), axis=0)
                vec[1] = vec[1] + jnp.sum(gy.reshape(lanes // 8, 8, width), axis=0)
                e = gy * g_ref[...]
                gm = dy_ref[rows, :].astype(F32) + inv * (
                    e
                    - jnp.mean(e, axis=-1, keepdims=True)
                    - hat * jnp.mean(e * hat, axis=-1, keepdims=True)
                )
                gm_ref[rows, :] = gm
                gb = gm.astype(BF16)
                gb_ref[rows, :] = gb
                ok = valid_ref[p]
                da_ref[p, pl.ds(pl.multiple_of(core * half, half), half), :] = (
                    mm(wo_own[...], gb, NT) * ok
                ).astype(BF16)
                da_ref[p, pl.ds(pl.multiple_of((1 - core) * half, half), half), :] = (
                    mm(wo_peer[...], gb, NT) * ok
                ).astype(BF16)
            vec_ref[0] = vec[0]
            vec_ref[1] = vec[1]

    return pl.pallas_call(
        body,
        grid_spec=pltpu.PrefetchScalarGridSpec(
            num_scalar_prefetch=1,
            grid=(steps,),
            in_specs=[
                whole(*attn_t.shape),
                whole(tokens, width),
                whole(tokens, width),
                whole(*valid.shape),
                whole(1, width),
                whole(1, width),
                whole(half, width),
                whole(half, width),
                ups,
                ups,
                pl.BlockSpec((fc, width), lambda i, m: (jnp.minimum(i, near - 1), 0)),
                pl.BlockSpec((fc, width), lambda i, m: (jnp.maximum(i - near, 0), 0)),
            ],
            out_specs=(
                whole(tokens, width),
                whole(tokens, width),
                whole(tokens, width),
                whole(width, tokens),
                acts,
                acts,
                whole(*attn_t.shape),
                whole(2, 8, width),
            ),
            scratch_shapes=[
                pltpu.VMEM((tokens, width), F32),
                pltpu.VMEM((tokens, width), F32),
                pltpu.VMEM((tokens, half), BF16),
                pltpu.VMEM((tokens, half), BF16),
                pltpu.VMEM((tokens, half), F32),
                pltpu.VMEM((tokens, half), F32),
            ],
        ),
        out_shape=(
            jax.ShapeDtypeStruct((tokens, width), BF16),
            jax.ShapeDtypeStruct((tokens, width), F32),
            jax.ShapeDtypeStruct((tokens, width), BF16),
            jax.ShapeDtypeStruct((width, tokens), BF16),
            jax.ShapeDtypeStruct((tokens, hidden), BF16),
            jax.ShapeDtypeStruct((tokens, hidden), BF16),
            jax.ShapeDtypeStruct(attn_t.shape, BF16),
            jax.ShapeDtypeStruct((2, 8, width), F32),
        ),
        compiler_params=params(),
        cost_estimate=cost(25),
        name="ffn_both_ways",
    )(meta, attn_t, x, dy, valid, gain, bias, wo, wo_p, up, up_p, dn, dn_p)


def up_grads(meta, h2, dup, far=None):
    width, tokens = h2.shape
    hidden = dup.shape[1]
    half = width // 2
    n = hidden // width
    own = far is not None

    def body(meta, h2_ref, dup_ref, *rest):
        j = pl.program_id(0)
        side = meta[2] if own else 1 - meta[2]
        value = mm(h2_ref[pl.ds(pl.multiple_of(side * half, half), half), :], dup_ref[...])
        if own:
            store_halves(j, n, value, *rest)
        else:
            rest[0][...] = value.astype(BF16)

    def column(j, m):
        return jnp.where(j < n // 2, m[4], 1 - m[4]) * (n // 2) + lax.rem(j, n // 2)

    block = lambda index: pl.BlockSpec((half, width), index)
    if own:
        out_specs = (
            block(lambda j, m: (0, jnp.minimum(j, n // 2 - 1))),
            block(lambda j, m: (0, jnp.maximum(j - n // 2, 0))),
        )
        out_shape = (jax.ShapeDtypeStruct((half, hidden // 2), BF16),) * 2
    else:
        out_specs = block(lambda j, m: (0, j))
        out_shape = jax.ShapeDtypeStruct((half, hidden), BF16)
    return pl.pallas_call(
        body,
        grid_spec=pltpu.PrefetchScalarGridSpec(
            num_scalar_prefetch=1,
            grid=(n,),
            in_specs=[
                pl.BlockSpec((width, tokens), lambda j, m: (0, 0)),
                pl.BlockSpec((tokens, width), lambda j, m: (0, column(j, m))),
                *([block(lambda j, m: (0, j))] if own else []),
            ],
            out_specs=out_specs,
        ),
        out_shape=out_shape,
        compiler_params=params(),
        cost_estimate=cost(0.2),
        name="up_gradient",
    )(meta, h2, dup, *([far] if own else []))


def store_halves(j, n, value, far_ref, keep_ref, send_ref):
    value = (value + far_ref[...].astype(F32)).astype(BF16)

    @pl.when(j < n // 2)
    def _():
        keep_ref[...] = value

    @pl.when(j >= n // 2)
    def _():
        send_ref[...] = value


def down_out_grads(meta, act, dy, attn_t, gb, far=None):
    tokens, width = dy.shape
    half = width // 2
    packs, _, lanes = attn_t.shape
    n = act.shape[1] // 2 // half
    quarter = half // n
    rows = half + quarter
    own = far is not None

    def block_at(j, m):
        return jnp.where(j < n // 2, m[3], 1 - m[3]) * (n // 2) + lax.rem(j, n // 2)

    def body(meta, act_ref, dy_ref, at_ref, gb_ref, *rest):
        j = pl.program_id(0)
        side = meta[2] if own else 1 - meta[2]
        at = pl.ds(pl.multiple_of(side * half + block_at(j, meta) * quarter, quarter), quarter)
        total = jnp.zeros((quarter, width), F32)
        for p in range(packs):
            total = total + mm(at_ref[p, at, :], gb_ref[p * lanes : (p + 1) * lanes, :])
        value = jnp.concatenate([mm(act_ref[...], dy_ref[...], TN), total], axis=0)
        if own:
            store_halves(j, n, value, *rest)
        else:
            rest[0][...] = value.astype(BF16)

    def column(j, m):
        return (m[2] if own else 1 - m[2]) * n + block_at(j, m)

    whole = lambda *shape: pl.BlockSpec(shape, lambda j, m: (0,) * len(shape))
    block = lambda index: pl.BlockSpec((rows, width), index)
    if own:
        out_specs = (
            block(lambda j, m: (jnp.minimum(j, n // 2 - 1), 0)),
            block(lambda j, m: (jnp.maximum(j - n // 2, 0), 0)),
        )
        out_shape = (jax.ShapeDtypeStruct((n // 2 * rows, width), BF16),) * 2
    else:
        out_specs = block(lambda j, m: (j, 0))
        out_shape = jax.ShapeDtypeStruct((n * rows, width), BF16)
    return pl.pallas_call(
        body,
        grid_spec=pltpu.PrefetchScalarGridSpec(
            num_scalar_prefetch=1,
            grid=(n,),
            in_specs=[
                pl.BlockSpec((tokens, half), lambda j, m: (0, column(j, m))),
                whole(tokens, width),
                whole(*attn_t.shape),
                whole(tokens, width),
                *([block(lambda j, m: (j, 0))] if own else []),
            ],
            out_specs=out_specs,
        ),
        out_shape=out_shape,
        compiler_params=params(),
        cost_estimate=cost(0.2),
        name="down_out_gradient",
    )(meta, act, dy, attn_t, gb, *([far] if own else []))


def assemble(meta, downs, ups):
    rows, width = downs[0].shape
    half = width // 2
    quarter = rows - half
    hidden = ups[0].shape[1] * 2

    def body(meta, down_aa, down_ab, down_ba, down_bb, up_a, up_b, down_ref, up_ref, out_ref):
        i = pl.program_id(0)

        def place(ref, value, swapped):
            lo, hi = value[:, :half].astype(F32), value[:, half:].astype(F32)
            ref[:, :half] = jnp.where(swapped == 0, lo, hi)
            ref[:, half:] = jnp.where(swapped == 0, hi, lo)

        down_x, down_y = i // 2 == meta[3], lax.rem(i, 2) == meta[4]
        own_x = jnp.where(down_y, down_aa[...], down_ab[...])
        down = jnp.where(down_x, own_x, jnp.where(down_y, down_ba[...], down_bb[...]))
        place(down_ref, down[:half], meta[5])
        place(out_ref, down[half:], meta[5])
        place(up_ref, jnp.where(i // 2 == meta[4], up_a[...], up_b[...]), meta[3])

    down = pl.BlockSpec((rows, width), lambda i, m: (0, 0))
    up = pl.BlockSpec((half, width), lambda i, m: (0, jnp.bitwise_xor(lax.rem(i, 2), m[5])))
    return pl.pallas_call(
        body,
        grid_spec=pltpu.PrefetchScalarGridSpec(
            num_scalar_prefetch=1,
            grid=(4,),
            in_specs=[down, down, down, down, up, up],
            out_specs=(
                pl.BlockSpec((half, width), lambda i, m: (i, 0)),
                pl.BlockSpec((half, width), lambda i, m: (0, i)),
                pl.BlockSpec((quarter, width), lambda i, m: (i, 0)),
            ),
        ),
        out_shape=(
            jax.ShapeDtypeStruct((4 * half, width), F32),
            jax.ShapeDtypeStruct((half, hidden), F32),
            jax.ShapeDtypeStruct((half, width), F32),
        ),
        compiler_params=params(),
        cost_estimate=cost(7),
        name="weight_gradients",
    )(meta, *downs, *ups)


def finish_body(x_ref, gm_ref, back_ref, g_ref, out_ref):
    hat, inv = norm_rows(x_ref[...].astype(F32))
    e = back_ref[...].astype(F32) * g_ref[...]
    out_ref[...] = gm_ref[...] + inv * (
        e - jnp.mean(e, axis=-1, keepdims=True) - hat * jnp.mean(e * hat, axis=-1, keepdims=True)
    )


def finish(x, gm, back, gain):
    tokens, width = x.shape
    rows = pl.BlockSpec((128, width), lambda i: (i, 0))
    return pl.pallas_call(
        finish_body,
        grid=(tokens // 128,),
        in_specs=[rows, rows, rows, pl.BlockSpec((1, width), lambda i: (0, 0))],
        out_specs=rows,
        out_shape=jax.ShapeDtypeStruct((tokens, width), F32),
        compiler_params=params(),
        cost_estimate=cost(4),
        name="first_norm_backward",
    )(x, gm, back, gain)


def flip(value, axis, mask):
    size = lax.axis_size(axis)
    return lax.ppermute(value, axis, [(i, i ^ mask) for i in range(size)])


def bit(axis, mask):
    return (lax.axis_index(axis) // mask) % 2


def halves(value, which, axis=0):
    n = value.shape[axis] // 2
    keep = lax.dynamic_slice_in_dim(value, which * n, n, axis)
    send = lax.dynamic_slice_in_dim(value, (1 - which) * n, n, axis)
    return keep, send


def join(own, other, which, axis=0):
    return jnp.where(
        which == 0,
        jnp.concatenate([own, other], axis=axis),
        jnp.concatenate([other, own], axis=axis),
    )


def add(a, b):
    return (a.astype(F32) + b.astype(F32)).astype(BF16)


def on_device(
    tokens, lengths, ln1_gain, ln1_bias, qkv_weight, q_gain, k_gain, out_weight,
    ln2_gain, ln2_bias, up_weight, down_weight, cotangent,
):
    micro, rows, local, width = tokens.shape
    n = lax.axis_size("seq")
    length = local * n
    every = micro * rows
    team = n // every
    heads = H // team
    hd = width // H
    half = width // 2
    idx = lax.axis_index("seq")
    core = lax.axis_index("fsdp")
    row, member = idx // team, idx % team
    direct = every == 2 and team == 4
    lengths = lengths.reshape(every, lengths.shape[-1])
    mine = tokens.reshape(every, local, width)

    def swap(value):
        return flip(value, "fsdp", 1)

    vec = jnp.concatenate([ln1_gain, ln1_bias, ln2_gain, ln2_bias, q_gain, k_gain])[None]
    vec_p = swap(vec)
    ordered = jnp.where(core == 0, jnp.concatenate([vec, vec_p]), jnp.concatenate([vec_p, vec])).astype(F32)
    g1, b1, g2, b2 = (ordered[:, k * half : (k + 1) * half].reshape(1, width) for k in range(4))
    gq = ordered[:, 4 * half : 4 * half + hd // 2].reshape(hd, 1)
    gk = ordered[:, 4 * half + hd // 2 :].reshape(hd, 1)

    w_own = lax.dynamic_slice_in_dim(
        qkv_weight.reshape(half, 3, width), member * heads * hd, heads * hd, 2
    ).reshape(half, 3 * heads * hd)
    w_t = jnp.transpose(join(w_own, swap(w_own), core))

    if direct:
        near = lax.dynamic_index_in_dim(mine, row, 0, keepdims=False)
        away = lax.dynamic_index_in_dim(mine, 1 - row, 0, keepdims=False)
        cut = local // 2
        far = flip(away, "seq", 4)

        def spread(own):
            one, two = flip(own, "seq", 1), flip(own, "seq", 2)
            return [(own,), (one,), (two,), (flip(two[:cut], "seq", 1), flip(one[cut:], "seq", 2))]

        slots = spread(near) + spread(far)
        spot = idx
    else:
        same_member = [[q * team + p for q in range(every)] for p in range(team)]
        same_row = [[q * team + p for p in range(team)] for q in range(every)]
        got = lax.all_to_all(mine, "seq", 0, 0, axis_index_groups=same_member, tiled=True)
        got = lax.all_gather(got, "seq", axis_index_groups=same_row)
        whole = jnp.swapaxes(got, 0, 1).reshape(length, width)
        slots = [(whole[s * (length // 8) : (s + 1) * (length // 8)],) for s in range(8)]
        spot = jnp.int32(0)
    meta = jnp.stack([spot, row, core, bit("rep", 1), bit("seq", 1), bit("seq", 2)]).astype(jnp.int32)

    out_p, up_p, down_p = swap(out_weight), swap(up_weight), swap(down_weight)

    with jax.named_scope("forward_attention"):
        qt, ka, kt, v, vt, x_row = make_qkv(meta, lengths, slots, w_t, g1, b1, gq, gk, heads, hd)
        attn, attn_f, logsum = attend(meta, lengths, qt, ka, vt, heads, hd)

    def exchange(value):
        return lax.all_to_all(value, "seq", 0, 0, tiled=True)

    packs = every * local // BLK
    if direct:
        attn_t = exchange(attn).reshape(packs, width, BLK)
    else:
        cut = jnp.moveaxis(attn.reshape(BLK * 0 + 8, heads * hd, BLK // local, local), 2, 1)
        got = exchange(cut.reshape(n, heads * hd, local))
        got = got.reshape(packs, every // packs, width, local)
        attn_t = jnp.swapaxes(got, 1, 2).reshape(packs, width, BLK)

    total = jnp.sum(lengths[:, :-1], axis=-1)
    places = idx * local + jnp.arange(local, dtype=jnp.int32)
    valid = (places[None] < total[:, None]).astype(F32).reshape(packs, 1, BLK)
    x_home = tokens.reshape(every * local, width)
    dy = cotangent.reshape(every * local, width)

    with jax.named_scope("feed_forward"):
        output, grad_mid, grad_branch, h2, act, dup, grad_attn, vec2 = ffn(
            meta, attn_t, x_home, dy, valid, g2, b2, out_weight, out_p, up_weight, up_p, down_weight, down_p
        )
    if direct:
        grad_o = exchange(grad_attn.reshape(n, heads * hd, BLK))
    else:
        cut = jnp.swapaxes(grad_attn.reshape(packs, width, every // packs, local), 1, 2)
        got = exchange(cut.reshape(n, heads * hd, local))
        got = got.reshape(8, BLK // local, heads * hd, local)
        grad_o = jnp.swapaxes(got, 1, 2).reshape(8, heads * hd, BLK)

    masks = [1 << k for k in range(n.bit_length() - 1)]
    x, y, z = ("rep", 1), ("seq", 1), ("seq", 2)

    def next_half(keep, got, way, axis):
        return halves(add(keep, got), bit(*way), axis)

    tie = lambda *values: lax.optimization_barrier(values)
    with jax.named_scope("weight_gradients"):
        far_d = swap(down_out_grads(meta, act, dy, attn_t, grad_branch))
        far_u = swap(up_grads(meta, h2, dup))
        down_k, down_s = down_out_grads(meta, act, dy, attn_t, grad_branch, far_d)
        up_k, up_s = up_grads(meta, h2, dup, far_u)
        got = flip(down_s, *x), flip(up_s, *y)
    grad_o = tie(grad_o, up_k, up_s, down_k, down_s)[0]
    go_back = lambda go, before: attend_back(
        meta, lengths, qt, ka, kt, v, attn_f, logsum, go, heads, hd, before
    )
    with jax.named_scope("backward_attention"):
        parts = go_back(grad_o, None)
    parts, *got = tie(parts, *got)
    with jax.named_scope("weight_gradients"):
        down_k, down_s = next_half(down_k, got[0], y, 0)
        up_k, up_s = next_half(up_k, got[1], z, 1)
        got = flip(down_s, *y), flip(up_s, *z)
    with jax.named_scope("backward_attention"):
        parts = go_back(grad_o, parts)
    parts, *got = tie(parts, *got)
    with jax.named_scope("weight_gradients"):
        down_k, down_s = next_half(down_k, got[0], z, 1)
        up_k, up_s = next_half(up_k, got[1], x, 1)
        got = flip(down_s, *z), flip(up_s, *x)
    parts, *got = tie(parts, *got)
    with jax.named_scope("weight_gradients"):
        down, up = add(down_k, got[0]), add(up_k, got[1])
        pieces = jnp.concatenate([down, up])
        for mask in masks[2:]:
            pieces = add(pieces, flip(pieces, "seq", mask))
    with jax.named_scope("backward_attention"):
        dq, dk, dv = parts
        back_a, back_b, dw_t = qkv_back(meta, x_row, dq, dk, dv, w_t, g1, b1, gq, gk, vec2, heads, hd)
    dw_t, pieces = tie(dw_t, pieces)
    down, up = jnp.split(pieces, [down.shape[0]])

    with jax.named_scope("first_round"):
        keep, send = halves(dw_t, core, 1)
        q_keep, q_send = next_half(keep, swap(send), x, 0)
        got = [flip(down, *z), flip(up, *x), flip(q_send, *x)]
        if direct:
            a = back_a.reshape(2, 2, 2, local, half)
            b = back_b.reshape(2, 2, 2, local, half)
            got += [flip(a[:, :, 1], *y), flip(b[:, 1], *z)]
        got = tie(*got)
        down = jnp.concatenate([down, got[0]], axis=1)
        up = jnp.concatenate([up, got[1]], axis=1)
        piece = add(q_keep, got[2])
        if direct:
            a, b = add(a[:, :, 0], got[3]), add(b[:, 0], got[4])
    with jax.named_scope("second_round"):
        rows_at = [mask for mask in masks if mask >= team]
        got = [flip(down, *y), flip(down, *x), flip(up, *z)]
        got += [flip(piece, "seq", mask) for mask in rows_at[:1]]
        if direct:
            got += [flip(a[:, 1], *z), flip(b[:, 1], *y)]
        got = tie(*got)
        downs = [down, got[0], got[1]]
        up = jnp.concatenate([up, got[2]], axis=1)
        if rows_at:
            piece = add(piece, got[3])
        for mask in rows_at[1:]:
            piece = add(piece, flip(piece, "seq", mask))
        if direct:
            a, b = add(a[:, 0], got[-2]), add(b[:, 0], got[-1])
    with jax.named_scope("third_round"):
        piece_y, up = tie(flip(piece, *y), up)
        piece = jnp.stack([piece, piece_y])
        if direct:
            mixed = jnp.concatenate([a, b], axis=-1)
            near, far = mixed[0], flip(mixed[1], "seq", 4)
            back = jnp.where(row == 0, jnp.stack([near, far]), jnp.stack([far, near])).reshape(every * local, width)
        else:
            whole = jnp.concatenate([back_a, back_b], axis=-1).reshape(every, team, local, width)
            whole = lax.psum_scatter(whole, "seq", scatter_dimension=1, axis_index_groups=same_row, tiled=True)
            back = lax.all_to_all(
                whole[:, 0], "seq", 0, 0, axis_index_groups=same_member, tiled=True
            ).reshape(every * local, width)
        downs.append(flip(downs[1], *x))
        piece_z, downs[3] = tie(flip(piece, *z), downs[3])
        pieces = [piece, piece_z, flip(piece, *x), flip(piece_z, *x)]
        ups = (up, flip(up, *y))
    grad_tokens = finish(x_home, grad_mid, back, g1)
    grad_qkv, small = assemble_qkv(meta, pieces, heads, hd)
    grad_down, grad_up, grad_out = assemble(meta, downs, ups)
    cuts = [small[k] for k in range(4)] + [small[4, : hd // 2], small[5, : hd // 2]]
    shape = tokens.shape
    return (
        output.reshape(shape), grad_tokens.reshape(shape), cuts[0], cuts[1], grad_qkv, cuts[4], cuts[5],
        grad_out, cuts[2], cuts[3], grad_up, grad_down,
    )


def solution(mesh):
    tok = P(None, ("rep", "fsdp"), "seq", None)
    one, two = P("fsdp"), P("fsdp", None)
    in_specs = (tok, P(None, ("rep", "fsdp"), None), one, one, two, one, one, two, one, one, two, two, tok)
    out_specs = (tok, tok, one, one, two, one, one, two, one, one, two, two)
    return jax.shard_map(on_device, mesh=mesh, in_specs=in_specs, out_specs=out_specs, check_vma=False)
```

```python
import functools

import jax
import jax.numpy as jnp
from jax import lax
from jax.experimental import pallas as pl
from jax.experimental.pallas import tpu as pltpu
from jax.sharding import PartitionSpec as P

H = 12
EPS = 1e-06
LOG2E = 1.4426950408889634
SHIFT = 512.0
BLK = 256
EXTRA = 32
NN = (((1,), (0,)), ((), ()))
NT = (((1,), (1,)), ((), ()))
TN = (((0,), (0,)), ((), ()))
F32 = jnp.float32
BF16 = jnp.bfloat16


def mm(a, b, dims=NN):
    return lax.dot_general(a, b, dims, preferred_element_type=F32)


def params(**kw):
    return pltpu.CompilerParams(vmem_limit_bytes=60 * 1024 * 1024, **kw)


def cost(us):
    return pl.CostEstimate(flops=int(us * 0.35e9), bytes_accessed=1024, transcendentals=0)


def norm_rows(v):
    center = jnp.mean(v, axis=-1, keepdims=True)
    centred = v - center
    inv = lax.rsqrt(jnp.mean(centred * centred, axis=-1, keepdims=True) + EPS)
    return centred * inv, inv


def norm_cols(v):
    center = jnp.mean(v, axis=0, keepdims=True)
    centred = v - center
    inv = lax.rsqrt(jnp.mean(centred * centred, axis=0, keepdims=True) + EPS)
    return centred * inv, inv


def bounds_of(len_ref, row):
    out = []
    total = jnp.int32(0)
    for j in range(len_ref.shape[1] - 1):
        total = total + len_ref[row, j]
        out.append(total)
    return out


def qkv_body(heads, hd, cuts, meta, len_ref, *refs):
    xs = []
    for count in cuts:
        xs.append(refs[:count])
        refs = refs[count:]
    w_ref, g_ref, b_ref, gq_ref, gk_ref = refs[:5]
    qt_ref, ka_ref, kt_ref, v_ref, vt_ref, x_ref, c = refs[-7:]
    wid = heads * hd
    bounds = bounds_of(len_ref, meta[1])
    for s in range(len(cuts)):

        @pl.when(pl.program_id(0) == s)
        def _():
            at = 0
            for ref in xs[s]:
                x_ref[at : at + ref.shape[0], :] = ref[...]
                at += ref.shape[0]

    hat, _ = norm_rows(x_ref[...].astype(F32))
    first = (hat * g_ref[...] + b_ref[...]).astype(BF16)
    qkv = mm(w_ref[...], first, NT)
    place = c * BLK + lax.broadcasted_iota(jnp.int32, (8, BLK), 1)
    ident = jnp.zeros((8, BLK), jnp.int32)
    place_k = c * BLK + lax.broadcasted_iota(jnp.int32, (BLK, 128), 0)
    ident_k = jnp.zeros((BLK, 128), jnp.int32)
    for bound in bounds:
        ident = ident + (place >= bound).astype(jnp.int32)
        ident_k = ident_k + (place_k >= bound).astype(jnp.int32)
    which = lax.broadcasted_iota(jnp.int32, (8, BLK), 0)
    hot = jnp.where((ident == which) & (which < len(bounds)), 16.0, 0.0)
    hot = jnp.concatenate([hot, jnp.zeros((hd - 8, BLK), F32)], axis=0)
    lane = lax.broadcasted_iota(jnp.int32, (BLK, 128), 1) - hd
    hot_k = jnp.where((ident_k == lane) & (lane < len(bounds)), SHIFT / 16.0, 0.0)
    for h in range(heads):
        q, _ = norm_cols(qkv[h * hd : (h + 1) * hd])
        k, _ = norm_cols(qkv[wid + h * hd : wid + (h + 1) * hd])
        q = (q * gq_ref[...]).astype(BF16).astype(F32) * (hd**-0.5)
        k = k * gk_ref[...]
        v = qkv[2 * wid + h * hd : 2 * wid + (h + 1) * hd]
        qt_ref[h] = jnp.concatenate([q, hot], axis=0).astype(BF16)
        kt_ref[h] = k.astype(BF16)
        vt_ref[h] = v.astype(BF16)
        both = jnp.transpose(jnp.concatenate([k, v], axis=0))
        ka_ref[h] = jnp.where(lane < 0, both, hot_k).astype(BF16)
        v_ref[h] = both[:, hd:].astype(BF16)


def make_qkv(meta, lengths, slots, w_t, gain, bias, gq, gk, heads, hd, before=None):
    cuts = tuple(len(one) for one in slots)
    blocks = 2 * len(cuts)
    width = slots[0][0].shape[1]
    length = blocks * BLK
    first = len(cuts) if before else 0
    spot = lambda i, m: jnp.bitwise_xor(m[0], first + i)
    whole = lambda value: pl.BlockSpec(value.shape, lambda i, m, n: (0,) * value.ndim)
    operands = [*sum(slots, ()), w_t, gain, bias, gq, gk]
    columns = lambda rows: pl.BlockSpec((heads, rows, BLK), lambda i, m, n: (0, 0, spot(i, m)))
    lines = lambda size: pl.BlockSpec((heads, BLK, size), lambda i, m, n: (0, spot(i, m), 0))

    def body(meta, len_ref, *refs):
        qkv_body(heads, hd, cuts, meta, len_ref, *refs, spot(pl.program_id(0), meta))

    more = list(before or ())
    return pl.pallas_call(
        body,
        grid_spec=pltpu.PrefetchScalarGridSpec(
            num_scalar_prefetch=2,
            grid=(len(cuts),),
            in_specs=[whole(value) for value in operands] + [pl.BlockSpec(memory_space=pl.ANY)] * len(more),
            out_specs=(
                columns(2 * hd),
                lines(2 * hd),
                columns(hd),
                lines(hd),
                columns(hd),
                pl.BlockSpec((BLK, width), lambda i, m, n: (spot(i, m), 0)),
            ),
        ),
        out_shape=(
            jax.ShapeDtypeStruct((heads, 2 * hd, length), BF16),
            jax.ShapeDtypeStruct((heads, length, 2 * hd), BF16),
            jax.ShapeDtypeStruct((heads, hd, length), BF16),
            jax.ShapeDtypeStruct((heads, length, hd), BF16),
            jax.ShapeDtypeStruct((heads, hd, length), BF16),
            jax.ShapeDtypeStruct((length, width), BF16),
        ),
        input_output_aliases={2 + len(operands) + k: k for k in range(len(more))},
        compiler_params=params(),
        cost_estimate=cost(6),
        name="qkv_forward",
    )(meta, lengths, *operands, *more)


def block_range(bounds, i):
    first = i * BLK
    last = first + BLK - 1
    lo = jnp.int32(0)
    hi = bounds[-1]
    for bound in bounds:
        lo = jnp.where(first >= bound, bound, lo)
    for bound in bounds[::-1]:
        hi = jnp.where(last < bound, bound, hi)
    lo_b = lo // BLK
    hi_b = (hi + BLK - 1) // BLK
    return lo_b, jnp.where(first >= bounds[-1], lo_b, hi_b)


def in_pairs(lo, hi, step, carry):
    pairs = (hi - lo) // 2
    carry = lax.fori_loop(0, pairs, lambda k, c: step([lo + 2 * k, lo + 2 * k + 1], c), carry)
    return lax.fori_loop(lo + 2 * pairs, hi, lambda b, c: step([b], c), carry)


def attend_body(heads, hd, meta, len_ref, qt_ref, ka_ref, vt_ref, o_ref, of_ref, ls_ref):
    i = pl.program_id(0)
    bounds = bounds_of(len_ref, meta[1])
    lo, hi = block_range(bounds, i)

    def step(blocks, carry):
        rows = [pl.ds(pl.multiple_of(b * BLK, BLK), BLK) for b in blocks]
        items = [(h, r) for r in rows for h in range(heads)]
        scores = [mm(ka_ref[h, r, :], qt_ref[h]) for h, r in items]
        expos = [jnp.exp2(one * LOG2E - SHIFT * LOG2E) for one in scores]
        out = list(carry)
        for expo, (h, r) in zip(expos, items):
            acc, total = out[h]
            total = total + jnp.sum(expo.reshape(BLK // 8, 8, BLK), axis=0)
            out[h] = (acc + mm(vt_ref[h, :, r], expo.astype(BF16)), total)
        return tuple(out)

    init = tuple((jnp.zeros((hd, BLK), F32), jnp.zeros((8, BLK), F32)) for _ in range(heads))
    done = in_pairs(lo, hi, step, init)
    for h in range(heads):
        acc, total = done[h]
        total = jnp.sum(total, axis=0, keepdims=True)
        live = total > 0.0
        safe = jnp.where(live, total, 1.0)
        out = jnp.where(live, acc * (1.0 / safe), 0.0)
        o_ref[0, h * hd : (h + 1) * hd, :] = out.astype(BF16)
        of_ref[h] = out
        ls_ref[h] = jnp.log2(safe) + SHIFT * LOG2E


def attend(meta, lengths, qt, ka, vt, heads, hd):
    length = qt.shape[2]
    blocks = length // BLK
    smem = pl.BlockSpec(memory_space=pltpu.SMEM)
    return pl.pallas_call(
        functools.partial(attend_body, heads, hd),
        grid=(blocks,),
        out_shape=(
            jax.ShapeDtypeStruct((blocks, heads * hd, BLK), BF16),
            jax.ShapeDtypeStruct((heads, hd, length), F32),
            jax.ShapeDtypeStruct((heads, 1, length), F32),
        ),
        in_specs=[
            smem,
            smem,
            pl.BlockSpec((heads, 2 * hd, BLK), lambda i: (0, 0, i)),
            pl.BlockSpec((heads, length, 2 * hd), lambda i: (0, 0, 0)),
            pl.BlockSpec((heads, hd, length), lambda i: (0, 0, 0)),
        ],
        out_specs=(
            pl.BlockSpec((1, heads * hd, BLK), lambda i: (i, 0, 0)),
            pl.BlockSpec((heads, hd, BLK), lambda i: (0, 0, i)),
            pl.BlockSpec((heads, 1, BLK), lambda i: (0, 0, i)),
        ),
        compiler_params=params(),
        cost_estimate=cost(25),
        name="attention_forward",
    )(meta, lengths, qt, ka, vt)


def attend_back_body(first, heads, hd, meta, len_ref, *refs):
    qt_ref, ka_ref, kt_ref, v_ref, of_ref, ls_ref, go_ref = refs[:7]
    dq_ref, dk_ref, dv_ref = refs[-3:]
    i = pl.program_id(0)
    bounds = bounds_of(len_ref, meta[1])
    lo, hi = block_range(bounds, i + first)

    @pl.when(i == 0)
    def _():
        if first:
            dk_ref[...] = refs[8][...]
            dv_ref[...] = refs[9][...]
        else:
            dk_ref[...] = jnp.zeros_like(dk_ref)
            dv_ref[...] = jnp.zeros_like(dv_ref)

    inner = []
    for h in range(heads):
        go = go_ref[0, h * hd : (h + 1) * hd, :].astype(F32)
        inner.append(jnp.sum(go * of_ref[h], axis=0, keepdims=True))

    def step(blocks, carry):
        rows = [pl.ds(pl.multiple_of(b * BLK, BLK), BLK) for b in blocks]
        items = [(h, r) for r in rows for h in range(heads)]
        gos = [go_ref[0, h * hd : (h + 1) * hd, :] for h in range(heads)]
        scores = [mm(ka_ref[h, r, :], qt_ref[h]) for h, r in items]
        grad_probs = [mm(v_ref[h, r, :], gos[h]) for h, r in items]
        probs = [jnp.exp2(one * LOG2E - ls_ref[h]) for one, (h, _) in zip(scores, items)]
        grads = [(p * (g - inner[h])).astype(BF16) for p, g, (h, _) in zip(probs, grad_probs, items)]
        out = list(carry)
        for p, g, (h, r) in zip(probs, grads, items):
            dv_ref[h, :, r] += mm(gos[h], p.astype(BF16), NT)
            dk_ref[h, :, r] += mm(qt_ref[h][:hd], g, NT)
            out[h] = out[h] + mm(kt_ref[h, :, r], g)
        return tuple(out)

    done = in_pairs(lo, hi, step, tuple(jnp.zeros((hd, BLK), F32) for _ in range(heads)))
    for h in range(heads):
        dq_ref[h] = done[h] * (hd**-0.5)


def attend_back(meta, lengths, qt, ka, kt, v, of, ls, go, heads, hd, before=None):
    length = qt.shape[2]
    count = length // BLK // 2
    first = count if before else 0
    smem = pl.BlockSpec(memory_space=pltpu.SMEM)
    whole = lambda *shape: pl.BlockSpec(shape, lambda i: (0, 0, 0))
    part = lambda *shape: pl.BlockSpec(shape, lambda i: (0, 0, first + i))
    more = [pl.BlockSpec(memory_space=pl.ANY), whole(heads, hd, length), whole(heads, hd, length)]
    return pl.pallas_call(
        functools.partial(attend_back_body, first, heads, hd),
        grid=(count,),
        out_shape=tuple(jax.ShapeDtypeStruct((heads, hd, length), F32) for _ in range(3)),
        in_specs=[
            smem,
            smem,
            part(heads, 2 * hd, BLK),
            whole(heads, length, 2 * hd),
            whole(heads, hd, length),
            whole(heads, length, hd),
            part(heads, hd, BLK),
            part(heads, 1, BLK),
            pl.BlockSpec((1, heads * hd, BLK), lambda i: (first + i, 0, 0)),
            *(more if before else []),
        ],
        out_specs=(part(heads, hd, BLK), whole(heads, hd, length), whole(heads, hd, length)),
        input_output_aliases={9: 0} if before else {},
        compiler_params=params(),
        cost_estimate=cost(15),
        name="attention_backward",
    )(meta, lengths, qt, ka, kt, v, of, ls, go, *(before or ()))


def qkv_back_body(
    heads, hd, meta, x_ref, *refs
):
    dq_ref, dk_ref, dv_ref, w_ref, g_ref, b_ref, gq_ref, gk_ref, vec2_ref = refs[:9]
    da_ref, db_ref, dw_ref, acc_ref, vec_ref, gain_ref = refs[9:]
    i = pl.program_id(0)
    wid = heads * hd

    @pl.when(i == 0)
    def _():
        acc_ref[...] = jnp.zeros_like(acc_ref)
        vec_ref[...] = jnp.zeros_like(vec_ref)
        gain_ref[...] = jnp.zeros_like(gain_ref)

    hat, _ = norm_rows(x_ref[...].astype(F32))
    first = (hat * g_ref[...] + b_ref[...]).astype(BF16)
    qk = mm(w_ref[: 2 * wid, :], first, NT)
    pieces = []
    for at, gain, grad in ((0, gq_ref, dq_ref), (1, gk_ref, dk_ref)):
        for h in range(heads):
            unit, inv = norm_cols(qk[at * wid + h * hd : at * wid + (h + 1) * hd])
            gy = grad[h]
            gain_ref[at] += gy * unit
            e = gy * gain[...]
            pieces.append(
                inv
                * (
                    e
                    - jnp.mean(e, axis=0, keepdims=True)
                    - unit * jnp.mean(e * unit, axis=0, keepdims=True)
                )
            )
    for h in range(heads):
        pieces.append(dv_ref[h])
    grad = jnp.concatenate(pieces, axis=0).astype(BF16)
    acc_ref[...] += mm(grad, first)
    back = mm(grad, w_ref[...], TN)
    vec_ref[0] += jnp.sum((back * hat).reshape(BLK // 8, 8, -1), axis=0)
    vec_ref[1] += jnp.sum(back.reshape(BLK // 8, 8, -1), axis=0)
    half = back.shape[1] // 2
    da_ref[0] = back[:, :half].astype(BF16)
    db_ref[0] = back[:, half:].astype(BF16)

    @pl.when(i == pl.num_programs(0) - 1)
    def _():
        dw_ref[: 3 * wid, :] = acc_ref[...].astype(BF16)
        lines = [jnp.sum(ref[k], axis=0, keepdims=True) for ref in (vec_ref, vec2_ref) for k in range(2)]
        width = dw_ref.shape[1]
        lane = lax.broadcasted_iota(jnp.int32, (hd, width), 1)
        item = lax.broadcasted_iota(jnp.int32, (hd, width), 0)
        spread = jnp.where(item < hd // 2, item, item - hd // 2 + width // 2)
        for k in range(2):
            total = lax.dot_general(
                jnp.ones((8, BLK), F32), gain_ref[k], NT, precision=lax.Precision.HIGHEST, preferred_element_type=F32
            )
            pick = (lane == spread).astype(F32)
            line = lax.dot_general(total, pick, NN, precision=lax.Precision.HIGHEST, preferred_element_type=F32)
            lines.append(line[:1])
        place = lax.broadcasted_iota(jnp.int32, (EXTRA, width), 0)
        below = jnp.zeros((EXTRA, width), F32)
        for k, one in enumerate(lines):
            below = jnp.where(place == k, one, below)
        dw_ref[3 * wid :, :] = below.astype(BF16)


def qkv_back(meta, x, dq, dk, dv, w_t, gain, bias, gq, gk, vec2, heads, hd):
    length, width = x.shape
    blocks = length // BLK
    whole = lambda *shape: pl.BlockSpec(shape, lambda i, m: (0,) * len(shape))
    part = pl.BlockSpec((heads, hd, BLK), lambda i, m: (0, 0, i))
    grads = pl.BlockSpec((1, BLK, width // 2), lambda i, m: (jnp.bitwise_xor(i, m[0]), 0, 0))
    return pl.pallas_call(
        functools.partial(qkv_back_body, heads, hd),
        grid_spec=pltpu.PrefetchScalarGridSpec(
            num_scalar_prefetch=1,
            grid=(blocks,),
            in_specs=[
                pl.BlockSpec((BLK, width), lambda i, m: (i, 0)),
                part,
                part,
                part,
                whole(*w_t.shape),
                whole(1, width),
                whole(1, width),
                whole(hd, 1),
                whole(hd, 1),
                whole(2, 8, width),
            ],
            out_specs=(
                grads,
                grads,
                whole(w_t.shape[0] + EXTRA, width),
            ),
            scratch_shapes=[
                pltpu.VMEM(w_t.shape, F32),
                pltpu.VMEM((2, 8, width), F32),
                pltpu.VMEM((2, hd, BLK), F32),
            ],
        ),
        out_shape=(
            jax.ShapeDtypeStruct((blocks, BLK, width // 2), BF16),
            jax.ShapeDtypeStruct((blocks, BLK, width // 2), BF16),
            jax.ShapeDtypeStruct((w_t.shape[0] + EXTRA, width), BF16),
        ),
        compiler_params=params(),
        cost_estimate=cost(17),
        name="qkv_backward",
    )(meta, x, dq, dk, dv, w_t, gain, bias, gq, gk, vec2)


def assemble_qkv(meta, pieces, heads, hd):
    _, part, half = pieces[0].shape
    team = 4
    wid = heads * hd
    turned = team * wid

    def body(meta, p00, p01, p10, p11, out_ref, vec_ref, all_s):
        t = pl.program_id(0)

        @pl.when(t == 0)
        def _():
            for y in range(2):
                at = jnp.bitwise_xor(meta[4], y)
                for z in range(2):
                    own_z = meta[5] == z
                    near, away = jnp.where(own_z, p00[at], p01[at]), jnp.where(own_z, p10[at], p11[at])
                    for x in range(2):
                        all_s[2 * z + y, x * part : (x + 1) * part, :] = jnp.where(meta[3] == x, near, away)
            total = jnp.zeros((EXTRA, half), F32)
            for p in range(team):
                total = total + all_s[p, 3 * wid :, :].astype(F32)
            vec_ref[...] = total

        rows = pl.ds(pl.multiple_of(t * wid, wid), wid)
        piece = jnp.concatenate([all_s[p, rows, :] for p in range(team)], axis=0)
        out_ref[...] = jnp.transpose(piece.astype(F32))

    whole = lambda *shape: pl.BlockSpec(shape, lambda i, m: (0,) * len(shape))
    return pl.pallas_call(
        body,
        grid_spec=pltpu.PrefetchScalarGridSpec(
            num_scalar_prefetch=1,
            grid=(3,),
            in_specs=[whole(2, part, half)] * 4,
            out_specs=(pl.BlockSpec((half, turned), lambda i, m: (0, i)), whole(EXTRA, half)),
            scratch_shapes=[pltpu.VMEM((team, 2 * part, half), BF16)],
        ),
        out_shape=(jax.ShapeDtypeStruct((half, 3 * turned), F32), jax.ShapeDtypeStruct((EXTRA, half), F32)),
        compiler_params=params(),
        cost_estimate=cost(5),
        name="first_projection_gradient",
    )(meta, *pieces)


def gelu_pair(u):
    a = jnp.abs(u)
    t = 1.0 / (1.0 + (0.3275911 * 0.7071067811865476) * a)
    poly = 1.061405429 * t - 1.453152027
    poly = poly * t + 1.421413741
    poly = poly * t - 0.284496736
    poly = poly * t + 0.254829592
    bell = jnp.exp(-0.5 * (u * u))
    tail = (0.5 * poly) * t * bell
    cdf = jnp.where(u >= 0.0, 1.0 - tail, tail)
    return u * cdf, cdf + u * (bell * 0.3989422804014327)


def ffn(meta, attn_t, x, dy, valid, gain, bias, wo, wo_p, up, up_p, dn, dn_p):
    tokens, width = x.shape
    hidden = up.shape[1]
    fc = 512
    steps = hidden // fc
    near = steps // 2
    packs, _, lanes = attn_t.shape
    whole = lambda *shape: pl.BlockSpec(shape, lambda i, m: (0,) * len(shape))
    ups = pl.BlockSpec((width // 2, fc), lambda i, m: (0, lax.rem(m[2] * near + i, steps)))
    acts = pl.BlockSpec((tokens, fc), lambda i, m: (0, lax.rem(m[2] * near + i, steps)))
    half = width // 2

    def body(meta, *refs):
        (at_ref, x_ref, dy_ref, valid_ref, g_ref, b_ref, wo_own, wo_peer, up_own, up_peer, dn_own, dn_peer) = refs[:12]
        (out_ref, gm_ref, gb_ref, h2_ref, act_ref, dup_ref, da_ref, vec_ref) = refs[12:20]
        (mid_s, acc_s, own_s, peer_s, gown_s, gpeer_s) = refs[20:]
        i = pl.program_id(0)
        core = meta[2]
        zero = core == 0

        @pl.when(i == 0)
        def _():
            for p in range(packs):
                rows = pl.ds(p * lanes, lanes)
                own = at_ref[p, pl.ds(pl.multiple_of(core * half, half), half), :]
                peer = at_ref[p, pl.ds(pl.multiple_of((1 - core) * half, half), half), :]
                mid = x_ref[rows, :].astype(F32) + mm(own, wo_own[...], TN) + mm(peer, wo_peer[...], TN)
                mid_s[rows, :] = mid
                acc_s[rows, :] = mid
                hat, _ = norm_rows(mid)
                second = (hat * g_ref[...] + b_ref[...]).astype(BF16)
                h2_ref[:, rows] = jnp.transpose(hat * g_ref[...] + b_ref[...]).astype(BF16)
                lo, hi = second[:, :half], second[:, half:]
                own_s[rows, :] = jnp.where(zero, lo, hi)
                peer_s[rows, :] = jnp.where(zero, hi, lo)
            gown_s[...] = jnp.zeros_like(gown_s)
            gpeer_s[...] = jnp.zeros_like(gpeer_s)

        down = jnp.where(i < near, dn_own[...], dn_peer[...])
        upper = mm(own_s[...], up_own[...]) + mm(peer_s[...], up_peer[...])
        act, slope = gelu_pair(upper)
        act = act.astype(BF16)
        grad = (mm(dy_ref[...], down, NT) * slope).astype(BF16)
        act_ref[...] = act
        dup_ref[...] = grad
        acc_s[...] += mm(act, down)
        gown_s[...] += mm(grad, up_own[...], NT)
        gpeer_s[...] += mm(grad, up_peer[...], NT)

        @pl.when(i == steps - 1)
        def _():
            out_ref[...] = acc_s[...].astype(BF16)
            vec = [jnp.zeros((8, width), F32), jnp.zeros((8, width), F32)]
            for p in range(packs):
                rows = pl.ds(p * lanes, lanes)
                hat, inv = norm_rows(mid_s[rows, :])
                a, b = gown_s[rows, :], gpeer_s[rows, :]
                gy = jnp.concatenate([jnp.where(zero, a, b), jnp.where(zero, b, a)], axis=1)
                vec[0] = vec[0] + jnp.sum((gy * hat).reshape(lanes // 8, 8, width), axis=0)
                vec[1] = vec[1] + jnp.sum(gy.reshape(lanes // 8, 8, width), axis=0)
                e = gy * g_ref[...]
                gm = dy_ref[rows, :].astype(F32) + inv * (
                    e
                    - jnp.mean(e, axis=-1, keepdims=True)
                    - hat * jnp.mean(e * hat, axis=-1, keepdims=True)
                )
                gm_ref[rows, :] = gm
                gb = gm.astype(BF16)
                gb_ref[rows, :] = gb
                ok = valid_ref[p]
                da_ref[p, pl.ds(pl.multiple_of(core * half, half), half), :] = (
                    mm(wo_own[...], gb, NT) * ok
                ).astype(BF16)
                da_ref[p, pl.ds(pl.multiple_of((1 - core) * half, half), half), :] = (
                    mm(wo_peer[...], gb, NT) * ok
                ).astype(BF16)
            vec_ref[0] = vec[0]
            vec_ref[1] = vec[1]

    return pl.pallas_call(
        body,
        grid_spec=pltpu.PrefetchScalarGridSpec(
            num_scalar_prefetch=1,
            grid=(steps,),
            in_specs=[
                whole(*attn_t.shape),
                whole(tokens, width),
                whole(tokens, width),
                whole(*valid.shape),
                whole(1, width),
                whole(1, width),
                whole(half, width),
                whole(half, width),
                ups,
                ups,
                pl.BlockSpec((fc, width), lambda i, m: (jnp.minimum(i, near - 1), 0)),
                pl.BlockSpec((fc, width), lambda i, m: (jnp.maximum(i - near, 0), 0)),
            ],
            out_specs=(
                whole(tokens, width),
                whole(tokens, width),
                whole(tokens, width),
                whole(width, tokens),
                acts,
                acts,
                whole(*attn_t.shape),
                whole(2, 8, width),
            ),
            scratch_shapes=[
                pltpu.VMEM((tokens, width), F32),
                pltpu.VMEM((tokens, width), F32),
                pltpu.VMEM((tokens, half), BF16),
                pltpu.VMEM((tokens, half), BF16),
                pltpu.VMEM((tokens, half), F32),
                pltpu.VMEM((tokens, half), F32),
            ],
        ),
        out_shape=(
            jax.ShapeDtypeStruct((tokens, width), BF16),
            jax.ShapeDtypeStruct((tokens, width), F32),
            jax.ShapeDtypeStruct((tokens, width), BF16),
            jax.ShapeDtypeStruct((width, tokens), BF16),
            jax.ShapeDtypeStruct((tokens, hidden), BF16),
            jax.ShapeDtypeStruct((tokens, hidden), BF16),
            jax.ShapeDtypeStruct(attn_t.shape, BF16),
            jax.ShapeDtypeStruct((2, 8, width), F32),
        ),
        compiler_params=params(),
        cost_estimate=cost(25),
        name="ffn_both_ways",
    )(meta, attn_t, x, dy, valid, gain, bias, wo, wo_p, up, up_p, dn, dn_p)


def up_grads(meta, h2, dup, far=None):
    width, tokens = h2.shape
    hidden = dup.shape[1]
    half = width // 2
    n = hidden // width
    own = far is not None

    def body(meta, h2_ref, dup_ref, *rest):
        j = pl.program_id(0)
        side = meta[2] if own else 1 - meta[2]
        value = mm(h2_ref[pl.ds(pl.multiple_of(side * half, half), half), :], dup_ref[...])
        if own:
            store_halves(j, n, value, *rest)
        else:
            rest[0][...] = value.astype(BF16)

    def column(j, m):
        return jnp.where(j < n // 2, m[4], 1 - m[4]) * (n // 2) + lax.rem(j, n // 2)

    block = lambda index: pl.BlockSpec((half, width), index)
    if own:
        out_specs = (
            block(lambda j, m: (0, jnp.minimum(j, n // 2 - 1))),
            block(lambda j, m: (0, jnp.maximum(j - n // 2, 0))),
        )
        out_shape = (jax.ShapeDtypeStruct((half, hidden // 2), BF16),) * 2
    else:
        out_specs = block(lambda j, m: (0, j))
        out_shape = jax.ShapeDtypeStruct((half, hidden), BF16)
    return pl.pallas_call(
        body,
        grid_spec=pltpu.PrefetchScalarGridSpec(
            num_scalar_prefetch=1,
            grid=(n,),
            in_specs=[
                pl.BlockSpec((width, tokens), lambda j, m: (0, 0)),
                pl.BlockSpec((tokens, width), lambda j, m: (0, column(j, m))),
                *([block(lambda j, m: (0, j))] if own else []),
            ],
            out_specs=out_specs,
        ),
        out_shape=out_shape,
        compiler_params=params(),
        cost_estimate=cost(0.2),
        name="up_gradient",
    )(meta, h2, dup, *([far] if own else []))


def store_halves(j, n, value, far_ref, keep_ref, send_ref):
    value = (value + far_ref[...].astype(F32)).astype(BF16)

    @pl.when(j < n // 2)
    def _():
        keep_ref[...] = value

    @pl.when(j >= n // 2)
    def _():
        send_ref[...] = value


def down_out_grads(meta, act, dy, attn_t, gb, far=None):
    tokens, width = dy.shape
    half = width // 2
    packs, _, lanes = attn_t.shape
    n = act.shape[1] // 2 // half
    quarter = half // n
    rows = half + quarter
    own = far is not None

    def block_at(j, m):
        return jnp.where(j < n // 2, m[3], 1 - m[3]) * (n // 2) + lax.rem(j, n // 2)

    def body(meta, act_ref, dy_ref, at_ref, gb_ref, *rest):
        j = pl.program_id(0)
        side = meta[2] if own else 1 - meta[2]
        at = pl.ds(pl.multiple_of(side * half + block_at(j, meta) * quarter, quarter), quarter)
        total = jnp.zeros((quarter, width), F32)
        for p in range(packs):
            total = total + mm(at_ref[p, at, :], gb_ref[p * lanes : (p + 1) * lanes, :])
        value = jnp.concatenate([mm(act_ref[...], dy_ref[...], TN), total], axis=0)
        if own:
            store_halves(j, n, value, *rest)
        else:
            rest[0][...] = value.astype(BF16)

    def column(j, m):
        return (m[2] if own else 1 - m[2]) * n + block_at(j, m)

    whole = lambda *shape: pl.BlockSpec(shape, lambda j, m: (0,) * len(shape))
    block = lambda index: pl.BlockSpec((rows, width), index)
    if own:
        out_specs = (
            block(lambda j, m: (jnp.minimum(j, n // 2 - 1), 0)),
            block(lambda j, m: (jnp.maximum(j - n // 2, 0), 0)),
        )
        out_shape = (jax.ShapeDtypeStruct((n // 2 * rows, width), BF16),) * 2
    else:
        out_specs = block(lambda j, m: (j, 0))
        out_shape = jax.ShapeDtypeStruct((n * rows, width), BF16)
    return pl.pallas_call(
        body,
        grid_spec=pltpu.PrefetchScalarGridSpec(
            num_scalar_prefetch=1,
            grid=(n,),
            in_specs=[
                pl.BlockSpec((tokens, half), lambda j, m: (0, column(j, m))),
                whole(tokens, width),
                whole(*attn_t.shape),
                whole(tokens, width),
                *([block(lambda j, m: (j, 0))] if own else []),
            ],
            out_specs=out_specs,
        ),
        out_shape=out_shape,
        compiler_params=params(),
        cost_estimate=cost(0.2),
        name="down_out_gradient",
    )(meta, act, dy, attn_t, gb, *([far] if own else []))


def place(ref, value, swapped):
    half = value.shape[1] // 2
    lo, hi = value[:, :half].astype(F32), value[:, half:].astype(F32)
    ref[:, :half] = jnp.where(swapped == 0, lo, hi)
    ref[:, half:] = jnp.where(swapped == 0, hi, lo)


def assemble_down(meta, downs):
    rows, width = downs[0].shape
    half = width // 2
    quarter = rows - half

    def body(meta, down_aa, down_ab, down_ba, down_bb, down_ref, out_ref):
        i = pl.program_id(0)
        down_x, down_y = i // 2 == meta[3], lax.rem(i, 2) == meta[4]
        own_x = jnp.where(down_y, down_aa[...], down_ab[...])
        down = jnp.where(down_x, own_x, jnp.where(down_y, down_ba[...], down_bb[...]))
        place(down_ref, down[:half], meta[5])
        place(out_ref, down[half:], meta[5])

    return pl.pallas_call(
        body,
        grid_spec=pltpu.PrefetchScalarGridSpec(
            num_scalar_prefetch=1,
            grid=(4,),
            in_specs=[pl.BlockSpec((rows, width), lambda i, m: (0, 0))] * 4,
            out_specs=(
                pl.BlockSpec((half, width), lambda i, m: (i, 0)),
                pl.BlockSpec((quarter, width), lambda i, m: (i, 0)),
            ),
        ),
        out_shape=(
            jax.ShapeDtypeStruct((4 * half, width), F32),
            jax.ShapeDtypeStruct((half, width), F32),
        ),
        compiler_params=params(),
        cost_estimate=cost(4),
        name="down_out_in_place",
    )(meta, *downs)


def assemble_up(meta, ups):
    half, width = ups[0].shape[0], ups[0].shape[1] // 2

    def body(meta, up_a, up_b, up_ref):
        place(up_ref, jnp.where(pl.program_id(0) // 2 == meta[4], up_a[...], up_b[...]), meta[3])

    return pl.pallas_call(
        body,
        grid_spec=pltpu.PrefetchScalarGridSpec(
            num_scalar_prefetch=1,
            grid=(4,),
            in_specs=[pl.BlockSpec((half, width), lambda i, m: (0, jnp.bitwise_xor(lax.rem(i, 2), m[5])))] * 2,
            out_specs=pl.BlockSpec((half, width), lambda i, m: (0, i)),
        ),
        out_shape=jax.ShapeDtypeStruct((half, 4 * width), F32),
        compiler_params=params(),
        cost_estimate=cost(4),
        name="up_in_place",
    )(meta, *ups)


def finish_body(x_ref, gm_ref, back_ref, g_ref, out_ref):
    hat, inv = norm_rows(x_ref[...].astype(F32))
    e = back_ref[...].astype(F32) * g_ref[...]
    out_ref[...] = gm_ref[...] + inv * (
        e - jnp.mean(e, axis=-1, keepdims=True) - hat * jnp.mean(e * hat, axis=-1, keepdims=True)
    )


def finish(x, gm, back, gain):
    tokens, width = x.shape
    rows = pl.BlockSpec((128, width), lambda i: (i, 0))
    return pl.pallas_call(
        finish_body,
        grid=(tokens // 128,),
        in_specs=[rows, rows, rows, pl.BlockSpec((1, width), lambda i: (0, 0))],
        out_specs=rows,
        out_shape=jax.ShapeDtypeStruct((tokens, width), F32),
        compiler_params=params(),
        cost_estimate=cost(4),
        name="first_norm_backward",
    )(x, gm, back, gain)


def flip(value, axis, mask):
    size = lax.axis_size(axis)
    return lax.ppermute(value, axis, [(i, i ^ mask) for i in range(size)])


def bit(axis, mask):
    return (lax.axis_index(axis) // mask) % 2


def halves(value, which, axis=0):
    n = value.shape[axis] // 2
    keep = lax.dynamic_slice_in_dim(value, which * n, n, axis)
    send = lax.dynamic_slice_in_dim(value, (1 - which) * n, n, axis)
    return keep, send


def join(own, other, which, axis=0):
    return jnp.where(
        which == 0,
        jnp.concatenate([own, other], axis=axis),
        jnp.concatenate([other, own], axis=axis),
    )


def add(a, b):
    return (a.astype(F32) + b.astype(F32)).astype(BF16)


def on_device(
    tokens, lengths, ln1_gain, ln1_bias, qkv_weight, q_gain, k_gain, out_weight,
    ln2_gain, ln2_bias, up_weight, down_weight, cotangent,
):
    micro, rows, local, width = tokens.shape
    n = lax.axis_size("seq")
    length = local * n
    every = micro * rows
    team = n // every
    heads = H // team
    hd = width // H
    half = width // 2
    idx = lax.axis_index("seq")
    core = lax.axis_index("fsdp")
    row, member = idx // team, idx % team
    direct = every == 2 and team == 4
    lengths = lengths.reshape(every, lengths.shape[-1])
    mine = tokens.reshape(every, local, width)

    def swap(value):
        return flip(value, "fsdp", 1)

    vec = jnp.concatenate([ln1_gain, ln1_bias, ln2_gain, ln2_bias, q_gain, k_gain])[None]
    vec_p = swap(vec)
    ordered = jnp.where(core == 0, jnp.concatenate([vec, vec_p]), jnp.concatenate([vec_p, vec])).astype(F32)
    g1, b1, g2, b2 = (ordered[:, k * half : (k + 1) * half].reshape(1, width) for k in range(4))
    gq = ordered[:, 4 * half : 4 * half + hd // 2].reshape(hd, 1)
    gk = ordered[:, 4 * half + hd // 2 :].reshape(hd, 1)

    w_own = lax.dynamic_slice_in_dim(
        qkv_weight.reshape(half, 3, width), member * heads * hd, heads * hd, 2
    ).reshape(half, 3 * heads * hd)
    w_t = jnp.transpose(join(w_own, swap(w_own), core))

    if direct:
        near = lax.dynamic_index_in_dim(mine, row, 0, keepdims=False)
        away = lax.dynamic_index_in_dim(mine, 1 - row, 0, keepdims=False)
        cut = local // 2
        far = flip(away, "seq", 4)

        def spread(own):
            one, two = flip(own, "seq", 1), flip(own, "seq", 2)
            return [(own,), (one,), (two,), (flip(two[:cut], "seq", 1), flip(one[cut:], "seq", 2))]

        slots = spread(near) + spread(far)
        spot = idx
    else:
        same_member = [[q * team + p for q in range(every)] for p in range(team)]
        same_row = [[q * team + p for p in range(team)] for q in range(every)]
        got = lax.all_to_all(mine, "seq", 0, 0, axis_index_groups=same_member, tiled=True)
        got = lax.all_gather(got, "seq", axis_index_groups=same_row)
        whole = jnp.swapaxes(got, 0, 1).reshape(length, width)
        slots = [(whole[s * (length // 8) : (s + 1) * (length // 8)],) for s in range(8)]
        spot = jnp.int32(0)
    meta = jnp.stack([spot, row, core, bit("rep", 1), bit("seq", 1), bit("seq", 2)]).astype(jnp.int32)

    out_p, up_p, down_p = swap(out_weight), swap(up_weight), swap(down_weight)

    with jax.named_scope("forward_attention"):
        near = make_qkv(meta, lengths, slots[:4], w_t, g1, b1, gq, gk, heads, hd)
        qt, ka, kt, v, vt, x_row = make_qkv(meta, lengths, slots[4:], w_t, g1, b1, gq, gk, heads, hd, near)
        attn, attn_f, logsum = attend(meta, lengths, qt, ka, vt, heads, hd)

    def exchange(value):
        return lax.all_to_all(value, "seq", 0, 0, tiled=True)

    packs = every * local // BLK
    if direct:
        attn_t = exchange(attn).reshape(packs, width, BLK)
    else:
        cut = jnp.moveaxis(attn.reshape(BLK * 0 + 8, heads * hd, BLK // local, local), 2, 1)
        got = exchange(cut.reshape(n, heads * hd, local))
        got = got.reshape(packs, every // packs, width, local)
        attn_t = jnp.swapaxes(got, 1, 2).reshape(packs, width, BLK)

    total = jnp.sum(lengths[:, :-1], axis=-1)
    places = idx * local + jnp.arange(local, dtype=jnp.int32)
    valid = (places[None] < total[:, None]).astype(F32).reshape(packs, 1, BLK)
    x_home = tokens.reshape(every * local, width)
    dy = cotangent.reshape(every * local, width)

    with jax.named_scope("feed_forward"):
        output, grad_mid, grad_branch, h2, act, dup, grad_attn, vec2 = ffn(
            meta, attn_t, x_home, dy, valid, g2, b2, out_weight, out_p, up_weight, up_p, down_weight, down_p
        )
    if direct:
        grad_o = exchange(grad_attn.reshape(n, heads * hd, BLK))
    else:
        cut = jnp.swapaxes(grad_attn.reshape(packs, width, every // packs, local), 1, 2)
        got = exchange(cut.reshape(n, heads * hd, local))
        got = got.reshape(8, BLK // local, heads * hd, local)
        grad_o = jnp.swapaxes(got, 1, 2).reshape(8, heads * hd, BLK)

    masks = [1 << k for k in range(n.bit_length() - 1)]
    x, y, z = ("rep", 1), ("seq", 1), ("seq", 2)

    def next_half(keep, got, way, axis):
        return halves(add(keep, got), bit(*way), axis)

    tie = lambda *values: lax.optimization_barrier(values)
    with jax.named_scope("weight_gradients"):
        far_d = swap(down_out_grads(meta, act, dy, attn_t, grad_branch))
        far_u = swap(up_grads(meta, h2, dup))
        down_k, down_s = down_out_grads(meta, act, dy, attn_t, grad_branch, far_d)
        up_k, up_s = up_grads(meta, h2, dup, far_u)
        got = flip(down_s, *x), flip(up_s, *y)
    grad_o = tie(grad_o, up_k, up_s, down_k, down_s)[0]
    go_back = lambda go, before: attend_back(
        meta, lengths, qt, ka, kt, v, attn_f, logsum, go, heads, hd, before
    )
    with jax.named_scope("backward_attention"):
        parts = go_back(grad_o, None)
    parts, *got = tie(parts, *got)
    with jax.named_scope("weight_gradients"):
        down_k, down_s = next_half(down_k, got[0], y, 0)
        up_k, up_s = next_half(up_k, got[1], z, 1)
        got = flip(down_s, *y), flip(up_s, *z)
    with jax.named_scope("backward_attention"):
        parts = go_back(grad_o, parts)
    parts, *got = tie(parts, *got)
    with jax.named_scope("weight_gradients"):
        down_k, down_s = next_half(down_k, got[0], z, 1)
        up_k, up_s = next_half(up_k, got[1], x, 1)
        got = flip(down_s, *z), flip(up_s, *x)
    parts, *got = tie(parts, *got)
    with jax.named_scope("weight_gradients"):
        down, up = add(down_k, got[0]), add(up_k, got[1])
        pieces = jnp.concatenate([down, up])
        for mask in masks[2:]:
            pieces = add(pieces, flip(pieces, "seq", mask))
    with jax.named_scope("backward_attention"):
        dq, dk, dv = parts
        back_a, back_b, dw_t = qkv_back(meta, x_row, dq, dk, dv, w_t, g1, b1, gq, gk, vec2, heads, hd)
    dw_t, pieces = tie(dw_t, pieces)
    down, up = jnp.split(pieces, [down.shape[0]])

    with jax.named_scope("first_round"):
        keep, send = halves(dw_t, core, 1)
        q_keep, q_send = next_half(keep, swap(send), x, 0)
        got = [flip(down, *z), flip(up, *x), flip(q_send, *x)]
        if direct:
            a = back_a.reshape(2, 2, 2, local, half)
            b = back_b.reshape(2, 2, 2, local, half)
            got += [flip(a[:, :, 1], *y), flip(b[:, 1], *z)]
        got = tie(*got)
        down = jnp.concatenate([down, got[0]], axis=1)
        up = jnp.concatenate([up, got[1]], axis=1)
        piece = add(q_keep, got[2])
        if direct:
            a, b = add(a[:, :, 0], got[3]), add(b[:, 0], got[4])
    with jax.named_scope("second_round"):
        rows_at = [mask for mask in masks if mask >= team]
        got = [flip(down, *y), flip(down, *x), flip(up, *z)]
        got += [flip(piece, "seq", mask) for mask in rows_at[:1]]
        if direct:
            got += [flip(a[:, 1], *z), flip(b[:, 1], *y)]
        got = tie(*got)
        downs = [down, got[0], got[1]]
        up = jnp.concatenate([up, got[2]], axis=1)
        if rows_at:
            piece = add(piece, got[3])
        for mask in rows_at[1:]:
            piece = add(piece, flip(piece, "seq", mask))
        if direct:
            a, b = add(a[:, 0], got[-2]), add(b[:, 0], got[-1])
    with jax.named_scope("third_round"):
        piece_y, up = tie(flip(piece, *y), up)
        piece = jnp.stack([piece, piece_y])
        if direct:
            mixed = jnp.concatenate([a, b], axis=-1)
            near, far = mixed[0], flip(mixed[1], "seq", 4)
            back = jnp.where(row == 0, jnp.stack([near, far]), jnp.stack([far, near])).reshape(every * local, width)
        else:
            whole = jnp.concatenate([back_a, back_b], axis=-1).reshape(every, team, local, width)
            whole = lax.psum_scatter(whole, "seq", scatter_dimension=1, axis_index_groups=same_row, tiled=True)
            back = lax.all_to_all(
                whole[:, 0], "seq", 0, 0, axis_index_groups=same_member, tiled=True
            ).reshape(every * local, width)
        downs.append(flip(downs[1], *x))
        piece_z, downs[3] = tie(flip(piece, *z), downs[3])
        pieces = [piece, piece_z, flip(piece, *x), flip(piece_z, *x)]
        ups = (up, flip(up, *y))
    grad_tokens = finish(x_home, grad_mid, back, g1)
    grad_qkv, small = assemble_qkv(meta, pieces, heads, hd)
    grad_down, grad_out = assemble_down(meta, downs)
    grad_up = assemble_up(meta, ups)
    cuts = [small[k] for k in range(4)] + [small[4, : hd // 2], small[5, : hd // 2]]
    shape = tokens.shape
    return (
        output.reshape(shape), grad_tokens.reshape(shape), cuts[0], cuts[1], grad_qkv, cuts[4], cuts[5],
        grad_out, cuts[2], cuts[3], grad_up, grad_down,
    )


def solution(mesh):
    tok = P(None, ("rep", "fsdp"), "seq", None)
    one, two = P("fsdp"), P("fsdp", None)
    in_specs = (tok, P(None, ("rep", "fsdp"), None), one, one, two, one, one, two, one, one, two, two, tok)
    out_specs = (tok, tok, one, one, two, one, one, two, one, one, two, two)
    return jax.shard_map(on_device, mesh=mesh, in_specs=in_specs, out_specs=out_specs, check_vma=False)
```

```python
import functools

import jax
import jax.numpy as jnp
from jax import lax
from jax.experimental import pallas as pl
from jax.experimental.pallas import tpu as pltpu
from jax.sharding import PartitionSpec as P

H = 12
EPS = 1e-06
LOG2E = 1.4426950408889634
SHIFT = 512.0
BLK = 256
EXTRA = 32
NN = (((1,), (0,)), ((), ()))
NT = (((1,), (1,)), ((), ()))
TN = (((0,), (0,)), ((), ()))
F32 = jnp.float32
BF16 = jnp.bfloat16


def mm(a, b, dims=NN):
    return lax.dot_general(a, b, dims, preferred_element_type=F32)


def params(**kw):
    return pltpu.CompilerParams(vmem_limit_bytes=60 * 1024 * 1024, **kw)


def cost(us):
    return pl.CostEstimate(flops=int(us * 0.35e9), bytes_accessed=1024, transcendentals=0)


def norm_rows(v):
    center = jnp.mean(v, axis=-1, keepdims=True)
    centred = v - center
    inv = lax.rsqrt(jnp.mean(centred * centred, axis=-1, keepdims=True) + EPS)
    return centred * inv, inv


def norm_cols(v):
    center = jnp.mean(v, axis=0, keepdims=True)
    centred = v - center
    inv = lax.rsqrt(jnp.mean(centred * centred, axis=0, keepdims=True) + EPS)
    return centred * inv, inv


def bounds_of(len_ref, row):
    out = []
    total = jnp.int32(0)
    for j in range(len_ref.shape[1] - 1):
        total = total + len_ref[row, j]
        out.append(total)
    return out


def qkv_body(heads, hd, cuts, meta, len_ref, *refs):
    xs = []
    for count in cuts:
        xs.append(refs[:count])
        refs = refs[count:]
    w_ref, g_ref, b_ref, gq_ref, gk_ref = refs[:5]
    qt_ref, ka_ref, kt_ref, v_ref, vt_ref, x_ref, c = refs[-7:]
    wid = heads * hd
    bounds = bounds_of(len_ref, meta[1])
    for s in range(len(cuts)):

        @pl.when(pl.program_id(0) == s)
        def _():
            at = 0
            for ref in xs[s]:
                x_ref[at : at + ref.shape[0], :] = ref[...]
                at += ref.shape[0]

    hat, _ = norm_rows(x_ref[...].astype(F32))
    first = (hat * g_ref[...] + b_ref[...]).astype(BF16)
    qkv = mm(w_ref[...], first, NT)
    place = c * BLK + lax.broadcasted_iota(jnp.int32, (8, BLK), 1)
    ident = jnp.zeros((8, BLK), jnp.int32)
    place_k = c * BLK + lax.broadcasted_iota(jnp.int32, (BLK, 128), 0)
    ident_k = jnp.zeros((BLK, 128), jnp.int32)
    for bound in bounds:
        ident = ident + (place >= bound).astype(jnp.int32)
        ident_k = ident_k + (place_k >= bound).astype(jnp.int32)
    which = lax.broadcasted_iota(jnp.int32, (8, BLK), 0)
    hot = jnp.where((ident == which) & (which < len(bounds)), 16.0, 0.0)
    hot = jnp.concatenate([hot, jnp.zeros((hd - 8, BLK), F32)], axis=0)
    lane = lax.broadcasted_iota(jnp.int32, (BLK, 128), 1) - hd
    hot_k = jnp.where((ident_k == lane) & (lane < len(bounds)), SHIFT / 16.0, 0.0)
    for h in range(heads):
        q, _ = norm_cols(qkv[h * hd : (h + 1) * hd])
        k, _ = norm_cols(qkv[wid + h * hd : wid + (h + 1) * hd])
        q = (q * gq_ref[...]).astype(BF16).astype(F32) * (hd**-0.5)
        k = k * gk_ref[...]
        v = qkv[2 * wid + h * hd : 2 * wid + (h + 1) * hd]
        qt_ref[h] = jnp.concatenate([q, hot], axis=0).astype(BF16)
        kt_ref[h] = k.astype(BF16)
        vt_ref[h] = v.astype(BF16)
        both = jnp.transpose(jnp.concatenate([k, v], axis=0))
        ka_ref[h] = jnp.where(lane < 0, both, hot_k).astype(BF16)
        v_ref[h] = both[:, hd:].astype(BF16)


def make_qkv(meta, lengths, slots, w_t, gain, bias, gq, gk, heads, hd, before=None):
    cuts = tuple(len(one) for one in slots)
    blocks = 2 * len(cuts)
    width = slots[0][0].shape[1]
    length = blocks * BLK
    first = len(cuts) if before else 0
    spot = lambda i, m: jnp.bitwise_xor(m[0], first + i)
    whole = lambda value: pl.BlockSpec(value.shape, lambda i, m, n: (0,) * value.ndim)
    operands = [*sum(slots, ()), w_t, gain, bias, gq, gk]
    columns = lambda rows: pl.BlockSpec((heads, rows, BLK), lambda i, m, n: (0, 0, spot(i, m)))
    lines = lambda size: pl.BlockSpec((heads, BLK, size), lambda i, m, n: (0, spot(i, m), 0))

    def body(meta, len_ref, *refs):
        qkv_body(heads, hd, cuts, meta, len_ref, *refs, spot(pl.program_id(0), meta))

    more = list(before or ())
    return pl.pallas_call(
        body,
        grid_spec=pltpu.PrefetchScalarGridSpec(
            num_scalar_prefetch=2,
            grid=(len(cuts),),
            in_specs=[whole(value) for value in operands] + [pl.BlockSpec(memory_space=pl.ANY)] * len(more),
            out_specs=(
                columns(2 * hd),
                lines(2 * hd),
                columns(hd),
                lines(hd),
                columns(hd),
                pl.BlockSpec((BLK, width), lambda i, m, n: (spot(i, m), 0)),
            ),
        ),
        out_shape=(
            jax.ShapeDtypeStruct((heads, 2 * hd, length), BF16),
            jax.ShapeDtypeStruct((heads, length, 2 * hd), BF16),
            jax.ShapeDtypeStruct((heads, hd, length), BF16),
            jax.ShapeDtypeStruct((heads, length, hd), BF16),
            jax.ShapeDtypeStruct((heads, hd, length), BF16),
            jax.ShapeDtypeStruct((length, width), BF16),
        ),
        input_output_aliases={2 + len(operands) + k: k for k in range(len(more))},
        compiler_params=params(),
        cost_estimate=cost(6),
        name="qkv_forward",
    )(meta, lengths, *operands, *more)


def block_range(bounds, i):
    first = i * BLK
    last = first + BLK - 1
    lo = jnp.int32(0)
    hi = bounds[-1]
    for bound in bounds:
        lo = jnp.where(first >= bound, bound, lo)
    for bound in bounds[::-1]:
        hi = jnp.where(last < bound, bound, hi)
    lo_b = lo // BLK
    hi_b = (hi + BLK - 1) // BLK
    return lo_b, jnp.where(first >= bounds[-1], lo_b, hi_b)


def in_pairs(lo, hi, step, carry):
    pairs = (hi - lo) // 2
    carry = lax.fori_loop(0, pairs, lambda k, c: step([lo + 2 * k, lo + 2 * k + 1], c), carry)
    return lax.fori_loop(lo + 2 * pairs, hi, lambda b, c: step([b], c), carry)


def attend_body(heads, hd, meta, len_ref, qt_ref, ka_ref, vt_ref, o_ref, of_ref, ls_ref):
    i = pl.program_id(0)
    bounds = bounds_of(len_ref, meta[1])
    lo, hi = block_range(bounds, i)

    def step(blocks, carry):
        rows = [pl.ds(pl.multiple_of(b * BLK, BLK), BLK) for b in blocks]
        items = [(h, r) for r in rows for h in range(heads)]
        scores = [mm(ka_ref[h, r, :], qt_ref[h]) for h, r in items]
        expos = [jnp.exp2(one * LOG2E - SHIFT * LOG2E) for one in scores]
        out = list(carry)
        for expo, (h, r) in zip(expos, items):
            acc, total = out[h]
            total = total + jnp.sum(expo.reshape(BLK // 8, 8, BLK), axis=0)
            out[h] = (acc + mm(vt_ref[h, :, r], expo.astype(BF16)), total)
        return tuple(out)

    init = tuple((jnp.zeros((hd, BLK), F32), jnp.zeros((8, BLK), F32)) for _ in range(heads))
    done = in_pairs(lo, hi, step, init)
    for h in range(heads):
        acc, total = done[h]
        total = jnp.sum(total, axis=0, keepdims=True)
        live = total > 0.0
        safe = jnp.where(live, total, 1.0)
        out = jnp.where(live, acc * (1.0 / safe), 0.0)
        o_ref[0, h * hd : (h + 1) * hd, :] = out.astype(BF16)
        of_ref[h] = out
        ls_ref[h] = jnp.log2(safe) + SHIFT * LOG2E


def attend(meta, lengths, qt, ka, vt, heads, hd):
    length = qt.shape[2]
    blocks = length // BLK
    smem = pl.BlockSpec(memory_space=pltpu.SMEM)
    return pl.pallas_call(
        functools.partial(attend_body, heads, hd),
        grid=(blocks,),
        out_shape=(
            jax.ShapeDtypeStruct((blocks, heads * hd, BLK), BF16),
            jax.ShapeDtypeStruct((heads, hd, length), F32),
            jax.ShapeDtypeStruct((heads, 1, length), F32),
        ),
        in_specs=[
            smem,
            smem,
            pl.BlockSpec((heads, 2 * hd, BLK), lambda i: (0, 0, i)),
            pl.BlockSpec((heads, length, 2 * hd), lambda i: (0, 0, 0)),
            pl.BlockSpec((heads, hd, length), lambda i: (0, 0, 0)),
        ],
        out_specs=(
            pl.BlockSpec((1, heads * hd, BLK), lambda i: (i, 0, 0)),
            pl.BlockSpec((heads, hd, BLK), lambda i: (0, 0, i)),
            pl.BlockSpec((heads, 1, BLK), lambda i: (0, 0, i)),
        ),
        compiler_params=params(),
        cost_estimate=cost(25),
        name="attention_forward",
    )(meta, lengths, qt, ka, vt)


def attend_back_body(first, heads, hd, meta, len_ref, *refs):
    qt_ref, ka_ref, kt_ref, v_ref, of_ref, ls_ref, go_ref = refs[:7]
    dq_ref, dk_ref, dv_ref = refs[-3:]
    i = pl.program_id(0)
    bounds = bounds_of(len_ref, meta[1])
    lo, hi = block_range(bounds, i + first)

    @pl.when(i == 0)
    def _():
        if first:
            dk_ref[...] = refs[8][...]
            dv_ref[...] = refs[9][...]
        else:
            dk_ref[...] = jnp.zeros_like(dk_ref)
            dv_ref[...] = jnp.zeros_like(dv_ref)

    inner = []
    for h in range(heads):
        go = go_ref[0, h * hd : (h + 1) * hd, :].astype(F32)
        inner.append(jnp.sum(go * of_ref[h], axis=0, keepdims=True))

    def step(blocks, carry):
        rows = [pl.ds(pl.multiple_of(b * BLK, BLK), BLK) for b in blocks]
        items = [(h, r) for r in rows for h in range(heads)]
        gos = [go_ref[0, h * hd : (h + 1) * hd, :] for h in range(heads)]
        scores = [mm(ka_ref[h, r, :], qt_ref[h]) for h, r in items]
        grad_probs = [mm(v_ref[h, r, :], gos[h]) for h, r in items]
        probs = [jnp.exp2(one * LOG2E - ls_ref[h]) for one, (h, _) in zip(scores, items)]
        grads = [(p * (g - inner[h])).astype(BF16) for p, g, (h, _) in zip(probs, grad_probs, items)]
        out = list(carry)
        for p, g, (h, r) in zip(probs, grads, items):
            dv_ref[h, :, r] += mm(gos[h], p.astype(BF16), NT)
            dk_ref[h, :, r] += mm(qt_ref[h][:hd], g, NT)
            out[h] = out[h] + mm(kt_ref[h, :, r], g)
        return tuple(out)

    done = in_pairs(lo, hi, step, tuple(jnp.zeros((hd, BLK), F32) for _ in range(heads)))
    for h in range(heads):
        dq_ref[h] = done[h] * (hd**-0.5)


def attend_back(meta, lengths, qt, ka, kt, v, of, ls, go, heads, hd, before=None):
    length = qt.shape[2]
    split = (5 * length) // (8 * BLK)
    first = split if before else 0
    count = length // BLK - split if before else split
    smem = pl.BlockSpec(memory_space=pltpu.SMEM)
    whole = lambda *shape: pl.BlockSpec(shape, lambda i: (0, 0, 0))
    part = lambda *shape: pl.BlockSpec(shape, lambda i: (0, 0, first + i))
    more = [pl.BlockSpec(memory_space=pl.ANY), whole(heads, hd, length), whole(heads, hd, length)]
    return pl.pallas_call(
        functools.partial(attend_back_body, first, heads, hd),
        grid=(count,),
        out_shape=tuple(jax.ShapeDtypeStruct((heads, hd, length), F32) for _ in range(3)),
        in_specs=[
            smem,
            smem,
            part(heads, 2 * hd, BLK),
            whole(heads, length, 2 * hd),
            whole(heads, hd, length),
            whole(heads, length, hd),
            part(heads, hd, BLK),
            part(heads, 1, BLK),
            pl.BlockSpec((1, heads * hd, BLK), lambda i: (first + i, 0, 0)),
            *(more if before else []),
        ],
        out_specs=(part(heads, hd, BLK), whole(heads, hd, length), whole(heads, hd, length)),
        input_output_aliases={9: 0} if before else {},
        compiler_params=params(),
        cost_estimate=cost(15),
        name="attention_backward",
    )(meta, lengths, qt, ka, kt, v, of, ls, go, *(before or ()))


def qkv_back_body(
    heads, hd, meta, x_ref, *refs
):
    dq_ref, dk_ref, dv_ref, w_ref, g_ref, b_ref, gq_ref, gk_ref, vec2_ref = refs[:9]
    da_ref, db_ref, dw_ref, acc_ref, vec_ref, gain_ref = refs[9:]
    i = pl.program_id(0)
    wid = heads * hd

    @pl.when(i == 0)
    def _():
        acc_ref[...] = jnp.zeros_like(acc_ref)
        vec_ref[...] = jnp.zeros_like(vec_ref)
        gain_ref[...] = jnp.zeros_like(gain_ref)

    hat, _ = norm_rows(x_ref[...].astype(F32))
    first = (hat * g_ref[...] + b_ref[...]).astype(BF16)
    qk = mm(w_ref[: 2 * wid, :], first, NT)
    pieces = []
    for at, gain, grad in ((0, gq_ref, dq_ref), (1, gk_ref, dk_ref)):
        for h in range(heads):
            unit, inv = norm_cols(qk[at * wid + h * hd : at * wid + (h + 1) * hd])
            gy = grad[h]
            gain_ref[at] += gy * unit
            e = gy * gain[...]
            pieces.append(
                inv
                * (
                    e
                    - jnp.mean(e, axis=0, keepdims=True)
                    - unit * jnp.mean(e * unit, axis=0, keepdims=True)
                )
            )
    for h in range(heads):
        pieces.append(dv_ref[h])
    grad = jnp.concatenate(pieces, axis=0).astype(BF16)
    acc_ref[...] += mm(grad, first)
    back = mm(grad, w_ref[...], TN)
    vec_ref[0] += jnp.sum((back * hat).reshape(BLK // 8, 8, -1), axis=0)
    vec_ref[1] += jnp.sum(back.reshape(BLK // 8, 8, -1), axis=0)
    half = back.shape[1] // 2
    da_ref[0] = back[:, :half].astype(BF16)
    db_ref[0] = back[:, half:].astype(BF16)

    @pl.when(i == pl.num_programs(0) - 1)
    def _():
        dw_ref[: 3 * wid, :] = acc_ref[...].astype(BF16)
        lines = [jnp.sum(ref[k], axis=0, keepdims=True) for ref in (vec_ref, vec2_ref) for k in range(2)]
        width = dw_ref.shape[1]
        lane = lax.broadcasted_iota(jnp.int32, (hd, width), 1)
        item = lax.broadcasted_iota(jnp.int32, (hd, width), 0)
        spread = jnp.where(item < hd // 2, item, item - hd // 2 + width // 2)
        for k in range(2):
            total = lax.dot_general(
                jnp.ones((8, BLK), F32), gain_ref[k], NT, precision=lax.Precision.HIGHEST, preferred_element_type=F32
            )
            pick = (lane == spread).astype(F32)
            line = lax.dot_general(total, pick, NN, precision=lax.Precision.HIGHEST, preferred_element_type=F32)
            lines.append(line[:1])
        place = lax.broadcasted_iota(jnp.int32, (EXTRA, width), 0)
        below = jnp.zeros((EXTRA, width), F32)
        for k, one in enumerate(lines):
            below = jnp.where(place == k, one, below)
        dw_ref[3 * wid :, :] = below.astype(BF16)


def qkv_back(meta, x, dq, dk, dv, w_t, gain, bias, gq, gk, vec2, heads, hd):
    length, width = x.shape
    blocks = length // BLK
    whole = lambda *shape: pl.BlockSpec(shape, lambda i, m: (0,) * len(shape))
    part = pl.BlockSpec((heads, hd, BLK), lambda i, m: (0, 0, i))
    grads = pl.BlockSpec((1, BLK, width // 2), lambda i, m: (jnp.bitwise_xor(i, m[0]), 0, 0))
    return pl.pallas_call(
        functools.partial(qkv_back_body, heads, hd),
        grid_spec=pltpu.PrefetchScalarGridSpec(
            num_scalar_prefetch=1,
            grid=(blocks,),
            in_specs=[
                pl.BlockSpec((BLK, width), lambda i, m: (i, 0)),
                part,
                part,
                part,
                whole(*w_t.shape),
                whole(1, width),
                whole(1, width),
                whole(hd, 1),
                whole(hd, 1),
                whole(2, 8, width),
            ],
            out_specs=(
                grads,
                grads,
                whole(w_t.shape[0] + EXTRA, width),
            ),
            scratch_shapes=[
                pltpu.VMEM(w_t.shape, F32),
                pltpu.VMEM((2, 8, width), F32),
                pltpu.VMEM((2, hd, BLK), F32),
            ],
        ),
        out_shape=(
            jax.ShapeDtypeStruct((blocks, BLK, width // 2), BF16),
            jax.ShapeDtypeStruct((blocks, BLK, width // 2), BF16),
            jax.ShapeDtypeStruct((w_t.shape[0] + EXTRA, width), BF16),
        ),
        compiler_params=params(),
        cost_estimate=cost(17),
        name="qkv_backward",
    )(meta, x, dq, dk, dv, w_t, gain, bias, gq, gk, vec2)


def assemble_qkv(meta, pieces, heads, hd):
    _, part, half = pieces[0].shape
    team = 4
    wid = heads * hd
    turned = team * wid

    def body(meta, p00, p01, p10, p11, out_ref, vec_ref, all_s):
        t = pl.program_id(0)

        @pl.when(t == 0)
        def _():
            for y in range(2):
                at = jnp.bitwise_xor(meta[4], y)
                for z in range(2):
                    own_z = meta[5] == z
                    near, away = jnp.where(own_z, p00[at], p01[at]), jnp.where(own_z, p10[at], p11[at])
                    for x in range(2):
                        all_s[2 * z + y, x * part : (x + 1) * part, :] = jnp.where(meta[3] == x, near, away)
            total = jnp.zeros((EXTRA, half), F32)
            for p in range(team):
                total = total + all_s[p, 3 * wid :, :].astype(F32)
            vec_ref[...] = total

        rows = pl.ds(pl.multiple_of(t * wid, wid), wid)
        piece = jnp.concatenate([all_s[p, rows, :] for p in range(team)], axis=0)
        out_ref[...] = jnp.transpose(piece.astype(F32))

    whole = lambda *shape: pl.BlockSpec(shape, lambda i, m: (0,) * len(shape))
    return pl.pallas_call(
        body,
        grid_spec=pltpu.PrefetchScalarGridSpec(
            num_scalar_prefetch=1,
            grid=(3,),
            in_specs=[whole(2, part, half)] * 4,
            out_specs=(pl.BlockSpec((half, turned), lambda i, m: (0, i)), whole(EXTRA, half)),
            scratch_shapes=[pltpu.VMEM((team, 2 * part, half), BF16)],
        ),
        out_shape=(jax.ShapeDtypeStruct((half, 3 * turned), F32), jax.ShapeDtypeStruct((EXTRA, half), F32)),
        compiler_params=params(),
        cost_estimate=cost(5),
        name="first_projection_gradient",
    )(meta, *pieces)


def gelu_pair(u):
    a = jnp.abs(u)
    t = 1.0 / (1.0 + (0.3275911 * 0.7071067811865476) * a)
    poly = 1.061405429 * t - 1.453152027
    poly = poly * t + 1.421413741
    poly = poly * t - 0.284496736
    poly = poly * t + 0.254829592
    bell = jnp.exp(-0.5 * (u * u))
    tail = (0.5 * poly) * t * bell
    cdf = jnp.where(u >= 0.0, 1.0 - tail, tail)
    return u * cdf, cdf + u * (bell * 0.3989422804014327)


def ffn(meta, attn_t, x, dy, valid, gain, bias, wo, wo_p, up, up_p, dn, dn_p):
    tokens, width = x.shape
    hidden = up.shape[1]
    fc = 512
    steps = hidden // fc
    near = steps // 2
    packs, _, lanes = attn_t.shape
    whole = lambda *shape: pl.BlockSpec(shape, lambda i, m: (0,) * len(shape))
    ups = pl.BlockSpec((width // 2, fc), lambda i, m: (0, lax.rem(m[2] * near + i, steps)))
    acts = pl.BlockSpec((tokens, fc), lambda i, m: (0, lax.rem(m[2] * near + i, steps)))
    half = width // 2

    def body(meta, *refs):
        (at_ref, x_ref, dy_ref, valid_ref, g_ref, b_ref, wo_own, wo_peer, up_own, up_peer, dn_own, dn_peer) = refs[:12]
        (out_ref, gm_ref, gb_ref, h2_ref, act_ref, dup_ref, da_ref, vec_ref) = refs[12:20]
        (mid_s, acc_s, own_s, peer_s, gown_s, gpeer_s) = refs[20:]
        i = pl.program_id(0)
        core = meta[2]
        zero = core == 0

        @pl.when(i == 0)
        def _():
            for p in range(packs):
                rows = pl.ds(p * lanes, lanes)
                own = at_ref[p, pl.ds(pl.multiple_of(core * half, half), half), :]
                peer = at_ref[p, pl.ds(pl.multiple_of((1 - core) * half, half), half), :]
                mid = x_ref[rows, :].astype(F32) + mm(own, wo_own[...], TN) + mm(peer, wo_peer[...], TN)
                mid_s[rows, :] = mid
                acc_s[rows, :] = mid
                hat, _ = norm_rows(mid)
                second = (hat * g_ref[...] + b_ref[...]).astype(BF16)
                h2_ref[:, rows] = jnp.transpose(hat * g_ref[...] + b_ref[...]).astype(BF16)
                lo, hi = second[:, :half], second[:, half:]
                own_s[rows, :] = jnp.where(zero, lo, hi)
                peer_s[rows, :] = jnp.where(zero, hi, lo)
            gown_s[...] = jnp.zeros_like(gown_s)
            gpeer_s[...] = jnp.zeros_like(gpeer_s)

        down = jnp.where(i < near, dn_own[...], dn_peer[...])
        upper = mm(own_s[...], up_own[...]) + mm(peer_s[...], up_peer[...])
        act, slope = gelu_pair(upper)
        act = act.astype(BF16)
        grad = (mm(dy_ref[...], down, NT) * slope).astype(BF16)
        act_ref[...] = act
        dup_ref[...] = grad
        acc_s[...] += mm(act, down)
        gown_s[...] += mm(grad, up_own[...], NT)
        gpeer_s[...] += mm(grad, up_peer[...], NT)

        @pl.when(i == steps - 1)
        def _():
            out_ref[...] = acc_s[...].astype(BF16)
            vec = [jnp.zeros((8, width), F32), jnp.zeros((8, width), F32)]
            for p in range(packs):
                rows = pl.ds(p * lanes, lanes)
                hat, inv = norm_rows(mid_s[rows, :])
                a, b = gown_s[rows, :], gpeer_s[rows, :]
                gy = jnp.concatenate([jnp.where(zero, a, b), jnp.where(zero, b, a)], axis=1)
                vec[0] = vec[0] + jnp.sum((gy * hat).reshape(lanes // 8, 8, width), axis=0)
                vec[1] = vec[1] + jnp.sum(gy.reshape(lanes // 8, 8, width), axis=0)
                e = gy * g_ref[...]
                gm = dy_ref[rows, :].astype(F32) + inv * (
                    e
                    - jnp.mean(e, axis=-1, keepdims=True)
                    - hat * jnp.mean(e * hat, axis=-1, keepdims=True)
                )
                gm_ref[rows, :] = gm
                gb = gm.astype(BF16)
                gb_ref[rows, :] = gb
                ok = valid_ref[p]
                da_ref[p, pl.ds(pl.multiple_of(core * half, half), half), :] = (
                    mm(wo_own[...], gb, NT) * ok
                ).astype(BF16)
                da_ref[p, pl.ds(pl.multiple_of((1 - core) * half, half), half), :] = (
                    mm(wo_peer[...], gb, NT) * ok
                ).astype(BF16)
            vec_ref[0] = vec[0]
            vec_ref[1] = vec[1]

    return pl.pallas_call(
        body,
        grid_spec=pltpu.PrefetchScalarGridSpec(
            num_scalar_prefetch=1,
            grid=(steps,),
            in_specs=[
                whole(*attn_t.shape),
                whole(tokens, width),
                whole(tokens, width),
                whole(*valid.shape),
                whole(1, width),
                whole(1, width),
                whole(half, width),
                whole(half, width),
                ups,
                ups,
                pl.BlockSpec((fc, width), lambda i, m: (jnp.minimum(i, near - 1), 0)),
                pl.BlockSpec((fc, width), lambda i, m: (jnp.maximum(i - near, 0), 0)),
            ],
            out_specs=(
                whole(tokens, width),
                whole(tokens, width),
                whole(tokens, width),
                whole(width, tokens),
                acts,
                acts,
                whole(*attn_t.shape),
                whole(2, 8, width),
            ),
            scratch_shapes=[
                pltpu.VMEM((tokens, width), F32),
                pltpu.VMEM((tokens, width), F32),
                pltpu.VMEM((tokens, half), BF16),
                pltpu.VMEM((tokens, half), BF16),
                pltpu.VMEM((tokens, half), F32),
                pltpu.VMEM((tokens, half), F32),
            ],
        ),
        out_shape=(
            jax.ShapeDtypeStruct((tokens, width), BF16),
            jax.ShapeDtypeStruct((tokens, width), F32),
            jax.ShapeDtypeStruct((tokens, width), BF16),
            jax.ShapeDtypeStruct((width, tokens), BF16),
            jax.ShapeDtypeStruct((tokens, hidden), BF16),
            jax.ShapeDtypeStruct((tokens, hidden), BF16),
            jax.ShapeDtypeStruct(attn_t.shape, BF16),
            jax.ShapeDtypeStruct((2, 8, width), F32),
        ),
        compiler_params=params(),
        cost_estimate=cost(25),
        name="ffn_both_ways",
    )(meta, attn_t, x, dy, valid, gain, bias, wo, wo_p, up, up_p, dn, dn_p)


def up_grads(meta, h2, dup, far=None):
    width, tokens = h2.shape
    hidden = dup.shape[1]
    half = width // 2
    n = hidden // width
    own = far is not None

    def body(meta, h2_ref, dup_ref, *rest):
        j = pl.program_id(0)
        side = meta[2] if own else 1 - meta[2]
        value = mm(h2_ref[pl.ds(pl.multiple_of(side * half, half), half), :], dup_ref[...])
        if own:
            store_halves(j, n, value, *rest)
        else:
            rest[0][...] = value.astype(BF16)

    def column(j, m):
        return jnp.where(j < n // 2, m[4], 1 - m[4]) * (n // 2) + lax.rem(j, n // 2)

    block = lambda index: pl.BlockSpec((half, width), index)
    if own:
        out_specs = (
            block(lambda j, m: (0, jnp.minimum(j, n // 2 - 1))),
            block(lambda j, m: (0, jnp.maximum(j - n // 2, 0))),
        )
        out_shape = (jax.ShapeDtypeStruct((half, hidden // 2), BF16),) * 2
    else:
        out_specs = block(lambda j, m: (0, j))
        out_shape = jax.ShapeDtypeStruct((half, hidden), BF16)
    return pl.pallas_call(
        body,
        grid_spec=pltpu.PrefetchScalarGridSpec(
            num_scalar_prefetch=1,
            grid=(n,),
            in_specs=[
                pl.BlockSpec((width, tokens), lambda j, m: (0, 0)),
                pl.BlockSpec((tokens, width), lambda j, m: (0, column(j, m))),
                *([block(lambda j, m: (0, j))] if own else []),
            ],
            out_specs=out_specs,
        ),
        out_shape=out_shape,
        compiler_params=params(),
        cost_estimate=cost(0.2),
        name="up_gradient",
    )(meta, h2, dup, *([far] if own else []))


def store_halves(j, n, value, far_ref, keep_ref, send_ref):
    value = (value + far_ref[...].astype(F32)).astype(BF16)

    @pl.when(j < n // 2)
    def _():
        keep_ref[...] = value

    @pl.when(j >= n // 2)
    def _():
        send_ref[...] = value


def down_out_grads(meta, act, dy, attn_t, gb, far=None):
    tokens, width = dy.shape
    half = width // 2
    packs, _, lanes = attn_t.shape
    n = act.shape[1] // 2 // half
    quarter = half // n
    rows = half + quarter
    own = far is not None

    def block_at(j, m):
        return jnp.where(j < n // 2, m[3], 1 - m[3]) * (n // 2) + lax.rem(j, n // 2)

    def body(meta, act_ref, dy_ref, at_ref, gb_ref, *rest):
        j = pl.program_id(0)
        side = meta[2] if own else 1 - meta[2]
        at = pl.ds(pl.multiple_of(side * half + block_at(j, meta) * quarter, quarter), quarter)
        total = jnp.zeros((quarter, width), F32)
        for p in range(packs):
            total = total + mm(at_ref[p, at, :], gb_ref[p * lanes : (p + 1) * lanes, :])
        value = jnp.concatenate([mm(act_ref[...], dy_ref[...], TN), total], axis=0)
        if own:
            store_halves(j, n, value, *rest)
        else:
            rest[0][...] = value.astype(BF16)

    def column(j, m):
        return (m[2] if own else 1 - m[2]) * n + block_at(j, m)

    whole = lambda *shape: pl.BlockSpec(shape, lambda j, m: (0,) * len(shape))
    block = lambda index: pl.BlockSpec((rows, width), index)
    if own:
        out_specs = (
            block(lambda j, m: (jnp.minimum(j, n // 2 - 1), 0)),
            block(lambda j, m: (jnp.maximum(j - n // 2, 0), 0)),
        )
        out_shape = (jax.ShapeDtypeStruct((n // 2 * rows, width), BF16),) * 2
    else:
        out_specs = block(lambda j, m: (j, 0))
        out_shape = jax.ShapeDtypeStruct((n * rows, width), BF16)
    return pl.pallas_call(
        body,
        grid_spec=pltpu.PrefetchScalarGridSpec(
            num_scalar_prefetch=1,
            grid=(n,),
            in_specs=[
                pl.BlockSpec((tokens, half), lambda j, m: (0, column(j, m))),
                whole(tokens, width),
                whole(*attn_t.shape),
                whole(tokens, width),
                *([block(lambda j, m: (j, 0))] if own else []),
            ],
            out_specs=out_specs,
        ),
        out_shape=out_shape,
        compiler_params=params(),
        cost_estimate=cost(0.2),
        name="down_out_gradient",
    )(meta, act, dy, attn_t, gb, *([far] if own else []))


def place(ref, value, swapped):
    half = value.shape[1] // 2
    lo, hi = value[:, :half].astype(F32), value[:, half:].astype(F32)
    ref[:, :half] = jnp.where(swapped == 0, lo, hi)
    ref[:, half:] = jnp.where(swapped == 0, hi, lo)


def assemble_down(meta, downs):
    rows, width = downs[0].shape
    half = width // 2
    quarter = rows - half

    def body(meta, down_aa, down_ab, down_ba, down_bb, down_ref, out_ref):
        i = pl.program_id(0)
        down_x, down_y = i // 2 == meta[3], lax.rem(i, 2) == meta[4]
        own_x = jnp.where(down_y, down_aa[...], down_ab[...])
        down = jnp.where(down_x, own_x, jnp.where(down_y, down_ba[...], down_bb[...]))
        place(down_ref, down[:half], meta[5])
        place(out_ref, down[half:], meta[5])

    return pl.pallas_call(
        body,
        grid_spec=pltpu.PrefetchScalarGridSpec(
            num_scalar_prefetch=1,
            grid=(4,),
            in_specs=[pl.BlockSpec((rows, width), lambda i, m: (0, 0))] * 4,
            out_specs=(
                pl.BlockSpec((half, width), lambda i, m: (i, 0)),
                pl.BlockSpec((quarter, width), lambda i, m: (i, 0)),
            ),
        ),
        out_shape=(
            jax.ShapeDtypeStruct((4 * half, width), F32),
            jax.ShapeDtypeStruct((half, width), F32),
        ),
        compiler_params=params(),
        cost_estimate=cost(4),
        name="down_out_in_place",
    )(meta, *downs)


def assemble_up(meta, ups):
    half, width = ups[0].shape[0], ups[0].shape[1] // 2

    def body(meta, up_a, up_b, up_ref):
        place(up_ref, jnp.where(pl.program_id(0) // 2 == meta[4], up_a[...], up_b[...]), meta[3])

    return pl.pallas_call(
        body,
        grid_spec=pltpu.PrefetchScalarGridSpec(
            num_scalar_prefetch=1,
            grid=(4,),
            in_specs=[pl.BlockSpec((half, width), lambda i, m: (0, jnp.bitwise_xor(lax.rem(i, 2), m[5])))] * 2,
            out_specs=pl.BlockSpec((half, width), lambda i, m: (0, i)),
        ),
        out_shape=jax.ShapeDtypeStruct((half, 4 * width), F32),
        compiler_params=params(),
        cost_estimate=cost(4),
        name="up_in_place",
    )(meta, *ups)


def finish_body(x_ref, gm_ref, back_ref, g_ref, out_ref):
    hat, inv = norm_rows(x_ref[...].astype(F32))
    e = back_ref[...].astype(F32) * g_ref[...]
    out_ref[...] = gm_ref[...] + inv * (
        e - jnp.mean(e, axis=-1, keepdims=True) - hat * jnp.mean(e * hat, axis=-1, keepdims=True)
    )


def finish(x, gm, back, gain):
    tokens, width = x.shape
    rows = pl.BlockSpec((128, width), lambda i: (i, 0))
    return pl.pallas_call(
        finish_body,
        grid=(tokens // 128,),
        in_specs=[rows, rows, rows, pl.BlockSpec((1, width), lambda i: (0, 0))],
        out_specs=rows,
        out_shape=jax.ShapeDtypeStruct((tokens, width), F32),
        compiler_params=params(),
        cost_estimate=cost(4),
        name="first_norm_backward",
    )(x, gm, back, gain)


def flip(value, axis, mask):
    size = lax.axis_size(axis)
    return lax.ppermute(value, axis, [(i, i ^ mask) for i in range(size)])


def bit(axis, mask):
    return (lax.axis_index(axis) // mask) % 2


def halves(value, which, axis=0):
    n = value.shape[axis] // 2
    keep = lax.dynamic_slice_in_dim(value, which * n, n, axis)
    send = lax.dynamic_slice_in_dim(value, (1 - which) * n, n, axis)
    return keep, send


def join(own, other, which, axis=0):
    return jnp.where(
        which == 0,
        jnp.concatenate([own, other], axis=axis),
        jnp.concatenate([other, own], axis=axis),
    )


def add(a, b):
    return (a.astype(F32) + b.astype(F32)).astype(BF16)


def on_device(
    tokens, lengths, ln1_gain, ln1_bias, qkv_weight, q_gain, k_gain, out_weight,
    ln2_gain, ln2_bias, up_weight, down_weight, cotangent,
):
    micro, rows, local, width = tokens.shape
    n = lax.axis_size("seq")
    length = local * n
    every = micro * rows
    team = n // every
    heads = H // team
    hd = width // H
    half = width // 2
    idx = lax.axis_index("seq")
    core = lax.axis_index("fsdp")
    row, member = idx // team, idx % team
    direct = every == 2 and team == 4
    lengths = lengths.reshape(every, lengths.shape[-1])
    mine = tokens.reshape(every, local, width)

    def swap(value):
        return flip(value, "fsdp", 1)

    vec = jnp.concatenate([ln1_gain, ln1_bias, ln2_gain, ln2_bias, q_gain, k_gain])[None]
    vec_p = swap(vec)
    ordered = jnp.where(core == 0, jnp.concatenate([vec, vec_p]), jnp.concatenate([vec_p, vec])).astype(F32)
    g1, b1, g2, b2 = (ordered[:, k * half : (k + 1) * half].reshape(1, width) for k in range(4))
    gq = ordered[:, 4 * half : 4 * half + hd // 2].reshape(hd, 1)
    gk = ordered[:, 4 * half + hd // 2 :].reshape(hd, 1)

    w_own = lax.dynamic_slice_in_dim(
        qkv_weight.reshape(half, 3, width), member * heads * hd, heads * hd, 2
    ).reshape(half, 3 * heads * hd)
    w_t = jnp.transpose(join(w_own, swap(w_own), core))

    if direct:
        near = lax.dynamic_index_in_dim(mine, row, 0, keepdims=False)
        away = lax.dynamic_index_in_dim(mine, 1 - row, 0, keepdims=False)
        cut = local // 2
        far = flip(away, "seq", 4)

        def spread(own):
            one, two = flip(own, "seq", 1), flip(own, "seq", 2)
            return [(own,), (one,), (two,), (flip(two[:cut], "seq", 1), flip(one[cut:], "seq", 2))]

        slots = spread(near) + spread(far)
        spot = idx
    else:
        same_member = [[q * team + p for q in range(every)] for p in range(team)]
        same_row = [[q * team + p for p in range(team)] for q in range(every)]
        got = lax.all_to_all(mine, "seq", 0, 0, axis_index_groups=same_member, tiled=True)
        got = lax.all_gather(got, "seq", axis_index_groups=same_row)
        whole = jnp.swapaxes(got, 0, 1).reshape(length, width)
        slots = [(whole[s * (length // 8) : (s + 1) * (length // 8)],) for s in range(8)]
        spot = jnp.int32(0)
    meta = jnp.stack([spot, row, core, bit("rep", 1), bit("seq", 1), bit("seq", 2)]).astype(jnp.int32)

    out_p, up_p, down_p = swap(out_weight), swap(up_weight), swap(down_weight)

    with jax.named_scope("forward_attention"):
        near = make_qkv(meta, lengths, slots[:4], w_t, g1, b1, gq, gk, heads, hd)
        qt, ka, kt, v, vt, x_row = make_qkv(meta, lengths, slots[4:], w_t, g1, b1, gq, gk, heads, hd, near)
        attn, attn_f, logsum = attend(meta, lengths, qt, ka, vt, heads, hd)

    def exchange(value):
        return lax.all_to_all(value, "seq", 0, 0, tiled=True)

    packs = every * local // BLK
    if direct:
        attn_t = exchange(attn).reshape(packs, width, BLK)
    else:
        cut = jnp.moveaxis(attn.reshape(BLK * 0 + 8, heads * hd, BLK // local, local), 2, 1)
        got = exchange(cut.reshape(n, heads * hd, local))
        got = got.reshape(packs, every // packs, width, local)
        attn_t = jnp.swapaxes(got, 1, 2).reshape(packs, width, BLK)

    total = jnp.sum(lengths[:, :-1], axis=-1)
    places = idx * local + jnp.arange(local, dtype=jnp.int32)
    valid = (places[None] < total[:, None]).astype(F32).reshape(packs, 1, BLK)
    x_home = tokens.reshape(every * local, width)
    dy = cotangent.reshape(every * local, width)

    with jax.named_scope("feed_forward"):
        output, grad_mid, grad_branch, h2, act, dup, grad_attn, vec2 = ffn(
            meta, attn_t, x_home, dy, valid, g2, b2, out_weight, out_p, up_weight, up_p, down_weight, down_p
        )
    if direct:
        grad_o = exchange(grad_attn.reshape(n, heads * hd, BLK))
    else:
        cut = jnp.swapaxes(grad_attn.reshape(packs, width, every // packs, local), 1, 2)
        got = exchange(cut.reshape(n, heads * hd, local))
        got = got.reshape(8, BLK // local, heads * hd, local)
        grad_o = jnp.swapaxes(got, 1, 2).reshape(8, heads * hd, BLK)

    masks = [1 << k for k in range(n.bit_length() - 1)]
    x, y, z = ("rep", 1), ("seq", 1), ("seq", 2)

    def next_half(keep, got, way, axis):
        return halves(add(keep, got), bit(*way), axis)

    tie = lambda *values: lax.optimization_barrier(values)
    with jax.named_scope("weight_gradients"):
        far_d = swap(down_out_grads(meta, act, dy, attn_t, grad_branch))
        far_u = swap(up_grads(meta, h2, dup))
        down_k, down_s = down_out_grads(meta, act, dy, attn_t, grad_branch, far_d)
        up_k, up_s = up_grads(meta, h2, dup, far_u)
        got = flip(down_s, *x), flip(up_s, *y)
    grad_o = tie(grad_o, up_k, up_s, down_k, down_s)[0]
    go_back = lambda go, before: attend_back(
        meta, lengths, qt, ka, kt, v, attn_f, logsum, go, heads, hd, before
    )
    with jax.named_scope("backward_attention"):
        parts = go_back(grad_o, None)
    parts, *got = tie(parts, *got)
    with jax.named_scope("weight_gradients"):
        down_k, down_s = next_half(down_k, got[0], y, 0)
        up_k, up_s = next_half(up_k, got[1], z, 1)
        got = flip(down_s, *y), flip(up_s, *z)
    with jax.named_scope("backward_attention"):
        parts = go_back(grad_o, parts)
    parts, *got = tie(parts, *got)
    with jax.named_scope("weight_gradients"):
        down_k, down_s = next_half(down_k, got[0], z, 1)
        up_k, up_s = next_half(up_k, got[1], x, 1)
        got = flip(down_s, *z), flip(up_s, *x)
    parts, *got = tie(parts, *got)
    with jax.named_scope("weight_gradients"):
        down, up = add(down_k, got[0]), add(up_k, got[1])
        pieces = jnp.concatenate([down, up])
        for mask in masks[2:]:
            pieces = add(pieces, flip(pieces, "seq", mask))
    with jax.named_scope("backward_attention"):
        dq, dk, dv = parts
        back_a, back_b, dw_t = qkv_back(meta, x_row, dq, dk, dv, w_t, g1, b1, gq, gk, vec2, heads, hd)
    dw_t, pieces = tie(dw_t, pieces)
    down, up = jnp.split(pieces, [down.shape[0]])

    with jax.named_scope("first_round"):
        keep, send = halves(dw_t, core, 1)
        q_keep, q_send = next_half(keep, swap(send), x, 0)
        got = [flip(down, *z), flip(up, *x), flip(q_send, *x)]
        if direct:
            a = back_a.reshape(2, 2, 2, local, half)
            b = back_b.reshape(2, 2, 2, local, half)
            got += [flip(a[:, :, 1], *y), flip(b[:, 1], *z)]
        got = tie(*got)
        down = jnp.concatenate([down, got[0]], axis=1)
        up = jnp.concatenate([up, got[1]], axis=1)
        piece = add(q_keep, got[2])
        if direct:
            a, b = add(a[:, :, 0], got[3]), add(b[:, 0], got[4])
    with jax.named_scope("second_round"):
        rows_at = [mask for mask in masks if mask >= team]
        got = [flip(down, *y), flip(down, *x), flip(up, *z)]
        got += [flip(piece, "seq", mask) for mask in rows_at[:1]]
        if direct:
            got += [flip(a[:, 1], *z), flip(b[:, 1], *y)]
        got = tie(*got)
        downs = [down, got[0], got[1]]
        up = jnp.concatenate([up, got[2]], axis=1)
        if rows_at:
            piece = add(piece, got[3])
        for mask in rows_at[1:]:
            piece = add(piece, flip(piece, "seq", mask))
        if direct:
            a, b = add(a[:, 0], got[-2]), add(b[:, 0], got[-1])
    with jax.named_scope("third_round"):
        piece_y, up = tie(flip(piece, *y), up)
        piece = jnp.stack([piece, piece_y])
        if direct:
            mixed = jnp.concatenate([a, b], axis=-1)
            near, far = mixed[0], flip(mixed[1], "seq", 4)
            back = jnp.where(row == 0, jnp.stack([near, far]), jnp.stack([far, near])).reshape(every * local, width)
        else:
            whole = jnp.concatenate([back_a, back_b], axis=-1).reshape(every, team, local, width)
            whole = lax.psum_scatter(whole, "seq", scatter_dimension=1, axis_index_groups=same_row, tiled=True)
            back = lax.all_to_all(
                whole[:, 0], "seq", 0, 0, axis_index_groups=same_member, tiled=True
            ).reshape(every * local, width)
        downs.append(flip(downs[1], *x))
        piece_z, downs[3] = tie(flip(piece, *z), downs[3])
        grad_down, grad_out = assemble_down(meta, downs)
        piece_z, grad_down, grad_out = tie(piece_z, grad_down, grad_out)
        pieces = [piece, piece_z, flip(piece, *x), flip(piece_z, *x)]
        ups = (up, flip(up, *y))
    grad_tokens = finish(x_home, grad_mid, back, g1)
    grad_up, grad_tokens = tie(assemble_up(meta, ups), grad_tokens)
    pieces[3], grad_up = tie(pieces[3], grad_up)
    grad_qkv, small = assemble_qkv(meta, pieces, heads, hd)
    cuts = [small[k] for k in range(4)] + [small[4, : hd // 2], small[5, : hd // 2]]
    shape = tokens.shape
    return (
        output.reshape(shape), grad_tokens.reshape(shape), cuts[0], cuts[1], grad_qkv, cuts[4], cuts[5],
        grad_out, cuts[2], cuts[3], grad_up, grad_down,
    )


def solution(mesh):
    tok = P(None, ("rep", "fsdp"), "seq", None)
    one, two = P("fsdp"), P("fsdp", None)
    in_specs = (tok, P(None, ("rep", "fsdp"), None), one, one, two, one, one, two, one, one, two, two, tok)
    out_specs = (tok, tok, one, one, two, one, one, two, one, one, two, two)
    return jax.shard_map(on_device, mesh=mesh, in_specs=in_specs, out_specs=out_specs, check_vma=False)
```

```python
import functools

import jax
import jax.numpy as jnp
from jax import lax
from jax.experimental import pallas as pl
from jax.experimental.pallas import tpu as pltpu
from jax.sharding import PartitionSpec as P

H = 12
EPS = 1e-06
LOG2E = 1.4426950408889634
SHIFT = 512.0
BLK = 256
EXTRA = 32
NN = (((1,), (0,)), ((), ()))
NT = (((1,), (1,)), ((), ()))
TN = (((0,), (0,)), ((), ()))
F32 = jnp.float32
BF16 = jnp.bfloat16


def mm(a, b, dims=NN):
    return lax.dot_general(a, b, dims, preferred_element_type=F32)


def params(**kw):
    return pltpu.CompilerParams(vmem_limit_bytes=60 * 1024 * 1024, **kw)


def cost(us):
    return pl.CostEstimate(flops=int(us * 0.35e9), bytes_accessed=1024, transcendentals=0)


def norm_rows(v):
    center = jnp.mean(v, axis=-1, keepdims=True)
    centred = v - center
    inv = lax.rsqrt(jnp.mean(centred * centred, axis=-1, keepdims=True) + EPS)
    return centred * inv, inv


def norm_cols(v):
    center = jnp.mean(v, axis=0, keepdims=True)
    centred = v - center
    inv = lax.rsqrt(jnp.mean(centred * centred, axis=0, keepdims=True) + EPS)
    return centred * inv, inv


def bounds_of(len_ref, row):
    out = []
    total = jnp.int32(0)
    for j in range(len_ref.shape[1] - 1):
        total = total + len_ref[row, j]
        out.append(total)
    return out


def qkv_body(heads, hd, cuts, meta, len_ref, *refs):
    xs = []
    for count in cuts:
        xs.append(refs[:count])
        refs = refs[count:]
    w_ref, g_ref, b_ref, gq_ref, gk_ref = refs[:5]
    qt_ref, ka_ref, kt_ref, v_ref, vt_ref, x_ref, c = refs[-7:]
    wid = heads * hd
    bounds = bounds_of(len_ref, meta[1])
    for s in range(len(cuts)):

        @pl.when(pl.program_id(0) == s)
        def _():
            at = 0
            for ref in xs[s]:
                x_ref[at : at + ref.shape[0], :] = ref[...]
                at += ref.shape[0]

    hat, _ = norm_rows(x_ref[...].astype(F32))
    first = (hat * g_ref[...] + b_ref[...]).astype(BF16)
    qkv = mm(w_ref[...], first, NT)
    place = c * BLK + lax.broadcasted_iota(jnp.int32, (8, BLK), 1)
    ident = jnp.zeros((8, BLK), jnp.int32)
    place_k = c * BLK + lax.broadcasted_iota(jnp.int32, (BLK, 128), 0)
    ident_k = jnp.zeros((BLK, 128), jnp.int32)
    for bound in bounds:
        ident = ident + (place >= bound).astype(jnp.int32)
        ident_k = ident_k + (place_k >= bound).astype(jnp.int32)
    which = lax.broadcasted_iota(jnp.int32, (8, BLK), 0)
    hot = jnp.where((ident == which) & (which < len(bounds)), 16.0, 0.0)
    hot = jnp.concatenate([hot, jnp.zeros((hd - 8, BLK), F32)], axis=0)
    lane = lax.broadcasted_iota(jnp.int32, (BLK, 128), 1) - hd
    hot_k = jnp.where((ident_k == lane) & (lane < len(bounds)), SHIFT / 16.0, 0.0)
    for h in range(heads):
        q, _ = norm_cols(qkv[h * hd : (h + 1) * hd])
        k, _ = norm_cols(qkv[wid + h * hd : wid + (h + 1) * hd])
        q = (q * gq_ref[...]).astype(BF16).astype(F32) * (hd**-0.5)
        k = k * gk_ref[...]
        v = qkv[2 * wid + h * hd : 2 * wid + (h + 1) * hd]
        qt_ref[h] = jnp.concatenate([q, hot], axis=0).astype(BF16)
        kt_ref[h] = k.astype(BF16)
        vt_ref[h] = v.astype(BF16)
        both = jnp.transpose(jnp.concatenate([k, v], axis=0))
        ka_ref[h] = jnp.where(lane < 0, both, hot_k).astype(BF16)
        v_ref[h] = both[:, hd:].astype(BF16)


def make_qkv(meta, lengths, slots, w_t, gain, bias, gq, gk, heads, hd, before=None):
    cuts = tuple(len(one) for one in slots)
    blocks = 2 * len(cuts)
    width = slots[0][0].shape[1]
    length = blocks * BLK
    first = len(cuts) if before else 0
    spot = lambda i, m: jnp.bitwise_xor(m[0], first + i)
    whole = lambda value: pl.BlockSpec(value.shape, lambda i, m, n: (0,) * value.ndim)
    operands = [*sum(slots, ()), w_t, gain, bias, gq, gk]
    columns = lambda rows: pl.BlockSpec((heads, rows, BLK), lambda i, m, n: (0, 0, spot(i, m)))
    lines = lambda size: pl.BlockSpec((heads, BLK, size), lambda i, m, n: (0, spot(i, m), 0))

    def body(meta, len_ref, *refs):
        qkv_body(heads, hd, cuts, meta, len_ref, *refs, spot(pl.program_id(0), meta))

    more = list(before or ())
    return pl.pallas_call(
        body,
        grid_spec=pltpu.PrefetchScalarGridSpec(
            num_scalar_prefetch=2,
            grid=(len(cuts),),
            in_specs=[whole(value) for value in operands] + [pl.BlockSpec(memory_space=pl.ANY)] * len(more),
            out_specs=(
                columns(2 * hd),
                lines(2 * hd),
                columns(hd),
                lines(hd),
                columns(hd),
                pl.BlockSpec((BLK, width), lambda i, m, n: (spot(i, m), 0)),
            ),
        ),
        out_shape=(
            jax.ShapeDtypeStruct((heads, 2 * hd, length), BF16),
            jax.ShapeDtypeStruct((heads, length, 2 * hd), BF16),
            jax.ShapeDtypeStruct((heads, hd, length), BF16),
            jax.ShapeDtypeStruct((heads, length, hd), BF16),
            jax.ShapeDtypeStruct((heads, hd, length), BF16),
            jax.ShapeDtypeStruct((length, width), BF16),
        ),
        input_output_aliases={2 + len(operands) + k: k for k in range(len(more))},
        compiler_params=params(),
        cost_estimate=cost(6),
        name="qkv_forward",
    )(meta, lengths, *operands, *more)


def block_range(bounds, i):
    first = i * BLK
    last = first + BLK - 1
    lo = jnp.int32(0)
    hi = bounds[-1]
    for bound in bounds:
        lo = jnp.where(first >= bound, bound, lo)
    for bound in bounds[::-1]:
        hi = jnp.where(last < bound, bound, hi)
    lo_b = lo // BLK
    hi_b = (hi + BLK - 1) // BLK
    return lo_b, jnp.where(first >= bounds[-1], lo_b, hi_b)


def in_pairs(lo, hi, step, carry):
    pairs = (hi - lo) // 2
    carry = lax.fori_loop(0, pairs, lambda k, c: step([lo + 2 * k, lo + 2 * k + 1], c), carry)
    return lax.fori_loop(lo + 2 * pairs, hi, lambda b, c: step([b], c), carry)


def attend_body(heads, hd, meta, len_ref, qt_ref, ka_ref, vt_ref, o_ref, of_ref, ls_ref):
    i = pl.program_id(0)
    bounds = bounds_of(len_ref, meta[1])
    lo, hi = block_range(bounds, i)

    def step(blocks, carry):
        rows = [pl.ds(pl.multiple_of(b * BLK, BLK), BLK) for b in blocks]
        items = [(h, r) for r in rows for h in range(heads)]
        scores = [mm(ka_ref[h, r, :], qt_ref[h]) for h, r in items]
        expos = [jnp.exp2(one * LOG2E - SHIFT * LOG2E) for one in scores]
        out = list(carry)
        for expo, (h, r) in zip(expos, items):
            acc, total = out[h]
            total = total + jnp.sum(expo.reshape(BLK // 8, 8, BLK), axis=0)
            out[h] = (acc + mm(vt_ref[h, :, r], expo.astype(BF16)), total)
        return tuple(out)

    init = tuple((jnp.zeros((hd, BLK), F32), jnp.zeros((8, BLK), F32)) for _ in range(heads))
    done = in_pairs(lo, hi, step, init)
    for h in range(heads):
        acc, total = done[h]
        total = jnp.sum(total, axis=0, keepdims=True)
        live = total > 0.0
        safe = jnp.where(live, total, 1.0)
        out = jnp.where(live, acc * (1.0 / safe), 0.0)
        o_ref[0, h * hd : (h + 1) * hd, :] = out.astype(BF16)
        of_ref[h] = out
        ls_ref[h] = jnp.log2(safe) + SHIFT * LOG2E


def attend(meta, lengths, qt, ka, vt, heads, hd):
    length = qt.shape[2]
    blocks = length // BLK
    smem = pl.BlockSpec(memory_space=pltpu.SMEM)
    return pl.pallas_call(
        functools.partial(attend_body, heads, hd),
        grid=(blocks,),
        out_shape=(
            jax.ShapeDtypeStruct((blocks, heads * hd, BLK), BF16),
            jax.ShapeDtypeStruct((heads, hd, length), F32),
            jax.ShapeDtypeStruct((heads, 1, length), F32),
        ),
        in_specs=[
            smem,
            smem,
            pl.BlockSpec((heads, 2 * hd, BLK), lambda i: (0, 0, i)),
            pl.BlockSpec((heads, length, 2 * hd), lambda i: (0, 0, 0)),
            pl.BlockSpec((heads, hd, length), lambda i: (0, 0, 0)),
        ],
        out_specs=(
            pl.BlockSpec((1, heads * hd, BLK), lambda i: (i, 0, 0)),
            pl.BlockSpec((heads, hd, BLK), lambda i: (0, 0, i)),
            pl.BlockSpec((heads, 1, BLK), lambda i: (0, 0, i)),
        ),
        compiler_params=params(),
        cost_estimate=cost(25),
        name="attention_forward",
    )(meta, lengths, qt, ka, vt)


def attend_back_body(first, heads, hd, meta, len_ref, *refs):
    qt_ref, ka_ref, kt_ref, v_ref, of_ref, ls_ref, go_ref = refs[:7]
    dq_ref, dk_ref, dv_ref = refs[-3:]
    i = pl.program_id(0)
    bounds = bounds_of(len_ref, meta[1])
    lo, hi = block_range(bounds, i + first)

    @pl.when(i == 0)
    def _():
        if first:
            dk_ref[...] = refs[8][...]
            dv_ref[...] = refs[9][...]
        else:
            dk_ref[...] = jnp.zeros_like(dk_ref)
            dv_ref[...] = jnp.zeros_like(dv_ref)

    inner = []
    for h in range(heads):
        go = go_ref[0, h * hd : (h + 1) * hd, :].astype(F32)
        inner.append(jnp.sum(go * of_ref[h], axis=0, keepdims=True))

    def step(blocks, carry):
        rows = [pl.ds(pl.multiple_of(b * BLK, BLK), BLK) for b in blocks]
        items = [(h, r) for r in rows for h in range(heads)]
        gos = [go_ref[0, h * hd : (h + 1) * hd, :] for h in range(heads)]
        scores = [mm(ka_ref[h, r, :], qt_ref[h]) for h, r in items]
        grad_probs = [mm(v_ref[h, r, :], gos[h]) for h, r in items]
        probs = [jnp.exp2(one * LOG2E - ls_ref[h]) for one, (h, _) in zip(scores, items)]
        grads = [(p * (g - inner[h])).astype(BF16) for p, g, (h, _) in zip(probs, grad_probs, items)]
        out = list(carry)
        for p, g, (h, r) in zip(probs, grads, items):
            dv_ref[h, :, r] += mm(gos[h], p.astype(BF16), NT)
            dk_ref[h, :, r] += mm(qt_ref[h][:hd], g, NT)
            out[h] = out[h] + mm(kt_ref[h, :, r], g)
        return tuple(out)

    done = in_pairs(lo, hi, step, tuple(jnp.zeros((hd, BLK), F32) for _ in range(heads)))
    for h in range(heads):
        dq_ref[h] = done[h] * (hd**-0.5)


def attend_back(meta, lengths, qt, ka, kt, v, of, ls, go, heads, hd, before=None):
    length = qt.shape[2]
    split = (5 * length) // (8 * BLK)
    first = split if before else 0
    count = length // BLK - split if before else split
    smem = pl.BlockSpec(memory_space=pltpu.SMEM)
    whole = lambda *shape: pl.BlockSpec(shape, lambda i: (0, 0, 0))
    part = lambda *shape: pl.BlockSpec(shape, lambda i: (0, 0, first + i))
    more = [pl.BlockSpec(memory_space=pl.ANY), whole(heads, hd, length), whole(heads, hd, length)]
    return pl.pallas_call(
        functools.partial(attend_back_body, first, heads, hd),
        grid=(count,),
        out_shape=tuple(jax.ShapeDtypeStruct((heads, hd, length), F32) for _ in range(3)),
        in_specs=[
            smem,
            smem,
            part(heads, 2 * hd, BLK),
            whole(heads, length, 2 * hd),
            whole(heads, hd, length),
            whole(heads, length, hd),
            part(heads, hd, BLK),
            part(heads, 1, BLK),
            pl.BlockSpec((1, heads * hd, BLK), lambda i: (first + i, 0, 0)),
            *(more if before else []),
        ],
        out_specs=(part(heads, hd, BLK), whole(heads, hd, length), whole(heads, hd, length)),
        input_output_aliases={9: 0} if before else {},
        compiler_params=params(),
        cost_estimate=cost(15),
        name="attention_backward",
    )(meta, lengths, qt, ka, kt, v, of, ls, go, *(before or ()))


def qkv_back_body(
    heads, hd, meta, x_ref, *refs
):
    dq_ref, dk_ref, dv_ref, w_ref, g_ref, b_ref, gq_ref, gk_ref, vec2_ref = refs[:9]
    da_ref, db_ref, dw_ref, acc_ref, vec_ref, gain_ref = refs[9:]
    i = pl.program_id(0)
    wid = heads * hd

    @pl.when(i == 0)
    def _():
        acc_ref[...] = jnp.zeros_like(acc_ref)
        vec_ref[...] = jnp.zeros_like(vec_ref)
        gain_ref[...] = jnp.zeros_like(gain_ref)

    hat, _ = norm_rows(x_ref[...].astype(F32))
    first = (hat * g_ref[...] + b_ref[...]).astype(BF16)
    qk = mm(w_ref[: 2 * wid, :], first, NT)
    pieces = []
    for at, gain, grad in ((0, gq_ref, dq_ref), (1, gk_ref, dk_ref)):
        for h in range(heads):
            unit, inv = norm_cols(qk[at * wid + h * hd : at * wid + (h + 1) * hd])
            gy = grad[h]
            gain_ref[at] += gy * unit
            e = gy * gain[...]
            pieces.append(
                inv
                * (
                    e
                    - jnp.mean(e, axis=0, keepdims=True)
                    - unit * jnp.mean(e * unit, axis=0, keepdims=True)
                )
            )
    for h in range(heads):
        pieces.append(dv_ref[h])
    grad = jnp.concatenate(pieces, axis=0).astype(BF16)
    acc_ref[...] += mm(grad, first)
    back = mm(grad, w_ref[...], TN)
    vec_ref[0] += jnp.sum((back * hat).reshape(BLK // 8, 8, -1), axis=0)
    vec_ref[1] += jnp.sum(back.reshape(BLK // 8, 8, -1), axis=0)
    half = back.shape[1] // 2
    da_ref[0] = back[:, :half].astype(BF16)
    db_ref[0] = back[:, half:].astype(BF16)

    @pl.when(i == pl.num_programs(0) - 1)
    def _():
        dw_ref[: 3 * wid, :] = acc_ref[...].astype(BF16)
        lines = [jnp.sum(ref[k], axis=0, keepdims=True) for ref in (vec_ref, vec2_ref) for k in range(2)]
        width = dw_ref.shape[1]
        lane = lax.broadcasted_iota(jnp.int32, (hd, width), 1)
        item = lax.broadcasted_iota(jnp.int32, (hd, width), 0)
        spread = jnp.where(item < hd // 2, item, item - hd // 2 + width // 2)
        for k in range(2):
            total = lax.dot_general(
                jnp.ones((8, BLK), F32), gain_ref[k], NT, precision=lax.Precision.HIGHEST, preferred_element_type=F32
            )
            pick = (lane == spread).astype(F32)
            line = lax.dot_general(total, pick, NN, precision=lax.Precision.HIGHEST, preferred_element_type=F32)
            lines.append(line[:1])
        place = lax.broadcasted_iota(jnp.int32, (EXTRA, width), 0)
        below = jnp.zeros((EXTRA, width), F32)
        for k, one in enumerate(lines):
            below = jnp.where(place == k, one, below)
        dw_ref[3 * wid :, :] = below.astype(BF16)


def qkv_back(meta, x, dq, dk, dv, w_t, gain, bias, gq, gk, vec2, heads, hd):
    length, width = x.shape
    blocks = length // BLK
    whole = lambda *shape: pl.BlockSpec(shape, lambda i, m: (0,) * len(shape))
    part = pl.BlockSpec((heads, hd, BLK), lambda i, m: (0, 0, i))
    grads = pl.BlockSpec((1, BLK, width // 2), lambda i, m: (jnp.bitwise_xor(i, m[0]), 0, 0))
    return pl.pallas_call(
        functools.partial(qkv_back_body, heads, hd),
        grid_spec=pltpu.PrefetchScalarGridSpec(
            num_scalar_prefetch=1,
            grid=(blocks,),
            in_specs=[
                pl.BlockSpec((BLK, width), lambda i, m: (i, 0)),
                part,
                part,
                part,
                whole(*w_t.shape),
                whole(1, width),
                whole(1, width),
                whole(hd, 1),
                whole(hd, 1),
                whole(2, 8, width),
            ],
            out_specs=(
                grads,
                grads,
                whole(w_t.shape[0] + EXTRA, width),
            ),
            scratch_shapes=[
                pltpu.VMEM(w_t.shape, F32),
                pltpu.VMEM((2, 8, width), F32),
                pltpu.VMEM((2, hd, BLK), F32),
            ],
        ),
        out_shape=(
            jax.ShapeDtypeStruct((blocks, BLK, width // 2), BF16),
            jax.ShapeDtypeStruct((blocks, BLK, width // 2), BF16),
            jax.ShapeDtypeStruct((w_t.shape[0] + EXTRA, width), BF16),
        ),
        compiler_params=params(),
        cost_estimate=cost(17),
        name="qkv_backward",
    )(meta, x, dq, dk, dv, w_t, gain, bias, gq, gk, vec2)


def assemble_qkv(meta, pieces, heads, hd):
    _, part, half = pieces[0].shape
    team = 4
    wid = heads * hd
    turned = team * wid

    def body(meta, p00, p01, p10, p11, out_ref, vec_ref, all_s):
        t = pl.program_id(0)

        @pl.when(t == 0)
        def _():
            for y in range(2):
                at = jnp.bitwise_xor(meta[4], y)
                for z in range(2):
                    own_z = meta[5] == z
                    near, away = jnp.where(own_z, p00[at], p01[at]), jnp.where(own_z, p10[at], p11[at])
                    for x in range(2):
                        all_s[2 * z + y, x * part : (x + 1) * part, :] = jnp.where(meta[3] == x, near, away)
            total = jnp.zeros((EXTRA, half), F32)
            for p in range(team):
                total = total + all_s[p, 3 * wid :, :].astype(F32)
            vec_ref[...] = total

        rows = pl.ds(pl.multiple_of(t * wid, wid), wid)
        piece = jnp.concatenate([all_s[p, rows, :] for p in range(team)], axis=0)
        out_ref[...] = jnp.transpose(piece.astype(F32))

    whole = lambda *shape: pl.BlockSpec(shape, lambda i, m: (0,) * len(shape))
    return pl.pallas_call(
        body,
        grid_spec=pltpu.PrefetchScalarGridSpec(
            num_scalar_prefetch=1,
            grid=(3,),
            in_specs=[whole(2, part, half)] * 4,
            out_specs=(pl.BlockSpec((half, turned), lambda i, m: (0, i)), whole(EXTRA, half)),
            scratch_shapes=[pltpu.VMEM((team, 2 * part, half), BF16)],
        ),
        out_shape=(jax.ShapeDtypeStruct((half, 3 * turned), F32), jax.ShapeDtypeStruct((EXTRA, half), F32)),
        compiler_params=params(),
        cost_estimate=cost(5),
        name="first_projection_gradient",
    )(meta, *pieces)


def gelu_pair(u):
    a = jnp.abs(u)
    t = 1.0 / (1.0 + (0.3275911 * 0.7071067811865476) * a)
    poly = 1.061405429 * t - 1.453152027
    poly = poly * t + 1.421413741
    poly = poly * t - 0.284496736
    poly = poly * t + 0.254829592
    bell = jnp.exp(-0.5 * (u * u))
    tail = (0.5 * poly) * t * bell
    cdf = jnp.where(u >= 0.0, 1.0 - tail, tail)
    return u * cdf, cdf + u * (bell * 0.3989422804014327)


def ffn(meta, attn_t, x, dy, valid, gain, bias, wo, wo_p, up, up_p, dn, dn_p):
    tokens, width = x.shape
    hidden = up.shape[1]
    fc = 512
    steps = hidden // fc
    near = steps // 2
    packs, _, lanes = attn_t.shape
    whole = lambda *shape: pl.BlockSpec(shape, lambda i, m: (0,) * len(shape))
    ups = pl.BlockSpec((width // 2, fc), lambda i, m: (0, lax.rem(m[2] * near + i, steps)))
    acts = pl.BlockSpec((tokens, fc), lambda i, m: (0, lax.rem(m[2] * near + i, steps)))
    half = width // 2

    def body(meta, *refs):
        (at_ref, x_ref, dy_ref, valid_ref, g_ref, b_ref, wo_own, wo_peer, up_own, up_peer, dn_own, dn_peer) = refs[:12]
        (out_ref, gm_ref, gb_ref, h2_ref, act_ref, dup_ref, da_ref, vec_ref) = refs[12:20]
        (mid_s, acc_s, own_s, peer_s, gown_s, gpeer_s) = refs[20:]
        i = pl.program_id(0)
        core = meta[2]
        zero = core == 0

        @pl.when(i == 0)
        def _():
            for p in range(packs):
                rows = pl.ds(p * lanes, lanes)
                own = at_ref[p, pl.ds(pl.multiple_of(core * half, half), half), :]
                peer = at_ref[p, pl.ds(pl.multiple_of((1 - core) * half, half), half), :]
                mid = x_ref[rows, :].astype(F32) + mm(own, wo_own[...], TN) + mm(peer, wo_peer[...], TN)
                mid_s[rows, :] = mid
                acc_s[rows, :] = mid
                hat, _ = norm_rows(mid)
                second = (hat * g_ref[...] + b_ref[...]).astype(BF16)
                h2_ref[:, rows] = jnp.transpose(hat * g_ref[...] + b_ref[...]).astype(BF16)
                lo, hi = second[:, :half], second[:, half:]
                own_s[rows, :] = jnp.where(zero, lo, hi)
                peer_s[rows, :] = jnp.where(zero, hi, lo)
            gown_s[...] = jnp.zeros_like(gown_s)
            gpeer_s[...] = jnp.zeros_like(gpeer_s)

        down = jnp.where(i < near, dn_own[...], dn_peer[...])
        upper = mm(own_s[...], up_own[...]) + mm(peer_s[...], up_peer[...])
        act, slope = gelu_pair(upper)
        act = act.astype(BF16)
        grad = (mm(dy_ref[...], down, NT) * slope).astype(BF16)
        act_ref[...] = act
        dup_ref[...] = grad
        acc_s[...] += mm(act, down)
        gown_s[...] += mm(grad, up_own[...], NT)
        gpeer_s[...] += mm(grad, up_peer[...], NT)

        @pl.when(i == steps - 1)
        def _():
            out_ref[...] = acc_s[...].astype(BF16)
            vec = [jnp.zeros((8, width), F32), jnp.zeros((8, width), F32)]
            for p in range(packs):
                rows = pl.ds(p * lanes, lanes)
                hat, inv = norm_rows(mid_s[rows, :])
                a, b = gown_s[rows, :], gpeer_s[rows, :]
                gy = jnp.concatenate([jnp.where(zero, a, b), jnp.where(zero, b, a)], axis=1)
                vec[0] = vec[0] + jnp.sum((gy * hat).reshape(lanes // 8, 8, width), axis=0)
                vec[1] = vec[1] + jnp.sum(gy.reshape(lanes // 8, 8, width), axis=0)
                e = gy * g_ref[...]
                gm = dy_ref[rows, :].astype(F32) + inv * (
                    e
                    - jnp.mean(e, axis=-1, keepdims=True)
                    - hat * jnp.mean(e * hat, axis=-1, keepdims=True)
                )
                gm_ref[rows, :] = gm
                gb = gm.astype(BF16)
                gb_ref[rows, :] = gb
                ok = valid_ref[p]
                da_ref[p, pl.ds(pl.multiple_of(core * half, half), half), :] = (
                    mm(wo_own[...], gb, NT) * ok
                ).astype(BF16)
                da_ref[p, pl.ds(pl.multiple_of((1 - core) * half, half), half), :] = (
                    mm(wo_peer[...], gb, NT) * ok
                ).astype(BF16)
            vec_ref[0] = vec[0]
            vec_ref[1] = vec[1]

    return pl.pallas_call(
        body,
        grid_spec=pltpu.PrefetchScalarGridSpec(
            num_scalar_prefetch=1,
            grid=(steps,),
            in_specs=[
                whole(*attn_t.shape),
                whole(tokens, width),
                whole(tokens, width),
                whole(*valid.shape),
                whole(1, width),
                whole(1, width),
                whole(half, width),
                whole(half, width),
                ups,
                ups,
                pl.BlockSpec((fc, width), lambda i, m: (jnp.minimum(i, near - 1), 0)),
                pl.BlockSpec((fc, width), lambda i, m: (jnp.maximum(i - near, 0), 0)),
            ],
            out_specs=(
                whole(tokens, width),
                whole(tokens, width),
                whole(tokens, width),
                whole(width, tokens),
                acts,
                acts,
                whole(*attn_t.shape),
                whole(2, 8, width),
            ),
            scratch_shapes=[
                pltpu.VMEM((tokens, width), F32),
                pltpu.VMEM((tokens, width), F32),
                pltpu.VMEM((tokens, half), BF16),
                pltpu.VMEM((tokens, half), BF16),
                pltpu.VMEM((tokens, half), F32),
                pltpu.VMEM((tokens, half), F32),
            ],
        ),
        out_shape=(
            jax.ShapeDtypeStruct((tokens, width), BF16),
            jax.ShapeDtypeStruct((tokens, width), F32),
            jax.ShapeDtypeStruct((tokens, width), BF16),
            jax.ShapeDtypeStruct((width, tokens), BF16),
            jax.ShapeDtypeStruct((tokens, hidden), BF16),
            jax.ShapeDtypeStruct((tokens, hidden), BF16),
            jax.ShapeDtypeStruct(attn_t.shape, BF16),
            jax.ShapeDtypeStruct((2, 8, width), F32),
        ),
        compiler_params=params(),
        cost_estimate=cost(25),
        name="ffn_both_ways",
    )(meta, attn_t, x, dy, valid, gain, bias, wo, wo_p, up, up_p, dn, dn_p)


def up_grads(meta, h2, dup, far=None):
    width, tokens = h2.shape
    hidden = dup.shape[1]
    half = width // 2
    n = hidden // width
    own = far is not None

    def body(meta, h2_ref, dup_ref, *rest):
        j = pl.program_id(0)
        side = meta[2] if own else 1 - meta[2]
        value = mm(h2_ref[pl.ds(pl.multiple_of(side * half, half), half), :], dup_ref[...])
        if own:
            store_halves(j, n, value, *rest)
        else:
            rest[0][...] = value.astype(BF16)

    def column(j, m):
        return jnp.where(j < n // 2, m[4], 1 - m[4]) * (n // 2) + lax.rem(j, n // 2)

    block = lambda index: pl.BlockSpec((half, width), index)
    if own:
        out_specs = (
            block(lambda j, m: (0, jnp.minimum(j, n // 2 - 1))),
            block(lambda j, m: (0, jnp.maximum(j - n // 2, 0))),
        )
        out_shape = (jax.ShapeDtypeStruct((half, hidden // 2), BF16),) * 2
    else:
        out_specs = block(lambda j, m: (0, j))
        out_shape = jax.ShapeDtypeStruct((half, hidden), BF16)
    return pl.pallas_call(
        body,
        grid_spec=pltpu.PrefetchScalarGridSpec(
            num_scalar_prefetch=1,
            grid=(n,),
            in_specs=[
                pl.BlockSpec((width, tokens), lambda j, m: (0, 0)),
                pl.BlockSpec((tokens, width), lambda j, m: (0, column(j, m))),
                *([block(lambda j, m: (0, j))] if own else []),
            ],
            out_specs=out_specs,
        ),
        out_shape=out_shape,
        compiler_params=params(),
        cost_estimate=cost(0.2),
        name="up_gradient",
    )(meta, h2, dup, *([far] if own else []))


def store_halves(j, n, value, far_ref, keep_ref, send_ref):
    value = (value + far_ref[...].astype(F32)).astype(BF16)

    @pl.when(j < n // 2)
    def _():
        keep_ref[...] = value

    @pl.when(j >= n // 2)
    def _():
        send_ref[...] = value


def down_out_grads(meta, act, dy, attn_t, gb, far=None):
    tokens, width = dy.shape
    half = width // 2
    packs, _, lanes = attn_t.shape
    n = act.shape[1] // 2 // half
    quarter = half // n
    rows = half + quarter
    own = far is not None

    def block_at(j, m):
        return jnp.where(j < n // 2, m[3], 1 - m[3]) * (n // 2) + lax.rem(j, n // 2)

    def body(meta, act_ref, dy_ref, at_ref, gb_ref, *rest):
        j = pl.program_id(0)
        side = meta[2] if own else 1 - meta[2]
        at = pl.ds(pl.multiple_of(side * half + block_at(j, meta) * quarter, quarter), quarter)
        total = jnp.zeros((quarter, width), F32)
        for p in range(packs):
            total = total + mm(at_ref[p, at, :], gb_ref[p * lanes : (p + 1) * lanes, :])
        value = jnp.concatenate([mm(act_ref[...], dy_ref[...], TN), total], axis=0)
        if own:
            store_halves(j, n, value, *rest)
        else:
            rest[0][...] = value.astype(BF16)

    def column(j, m):
        return (m[2] if own else 1 - m[2]) * n + block_at(j, m)

    whole = lambda *shape: pl.BlockSpec(shape, lambda j, m: (0,) * len(shape))
    block = lambda index: pl.BlockSpec((rows, width), index)
    if own:
        out_specs = (
            block(lambda j, m: (jnp.minimum(j, n // 2 - 1), 0)),
            block(lambda j, m: (jnp.maximum(j - n // 2, 0), 0)),
        )
        out_shape = (jax.ShapeDtypeStruct((n // 2 * rows, width), BF16),) * 2
    else:
        out_specs = block(lambda j, m: (j, 0))
        out_shape = jax.ShapeDtypeStruct((n * rows, width), BF16)
    return pl.pallas_call(
        body,
        grid_spec=pltpu.PrefetchScalarGridSpec(
            num_scalar_prefetch=1,
            grid=(n,),
            in_specs=[
                pl.BlockSpec((tokens, half), lambda j, m: (0, column(j, m))),
                whole(tokens, width),
                whole(*attn_t.shape),
                whole(tokens, width),
                *([block(lambda j, m: (j, 0))] if own else []),
            ],
            out_specs=out_specs,
        ),
        out_shape=out_shape,
        compiler_params=params(),
        cost_estimate=cost(0.2),
        name="down_out_gradient",
    )(meta, act, dy, attn_t, gb, *([far] if own else []))


def place(ref, value, swapped):
    half = value.shape[1] // 2
    lo, hi = value[:, :half].astype(F32), value[:, half:].astype(F32)
    ref[:, :half] = jnp.where(swapped == 0, lo, hi)
    ref[:, half:] = jnp.where(swapped == 0, hi, lo)


def assemble_down(meta, downs):
    rows, width = downs[0].shape
    half = width // 2
    quarter = rows - half

    def body(meta, down_aa, down_ab, down_ba, down_bb, down_ref, out_ref):
        i = pl.program_id(0)
        down_x, down_y = i // 2 == meta[3], lax.rem(i, 2) == meta[4]
        own_x = jnp.where(down_y, down_aa[...], down_ab[...])
        down = jnp.where(down_x, own_x, jnp.where(down_y, down_ba[...], down_bb[...]))
        place(down_ref, down[:half], meta[5])
        place(out_ref, down[half:], meta[5])

    return pl.pallas_call(
        body,
        grid_spec=pltpu.PrefetchScalarGridSpec(
            num_scalar_prefetch=1,
            grid=(4,),
            in_specs=[pl.BlockSpec((rows, width), lambda i, m: (0, 0))] * 4,
            out_specs=(
                pl.BlockSpec((half, width), lambda i, m: (i, 0)),
                pl.BlockSpec((quarter, width), lambda i, m: (i, 0)),
            ),
        ),
        out_shape=(
            jax.ShapeDtypeStruct((4 * half, width), F32),
            jax.ShapeDtypeStruct((half, width), F32),
        ),
        compiler_params=params(),
        cost_estimate=cost(4),
        name="down_out_in_place",
    )(meta, *downs)


def assemble_up(meta, ups):
    half, width = ups[0].shape[0], ups[0].shape[1] // 2

    def body(meta, up_a, up_b, up_ref):
        place(up_ref, jnp.where(pl.program_id(0) // 2 == meta[4], up_a[...], up_b[...]), meta[3])

    return pl.pallas_call(
        body,
        grid_spec=pltpu.PrefetchScalarGridSpec(
            num_scalar_prefetch=1,
            grid=(4,),
            in_specs=[pl.BlockSpec((half, width), lambda i, m: (0, jnp.bitwise_xor(lax.rem(i, 2), m[5])))] * 2,
            out_specs=pl.BlockSpec((half, width), lambda i, m: (0, i)),
        ),
        out_shape=jax.ShapeDtypeStruct((half, 4 * width), F32),
        compiler_params=params(),
        cost_estimate=cost(4),
        name="up_in_place",
    )(meta, *ups)


def finish_body(x_ref, gm_ref, back_ref, g_ref, out_ref):
    hat, inv = norm_rows(x_ref[...].astype(F32))
    e = back_ref[...].astype(F32) * g_ref[...]
    out_ref[...] = gm_ref[...] + inv * (
        e - jnp.mean(e, axis=-1, keepdims=True) - hat * jnp.mean(e * hat, axis=-1, keepdims=True)
    )


def finish(x, gm, back, gain):
    tokens, width = x.shape
    rows = pl.BlockSpec((128, width), lambda i: (i, 0))
    return pl.pallas_call(
        finish_body,
        grid=(tokens // 128,),
        in_specs=[rows, rows, rows, pl.BlockSpec((1, width), lambda i: (0, 0))],
        out_specs=rows,
        out_shape=jax.ShapeDtypeStruct((tokens, width), F32),
        compiler_params=params(),
        cost_estimate=cost(4),
        name="first_norm_backward",
    )(x, gm, back, gain)


def flip(value, axis, mask):
    size = lax.axis_size(axis)
    return lax.ppermute(value, axis, [(i, i ^ mask) for i in range(size)])


def bit(axis, mask):
    return (lax.axis_index(axis) // mask) % 2


def halves(value, which, axis=0):
    n = value.shape[axis] // 2
    keep = lax.dynamic_slice_in_dim(value, which * n, n, axis)
    send = lax.dynamic_slice_in_dim(value, (1 - which) * n, n, axis)
    return keep, send


def join(own, other, which, axis=0):
    return jnp.where(
        which == 0,
        jnp.concatenate([own, other], axis=axis),
        jnp.concatenate([other, own], axis=axis),
    )


def add(a, b):
    return (a.astype(F32) + b.astype(F32)).astype(BF16)


def on_device(
    tokens, lengths, ln1_gain, ln1_bias, qkv_weight, q_gain, k_gain, out_weight,
    ln2_gain, ln2_bias, up_weight, down_weight, cotangent,
):
    micro, rows, local, width = tokens.shape
    n = lax.axis_size("seq")
    length = local * n
    every = micro * rows
    team = n // every
    heads = H // team
    hd = width // H
    half = width // 2
    idx = lax.axis_index("seq")
    core = lax.axis_index("fsdp")
    row, member = idx // team, idx % team
    direct = every == 2 and team == 4
    lengths = lengths.reshape(every, lengths.shape[-1])
    mine = tokens.reshape(every, local, width)

    def swap(value):
        return flip(value, "fsdp", 1)

    vec = jnp.concatenate([ln1_gain, ln1_bias, ln2_gain, ln2_bias, q_gain, k_gain])[None]
    vec_p = swap(vec)
    ordered = jnp.where(core == 0, jnp.concatenate([vec, vec_p]), jnp.concatenate([vec_p, vec])).astype(F32)
    g1, b1, g2, b2 = (ordered[:, k * half : (k + 1) * half].reshape(1, width) for k in range(4))
    gq = ordered[:, 4 * half : 4 * half + hd // 2].reshape(hd, 1)
    gk = ordered[:, 4 * half + hd // 2 :].reshape(hd, 1)

    w_own = lax.dynamic_slice_in_dim(
        qkv_weight.reshape(half, 3, width), member * heads * hd, heads * hd, 2
    ).reshape(half, 3 * heads * hd)
    w_t = jnp.transpose(join(w_own, swap(w_own), core))

    if direct:
        near = lax.dynamic_index_in_dim(mine, row, 0, keepdims=False)
        away = lax.dynamic_index_in_dim(mine, 1 - row, 0, keepdims=False)
        cut = local // 2
        far = flip(away, "seq", 4)

        def spread(own):
            one, two = flip(own, "seq", 1), flip(own, "seq", 2)
            return [(own,), (one,), (two,), (flip(two[:cut], "seq", 1), flip(one[cut:], "seq", 2))]

        slots = spread(near) + spread(far)
        spot = idx
    else:
        same_member = [[q * team + p for q in range(every)] for p in range(team)]
        same_row = [[q * team + p for p in range(team)] for q in range(every)]
        got = lax.all_to_all(mine, "seq", 0, 0, axis_index_groups=same_member, tiled=True)
        got = lax.all_gather(got, "seq", axis_index_groups=same_row)
        whole = jnp.swapaxes(got, 0, 1).reshape(length, width)
        slots = [(whole[s * (length // 8) : (s + 1) * (length // 8)],) for s in range(8)]
        spot = jnp.int32(0)
    meta = jnp.stack([spot, row, core, bit("rep", 1), bit("seq", 1), bit("seq", 2)]).astype(jnp.int32)

    out_p, up_p, down_p = swap(out_weight), swap(up_weight), swap(down_weight)

    with jax.named_scope("forward_attention"):
        near = make_qkv(meta, lengths, slots[:4], w_t, g1, b1, gq, gk, heads, hd)
        qt, ka, kt, v, vt, x_row = make_qkv(meta, lengths, slots[4:], w_t, g1, b1, gq, gk, heads, hd, near)
        attn, attn_f, logsum = attend(meta, lengths, qt, ka, vt, heads, hd)

    def exchange(value):
        return lax.all_to_all(value, "seq", 0, 0, tiled=True)

    packs = every * local // BLK
    if direct:
        attn_t = exchange(attn).reshape(packs, width, BLK)
    else:
        cut = jnp.moveaxis(attn.reshape(BLK * 0 + 8, heads * hd, BLK // local, local), 2, 1)
        got = exchange(cut.reshape(n, heads * hd, local))
        got = got.reshape(packs, every // packs, width, local)
        attn_t = jnp.swapaxes(got, 1, 2).reshape(packs, width, BLK)

    total = jnp.sum(lengths[:, :-1], axis=-1)
    places = idx * local + jnp.arange(local, dtype=jnp.int32)
    valid = (places[None] < total[:, None]).astype(F32).reshape(packs, 1, BLK)
    x_home = tokens.reshape(every * local, width)
    dy = cotangent.reshape(every * local, width)

    with jax.named_scope("feed_forward"):
        output, grad_mid, grad_branch, h2, act, dup, grad_attn, vec2 = ffn(
            meta, attn_t, x_home, dy, valid, g2, b2, out_weight, out_p, up_weight, up_p, down_weight, down_p
        )
    if direct:
        grad_o = exchange(grad_attn.reshape(n, heads * hd, BLK))
    else:
        cut = jnp.swapaxes(grad_attn.reshape(packs, width, every // packs, local), 1, 2)
        got = exchange(cut.reshape(n, heads * hd, local))
        got = got.reshape(8, BLK // local, heads * hd, local)
        grad_o = jnp.swapaxes(got, 1, 2).reshape(8, heads * hd, BLK)

    masks = [1 << k for k in range(n.bit_length() - 1)]
    x, y, z = ("rep", 1), ("seq", 1), ("seq", 2)

    def next_half(keep, got, way, axis):
        return halves(add(keep, got), bit(*way), axis)

    tie = lambda *values: lax.optimization_barrier(values)
    with jax.named_scope("weight_gradients"):
        far_d = swap(down_out_grads(meta, act, dy, attn_t, grad_branch))
        far_u = swap(up_grads(meta, h2, dup))
        down_k, down_s = down_out_grads(meta, act, dy, attn_t, grad_branch, far_d)
        up_k, up_s = up_grads(meta, h2, dup, far_u)
        got = flip(down_s, *x), flip(up_s, *y)
    grad_o = tie(grad_o, up_k, up_s, down_k, down_s)[0]
    go_back = lambda go, before: attend_back(
        meta, lengths, qt, ka, kt, v, attn_f, logsum, go, heads, hd, before
    )
    with jax.named_scope("backward_attention"):
        parts = go_back(grad_o, None)
    parts, *got = tie(parts, *got)
    with jax.named_scope("weight_gradients"):
        down_k, down_s = next_half(down_k, got[0], y, 0)
        up_k, up_s = next_half(up_k, got[1], z, 1)
        got = flip(down_s, *y), flip(up_s, *z)
    with jax.named_scope("backward_attention"):
        parts = go_back(grad_o, parts)
    parts, *got = tie(parts, *got)
    with jax.named_scope("weight_gradients"):
        down_k, down_s = next_half(down_k, got[0], z, 1)
        up_k, up_s = next_half(up_k, got[1], x, 1)
        got = flip(down_s, *z), flip(up_s, *x)
    parts, *got = tie(parts, *got)
    with jax.named_scope("weight_gradients"):
        down, up = add(down_k, got[0]), add(up_k, got[1])
        pieces = jnp.concatenate([down, up])
        for mask in masks[2:]:
            pieces = add(pieces, flip(pieces, "seq", mask))
    with jax.named_scope("backward_attention"):
        dq, dk, dv = parts
        back_a, back_b, dw_t = qkv_back(meta, x_row, dq, dk, dv, w_t, g1, b1, gq, gk, vec2, heads, hd)
    dw_t, pieces = tie(dw_t, pieces)
    down, up = jnp.split(pieces, [down.shape[0]])

    with jax.named_scope("first_round"):
        keep, send = halves(dw_t, core, 1)
        q_keep, q_send = next_half(keep, swap(send), x, 0)
        got = [flip(down, *z), flip(up, *x), flip(q_send, *x)]
        if direct:
            a = back_a.reshape(2, 2, 2, local, half)
            b = back_b.reshape(2, 2, 2, local, half)
            got += [flip(a[:, :, 1], *y), flip(b[:, 1], *z)]
        got = tie(*got)
        down = jnp.concatenate([down, got[0]], axis=1)
        up = jnp.concatenate([up, got[1]], axis=1)
        piece = add(q_keep, got[2])
        if direct:
            a, b = add(a[:, :, 0], got[3]), add(b[:, 0], got[4])
    with jax.named_scope("second_round"):
        rows_at = [mask for mask in masks if mask >= team]
        got = [flip(down, *y), flip(down, *x), flip(up, *z)]
        got += [flip(piece, "seq", mask) for mask in rows_at[:1]]
        if direct:
            got += [flip(a[:, 1], *z), flip(b[:, 1], *y)]
        got = tie(*got)
        downs = [down, got[0], got[1]]
        up = jnp.concatenate([up, got[2]], axis=1)
        if rows_at:
            piece = add(piece, got[3])
        for mask in rows_at[1:]:
            piece = add(piece, flip(piece, "seq", mask))
        if direct:
            a, b = add(a[:, 0], got[-2]), add(b[:, 0], got[-1])
    with jax.named_scope("third_round"):
        piece_y, up = tie(flip(piece, *y), up)
        piece = jnp.stack([piece, piece_y])
        if direct:
            mixed = jnp.concatenate([a, b], axis=-1)
            near, far = mixed[0], flip(mixed[1], "seq", 4)
            back = jnp.where(row == 0, jnp.stack([near, far]), jnp.stack([far, near])).reshape(every * local, width)
        else:
            whole = jnp.concatenate([back_a, back_b], axis=-1).reshape(every, team, local, width)
            whole = lax.psum_scatter(whole, "seq", scatter_dimension=1, axis_index_groups=same_row, tiled=True)
            back = lax.all_to_all(
                whole[:, 0], "seq", 0, 0, axis_index_groups=same_member, tiled=True
            ).reshape(every * local, width)
        downs.append(flip(downs[1], *x))
        piece_z, downs[3] = tie(flip(piece, *z), downs[3])
        grad_down, grad_out = assemble_down(meta, downs)
        piece_x = flip(piece, *x)
        piece_z, piece_x, grad_down, grad_out = tie(piece_z, piece_x, grad_down, grad_out)
        pieces = [piece, piece_z, piece_x, flip(piece_z, *x)]
        ups = (up, flip(up, *y))
    grad_tokens = finish(x_home, grad_mid, back, g1)
    grad_up, grad_tokens = tie(assemble_up(meta, ups), grad_tokens)
    pieces[3], grad_up = tie(pieces[3], grad_up)
    grad_qkv, small = assemble_qkv(meta, pieces, heads, hd)
    cuts = [small[k] for k in range(4)] + [small[4, : hd // 2], small[5, : hd // 2]]
    shape = tokens.shape
    return (
        output.reshape(shape), grad_tokens.reshape(shape), cuts[0], cuts[1], grad_qkv, cuts[4], cuts[5],
        grad_out, cuts[2], cuts[3], grad_up, grad_down,
    )


def solution(mesh):
    tok = P(None, ("rep", "fsdp"), "seq", None)
    one, two = P("fsdp"), P("fsdp", None)
    in_specs = (tok, P(None, ("rep", "fsdp"), None), one, one, two, one, one, two, one, one, two, two, tok)
    out_specs = (tok, tok, one, one, two, one, one, two, one, one, two, two)
    return jax.shard_map(on_device, mesh=mesh, in_specs=in_specs, out_specs=out_specs, check_vma=False)
```
